32 devices in a mesh: dp: 4 (over y, core), row: 2 (over x), col: 4 (over z).
Axes of the slice: x: 2, y: 2, z: 4, core: 2. Of those that a mesh axis runs over, the one named last changes fastest.
Arguments:
- layer_input: bfloat16 [12288, 1536], P(('dp', 'col'), 'row'), may hold values from -6 to 6
- attn_gain: float32 [1536], P('row'), may hold values from 0.25 to 1.75
- qkv_weight: bfloat16 [1536, 4608], P('row', 'col'), may hold values from -0.15625 to 0.15625
- forget_weight: bfloat16 [1536, 24], P('row', 'col'), may hold values from -0.15625 to 0.15625
- forget_bias: float32 [24], P('col'), may hold values from 2.5 to 7
- out_weight: bfloat16 [1536, 1536], P('col', 'row'), may hold values from -0.625 to 0.625
- ffn_gain: float32 [1536], P('row'), may hold values from 0.25 to 1.75
- gate_weight: bfloat16 [1536, 4096], P('row', 'col'), may hold values from -0.15625 to 0.15625
- up_weight: bfloat16 [1536, 4096], P('row', 'col'), may hold values from -0.15625 to 0.15625
- down_weight: bfloat16 [4096, 1536], P('col', 'row'), may hold values from -0.09375 to 0.09375
- prompt_doc: int32 [8, 1024], P(('dp', 'row')), may hold values from 0 to 3, never falling along the last dimension, each value on 1 to 512 neighbouring positions
- branch_seg: int32 [8, 512], P(('dp', 'row')), may hold values from 0 to 3, never falling along the last dimension, each value on 1 to 256 neighbouring positions
- branch_doc: int32 [8, 4], P(('dp', 'row')), may hold values from 0 to 3
- out_cotangent: bfloat16 [12288, 1536], P(('dp', 'col'), 'row'), may hold values from -6 to 6
Outputs:
- layer_output: bfloat16 [12288, 1536], P(('dp', 'col'), 'row')
- input_grad: bfloat16 [12288, 1536], P(('dp', 'col'), 'row')
- attn_gain_grad: float32 [1536], P('row')
- qkv_grad: float32 [1536, 4608], P('row', 'col')
- forget_grad: float32 [1536, 24], P('row', 'col')
- forget_bias_grad: float32 [24], P('col')
- out_grad: float32 [1536, 1536], P('col', 'row')
- ffn_gain_grad: float32 [1536], P('row')
- gate_grad: float32 [1536, 4096], P('row', 'col')
- up_grad: float32 [1536, 4096], P('row', 'col')
- down_grad: float32 [4096, 1536], P('col', 'row')
The draws below stay inside these ranges and needn't reach their ends.
Inputs may be any that keep to these rules, and one draw needn't show every extreme that they name: `prompt_doc`: in each group the prompt's documents are numbered 0 to 3 in order, every one present, each of 1 to 512 tokens, one of exactly 512. `branch_seg`: in each group the continuations are numbered 0 to 3 in order, every one present, each of 1 to 256 tokens, one of exactly 256.
All inputs are finite; a program needn't handle non-finite values.
Results may differ from the reference program's by a relative error of at most 0.023.
Values may be sent and summed in bfloat16 or wider, within the bound.
A program may use at most 192 MiB of HBM per device.

```python
import math
import jax
import jax.numpy as jnp
import numpy as np
from jax import lax

D = 1536
H = 24
DH = 64
FF = 4096
PROMPT = 1024
CONT_LEN = 128
CONTS = 4
DOCS = 4
GROUP_LEN = 1536
GROUPS = 8
TOKENS = 12288


def touch_ends(values, own_key, low, top_value):
    dims = values.shape
    place = [jax.random.randint(jax.random.fold_in(own_key, axis), (), 0, dims[axis]) for axis in range(len(dims))]
    values = values.at[tuple(place)].set(low)
    longest = dims.index(max(dims))
    place[longest] = (place[longest] + 1) % dims[longest]
    return values.at[tuple(place)].set(top_value)


def levels(rng, extent, split, smallest, top_value):
    def one(position, shards_of):
        heights = jax.random.uniform(jax.random.fold_in(jax.random.fold_in(rng, 6), position), (shards_of,), jnp.float32, smallest / len(split), top_value / len(split))
        return jnp.repeat(jnp.exp(heights), extent[position] // shards_of).reshape((-1,) + (1,) * (len(extent) - position - 1))

    gain = one(*split[0])
    for cut in split[1:]:
        gain = gain * one(*cut)
    return gain


def length_profile(number_of, total, most, slope):
    loads = [(1 << 20) // math.isqrt(standing ** slope) + 1 for standing in range(2, number_of + 1)]
    spare, counts = total - most - (number_of - 1), [1] * (number_of - 1)
    while spare > 0:
        movable = [i for i in range(number_of - 1) if counts[i] < most]
        mass, left = sum([loads[i] for i in movable]), spare
        for i in movable:
            more = min(most - counts[i], max(1, left * loads[i] // mass), spare)
            counts[i] = counts[i] + more
            spare = spare - more
    return np.array([most] + counts)


def uneven_parts(own_key, count, total, limit, slope):
    if count == 2:
        one = jax.random.randint(own_key, (), max(1, total - limit), min(limit, total - 1) + 1)
        return jnp.stack([one, total - one])
    sizes = jnp.asarray(length_profile(count, total, limit, slope), jnp.int32)
    couples = (count - 1) // 2
    source_of, receiver = sizes[1:1 + 2 * couples:2], sizes[2:2 + 2 * couples:2]
    slack = jnp.minimum(source_of - 1, limit - receiver)
    passed = jax.random.randint(jax.random.fold_in(own_key, 1), (couples,), 0, 1 << 20) % (slack + 1)
    sizes = sizes.at[1:1 + 2 * couples:2].set(source_of - passed).at[2:2 + 2 * couples:2].set(receiver + passed)
    return sizes[jax.random.permutation(jax.random.fold_in(own_key, 2), count)]


def normal_values(key, shape, deviation, limit, shards=(), held_as=jnp.bfloat16):
    entries = deviation * jax.random.normal(key, shape, jnp.float32)
    if shards:
        entries = entries * levels(key, shape, shards, -0.22, 0.18)
    return jnp.clip(entries, -limit, limit).astype(held_as)


def setup_inputs(seed: int = 0) -> dict:
    streams_of = jax.random.split(jax.random.key(seed), 15)
    layer_input = normal_values(streams_of[0], (TOKENS, D), 1.0, 6.0, ((0, 16), (1, 2)))
    attn_gain = jnp.clip(1.0 + 0.15 * jax.random.normal(streams_of[1], (D,), jnp.float32), 0.25, 1.75)
    qkv_weight = normal_values(streams_of[2], (D, 3 * D), D ** -0.5, 0.15625, ((0, 2), (1, 4)))
    forget_weight = normal_values(streams_of[3], (D, H), D ** -0.5, 0.15625, ((0, 2), (1, 4)))
    forget_bias = jnp.clip(2.5 + 4.5 * jax.random.uniform(streams_of[4], (H,), jnp.float32) ** levels(streams_of[4], (H,), ((0, 4),), -0.2, 0.2), 2.5, 7.0)
    out_weight = normal_values(streams_of[5], (D, D), (D // 16) ** -0.5, 0.625, ((0, 4), (1, 2)))
    ffn_gain = jnp.clip(1.0 + 0.15 * jax.random.normal(streams_of[6], (D,), jnp.float32), 0.25, 1.75)
    gate_weight = normal_values(streams_of[7], (D, FF), D ** -0.5, 0.15625, ((0, 2), (1, 4)))
    up_weight = normal_values(streams_of[8], (D, FF), D ** -0.5, 0.15625, ((0, 2), (1, 4)))
    down_weight = normal_values(streams_of[9], (FF, D), FF ** -0.5, 0.09375, ((0, 4), (1, 2)))
    prompt_doc = jax.vmap(lambda own: jnp.searchsorted(jnp.cumsum(uneven_parts(own, DOCS, PROMPT, PROMPT // 2, 2)), jnp.arange(PROMPT), side="right"))(jax.random.split(streams_of[10], GROUPS)).reshape((GROUPS, PROMPT)).astype(jnp.int32)
    branch_seg = jax.vmap(lambda own: jnp.searchsorted(jnp.cumsum(uneven_parts(own, CONTS, CONTS * CONT_LEN, 2 * CONT_LEN, 2)), jnp.arange(CONTS * CONT_LEN), side="right"))(jax.random.split(streams_of[11], GROUPS)).reshape((GROUPS, CONTS * CONT_LEN)).astype(jnp.int32)
    branch_doc = touch_ends(jax.random.randint(streams_of[12], (GROUPS, CONTS), 0, DOCS), jax.random.fold_in(streams_of[12], 1), 0, DOCS - 1).astype(jnp.int32)
    out_cotangent = normal_values(streams_of[13], (TOKENS, D), 1.0, 6.0, ((0, 16), (1, 2)))
    return {"layer_input": layer_input, "attn_gain": attn_gain, "qkv_weight": qkv_weight, "forget_weight": forget_weight, "forget_bias": forget_bias, "out_weight": out_weight, "ffn_gain": ffn_gain, "gate_weight": gate_weight, "up_weight": up_weight, "down_weight": down_weight, "prompt_doc": prompt_doc, "branch_seg": branch_seg, "branch_doc": branch_doc, "out_cotangent": out_cotangent}


EPS = 1e-06
MASKED = -1e+30
HIGH = lax.Precision.HIGHEST

@jax.custom_vjp
def low(v):
    return lax.optimization_barrier(v.astype(jnp.bfloat16)).astype(jnp.float32)

@jax.custom_vjp
def low_back(v):
    return v

def low_keep(v):
    return (low(v), None)

def low_pass(kept, grad):
    return (grad,)

def back_keep(v):
    return (v, None)

def back_low(kept, grad):
    return (low(grad),)
low.defvjp(low_keep, low_pass)
low_back.defvjp(back_keep, back_low)

def visible(row_start, doc_query, branch_query, doc_key, branch_key):
    pos_query = row_start + jnp.arange(doc_query.shape[0], dtype=jnp.int32)
    pos_key = jnp.arange(doc_key.shape[0], dtype=jnp.int32)
    causal = pos_key[None, :] <= pos_query[:, None]
    same_doc = doc_query[:, None] == doc_key[None, :]
    same_branch = (branch_key[None, :] < 0) | (branch_query[:, None] == branch_key[None, :])
    return causal & same_doc & same_branch

def decay_sums(log_rates, prompt_ids, branch_ids, branch_docs):
    prompt_len = prompt_ids.shape[0]
    prompt_part = log_rates[:prompt_len]
    branch_part = log_rates[prompt_len:]
    prompt_sums = jnp.cumsum(prompt_part, axis=0)
    doc_range = jnp.arange(DOCS, dtype=jnp.int32)
    doc_last = lax.optimization_barrier(jnp.sum((prompt_ids[None, :] <= doc_range[:, None]).astype(jnp.int32), axis=1)) - 1
    at_last = jnp.arange(prompt_len, dtype=jnp.int32)[None, :] == doc_last[:, None]
    doc_totals = lax.optimization_barrier(jnp.sum(jnp.where(at_last[:, :, None], prompt_sums[None], 0.0), axis=1))
    branch_range = jnp.arange(branch_docs.shape[0], dtype=jnp.int32)
    picked = branch_docs[:, None] == doc_range[None, :]
    branch_start = lax.optimization_barrier(jnp.sum(jnp.where(picked[:, :, None], doc_totals[None], 0.0), axis=1))
    earlier = branch_ids[None, :] < branch_range[:, None]
    skipped = lax.optimization_barrier(jnp.sum(jnp.where(earlier[:, :, None], branch_part[None], 0.0), axis=1))
    member = branch_ids[:, None] == branch_range[None, :]
    offsets = lax.optimization_barrier(jnp.sum(jnp.where(member[:, :, None], (branch_start - skipped)[None], 0.0), axis=1))
    decay_sum = jnp.concatenate([prompt_sums, jnp.cumsum(branch_part, axis=0) + offsets], axis=0)
    branch_doc_ids = lax.optimization_barrier(jnp.sum(jnp.where(member, branch_docs[None, :], 0), axis=1)).astype(jnp.int32)
    doc_ids = jnp.concatenate([prompt_ids.astype(jnp.int32), branch_doc_ids])
    branch_tags = jnp.concatenate([jnp.full((prompt_len,), -1, jnp.int32), branch_ids.astype(jnp.int32)])
    return (decay_sum, doc_ids, branch_tags)

def head_attention(head_items, allowed):
    head_query, head_keys, head_values, head_decay = head_items
    scores = jnp.dot(head_query, head_keys.T, precision=HIGH) * DH ** (-0.5) + head_decay[:, None] - head_decay[None, :]
    scores = jnp.where(allowed, low_back(scores), MASKED)
    probs = low(jax.nn.softmax(scores, axis=-1))
    return jnp.dot(probs, head_values, precision=HIGH)

def group_attention(group_items):
    group_qkv, group_rates, prompt_ids, branch_ids, branch_docs = group_items
    decay_sum, doc_ids, branch_tags = decay_sums(group_rates, prompt_ids, branch_ids, branch_docs)
    allowed = visible(0, doc_ids, branch_tags, doc_ids, branch_tags)
    heads_first = jnp.transpose(group_qkv, (1, 2, 0, 3))
    head_fn = jax.checkpoint(lambda head_items: head_attention(head_items, allowed))
    head_outs = lax.map(head_fn, (heads_first[:, 0], heads_first[:, 1], heads_first[:, 2], decay_sum.T))
    return jnp.transpose(head_outs, (1, 0, 2))

def reference(layer_input, attn_gain, qkv_weight, forget_weight, forget_bias, out_weight, ffn_gain, gate_weight, up_weight, down_weight, prompt_doc, branch_seg, branch_doc, out_cotangent):

    def forward(stream, gain_a, weight_qkv, weight_forget, bias_forget, weight_out, gain_b, weight_gate, weight_up, weight_down):
        row_count = stream.shape[0]
        rms_a = lax.rsqrt(lax.optimization_barrier(jnp.mean(stream * stream, axis=1, keepdims=True)) + EPS)
        normed_a = low(stream * rms_a * gain_a)
        projected = low(low_back(jnp.dot(normed_a, weight_qkv, precision=HIGH)))
        forget_logit = low_back(jnp.dot(normed_a, weight_forget, precision=HIGH) + bias_forget)
        log_rate = jax.nn.log_sigmoid(forget_logit)
        attended = lax.map(jax.checkpoint(group_attention), (projected.reshape(GROUPS, GROUP_LEN, H, 3, DH), log_rate.reshape(GROUPS, GROUP_LEN, H), prompt_doc, branch_seg, branch_doc))
        attended = low(low_back(attended.reshape(row_count, D)))
        resid = stream + low_back(jnp.dot(attended, weight_out, precision=HIGH))
        rms_b = lax.rsqrt(lax.optimization_barrier(jnp.mean(resid * resid, axis=1, keepdims=True)) + EPS)
        normed_b = low(resid * rms_b * gain_b)
        gate_pre = low_back(jnp.dot(normed_b, weight_gate, precision=HIGH))
        up_pre = low_back(jnp.dot(normed_b, weight_up, precision=HIGH))
        hidden = low(jax.nn.silu(gate_pre) * up_pre)
        return resid + low_back(jnp.dot(hidden, weight_down, precision=HIGH))
    params = (layer_input.astype(jnp.float32), attn_gain, qkv_weight.astype(jnp.float32), forget_weight.astype(jnp.float32), forget_bias, out_weight.astype(jnp.float32), ffn_gain, gate_weight.astype(jnp.float32), up_weight.astype(jnp.float32), down_weight.astype(jnp.float32))
    result, pullback = jax.vjp(forward, *params)
    grads = pullback(out_cotangent.astype(jnp.float32))
    return (result.astype(jnp.bfloat16), grads[0].astype(jnp.bfloat16), grads[1], grads[2], grads[3], grads[4], grads[5], grads[6], grads[7], grads[8], grads[9])
```

```python
import jax
import jax.numpy as jnp
from jax import lax
from jax.sharding import Mesh, PartitionSpec as P

D = 1536
DH = 64
DOCS = 4
QBLK = 512
EPS = 1e-06
MASKED = -1e30
LANES = 128
BF16 = jnp.bfloat16
F32 = jnp.float32


def swap(value, axis):
    return lax.ppermute(value, axis, [(0, 1), (1, 0)])


def xor_swap(value, axis, size, bit):
    return lax.ppermute(value, axis, [(i, i ^ bit) for i in range(size)])


def kxh(k, x, h):
    return (k * 2 + x) * 2 + h


def fetch_home_away(value):
    pairs = []
    for k in range(2):
        for x in range(2):
            for h in range(2):
                target = (k, 1 - x, h) if k == h else (1 - k, x, 1 - h)
                pairs.append((kxh(k, x, h), kxh(*target)))
    return lax.ppermute(value, ("k", "x", "h"), pairs)


def fetch_away(value):
    pairs = [
        (kxh(k, x, 1 - k), kxh(k, 1 - x, 1 - k)) for k in range(2) for x in range(2)
    ]
    return lax.ppermute(value, ("k", "x", "h"), pairs)


def gather_weight(shard, home, axis):
    first = fetch_home_away(shard)
    second = fetch_away(first)
    mine = jnp.where(home, shard, first)
    other = jnp.where(home, first, second)
    return jnp.concatenate([mine, other], axis=axis)


def reduce_weight(own, other, home, home_steps):
    total = own + swap(other.astype(BF16), "x").astype(F32)
    moved = lax.ppermute(
        total.astype(BF16), ("k", "h"), [(0 * 2 + 1, 0 * 2 + 0), (1 * 2 + 0, 1 * 2 + 1)]
    )
    total = (total + moved.astype(F32)).astype(BF16)
    for size, bit in home_steps:
        pairs = []
        for o in range(size):
            for k in range(2):
                pairs.append(((o * 2 + k) * 2 + k, ((o ^ bit) * 2 + k) * 2 + k))
        moved = lax.ppermute(total, ("o", "k", "h"), pairs)
        total = (total.astype(F32) + moved.astype(F32)).astype(BF16)
    moved = lax.ppermute(total, ("k", "h"), [(0, 2), (3, 1)])
    return jnp.where(home, total, moved).astype(F32)


def take_half(value, index):
    half = value.shape[0] // 2
    return lax.dynamic_slice_in_dim(value, index * half, half, 0)


def kx(k, x):
    return k * 2 + x


SPREAD_A = []
SPREAD_B = []
for _k in range(2):
    for _x in range(2):
        if _k == _x:
            SPREAD_A.append((kx(_k, _x), kx(1 - _k, _x)))
        else:
            SPREAD_A.append((kx(_k, _x), kx(_k, 1 - _x)))
            SPREAD_B.append((kx(_k, _x), kx(1 - _k, 1 - _x)))


def spread_tokens(block, core, same):
    near = take_half(block, core)
    far = take_half(block, 1 - core)
    first = lax.ppermute(jnp.where(same, far, near), ("k", "x"), SPREAD_A)
    second = lax.ppermute(far, ("k", "x"), SPREAD_B)
    own = jnp.where(same, near, first)
    other = jnp.where(same, first, second)
    return jnp.concatenate([own, other], axis=1)


def unspread_tokens(rows, core, same):
    half = rows.shape[1] // 2
    own, other = rows[:, :half], rows[:, half:]
    first = lax.ppermute(
        jnp.where(same, other, own), ("k", "x"), [(b, a) for a, b in SPREAD_A]
    )
    second = lax.ppermute(other, ("k", "x"), [(b, a) for a, b in SPREAD_B])
    near = jnp.where(same, own, first)
    far = jnp.where(same, first, second)
    low = jnp.where(core == 0, near, far)
    high = jnp.where(core == 0, far, near)
    return jnp.concatenate([low, high], axis=0)


def gather_blocks(block, psize):
    blocks = []
    for bit in range(psize):
        moved = block if bit == 0 else xor_swap(block, "p", psize, bit)
        blocks += [moved, swap(moved, "k")]
    return jnp.concatenate(blocks, axis=0)


def sum_blocks(partial, psize):
    size = partial.shape[0] // (2 * psize)
    parts = [partial[i * size : (i + 1) * size] for i in range(2 * psize)]
    total = None
    for bit in reversed(range(psize)):
        pair = parts[2 * bit] + swap(parts[2 * bit + 1].astype(BF16), "k").astype(F32)
        if bit:
            pair = xor_swap(pair.astype(BF16), "p", psize, bit).astype(F32)
        total = pair if total is None else total + pair
    return total


def reorder(rows, me, count):
    parts = rows.reshape((count, rows.shape[0] // count) + rows.shape[1:])
    taken = [lax.dynamic_index_in_dim(parts, j ^ me, 0, keepdims=False) for j in range(count)]
    return jnp.concatenate(taken, axis=0)


def contract_rows(left, right):
    return lax.dot_general(
        left, right, (((0,), (0,)), ((), ())), preferred_element_type=F32
    )


def contract_cols(left, right):
    return lax.dot_general(
        left, right, (((1,), (1,)), ((), ())), preferred_element_type=F32
    )


def matmul(left, right):
    return jnp.dot(left, right, preferred_element_type=F32)


def split3(value):
    high = lax.reduce_precision(value, 8, 7)
    rest = value - high
    mid = lax.reduce_precision(rest, 8, 7)
    return jnp.concatenate([high, mid, rest - mid], axis=1).astype(BF16)


def sum3(value):
    n = value.shape[1] // 3
    return value[:, :n] + value[:, n : 2 * n] + value[:, 2 * n :]


def visible(row_start, doc_query, branch_query, doc_key, branch_key):
    pos_query = row_start + jnp.arange(doc_query.shape[0], dtype=jnp.int32)
    pos_key = jnp.arange(doc_key.shape[0], dtype=jnp.int32)
    causal = pos_key[None, :] <= pos_query[:, None]
    same_doc = doc_query[:, None] == doc_key[None, :]
    same_branch = (branch_key[None, :] < 0) | (branch_query[:, None] == branch_key[None, :])
    return causal & same_doc & same_branch


def block_scores(query_block, key_rows, decay_query, decay_key, allowed):
    raw_scores = jnp.einsum(
        "qhd,khd->hqk", query_block, key_rows, preferred_element_type=jnp.float32
    )
    scores = raw_scores * DH ** (-0.5) + decay_query.T[:, :, None] - decay_key.T[:, None, :]
    return jnp.where(allowed[None], scores, MASKED)


def attention(qkv, decay_sum, doc_ids, branch_tags):
    group_len, heads = qkv.shape[0], qkv.shape[1]
    queries, key_rows, value_rows = qkv[:, :, 0], qkv[:, :, 1], qkv[:, :, 2]
    blocks = jnp.arange(group_len // QBLK, dtype=jnp.int32)

    def block_view(block_index):
        row_start = block_index * QBLK
        query_block = lax.dynamic_slice_in_dim(queries, row_start, QBLK, 0)
        decay_query = lax.dynamic_slice_in_dim(decay_sum, row_start, QBLK, 0)
        doc_query = lax.dynamic_slice_in_dim(doc_ids, row_start, QBLK, 0)
        branch_query = lax.dynamic_slice_in_dim(branch_tags, row_start, QBLK, 0)
        allowed = visible(row_start, doc_query, branch_query, doc_ids, branch_tags)
        scores = block_scores(query_block, key_rows, decay_query, decay_sum, allowed)
        return (row_start, query_block, scores)

    def forward_block(block_index):
        row_start, query_block, scores = block_view(block_index)
        row_max = jnp.max(scores, axis=2, keepdims=True)
        expo = jnp.exp(scores - row_max)
        row_total = jnp.sum(expo, axis=2, keepdims=True)
        probs = (expo / row_total).astype(BF16)
        attended_block = jnp.einsum(
            "hqk,khd->qhd", probs, value_rows, preferred_element_type=jnp.float32
        ).astype(BF16)
        return (attended_block, (row_max + jnp.log(row_total))[:, :, 0])

    attended_blocks, lse_blocks = lax.map(forward_block, blocks)
    attended = attended_blocks.reshape(group_len, heads * DH)

    def backward(grad_attended):
        def back_block(carry, block_index):
            key_acc, value_acc, decay_keys = carry
            row_start, query_block, scores = block_view(block_index)
            grad_block = lax.dynamic_slice_in_dim(grad_attended, row_start, QBLK, 0)
            lse_block = lax.dynamic_index_in_dim(lse_blocks, block_index, 0, keepdims=False)
            probs_star = jnp.exp(scores - lse_block[:, :, None])
            grad_probs = jnp.einsum(
                "qhd,khd->hqk", grad_block, value_rows, preferred_element_type=jnp.float32
            )
            row_delta = jnp.sum(probs_star * grad_probs, axis=2, keepdims=True)
            grad_scores = (probs_star * (grad_probs - row_delta)).astype(BF16)
            grad_query = jnp.einsum(
                "hqk,khd->qhd", grad_scores, key_rows, preferred_element_type=jnp.float32
            ) * DH ** (-0.5)
            key_acc = key_acc + jnp.einsum(
                "hqk,qhd->khd", grad_scores, query_block, preferred_element_type=jnp.float32
            )
            value_acc = value_acc + jnp.einsum(
                "hqk,qhd->khd", probs_star.astype(BF16), grad_block, preferred_element_type=F32
            )
            decay_rows = jnp.sum(grad_scores, axis=2, dtype=F32)
            decay_keys = decay_keys - jnp.sum(grad_scores, axis=1, dtype=F32)
            return ((key_acc, value_acc, decay_keys), (grad_query, decay_rows))

        zero_rows = jnp.zeros((group_len, heads, DH), F32)
        carried, stacked = lax.scan(
            back_block, (zero_rows, zero_rows, jnp.zeros((heads, group_len), F32)), blocks
        )
        key_acc, value_acc, decay_keys = carried
        query_blocks, decay_blocks = stacked
        grad_query = query_blocks.reshape(group_len, heads, DH)
        grad_decay = jnp.transpose(decay_blocks, (0, 2, 1)).reshape(group_len, heads) + decay_keys.T
        grad_qkv = (
            jnp.stack([grad_query, key_acc * DH ** (-0.5), value_acc], axis=2)
            .astype(BF16)
            .reshape(group_len, heads * 3 * DH)
        )
        return grad_qkv, grad_decay

    return attended, backward


def make_shards(osize, psize):
    count = 2 * psize
    home_steps = []
    bit = 1
    while bit < osize:
        home_steps.append((osize, bit))
        bit *= 2

    def shards(
        layer_input,
        attn_gain,
        qkv_weight,
        forget_weight,
        forget_bias,
        out_weight,
        ffn_gain,
        gate_weight,
        up_weight,
        down_weight,
        prompt_doc,
        branch_seg,
        branch_doc,
        out_cotangent,
    ):
        core, xpos = lax.axis_index("k"), lax.axis_index("x")
        hpos, ppos = lax.axis_index("h"), lax.axis_index("p")
        home = core == hpos
        same = core == xpos
        me = ppos * 2 + core
        heads = forget_weight.shape[1]

        prompt_len, branch_len = prompt_doc.shape[1], branch_seg.shape[1]
        packed = jnp.concatenate([prompt_doc[0], branch_seg[0], branch_doc[0]])
        sibling = swap(packed, "k")
        of_x = jnp.where(core == xpos, packed, sibling)
        of_peer = jnp.where(core == xpos, sibling, packed)
        from_peer = swap(of_peer, "x")
        packed = jnp.where(hpos == xpos, of_x, from_peer)
        prompt_ids = packed[:prompt_len]
        branch_ids = packed[prompt_len : prompt_len + branch_len]
        branch_docs = packed[prompt_len + branch_len :]

        gains = jnp.stack([attn_gain, ffn_gain])
        gains = jnp.concatenate([gains, swap(gains, "x")], axis=1)
        gain_a, gain_b = gains[0], gains[1]

        lane_pad = LANES - heads
        w_forget = gather_weight(
            jnp.concatenate([forget_weight, jnp.zeros((forget_weight.shape[0], lane_pad), BF16)], 1),
            home,
            0,
        )
        bias = jnp.where(home, forget_bias, lax.ppermute(forget_bias, ("k", "h"), [(1, 2), (2, 1)]))
        w_qkv = jnp.concatenate([gather_weight(qkv_weight, home, 0), w_forget], axis=1)
        w_out = gather_weight(out_weight, home, 1)
        w_gate = gather_weight(gate_weight, home, 0)
        w_up = gather_weight(up_weight, home, 0)
        w_down = gather_weight(down_weight, home, 1)

        stream = spread_tokens(layer_input, core, same).astype(F32)
        cot = spread_tokens(out_cotangent, core, same)
        cot_all = gather_blocks(cot, psize)
        cotangent = cot.astype(F32)

        rms_a = lax.rsqrt(jnp.sum(stream * stream, axis=1) / D + EPS)[:, None]
        normed_a_all = gather_blocks((stream * rms_a * gain_a).astype(BF16), psize)
        projected = reorder(matmul(normed_a_all, w_qkv), me, count)
        group_len = projected.shape[0]
        width = heads * 3 * DH
        qkv = projected[:, :width].astype(BF16).reshape(group_len, heads, 3, DH)
        forget_logit = projected[:, width : width + heads] + bias
        log_rate = jax.nn.log_sigmoid(forget_logit)

        member = branch_ids[:, None] == jnp.arange(branch_docs.shape[0])[None, :]
        branch_doc_ids = jnp.sum(jnp.where(member, branch_docs[None, :], 0), axis=1)
        doc_ids = jnp.concatenate([prompt_ids, branch_doc_ids])
        branch_tags = jnp.concatenate([jnp.full((prompt_len,), -1, jnp.int32), branch_ids])
        pos = jnp.arange(group_len, dtype=jnp.int32)
        key_prompt = branch_tags[None, :] < 0
        query_prompt = branch_tags[:, None] < 0
        causal = pos[None, :] <= pos[:, None]
        sums = jnp.where(
            query_prompt,
            causal,
            jnp.where(
                key_prompt,
                doc_ids[None, :] <= doc_ids[:, None],
                causal & (branch_tags[None, :] == branch_tags[:, None]),
            ),
        ).astype(BF16)
        decay_sum = sum3(matmul(sums, split3(log_rate)))

        attended, attention_back = attention(qkv, decay_sum, doc_ids, branch_tags)
        attended = reorder(attended, me, count)
        resid = stream + sum_blocks(matmul(attended, w_out), psize)
        rms_b = lax.rsqrt(jnp.sum(resid * resid, axis=1) / D + EPS)[:, None]
        normed_b_all = gather_blocks((resid * rms_b * gain_b).astype(BF16), psize)
        gate_pre = matmul(normed_b_all, w_gate)
        up_pre = matmul(normed_b_all, w_up)
        gate_sig = jax.nn.sigmoid(gate_pre)
        gate_act = gate_pre * gate_sig
        hidden = (gate_act * up_pre).astype(BF16)
        layer_output = (resid + sum_blocks(matmul(hidden, w_down), psize)).astype(BF16)
        layer_output = unspread_tokens(layer_output, core, same)

        feat = D // 2

        def reduce_rows(grad):
            return reduce_weight(grad[:feat], grad[feat:], home, home_steps)

        def reduce_cols(grad):
            return reduce_weight(grad[:, :feat], grad[:, feat:], home, home_steps)

        down_grad = reduce_cols(contract_rows(hidden, cot_all))
        grad_hidden = contract_cols(cot_all, w_down)
        grad_gate = (grad_hidden * up_pre * gate_sig * (1.0 + gate_pre * (1.0 - gate_sig))).astype(BF16)
        grad_up = (grad_hidden * gate_act).astype(BF16)
        gate_grad = reduce_rows(contract_rows(normed_b_all, grad_gate))
        up_grad = reduce_rows(contract_rows(normed_b_all, grad_up))
        grad_normed_b = sum_blocks(
            contract_cols(grad_gate, w_gate) + contract_cols(grad_up, w_up), psize
        )
        gained_b = gain_b * grad_normed_b
        inner_b = jnp.sum(resid * gained_b, axis=1)[:, None]
        ffn_gain_part = jnp.sum(grad_normed_b * resid * rms_b, axis=0)
        grad_resid = cotangent + rms_b * gained_b - resid * (rms_b * rms_b * rms_b) * inner_b / D
        grad_branch_all = gather_blocks(grad_resid.astype(BF16), psize)
        out_grad = reduce_cols(contract_rows(attended, grad_branch_all))
        grad_attended = reorder(contract_cols(grad_branch_all, w_out).astype(BF16), me, count)
        grad_qkv, grad_decay = attention_back(grad_attended.reshape(group_len, heads, DH))
        grad_log_rate = sum3(contract_rows(sums, split3(grad_decay)))
        grad_forget = (grad_log_rate * jax.nn.sigmoid(-forget_logit)).astype(BF16)
        forget_bias_part = jnp.sum(grad_forget, axis=0, dtype=F32)
        grad_proj = reorder(
            jnp.concatenate(
                [grad_qkv, grad_forget, jnp.zeros((group_len, lane_pad), BF16)], axis=1
            ),
            me,
            count,
        )
        proj_grad = reduce_rows(contract_rows(normed_a_all, grad_proj))
        qkv_grad, forget_grad = proj_grad[:, :width], proj_grad[:, width : width + heads]
        grad_normed_a = sum_blocks(contract_cols(grad_proj, w_qkv), psize)
        gained_a = gain_a * grad_normed_a
        inner_a = jnp.sum(stream * gained_a, axis=1)[:, None]
        attn_gain_part = jnp.sum(grad_normed_a * stream * rms_a, axis=0)
        input_grad = (
            grad_resid + rms_a * gained_a - stream * (rms_a * rms_a * rms_a) * inner_a / D
        ).astype(BF16)
        input_grad = unspread_tokens(input_grad, core, same)

        slots = jnp.where(
            (jnp.arange(2 * psize) == core * psize + ppos)[:, None], forget_bias_part[None, :], 0.0
        ).reshape(-1)
        small = jnp.concatenate([attn_gain_part[:feat], ffn_gain_part[:feat], slots])
        sent = jnp.concatenate([attn_gain_part[feat:], ffn_gain_part[feat:], slots])
        small = small + swap(sent, "x")
        small = lax.psum(small, ("o", "k", "h", "p"))
        bias_all = small[2 * feat :].reshape(2 * psize, heads)
        forget_bias_grad = lax.dynamic_index_in_dim(bias_all, hpos * psize + ppos, 0, keepdims=False)

        return (
            layer_output,
            input_grad,
            small[:feat],
            qkv_grad,
            forget_grad,
            forget_bias_grad,
            out_grad,
            small[feat : 2 * feat],
            gate_grad,
            up_grad,
            down_grad,
        )

    return shards


def solution(mesh):
    dp, row, col = mesh.shape["dp"], mesh.shape["row"], mesh.shape["col"]
    osize, psize = dp // 2, col // 2
    assert row == 2
    split = Mesh(mesh.devices.reshape(osize, 2, row, 2, psize), ("o", "k", "x", "h", "p"))
    tokens = P(("o", "k", "h", "p"), "x")
    rows_first = P("x", ("h", "p"))
    cols_first = P(("h", "p"), "x")
    groups = P(("o", "k", "x"), None)
    in_specs = (
        tokens,
        P("x"),
        rows_first,
        rows_first,
        P(("h", "p")),
        cols_first,
        P("x"),
        rows_first,
        rows_first,
        cols_first,
        groups,
        groups,
        groups,
        tokens,
    )
    out_specs = (
        tokens,
        tokens,
        P("x"),
        rows_first,
        rows_first,
        P(("h", "p")),
        cols_first,
        P("x"),
        rows_first,
        rows_first,
        cols_first,
    )
    return jax.shard_map(
        make_shards(osize, psize), mesh=split, in_specs=in_specs, out_specs=out_specs, check_vma=False
    )
```

```python
import functools

import jax
import jax.numpy as jnp
from jax import lax
from jax.experimental import pallas as pl
from jax.experimental.pallas import tpu as pltpu
from jax.sharding import Mesh, PartitionSpec as P

D = 1536
DH = 64
DOCS = 4
TILE = 256
EPS = 1e-06
MASKED = -1e30
LANES = 128
BF16 = jnp.bfloat16
F32 = jnp.float32


def swap(value, axis):
    return lax.ppermute(value, axis, [(0, 1), (1, 0)])


def xor_swap(value, axis, size, bit):
    return lax.ppermute(value, axis, [(i, i ^ bit) for i in range(size)])


def kxh(k, x, h):
    return (k * 2 + x) * 2 + h


def fetch_home_away(value):
    pairs = []
    for k in range(2):
        for x in range(2):
            for h in range(2):
                target = (k, 1 - x, h) if k == h else (1 - k, x, 1 - h)
                pairs.append((kxh(k, x, h), kxh(*target)))
    return lax.ppermute(value, ("k", "x", "h"), pairs)


def fetch_away(value):
    pairs = [
        (kxh(k, x, 1 - k), kxh(k, 1 - x, 1 - k)) for k in range(2) for x in range(2)
    ]
    return lax.ppermute(value, ("k", "x", "h"), pairs)


def gather_weight(shard, home, axis):
    first = fetch_home_away(shard)
    second = fetch_away(first)
    mine = jnp.where(home, shard, first)
    other = jnp.where(home, first, second)
    return jnp.concatenate([mine, other], axis=axis)


def reduce_weight(own, other, home, home_steps):
    total = own + swap(other.astype(BF16), "x").astype(F32)
    moved = lax.ppermute(
        total.astype(BF16), ("k", "h"), [(0 * 2 + 1, 0 * 2 + 0), (1 * 2 + 0, 1 * 2 + 1)]
    )
    total = (total + moved.astype(F32)).astype(BF16)
    for size, bit in home_steps:
        pairs = []
        for o in range(size):
            for k in range(2):
                pairs.append(((o * 2 + k) * 2 + k, ((o ^ bit) * 2 + k) * 2 + k))
        moved = lax.ppermute(total, ("o", "k", "h"), pairs)
        total = (total.astype(F32) + moved.astype(F32)).astype(BF16)
    moved = lax.ppermute(total, ("k", "h"), [(0, 2), (3, 1)])
    return jnp.where(home, total, moved).astype(F32)


def take_half(value, index):
    half = value.shape[0] // 2
    return lax.dynamic_slice_in_dim(value, index * half, half, 0)


def kx(k, x):
    return k * 2 + x


SPREAD_A = []
SPREAD_B = []
for _k in range(2):
    for _x in range(2):
        if _k == _x:
            SPREAD_A.append((kx(_k, _x), kx(1 - _k, _x)))
        else:
            SPREAD_A.append((kx(_k, _x), kx(_k, 1 - _x)))
            SPREAD_B.append((kx(_k, _x), kx(1 - _k, 1 - _x)))


def spread_tokens(block, core, same):
    near = take_half(block, core)
    far = take_half(block, 1 - core)
    first = lax.ppermute(jnp.where(same, far, near), ("k", "x"), SPREAD_A)
    second = lax.ppermute(far, ("k", "x"), SPREAD_B)
    own = jnp.where(same, near, first)
    other = jnp.where(same, first, second)
    return jnp.concatenate([own, other], axis=1)


def unspread_tokens(rows, core, same):
    half = rows.shape[1] // 2
    own, other = rows[:, :half], rows[:, half:]
    first = lax.ppermute(
        jnp.where(same, other, own), ("k", "x"), [(b, a) for a, b in SPREAD_A]
    )
    second = lax.ppermute(other, ("k", "x"), [(b, a) for a, b in SPREAD_B])
    near = jnp.where(same, own, first)
    far = jnp.where(same, first, second)
    low = jnp.where(core == 0, near, far)
    high = jnp.where(core == 0, far, near)
    return jnp.concatenate([low, high], axis=0)


def gather_blocks(block, psize):
    blocks = []
    for bit in range(psize):
        moved = block if bit == 0 else xor_swap(block, "p", psize, bit)
        blocks += [moved, swap(moved, "k")]
    return jnp.concatenate(blocks, axis=0)


def sum_blocks(partial, psize):
    size = partial.shape[0] // (2 * psize)
    parts = [partial[i * size : (i + 1) * size] for i in range(2 * psize)]
    total = None
    for bit in reversed(range(psize)):
        pair = parts[2 * bit] + swap(parts[2 * bit + 1].astype(BF16), "k").astype(F32)
        if bit:
            pair = xor_swap(pair.astype(BF16), "p", psize, bit).astype(F32)
        total = pair if total is None else total + pair
    return total


def contract_rows(left, right):
    return lax.dot_general(
        left, right, (((0,), (0,)), ((), ())), preferred_element_type=F32
    )


def contract_cols(left, right):
    return lax.dot_general(
        left, right, (((1,), (1,)), ((), ())), preferred_element_type=F32
    )


def matmul(left, right):
    return jnp.dot(left, right, preferred_element_type=F32)


def dot_nn(left, right):
    return lax.dot_general(left, right, (((1,), (0,)), ((), ())), preferred_element_type=F32)


def dot_nt(left, right):
    return lax.dot_general(left, right, (((1,), (1,)), ((), ())), preferred_element_type=F32)


def tile_mask(qrow, kcol, rows, cols, i, j):
    key_pos = j * TILE + lax.broadcasted_iota(jnp.int32, (TILE, TILE), 0)
    query_pos = i * TILE + lax.broadcasted_iota(jnp.int32, (TILE, TILE), 1)
    code = kcol[pl.ds(pl.multiple_of(j * TILE, TILE), TILE), 0:1]
    first = qrow[0:1, pl.ds(pl.multiple_of(i * TILE, TILE), TILE)]
    second = qrow[1:2, pl.ds(pl.multiple_of(i * TILE, TILE), TILE)]
    seen = (key_pos <= query_pos) & ((code == first) | (code == second))
    return jnp.where(seen, 0.0, MASKED)


def split_parts(value):
    high = value.astype(BF16)
    rest = value - high.astype(F32)
    mid = rest.astype(BF16)
    low = (rest - mid.astype(F32)).astype(BF16)
    return high, mid, low


def lane(shape):
    return lax.broadcasted_iota(jnp.int32, shape, 1)


def decay_map(pos_a, tag_a, limit_a, pos_b, tag_b, doc_b):
    adds = ((pos_b <= pos_a) & (tag_a == tag_b)) | (doc_b <= limit_a)
    return jnp.where(adds, 1.0, 0.0).astype(BF16)


def forward_kernel(
    heads, count, prompt_len, flags, qkv_hbm, logit_hbm, kcol, qrow, att_hbm, ot_hbm, lse_ref,
    qp_hbm, kp_hbm, vp_hbm, qkv, logit, qp, kp, vp, vt, rates, attended, ot, mask, m_ref, l_ref,
    in_sem, out_sem, keep_sem,
):
    me = lax.axis_index("p") * 2 + lax.axis_index("k")
    total = qkv.shape[0]
    size = total // count
    tiles = total // TILE
    loads = []
    for b in range(count):
        rows = pl.ds(b * size, size)
        loads.append(pltpu.make_async_copy(logit_hbm.at[b ^ me], logit.at[rows], in_sem.at[b]))
        loads.append(pltpu.make_async_copy(qkv_hbm.at[b ^ me], qkv.at[rows], in_sem.at[count + b]))
    for load in loads:
        load.start()
    for load in loads[::2]:
        load.wait()
    value = logit[...]
    rate = jnp.minimum(value, 0.0) - jnp.log1p(jnp.exp(-jnp.abs(value)))
    rate = jnp.where(lane(rate.shape) < heads, rate, 0.0)
    high, mid, low = split_parts(rate)
    packed = high.astype(F32) + pltpu.roll(mid.astype(F32), 8, 1) + pltpu.roll(low.astype(F32), 16, 1)
    rates[...] = packed.astype(BF16)
    for load in loads[1::2]:
        load.wait()
    place_row = lax.broadcasted_iota(jnp.int32, (LANES, LANES), 0)
    place_col = lax.broadcasted_iota(jnp.int32, (LANES, LANES), 1)

    def prepare(t, carry):
        rows = pl.ds(pl.multiple_of(t * TILE, TILE), TILE)

        def add_rates(u, acc):
            others = pl.ds(pl.multiple_of(u * TILE, TILE), TILE)
            pos_a = t * TILE + lax.broadcasted_iota(jnp.int32, (TILE, TILE), 0)
            pos_b = u * TILE + lax.broadcasted_iota(jnp.int32, (TILE, TILE), 1)
            adds = decay_map(
                pos_a, kcol[rows, 1:2], kcol[rows, 2:3], pos_b, qrow[2:3, others], qrow[3:4, others]
            )
            return acc + dot_nn(adds, rates[others, :])

        sums = lax.fori_loop(0, t + 1, add_rates, jnp.zeros((TILE, LANES), F32))
        decay = sums + pltpu.roll(sums, LANES - 8, 1) + pltpu.roll(sums, LANES - 16, 1)
        decay = jnp.where(lane(decay.shape) < heads, -decay, 0.0)
        high, mid, low = split_parts(decay)
        parts = (
            high.astype(F32) + pltpu.roll(mid.astype(F32), 8, 1) + pltpu.roll(low.astype(F32), 16, 1)
        ).astype(BF16)
        lanes = lane((TILE, LANES))
        for h in range(heads):
            base = 3 * DH * h
            query = qkv[rows, base : base + DH].astype(F32) * DH ** (-0.5)
            key = qkv[rows, base + DH : base + 2 * DH]
            worth = qkv[rows, base + 2 * DH : base + 3 * DH]
            ones = jnp.where((lanes >= DH) & (lanes < DH + 3), 1.0, 0.0)[:, :DH]
            ones = jnp.where(lane((TILE, DH)) < 3, 1.0, 0.0)
            qp[h, rows, :] = jnp.concatenate([query, ones], axis=1).astype(BF16)
            spread = jnp.where(
                (place_col >= DH) & (place_col < DH + 3) & (place_row == 8 * (place_col - DH) + h), 1.0, 0.0
            ).astype(BF16)
            extra = dot_nn(parts, spread)
            extra = jnp.where(lanes == DH + 3, 1.0, extra)
            key_wide = jnp.concatenate([key.astype(F32), extra[:, DH:]], axis=1)
            kp[h, rows, :] = key_wide.astype(BF16)
            vp[h, rows, :] = worth
            vt[h, :, rows] = worth.astype(F32).T.astype(BF16)
        return carry

    lax.fori_loop(0, tiles, prepare, 0)
    keeps = [
        pltpu.make_async_copy(qp, qp_hbm, keep_sem.at[0]),
        pltpu.make_async_copy(kp, kp_hbm, keep_sem.at[1]),
        pltpu.make_async_copy(vp, vp_hbm, keep_sem.at[2]),
    ]
    for keep in keeps:
        keep.start()

    def query_tile(i, carry):
        cols = pl.ds(pl.multiple_of(i * TILE, TILE), TILE)
        m_ref[...] = jnp.full(m_ref.shape, MASKED, F32)
        l_ref[...] = jnp.zeros(l_ref.shape, F32)
        ot[:, cols] = jnp.zeros((heads * DH, TILE), F32)

        def key_tile(j, inner):
            @pl.when(flags[i * tiles + j] > 0)
            def _():
                rows = pl.ds(pl.multiple_of(j * TILE, TILE), TILE)
                mask[...] = tile_mask(qrow, kcol, None, None, i, j)
                for h in range(heads):
                    scores = dot_nt(kp[h, rows, :], qp[h, cols, :]) + mask[...]
                    before = m_ref[h : h + 1, :]
                    top = jnp.maximum(before, jnp.max(scores, axis=0, keepdims=True))
                    expo = jnp.exp(scores - top)
                    shrink = jnp.exp(before - top)
                    m_ref[h : h + 1, :] = top
                    l_ref[h : h + 1, :] = l_ref[h : h + 1, :] * shrink + jnp.sum(expo, axis=0, keepdims=True)
                    part = dot_nn(vt[h, :, rows], expo.astype(BF16))
                    span = pl.ds(h * DH, DH)
                    ot[span, cols] = ot[span, cols] * shrink + part

            return inner

        lax.fori_loop(0, i + 1, key_tile, 0)
        for h in range(heads):
            span = pl.ds(h * DH, DH)
            ot[span, cols] = ot[span, cols] / l_ref[h : h + 1, :]
        lse_ref[:, cols] = m_ref[...] + jnp.log(l_ref[...])
        attended[cols, :] = ot[:, cols].T.astype(BF16)
        return carry

    lse_ref[...] = jnp.zeros(lse_ref.shape, F32)
    lax.fori_loop(0, tiles, query_tile, 0)
    stores = [pltpu.make_async_copy(ot, ot_hbm, keep_sem.at[3])]
    for b in range(count):
        stores.append(
            pltpu.make_async_copy(attended.at[pl.ds(b * size, size)], att_hbm.at[b ^ me], out_sem.at[b])
        )
    for store in stores:
        store.start()
    for copy in keeps + stores:
        copy.wait()


def attention_forward(qkv, logit, kcol, qrow, flags, heads, prompt_len):
    count, size, width = qkv.shape
    total = count * size
    any_spec = pl.BlockSpec(memory_space=pl.ANY)
    vmem = pl.BlockSpec(memory_space=pltpu.VMEM)
    shape = jax.ShapeDtypeStruct
    return pl.pallas_call(
        functools.partial(forward_kernel, heads, count, prompt_len),
        out_shape=(
            shape((count, size, heads * DH), BF16),
            shape((heads * DH, total), F32),
            shape((8, total), F32),
            shape((heads, total, LANES), BF16),
            shape((heads, total, LANES), BF16),
            shape((heads, total, DH), BF16),
        ),
        in_specs=[pl.BlockSpec(memory_space=pltpu.SMEM), any_spec, any_spec, vmem, vmem],
        out_specs=(any_spec, any_spec, vmem, any_spec, any_spec, any_spec),
        scratch_shapes=[
            pltpu.VMEM((total, width), BF16),
            pltpu.VMEM((total, LANES), F32),
            pltpu.VMEM((heads, total, LANES), BF16),
            pltpu.VMEM((heads, total, LANES), BF16),
            pltpu.VMEM((heads, total, DH), BF16),
            pltpu.VMEM((heads, DH, total), BF16),
            pltpu.VMEM((total, LANES), BF16),
            pltpu.VMEM((total, heads * DH), BF16),
            pltpu.VMEM((heads * DH, total), F32),
            pltpu.VMEM((TILE, TILE), F32),
            pltpu.VMEM((8, TILE), F32),
            pltpu.VMEM((8, TILE), F32),
            pltpu.SemaphoreType.DMA((2 * count,)),
            pltpu.SemaphoreType.DMA((count,)),
            pltpu.SemaphoreType.DMA((4,)),
        ],
        compiler_params=pltpu.CompilerParams(vmem_limit_bytes=48 << 20),
        cost_estimate=pl.CostEstimate(flops=20_000_000_000, bytes_accessed=30_000_000, transcendentals=0),
        name="attention_forward",
    )(flags, qkv, logit, kcol, qrow)


def backward_kernel(
    heads, count, prompt_len, flags, gatt_hbm, ot_ref, lse_ref, qp, kp, vp, logit_hbm, kcol, qrow,
    grad_hbm, bias_ref, gatt, logit, gout, kt, delta, dqt, dk, dv, mask, decay, grad, in_sem, out_sem,
):
    me = lax.axis_index("p") * 2 + lax.axis_index("k")
    total = gatt.shape[0]
    size = total // count
    tiles = total // TILE
    loads = []
    for b in range(count):
        rows = pl.ds(b * size, size)
        loads.append(pltpu.make_async_copy(gatt_hbm.at[b ^ me], gatt.at[rows], in_sem.at[b]))
        loads.append(pltpu.make_async_copy(logit_hbm.at[b ^ me], logit.at[rows], in_sem.at[count + b]))
    for load in loads:
        load.start()
    for load in loads:
        load.wait()
    dqt[...] = jnp.zeros(dqt.shape, F32)
    delta[...] = jnp.zeros(delta.shape, F32)

    def prepare(t, carry):
        rows = pl.ds(pl.multiple_of(t * TILE, TILE), TILE)
        turned = gatt[rows, :].astype(F32).T * ot_ref[:, rows]
        for h in range(heads):
            gout[h, rows, :] = gatt[rows, h * DH : (h + 1) * DH]
            kt[h, :, rows] = kp[h, rows, :].astype(F32).T[: DH + 8].astype(BF16)
            delta[h : h + 1, rows] = jnp.sum(turned[h * DH : (h + 1) * DH], axis=0, keepdims=True)
        return carry

    lax.fori_loop(0, tiles, prepare, 0)
    lanes = lane((TILE, LANES))

    def key_tile(j, carry):
        rows = pl.ds(pl.multiple_of(j * TILE, TILE), TILE)
        dk[...] = jnp.zeros(dk.shape, F32)
        dv[...] = jnp.zeros(dv.shape, F32)

        def query_tile(i, inner):
            @pl.when(flags[i * tiles + j] > 0)
            def _():
                cols = pl.ds(pl.multiple_of(i * TILE, TILE), TILE)
                mask[...] = tile_mask(qrow, kcol, None, None, i, j)
                for h in range(heads):
                    scores = dot_nt(kp[h, rows, :], qp[h, cols, :]) + mask[...]
                    probs = jnp.exp(scores - lse_ref[h : h + 1, cols])
                    grad_probs = dot_nt(vp[h, rows, :], gout[h, cols, :])
                    grad_scores = (probs * (grad_probs - delta[h : h + 1, cols])).astype(BF16)
                    dv[h] += dot_nn(probs.astype(BF16), gout[h, cols, :])
                    dk[h] += dot_nn(grad_scores, qp[h, cols, :])
                    dqt[h, :, cols] += dot_nn(kt[h, :, rows], grad_scores)

            return inner

        lax.fori_loop(j, tiles, query_tile, 0)
        keys = jnp.zeros((TILE, LANES), F32)
        for h in range(heads):
            grad_key = dk[h]
            keys += jnp.where(lanes == h, pltpu.roll(grad_key, LANES - DH + h, 1), 0.0)
            grad[rows, (3 * h + 1) * DH : (3 * h + 3) * DH] = jnp.concatenate(
                [grad_key[:, :DH], dv[h]], axis=1
            ).astype(BF16)
        decay[rows, :] = -keys
        return carry

    lax.fori_loop(0, tiles, key_tile, 0)

    def finish(t, carry):
        rows = pl.ds(pl.multiple_of(t * TILE, TILE), TILE)
        queries = jnp.zeros((TILE, LANES), F32)
        for h in range(heads):
            turned = jnp.concatenate([dqt[h, :, rows], jnp.zeros((LANES - DH - 8, TILE), F32)], axis=0).T
            queries += jnp.where(lanes == h, pltpu.roll(turned, LANES - DH - 3 + h, 1), 0.0)
            grad[rows, 3 * h * DH : (3 * h + 1) * DH] = (turned[:, :DH] * DH ** (-0.5)).astype(BF16)
        whole = decay[rows, :] + queries
        high, mid, low = split_parts(whole)
        decay[rows, :] = (
            high.astype(F32) + pltpu.roll(mid.astype(F32), 8, 1) + pltpu.roll(low.astype(F32), 16, 1)
        )
        return carry

    lax.fori_loop(0, tiles, finish, 0)

    def rates(t, bias):
        rows = pl.ds(pl.multiple_of(t * TILE, TILE), TILE)

        def add_decays(u, acc):
            others = pl.ds(pl.multiple_of(u * TILE, TILE), TILE)
            pos_b = t * TILE + lax.broadcasted_iota(jnp.int32, (TILE, TILE), 0)
            pos_a = u * TILE + lax.broadcasted_iota(jnp.int32, (TILE, TILE), 1)
            adds = decay_map(
                pos_a, qrow[2:3, others], qrow[4:5, others], pos_b, kcol[rows, 1:2], kcol[rows, 3:4]
            )
            return acc + dot_nn(adds, decay[others, :].astype(BF16))

        sums = lax.fori_loop(t, tiles, add_decays, jnp.zeros((TILE, LANES), F32))
        grad_rate = sums + pltpu.roll(sums, LANES - 8, 1) + pltpu.roll(sums, LANES - 16, 1)
        value = logit[rows, :]
        grad_forget = grad_rate / (1.0 + jnp.exp(value))
        grad_forget = jnp.where(lanes < heads, grad_forget, 0.0).astype(BF16)
        grad[rows, 3 * DH * heads :] = grad_forget
        return bias + jnp.sum(grad_forget.astype(F32), axis=0, keepdims=True)

    bias_ref[...] = jnp.broadcast_to(
        lax.fori_loop(0, tiles, rates, jnp.zeros((1, LANES), F32)), bias_ref.shape
    )
    stores = []
    for b in range(count):
        stores.append(
            pltpu.make_async_copy(grad.at[pl.ds(b * size, size)], grad_hbm.at[b ^ me], out_sem.at[b])
        )
    for store in stores:
        store.start()
    for store in stores:
        store.wait()


def attention_backward(grad_attended, saved, logit, kcol, qrow, flags, heads, prompt_len):
    ot, lse, qp, kp, vp = saved
    count, size, width = grad_attended.shape
    total = count * size
    any_spec = pl.BlockSpec(memory_space=pl.ANY)
    vmem = pl.BlockSpec(memory_space=pltpu.VMEM)
    shape = jax.ShapeDtypeStruct
    out_width = 3 * DH * heads + LANES
    return pl.pallas_call(
        functools.partial(backward_kernel, heads, count, prompt_len),
        out_shape=(shape((count, size, out_width), BF16), shape((8, LANES), F32)),
        in_specs=[pl.BlockSpec(memory_space=pltpu.SMEM), any_spec]
        + [vmem] * 5
        + [any_spec, vmem, vmem],
        out_specs=(any_spec, vmem),
        scratch_shapes=[
            pltpu.VMEM((total, width), BF16),
            pltpu.VMEM((total, LANES), F32),
            pltpu.VMEM((heads, total, DH), BF16),
            pltpu.VMEM((heads, DH + 8, total), BF16),
            pltpu.VMEM((8, total), F32),
            pltpu.VMEM((heads, DH + 8, total), F32),
            pltpu.VMEM((heads, TILE, LANES), F32),
            pltpu.VMEM((heads, TILE, DH), F32),
            pltpu.VMEM((TILE, TILE), F32),
            pltpu.VMEM((total, LANES), F32),
            pltpu.VMEM((total, out_width), BF16),
            pltpu.SemaphoreType.DMA((2 * count,)),
            pltpu.SemaphoreType.DMA((count,)),
        ],
        compiler_params=pltpu.CompilerParams(vmem_limit_bytes=56 << 20),
        cost_estimate=pl.CostEstimate(flops=50_000_000_000, bytes_accessed=30_000_000, transcendentals=0),
        name="attention_backward",
    )(flags, grad_attended, ot, lse, qp, kp, vp, logit, kcol, qrow)


def group_codes(prompt_ids, branch_ids, branch_docs):
    prompt_len = prompt_ids.shape[0]
    member = branch_ids[:, None] == jnp.arange(branch_docs.shape[0])[None, :]
    branch_doc_ids = jnp.sum(jnp.where(member, branch_docs[None, :], 0), axis=1)
    key_code = jnp.concatenate([prompt_ids, DOCS + branch_ids])
    first = jnp.concatenate([prompt_ids, branch_doc_ids])
    tag = jnp.concatenate([jnp.full_like(prompt_ids, -1), branch_ids])
    limit = jnp.concatenate([jnp.full_like(prompt_ids, -1), branch_doc_ids])
    prompt_code = jnp.concatenate([prompt_ids, jnp.full_like(branch_ids, DOCS)])
    total = key_code.shape[0]
    none = jnp.zeros_like(tag)
    kcol = jnp.stack([key_code, tag, limit, prompt_code] + [none] * 4, axis=1)
    qrow = jnp.stack([first, key_code, tag, prompt_code, limit] + [none] * 3, axis=0)
    tiles = total // TILE
    kinds = jnp.arange(2 * DOCS)
    key_bits = jnp.any(key_code.reshape(tiles, TILE, 1) == kinds, axis=1)
    query_bits = key_bits | jnp.any(first.reshape(tiles, TILE, 1) == kinds, axis=1)
    order = jnp.arange(tiles)
    meets = jnp.any(query_bits[:, None, :] & key_bits[None, :, :], axis=2)
    flags = (meets & (order[None, :] <= order[:, None])).astype(jnp.int32).reshape(-1)
    return kcol, qrow, flags


def make_shards(osize, psize):
    count = 2 * psize
    home_steps = []
    bit = 1
    while bit < osize:
        home_steps.append((osize, bit))
        bit *= 2

    def shards(
        layer_input,
        attn_gain,
        qkv_weight,
        forget_weight,
        forget_bias,
        out_weight,
        ffn_gain,
        gate_weight,
        up_weight,
        down_weight,
        prompt_doc,
        branch_seg,
        branch_doc,
        out_cotangent,
    ):
        core, xpos = lax.axis_index("k"), lax.axis_index("x")
        hpos, ppos = lax.axis_index("h"), lax.axis_index("p")
        home = core == hpos
        same = core == xpos
        me = ppos * 2 + core
        heads = forget_weight.shape[1]

        prompt_len, branch_len = prompt_doc.shape[1], branch_seg.shape[1]
        packed = jnp.concatenate([prompt_doc[0], branch_seg[0], branch_doc[0]])
        sibling = swap(packed, "k")
        of_x = jnp.where(core == xpos, packed, sibling)
        of_peer = jnp.where(core == xpos, sibling, packed)
        from_peer = swap(of_peer, "x")
        packed = jnp.where(hpos == xpos, of_x, from_peer)
        prompt_ids = packed[:prompt_len]
        branch_ids = packed[prompt_len : prompt_len + branch_len]
        branch_docs = packed[prompt_len + branch_len :]

        gains = jnp.stack([attn_gain, ffn_gain])
        gains = jnp.concatenate([gains, swap(gains, "x")], axis=1)
        gain_a, gain_b = gains[0], gains[1]

        lane_pad = LANES - heads
        w_forget = gather_weight(
            jnp.concatenate([forget_weight, jnp.zeros((forget_weight.shape[0], lane_pad), BF16)], 1),
            home,
            0,
        )
        bias = jnp.where(home, forget_bias, lax.ppermute(forget_bias, ("k", "h"), [(1, 2), (2, 1)]))
        bias = jnp.concatenate([bias, jnp.zeros((lane_pad,), F32)])
        w_qkv = jnp.concatenate([gather_weight(qkv_weight, home, 0), w_forget], axis=1)
        w_out = gather_weight(out_weight, home, 1)
        w_gate = gather_weight(gate_weight, home, 0)
        w_up = gather_weight(up_weight, home, 0)
        w_down = gather_weight(down_weight, home, 1)

        stream = spread_tokens(layer_input, core, same).astype(F32)
        cot = spread_tokens(out_cotangent, core, same)
        cot_all = gather_blocks(cot, psize)
        cotangent = cot.astype(F32)

        rms_a = lax.rsqrt(jnp.sum(stream * stream, axis=1) / D + EPS)[:, None]
        normed_a_all = gather_blocks((stream * rms_a * gain_a).astype(BF16), psize)
        projected = matmul(normed_a_all, w_qkv)
        width = heads * 3 * DH
        qkv = projected[:, :width].astype(BF16).reshape(count, -1, width)
        logit = projected[:, width:] + bias
        logit = logit.reshape(count, -1, LANES)
        kcol, qrow, flags = group_codes(prompt_ids, branch_ids, branch_docs)
        attended, *saved = attention_forward(qkv, logit, kcol, qrow, flags, heads, prompt_len)
        attended = attended.reshape(-1, heads * DH)
        resid = stream + sum_blocks(matmul(attended, w_out), psize)
        rms_b = lax.rsqrt(jnp.sum(resid * resid, axis=1) / D + EPS)[:, None]
        normed_b_all = gather_blocks((resid * rms_b * gain_b).astype(BF16), psize)
        gate_pre = matmul(normed_b_all, w_gate)
        up_pre = matmul(normed_b_all, w_up)
        gate_sig = jax.nn.sigmoid(gate_pre)
        gate_act = gate_pre * gate_sig
        hidden = (gate_act * up_pre).astype(BF16)
        layer_output = (resid + sum_blocks(matmul(hidden, w_down), psize)).astype(BF16)
        layer_output = unspread_tokens(layer_output, core, same)

        feat = D // 2

        def reduce_rows(grad):
            return reduce_weight(grad[:feat], grad[feat:], home, home_steps)

        def reduce_cols(grad):
            return reduce_weight(grad[:, :feat], grad[:, feat:], home, home_steps)

        down_grad = reduce_cols(contract_rows(hidden, cot_all))
        grad_hidden = contract_cols(cot_all, w_down)
        grad_gate = (grad_hidden * up_pre * gate_sig * (1.0 + gate_pre * (1.0 - gate_sig))).astype(BF16)
        grad_up = (grad_hidden * gate_act).astype(BF16)
        gate_grad = reduce_rows(contract_rows(normed_b_all, grad_gate))
        up_grad = reduce_rows(contract_rows(normed_b_all, grad_up))
        grad_normed_b = sum_blocks(
            contract_cols(grad_gate, w_gate) + contract_cols(grad_up, w_up), psize
        )
        gained_b = gain_b * grad_normed_b
        inner_b = jnp.sum(resid * gained_b, axis=1)[:, None]
        ffn_gain_part = jnp.sum(grad_normed_b * resid * rms_b, axis=0)
        grad_resid = cotangent + rms_b * gained_b - resid * (rms_b * rms_b * rms_b) * inner_b / D
        grad_branch_all = gather_blocks(grad_resid.astype(BF16), psize)
        out_grad = reduce_cols(contract_rows(attended, grad_branch_all))
        grad_attended = contract_cols(grad_branch_all, w_out).astype(BF16)
        grad_proj, bias_sums = attention_backward(
            grad_attended.reshape(count, -1, heads * DH), saved, logit, kcol, qrow, flags, heads, prompt_len
        )
        grad_proj = grad_proj.reshape(-1, width + LANES)
        forget_bias_part = bias_sums[0, :heads]
        proj_grad = reduce_rows(contract_rows(normed_a_all, grad_proj))
        qkv_grad, forget_grad = proj_grad[:, :width], proj_grad[:, width : width + heads]
        grad_normed_a = sum_blocks(contract_cols(grad_proj, w_qkv), psize)
        gained_a = gain_a * grad_normed_a
        inner_a = jnp.sum(stream * gained_a, axis=1)[:, None]
        attn_gain_part = jnp.sum(grad_normed_a * stream * rms_a, axis=0)
        input_grad = (
            grad_resid + rms_a * gained_a - stream * (rms_a * rms_a * rms_a) * inner_a / D
        ).astype(BF16)
        input_grad = unspread_tokens(input_grad, core, same)

        slots = jnp.where(
            (jnp.arange(2 * psize) == core * psize + ppos)[:, None], forget_bias_part[None, :], 0.0
        ).reshape(-1)
        small = jnp.concatenate([attn_gain_part[:feat], ffn_gain_part[:feat], slots])
        sent = jnp.concatenate([attn_gain_part[feat:], ffn_gain_part[feat:], slots])
        small = small + swap(sent, "x")
        small = lax.psum(small, ("o", "k", "h", "p"))
        bias_all = small[2 * feat :].reshape(2 * psize, heads)
        forget_bias_grad = lax.dynamic_index_in_dim(bias_all, hpos * psize + ppos, 0, keepdims=False)

        return (
            layer_output,
            input_grad,
            small[:feat],
            qkv_grad,
            forget_grad,
            forget_bias_grad,
            out_grad,
            small[feat : 2 * feat],
            gate_grad,
            up_grad,
            down_grad,
        )

    return shards


def solution(mesh):
    dp, row, col = mesh.shape["dp"], mesh.shape["row"], mesh.shape["col"]
    osize, psize = dp // 2, col // 2
    assert row == 2
    split = Mesh(mesh.devices.reshape(osize, 2, row, 2, psize), ("o", "k", "x", "h", "p"))
    tokens = P(("o", "k", "h", "p"), "x")
    rows_first = P("x", ("h", "p"))
    cols_first = P(("h", "p"), "x")
    groups = P(("o", "k", "x"), None)
    in_specs = (
        tokens,
        P("x"),
        rows_first,
        rows_first,
        P(("h", "p")),
        cols_first,
        P("x"),
        rows_first,
        rows_first,
        cols_first,
        groups,
        groups,
        groups,
        tokens,
    )
    out_specs = (
        tokens,
        tokens,
        P("x"),
        rows_first,
        rows_first,
        P(("h", "p")),
        cols_first,
        P("x"),
        rows_first,
        rows_first,
        cols_first,
    )
    return jax.shard_map(
        make_shards(osize, psize), mesh=split, in_specs=in_specs, out_specs=out_specs, check_vma=False
    )
```

```python
import functools

import jax
import jax.numpy as jnp
from jax import lax
from jax.experimental import pallas as pl
from jax.experimental.pallas import tpu as pltpu
from jax.sharding import Mesh, PartitionSpec as P

D = 1536
DH = 64
DOCS = 4
TILE = 256
EPS = 1e-06
MASKED = -1e30
LANES = 128
BF16 = jnp.bfloat16
F32 = jnp.float32


def swap(value, axis):
    return lax.ppermute(value, axis, [(0, 1), (1, 0)])


def xor_swap(value, axis, size, bit):
    return lax.ppermute(value, axis, [(i, i ^ bit) for i in range(size)])


def kxh(k, x, h):
    return (k * 2 + x) * 2 + h


def fetch_home_away(value):
    pairs = []
    for k in range(2):
        for x in range(2):
            for h in range(2):
                target = (k, 1 - x, h) if k == h else (1 - k, x, 1 - h)
                pairs.append((kxh(k, x, h), kxh(*target)))
    return lax.ppermute(value, ("k", "x", "h"), pairs)


def fetch_away(value):
    pairs = [
        (kxh(k, x, 1 - k), kxh(k, 1 - x, 1 - k)) for k in range(2) for x in range(2)
    ]
    return lax.ppermute(value, ("k", "x", "h"), pairs)


def tie(value, *others):
    return lax.optimization_barrier((value,) + others)[0]


def join_weight(shard, first, second, home, axis):
    mine = jnp.where(home, shard, first)
    other = jnp.where(home, first, second)
    return jnp.concatenate([mine, other], axis=axis)


def add_parts(kept, moved):
    return (kept.astype(F32) + moved.astype(F32)).astype(BF16)


def to_home(value):
    return lax.ppermute(value, ("k", "h"), [(1, 0), (2, 3)])


def from_home(value):
    return lax.ppermute(value, ("k", "h"), [(0, 2), (3, 1)])


def home_swap(value, size, bit):
    pairs = []
    for o in range(size):
        for k in range(2):
            pairs.append(((o * 2 + k) * 2 + k, ((o ^ bit) * 2 + k) * 2 + k))
    return lax.ppermute(value, ("o", "k", "h"), pairs)


def bits_of(size):
    return [1 << i for i in range(size.bit_length() - 1)]


def split_rows(value, high):
    half = value.shape[0] // 2
    low_rows, high_rows = value[:half], value[half:]
    return jnp.where(high, high_rows, low_rows), jnp.where(high, low_rows, high_rows)


def merge_rows(kept, moved, high):
    return jnp.concatenate([jnp.where(high, moved, kept), jnp.where(high, kept, moved)], axis=0)


def take_half(value, index):
    half = value.shape[0] // 2
    return lax.dynamic_slice_in_dim(value, index * half, half, 0)


def kx(k, x):
    return k * 2 + x


SPREAD_A = []
SPREAD_B = []
for _k in range(2):
    for _x in range(2):
        if _k == _x:
            SPREAD_A.append((kx(_k, _x), kx(1 - _k, _x)))
        else:
            SPREAD_A.append((kx(_k, _x), kx(_k, 1 - _x)))
            SPREAD_B.append((kx(_k, _x), kx(1 - _k, 1 - _x)))


def spread_tokens(block, core, same):
    near = take_half(block, core)
    far = take_half(block, 1 - core)
    first = lax.ppermute(jnp.where(same, far, near), ("k", "x"), SPREAD_A)
    second = lax.ppermute(far, ("k", "x"), SPREAD_B)
    own = jnp.where(same, near, first)
    other = jnp.where(same, first, second)
    return jnp.concatenate([own, other], axis=1)


def unspread_parts(rows, same):
    half = rows.shape[1] // 2
    own, other = rows[:, :half], rows[:, half:]
    return own, jnp.where(same, other, own), other


def unspread_moves(near, far):
    first = lax.ppermute(near, ("k", "x"), [(b, a) for a, b in SPREAD_A])
    second = lax.ppermute(far, ("k", "x"), [(b, a) for a, b in SPREAD_B])
    return first, second


def unspread_join(own, first, second, core, same):
    near = jnp.where(same, own, first)
    far = jnp.where(same, first, second)
    low = jnp.where(core == 0, near, far)
    high = jnp.where(core == 0, far, near)
    return jnp.concatenate([low, high], axis=0)


def contract_rows(left, right):
    return lax.dot_general(
        left, right, (((0,), (0,)), ((), ())), preferred_element_type=F32
    )


def contract_cols(left, right):
    return lax.dot_general(
        left, right, (((1,), (1,)), ((), ())), preferred_element_type=F32
    )


def matmul(left, right):
    return jnp.dot(left, right, preferred_element_type=F32)


def dot_nn(left, right):
    return lax.dot_general(left, right, (((1,), (0,)), ((), ())), preferred_element_type=F32)


def dot_nt(left, right):
    return lax.dot_general(left, right, (((1,), (1,)), ((), ())), preferred_element_type=F32)


def tile_mask(qrow, kcol, rows, cols, i, j):
    key_pos = j * TILE + lax.broadcasted_iota(jnp.int32, (TILE, TILE), 0)
    query_pos = i * TILE + lax.broadcasted_iota(jnp.int32, (TILE, TILE), 1)
    code = kcol[pl.ds(pl.multiple_of(j * TILE, TILE), TILE), 0:1]
    first = qrow[0:1, pl.ds(pl.multiple_of(i * TILE, TILE), TILE)]
    second = qrow[1:2, pl.ds(pl.multiple_of(i * TILE, TILE), TILE)]
    seen = (key_pos <= query_pos) & ((code == first) | (code == second))
    return jnp.where(seen, 0.0, MASKED)


def split_parts(value):
    high = value.astype(BF16)
    rest = value - high.astype(F32)
    mid = rest.astype(BF16)
    low = (rest - mid.astype(F32)).astype(BF16)
    return high, mid, low


def lane(shape):
    return lax.broadcasted_iota(jnp.int32, shape, 1)


def decay_map(pos_a, tag_a, limit_a, pos_b, tag_b, doc_b):
    adds = ((pos_b <= pos_a) & (tag_a == tag_b)) | (doc_b <= limit_a)
    return jnp.where(adds, 1.0, 0.0).astype(BF16)


def forward_kernel(
    heads, count, prompt_len, flags, qkv_hbm, logit_hbm, kcol, qrow, att_hbm, ot_hbm, lse_ref,
    qp_hbm, kp_hbm, vp_hbm, qkv, logit, qp, kp, vp, vt, rates, attended, ot, mask, m_ref, l_ref,
    in_sem, out_sem, keep_sem,
):
    me = lax.axis_index("p") * 2 + lax.axis_index("k")
    total = qkv.shape[0]
    size = total // count
    tiles = total // TILE
    loads = []
    for b in range(count):
        rows = pl.ds(b * size, size)
        loads.append(pltpu.make_async_copy(logit_hbm.at[b ^ me], logit.at[rows], in_sem.at[b]))
        loads.append(pltpu.make_async_copy(qkv_hbm.at[b ^ me], qkv.at[rows], in_sem.at[count + b]))
    for load in loads:
        load.start()
    for load in loads[::2]:
        load.wait()
    value = logit[...]
    rate = jnp.minimum(value, 0.0) - jnp.log1p(jnp.exp(-jnp.abs(value)))
    rate = jnp.where(lane(rate.shape) < heads, rate, 0.0)
    high, mid, low = split_parts(rate)
    packed = high.astype(F32) + pltpu.roll(mid.astype(F32), 8, 1) + pltpu.roll(low.astype(F32), 16, 1)
    rates[...] = packed.astype(BF16)
    for load in loads[1::2]:
        load.wait()
    place_row = lax.broadcasted_iota(jnp.int32, (LANES, LANES), 0)
    place_col = lax.broadcasted_iota(jnp.int32, (LANES, LANES), 1)

    def prepare(t, carry):
        rows = pl.ds(pl.multiple_of(t * TILE, TILE), TILE)

        def add_rates(u, acc):
            others = pl.ds(pl.multiple_of(u * TILE, TILE), TILE)
            pos_a = t * TILE + lax.broadcasted_iota(jnp.int32, (TILE, TILE), 0)
            pos_b = u * TILE + lax.broadcasted_iota(jnp.int32, (TILE, TILE), 1)
            adds = decay_map(
                pos_a, kcol[rows, 1:2], kcol[rows, 2:3], pos_b, qrow[2:3, others], qrow[3:4, others]
            )
            return acc + dot_nn(adds, rates[others, :])

        sums = lax.fori_loop(0, t + 1, add_rates, jnp.zeros((TILE, LANES), F32))
        decay = sums + pltpu.roll(sums, LANES - 8, 1) + pltpu.roll(sums, LANES - 16, 1)
        decay = jnp.where(lane(decay.shape) < heads, -decay, 0.0)
        high, mid, low = split_parts(decay)
        parts = (
            high.astype(F32) + pltpu.roll(mid.astype(F32), 8, 1) + pltpu.roll(low.astype(F32), 16, 1)
        ).astype(BF16)
        lanes = lane((TILE, LANES))
        for h in range(heads):
            base = 3 * DH * h
            query = qkv[rows, base : base + DH].astype(F32) * DH ** (-0.5)
            key = qkv[rows, base + DH : base + 2 * DH]
            worth = qkv[rows, base + 2 * DH : base + 3 * DH]
            ones = jnp.where((lanes >= DH) & (lanes < DH + 3), 1.0, 0.0)[:, :DH]
            ones = jnp.where(lane((TILE, DH)) < 3, 1.0, 0.0)
            qp[h, rows, :] = jnp.concatenate([query, ones], axis=1).astype(BF16)
            spread = jnp.where(
                (place_col >= DH) & (place_col < DH + 3) & (place_row == 8 * (place_col - DH) + h), 1.0, 0.0
            ).astype(BF16)
            extra = dot_nn(parts, spread)
            extra = jnp.where(lanes == DH + 3, 1.0, extra)
            key_wide = jnp.concatenate([key.astype(F32), extra[:, DH:]], axis=1)
            kp[h, rows, :] = key_wide.astype(BF16)
            vp[h, rows, :] = worth
            vt[h, :, rows] = worth.astype(F32).T.astype(BF16)
        return carry

    lax.fori_loop(0, tiles, prepare, 0)
    keeps = [
        pltpu.make_async_copy(qp, qp_hbm, keep_sem.at[0]),
        pltpu.make_async_copy(kp, kp_hbm, keep_sem.at[1]),
        pltpu.make_async_copy(vp, vp_hbm, keep_sem.at[2]),
    ]
    for keep in keeps:
        keep.start()

    def query_tile(i, carry):
        cols = pl.ds(pl.multiple_of(i * TILE, TILE), TILE)
        m_ref[...] = jnp.full(m_ref.shape, MASKED, F32)
        l_ref[...] = jnp.zeros(l_ref.shape, F32)
        ot[:, cols] = jnp.zeros((heads * DH, TILE), F32)

        def key_tile(j, inner):
            @pl.when(flags[i * tiles + j] > 0)
            def _():
                rows = pl.ds(pl.multiple_of(j * TILE, TILE), TILE)
                mask[...] = tile_mask(qrow, kcol, None, None, i, j)
                for h in range(heads):
                    scores = dot_nt(kp[h, rows, :], qp[h, cols, :]) + mask[...]
                    before = m_ref[h : h + 1, :]
                    top = jnp.maximum(before, jnp.max(scores, axis=0, keepdims=True))
                    expo = jnp.exp(scores - top)
                    shrink = jnp.exp(before - top)
                    m_ref[h : h + 1, :] = top
                    l_ref[h : h + 1, :] = l_ref[h : h + 1, :] * shrink + jnp.sum(expo, axis=0, keepdims=True)
                    part = dot_nn(vt[h, :, rows], expo.astype(BF16))
                    span = pl.ds(h * DH, DH)
                    ot[span, cols] = ot[span, cols] * shrink + part

            return inner

        lax.fori_loop(0, i + 1, key_tile, 0)
        for h in range(heads):
            span = pl.ds(h * DH, DH)
            ot[span, cols] = ot[span, cols] / l_ref[h : h + 1, :]
        lse_ref[:, cols] = m_ref[...] + jnp.log(l_ref[...])
        attended[cols, :] = ot[:, cols].T.astype(BF16)
        return carry

    lse_ref[...] = jnp.zeros(lse_ref.shape, F32)
    lax.fori_loop(0, tiles, query_tile, 0)
    stores = [pltpu.make_async_copy(ot, ot_hbm, keep_sem.at[3])]
    for b in range(count):
        stores.append(
            pltpu.make_async_copy(attended.at[pl.ds(b * size, size)], att_hbm.at[b ^ me], out_sem.at[b])
        )
    for store in stores:
        store.start()
    for copy in keeps + stores:
        copy.wait()


def attention_forward(qkv, logit, kcol, qrow, flags, heads, prompt_len):
    count, size, width = qkv.shape
    total = count * size
    any_spec = pl.BlockSpec(memory_space=pl.ANY)
    vmem = pl.BlockSpec(memory_space=pltpu.VMEM)
    shape = jax.ShapeDtypeStruct
    return pl.pallas_call(
        functools.partial(forward_kernel, heads, count, prompt_len),
        out_shape=(
            shape((count, size, heads * DH), BF16),
            shape((heads * DH, total), F32),
            shape((8, total), F32),
            shape((heads, total, LANES), BF16),
            shape((heads, total, LANES), BF16),
            shape((heads, total, DH), BF16),
        ),
        in_specs=[pl.BlockSpec(memory_space=pltpu.SMEM), any_spec, any_spec, vmem, vmem],
        out_specs=(any_spec, any_spec, vmem, any_spec, any_spec, any_spec),
        scratch_shapes=[
            pltpu.VMEM((total, width), BF16),
            pltpu.VMEM((total, LANES), F32),
            pltpu.VMEM((heads, total, LANES), BF16),
            pltpu.VMEM((heads, total, LANES), BF16),
            pltpu.VMEM((heads, total, DH), BF16),
            pltpu.VMEM((heads, DH, total), BF16),
            pltpu.VMEM((total, LANES), BF16),
            pltpu.VMEM((total, heads * DH), BF16),
            pltpu.VMEM((heads * DH, total), F32),
            pltpu.VMEM((TILE, TILE), F32),
            pltpu.VMEM((8, TILE), F32),
            pltpu.VMEM((8, TILE), F32),
            pltpu.SemaphoreType.DMA((2 * count,)),
            pltpu.SemaphoreType.DMA((count,)),
            pltpu.SemaphoreType.DMA((4,)),
        ],
        compiler_params=pltpu.CompilerParams(vmem_limit_bytes=48 << 20),
        cost_estimate=pl.CostEstimate(flops=20_000_000_000, bytes_accessed=30_000_000, transcendentals=0),
        name="attention_forward",
    )(flags, qkv, logit, kcol, qrow)


def backward_kernel(
    heads, count, prompt_len, flags, gatt_hbm, ot_ref, lse_ref, qp, kp, vp, logit_hbm, kcol, qrow,
    grad_hbm, bias_ref, gatt, logit, gout, kt, delta, dqt, dk, dv, mask, decay, grad, in_sem, out_sem,
):
    me = lax.axis_index("p") * 2 + lax.axis_index("k")
    total = gatt.shape[0]
    size = total // count
    tiles = total // TILE
    loads = []
    for b in range(count):
        rows = pl.ds(b * size, size)
        loads.append(pltpu.make_async_copy(gatt_hbm.at[b ^ me], gatt.at[rows], in_sem.at[b]))
        loads.append(pltpu.make_async_copy(logit_hbm.at[b ^ me], logit.at[rows], in_sem.at[count + b]))
    for load in loads:
        load.start()
    for load in loads:
        load.wait()
    dqt[...] = jnp.zeros(dqt.shape, F32)
    delta[...] = jnp.zeros(delta.shape, F32)

    def prepare(t, carry):
        rows = pl.ds(pl.multiple_of(t * TILE, TILE), TILE)
        turned = gatt[rows, :].astype(F32).T * ot_ref[:, rows]
        for h in range(heads):
            gout[h, rows, :] = gatt[rows, h * DH : (h + 1) * DH]
            kt[h, :, rows] = kp[h, rows, :].astype(F32).T[: DH + 8].astype(BF16)
            delta[h : h + 1, rows] = jnp.sum(turned[h * DH : (h + 1) * DH], axis=0, keepdims=True)
        return carry

    lax.fori_loop(0, tiles, prepare, 0)
    lanes = lane((TILE, LANES))

    def key_tile(j, carry):
        rows = pl.ds(pl.multiple_of(j * TILE, TILE), TILE)
        dk[...] = jnp.zeros(dk.shape, F32)
        dv[...] = jnp.zeros(dv.shape, F32)

        def query_tile(i, inner):
            @pl.when(flags[i * tiles + j] > 0)
            def _():
                cols = pl.ds(pl.multiple_of(i * TILE, TILE), TILE)
                mask[...] = tile_mask(qrow, kcol, None, None, i, j)
                for h in range(heads):
                    scores = dot_nt(kp[h, rows, :], qp[h, cols, :]) + mask[...]
                    probs = jnp.exp(scores - lse_ref[h : h + 1, cols])
                    grad_probs = dot_nt(vp[h, rows, :], gout[h, cols, :])
                    grad_scores = (probs * (grad_probs - delta[h : h + 1, cols])).astype(BF16)
                    dv[h] += dot_nn(probs.astype(BF16), gout[h, cols, :])
                    dk[h] += dot_nn(grad_scores, qp[h, cols, :])
                    dqt[h, :, cols] += dot_nn(kt[h, :, rows], grad_scores)

            return inner

        lax.fori_loop(j, tiles, query_tile, 0)
        keys = jnp.zeros((TILE, LANES), F32)
        for h in range(heads):
            grad_key = dk[h]
            keys += jnp.where(lanes == h, pltpu.roll(grad_key, LANES - DH + h, 1), 0.0)
            grad[rows, (3 * h + 1) * DH : (3 * h + 3) * DH] = jnp.concatenate(
                [grad_key[:, :DH], dv[h]], axis=1
            ).astype(BF16)
        decay[rows, :] = -keys
        return carry

    lax.fori_loop(0, tiles, key_tile, 0)

    def finish(t, carry):
        rows = pl.ds(pl.multiple_of(t * TILE, TILE), TILE)
        queries = jnp.zeros((TILE, LANES), F32)
        for h in range(heads):
            turned = jnp.concatenate([dqt[h, :, rows], jnp.zeros((LANES - DH - 8, TILE), F32)], axis=0).T
            queries += jnp.where(lanes == h, pltpu.roll(turned, LANES - DH - 3 + h, 1), 0.0)
            grad[rows, 3 * h * DH : (3 * h + 1) * DH] = (turned[:, :DH] * DH ** (-0.5)).astype(BF16)
        whole = decay[rows, :] + queries
        high, mid, low = split_parts(whole)
        decay[rows, :] = (
            high.astype(F32) + pltpu.roll(mid.astype(F32), 8, 1) + pltpu.roll(low.astype(F32), 16, 1)
        )
        return carry

    lax.fori_loop(0, tiles, finish, 0)

    def rates(t, bias):
        rows = pl.ds(pl.multiple_of(t * TILE, TILE), TILE)

        def add_decays(u, acc):
            others = pl.ds(pl.multiple_of(u * TILE, TILE), TILE)
            pos_b = t * TILE + lax.broadcasted_iota(jnp.int32, (TILE, TILE), 0)
            pos_a = u * TILE + lax.broadcasted_iota(jnp.int32, (TILE, TILE), 1)
            adds = decay_map(
                pos_a, qrow[2:3, others], qrow[4:5, others], pos_b, kcol[rows, 1:2], kcol[rows, 3:4]
            )
            return acc + dot_nn(adds, decay[others, :].astype(BF16))

        sums = lax.fori_loop(t, tiles, add_decays, jnp.zeros((TILE, LANES), F32))
        grad_rate = sums + pltpu.roll(sums, LANES - 8, 1) + pltpu.roll(sums, LANES - 16, 1)
        value = logit[rows, :]
        grad_forget = grad_rate / (1.0 + jnp.exp(value))
        grad_forget = jnp.where(lanes < heads, grad_forget, 0.0).astype(BF16)
        grad[rows, 3 * DH * heads :] = grad_forget
        return bias + jnp.sum(grad_forget.astype(F32), axis=0, keepdims=True)

    bias_ref[...] = jnp.broadcast_to(
        lax.fori_loop(0, tiles, rates, jnp.zeros((1, LANES), F32)), bias_ref.shape
    )
    stores = []
    for b in range(count):
        stores.append(
            pltpu.make_async_copy(grad.at[pl.ds(b * size, size)], grad_hbm.at[b ^ me], out_sem.at[b])
        )
    for store in stores:
        store.start()
    for store in stores:
        store.wait()


def attention_backward(grad_attended, saved, logit, kcol, qrow, flags, heads, prompt_len):
    ot, lse, qp, kp, vp = saved
    count, size, width = grad_attended.shape
    total = count * size
    any_spec = pl.BlockSpec(memory_space=pl.ANY)
    vmem = pl.BlockSpec(memory_space=pltpu.VMEM)
    shape = jax.ShapeDtypeStruct
    out_width = 3 * DH * heads + LANES
    return pl.pallas_call(
        functools.partial(backward_kernel, heads, count, prompt_len),
        out_shape=(shape((count, size, out_width), BF16), shape((8, LANES), F32)),
        in_specs=[pl.BlockSpec(memory_space=pltpu.SMEM), any_spec]
        + [vmem] * 5
        + [any_spec, vmem, vmem],
        out_specs=(any_spec, vmem),
        scratch_shapes=[
            pltpu.VMEM((total, width), BF16),
            pltpu.VMEM((total, LANES), F32),
            pltpu.VMEM((heads, total, DH), BF16),
            pltpu.VMEM((heads, DH + 8, total), BF16),
            pltpu.VMEM((8, total), F32),
            pltpu.VMEM((heads, DH + 8, total), F32),
            pltpu.VMEM((heads, TILE, LANES), F32),
            pltpu.VMEM((heads, TILE, DH), F32),
            pltpu.VMEM((TILE, TILE), F32),
            pltpu.VMEM((total, LANES), F32),
            pltpu.VMEM((total, out_width), BF16),
            pltpu.SemaphoreType.DMA((2 * count,)),
            pltpu.SemaphoreType.DMA((count,)),
        ],
        compiler_params=pltpu.CompilerParams(vmem_limit_bytes=56 << 20),
        cost_estimate=pl.CostEstimate(flops=50_000_000_000, bytes_accessed=30_000_000, transcendentals=0),
        name="attention_backward",
    )(flags, grad_attended, ot, lse, qp, kp, vp, logit, kcol, qrow)


def group_codes(prompt_ids, branch_ids, branch_docs):
    prompt_len = prompt_ids.shape[0]
    member = branch_ids[:, None] == jnp.arange(branch_docs.shape[0])[None, :]
    branch_doc_ids = jnp.sum(jnp.where(member, branch_docs[None, :], 0), axis=1)
    key_code = jnp.concatenate([prompt_ids, DOCS + branch_ids])
    first = jnp.concatenate([prompt_ids, branch_doc_ids])
    tag = jnp.concatenate([jnp.full_like(prompt_ids, -1), branch_ids])
    limit = jnp.concatenate([jnp.full_like(prompt_ids, -1), branch_doc_ids])
    prompt_code = jnp.concatenate([prompt_ids, jnp.full_like(branch_ids, DOCS)])
    total = key_code.shape[0]
    none = jnp.zeros_like(tag)
    kcol = jnp.stack([key_code, tag, limit, prompt_code] + [none] * 4, axis=1)
    qrow = jnp.stack([first, key_code, tag, prompt_code, limit] + [none] * 3, axis=0)
    tiles = total // TILE
    kinds = jnp.arange(2 * DOCS)
    key_bits = jnp.any(key_code.reshape(tiles, TILE, 1) == kinds, axis=1)
    query_bits = key_bits | jnp.any(first.reshape(tiles, TILE, 1) == kinds, axis=1)
    order = jnp.arange(tiles)
    meets = jnp.any(query_bits[:, None, :] & key_bits[None, :, :], axis=2)
    flags = (meets & (order[None, :] <= order[:, None])).astype(jnp.int32).reshape(-1)
    return kcol, qrow, flags


class Wires:
    def __init__(self, send_sem, recv_sem, local_sem):
        self.send_sem, self.recv_sem, self.local_sem = send_sem, recv_sem, local_sem
        self.used, self.local_used = 0, 0
        self.k, self.x = lax.axis_index("k"), lax.axis_index("x")
        self.h, self.p, self.o = lax.axis_index("h"), lax.axis_index("p"), lax.axis_index("o")
        self.home = self.k == self.h
        self.same = self.k == self.x
        self.pending = []

    def slot(self):
        self.used += 1
        return self.used - 1

    def copy(self, source, target, device, slot):
        return pltpu.make_async_remote_copy(
            src_ref=source,
            dst_ref=target,
            send_sem=self.send_sem.at[slot],
            recv_sem=self.recv_sem.at[slot],
            device_id=device,
            device_id_type=pl.DeviceIdType.MESH,
        )

    def send(self, source, target, device):
        copy = self.copy(source, target, device, self.slot())
        copy.start()
        self.pending.append(copy.wait_send)
        return copy

    def local(self, source, target):
        copy = pltpu.make_async_copy(source, target, self.local_sem.at[self.local_used])
        self.local_used += 1
        copy.start()
        return copy

    def greet(self, devices):
        barrier = pltpu.get_barrier_semaphore()
        for device in devices:
            pl.semaphore_signal(
                barrier, inc=1, device_id=device, device_id_type=pl.DeviceIdType.MESH
            )
        pl.semaphore_wait(barrier, len(devices))

    def close(self):
        for wait in self.pending:
            wait()


def row_spans(total, pieces):
    size = total // pieces
    return [pl.ds(i * size, size) for i in range(pieces)]


class Fetch:
    def __init__(self, wires, shard, target, stage, pieces, got=None, keep=None):
        w = self.wires = wires
        self.shard, self.target, self.stage, self.got, self.keep = shard, target, stage, got, keep
        self.count = pieces
        self.half_rows = shard.shape[0] // 2
        self.size = self.half_rows // pieces
        self.by_columns = len(target.shape) == 2
        self.first = [w.slot() for _ in range(pieces)]
        self.over = [w.slot() for _ in range(pieces)]
        self.second = [w.slot() for _ in range(2 * pieces)]
        self.local_slot = w.local_used
        w.local_used += 2

    def rows(self, i, mine=True):
        bit = self.wires.o % 2
        bit = bit if mine else 1 - bit
        return pl.ds(pl.multiple_of(bit * self.half_rows + i * self.size, 16), self.size)

    def place(self, half, span):
        if self.by_columns:
            width = self.shard.shape[1]
            return self.target.at[span, pl.ds(half * width, width)]
        return self.target.at[half, span]

    def first_copy(self, i, home):
        w, span = self.wires, self.rows(i)
        if home:
            return w.copy(self.shard.at[span], self.place(1, span), {"x": 1 - w.x}, self.first[i])
        device = {"k": 1 - w.k, "h": 1 - w.h}
        return w.copy(self.shard.at[span], self.place(0, span), device, self.first[i])

    def have(self, i, half):
        if self.got is None:
            return self.place(half, self.rows(i))
        return self.got.at[pl.ds(i * self.size, self.size)]

    def over_copy(self, i, home):
        w, half = self.wires, 1 if home else 0
        return w.copy(self.have(i, half), self.place(half, self.rows(i)), {"o": w.o ^ 1}, self.over[i])

    def second_copy(self, i, mine):
        w, span = self.wires, self.rows(i, mine)
        source = self.have(i, 0) if mine else self.place(0, span)
        slot = self.second[i if mine else self.count + i]
        return w.copy(source, self.place(1, span), {"x": 1 - w.x}, slot)

    def shard_load(self):
        return pltpu.make_async_copy(self.shard, self.stage, self.wires.local_sem.at[self.local_slot])

    def shard_store(self):
        whole = pl.ds(0, self.shard.shape[0])
        return pltpu.make_async_copy(
            self.stage, self.place(0, whole), self.wires.local_sem.at[self.local_slot]
        )

    def got_load(self):
        return pltpu.make_async_copy(self.got, self.keep, self.wires.local_sem.at[self.local_slot + 1])

    def got_store(self, half):
        bit = self.wires.o % 2
        span = pl.ds(pl.multiple_of(bit * self.half_rows, 16), self.half_rows)
        return pltpu.make_async_copy(
            self.keep, self.place(half, span), self.wires.local_sem.at[self.local_slot + 1]
        )

    def either(self, at_home, away):
        pl.when(self.wires.home)(at_home)
        pl.when(jnp.logical_not(self.wires.home))(away)

    def load(self):
        pl.when(self.wires.home)(lambda: self.shard_load().start())
        if self.got is not None:
            self.got_load().start()

    def start(self):
        if self.got is not None:
            for i in range(self.count):
                self.relay(i)
            return

        def go(home):
            for i in range(self.count):
                self.first_copy(i, home).start()

        self.either(lambda: go(True), lambda: go(False))

    def store(self):
        def at_home():
            self.shard_load().wait()
            self.shard_store().start()
            if self.got is not None:
                self.got_load().wait()
                self.got_store(1).start()

        def away():
            if self.got is not None:
                self.got_load().wait()
                self.got_store(0).start()

        self.either(at_home, away)

    def relay(self, i):
        def at_home():
            if self.got is None:
                self.first_copy(i, True).wait_recv()
            self.over_copy(i, True).start()

        def away():
            if self.got is None:
                self.first_copy(i, False).wait_recv()
            self.over_copy(i, False).start()
            self.second_copy(i, True).start()

        self.either(at_home, away)

    def relay_over(self, i):
        def away():
            self.over_copy(i, False).wait_recv()
            self.second_copy(i, False).start()

        pl.when(jnp.logical_not(self.wires.home))(away)

    def wait(self):
        def at_home():
            for i in range(self.count):
                if self.got is None:
                    self.first_copy(i, True).wait_send()
                self.over_copy(i, True).wait()
            self.shard_store().wait()
            if self.got is not None:
                self.got_store(1).wait()

        def away():
            for i in range(self.count):
                if self.got is None:
                    self.first_copy(i, False).wait_send()
                self.over_copy(i, False).wait_send()
                self.second_copy(i, True).wait()
                self.second_copy(i, False).wait()
            if self.got is not None:
                self.got_store(0).wait()

        self.either(at_home, away)


def partners(wires, psize, away=False, peers=True, over_o=0):
    devices = [{"k": 1 - wires.k}]
    if peers:
        devices += [{"p": wires.p ^ bit} for bit in range(1, psize)]
    devices += [{"x": 1 - wires.x}]
    devices += [{"k": 1 - wires.k, "x": 1 - wires.x}]
    if away:
        devices += [{"k": 1 - wires.k, "h": 1 - wires.h}, {"h": 1 - wires.h}]
    bit = 1
    while bit < over_o:
        devices += [{"o": wires.o ^ bit}]
        bit *= 2
    return devices


class Share:
    def __init__(self, wires, psize, own, g, spans):
        self.wires, self.psize, self.own, self.g, self.spans = wires, psize, own, g, spans
        self.near, self.far, self.kept, self.passed = [], {}, [], []

    def send(self, i):
        w, span = self.wires, self.spans[i]
        for bit in range(1, self.psize):
            self.far[bit, i] = w.send(self.own.at[span], self.g.at[2 * bit, span], {"p": w.p ^ bit})
        self.near.append(w.send(self.own.at[span], self.g.at[1, span], {"k": 1 - w.k}))
        self.kept.append(w.local(self.own.at[span], self.g.at[0, span]))

    def relay(self, i):
        w, span = self.wires, self.spans[i]
        for bit in range(1, self.psize):
            self.far[bit, i].wait_recv()
            self.passed.append(
                w.send(self.g.at[2 * bit, span], self.g.at[2 * bit + 1, span], {"k": 1 - w.k})
            )

    def wait(self):
        for copy in self.near + self.passed:
            copy.wait_recv()
        for copy in self.kept:
            copy.wait()


class Reduce:
    def __init__(self, wires, psize, part, near, mid, far, spans):
        self.wires, self.psize, self.part = wires, psize, part
        self.near, self.mid, self.far, self.spans = near, mid, far, spans
        self.near_copies, self.far_copies = {}, {}

    def start(self):
        w = self.wires
        for bit in reversed(range(self.psize)):
            for i, span in enumerate(self.spans):
                self.near_copies[bit, i] = w.send(
                    self.part.at[2 * bit + 1, span], self.near.at[bit, span], {"k": 1 - w.k}
                )
        for bit in reversed(range(1, self.psize)):
            for i, span in enumerate(self.spans):
                self.near_copies[bit, i].wait_recv()
                self.mid[bit - 1, span] = (
                    self.part[2 * bit, span].astype(F32) + self.near[bit, span].astype(F32)
                ).astype(BF16)
                self.far_copies[bit, i] = w.send(
                    self.mid.at[bit - 1, span], self.far.at[bit - 1, span], {"p": w.p ^ bit}
                )

    def rows(self, i):
        span = self.spans[i]
        self.near_copies[0, i].wait_recv()
        total = self.part[0, span].astype(F32) + self.near[0, span].astype(F32)
        for bit in range(1, self.psize):
            self.far_copies[bit, i].wait_recv()
            total = total + self.far[bit - 1, span].astype(F32)
        return total


PIECES = 3


def inverse_rms(value):
    return lax.rsqrt(jnp.sum(value * value, axis=1, keepdims=True) / D + EPS)


def norm_back(grad, value, base, gain):
    rms = inverse_rms(value)
    gained = gain * grad
    inner = jnp.sum(value * gained, axis=1, keepdims=True)
    result = base + rms * gained - value * (rms * rms * rms) * inner / D
    return result, jnp.sum(grad * value * rms, axis=0, keepdims=True)


def enter_kernel(
    psize, x_ref, gain_ref, qkv_shard, forget_shard, out_shard, xin, g, proj, out,
    own, qkv_stage, forget_stage, out_stage, send_sem, recv_sem, local_sem,
):
    w = Wires(send_sem, recv_sem, local_sem)
    width = qkv_shard.shape[1]
    qkv = Fetch(w, qkv_shard, proj.at[:, :, pl.ds(0, width)], qkv_stage, 3)
    forget = Fetch(
        w, forget_shard, proj.at[:, :, pl.ds(width, forget_shard.shape[1])], forget_stage, 1
    )
    out_fetch = Fetch(w, out_shard, out, out_stage, 1)
    for fetch in (qkv, forget, out_fetch):
        fetch.load()
    w.greet(partners(w, psize, away=True, over_o=2))
    rows, half = own.shape[0], x_ref.shape[1]
    spans = row_spans(rows, PIECES)
    size = rows // PIECES
    def spread(source, target, pieces):
        count = len(pieces)
        to_near = [w.slot() for _ in pieces]
        to_far = [w.slot() for _ in pieces]
        kept = [w.local_used + i for i in range(count)]
        w.local_used += count

        def piece(base, i):
            start, length = pieces[i]
            return source.at[pl.ds(pl.multiple_of(base * rows + start, 8), length)]

        def span(i):
            return pl.ds(pieces[i][0], pieces[i][1])

        left, right = pl.ds(0, half), pl.ds(half, half)

        def same_keep(i):
            return pltpu.make_async_copy(piece(w.k, i), target.at[span(i), left], local_sem.at[kept[i]])

        def same_send(i):
            return w.copy(piece(1 - w.k, i), target.at[span(i), left], {"k": 1 - w.k}, to_near[i])

        def cross_near(i):
            return w.copy(piece(w.k, i), target.at[span(i), right], {"x": 1 - w.x}, to_near[i])

        def cross_far(i):
            return w.copy(
                piece(1 - w.k, i), target.at[span(i), right], {"k": 1 - w.k, "x": 1 - w.x}, to_far[i]
            )

        def start():
            @pl.when(w.same)
            def _():
                for i in range(count):
                    same_send(i).start()
                    same_keep(i).start()

            @pl.when(jnp.logical_not(w.same))
            def _():
                for i in range(count):
                    cross_near(i).start()
                    cross_far(i).start()

        def arrive(i):
            @pl.when(w.same)
            def _():
                same_keep(i).wait()
                same_send(i).wait_recv()

            @pl.when(jnp.logical_not(w.same))
            def _():
                cross_near(i).wait_recv()
                cross_far(i).wait_recv()

        def close():
            @pl.when(w.same)
            def _():
                for i in range(count):
                    same_send(i).wait_send()

            @pl.when(jnp.logical_not(w.same))
            def _():
                for i in range(count):
                    cross_near(i).wait_send()
                    cross_far(i).wait_send()

        return start, arrive, close

    start, arrive, close = spread(x_ref, xin, [(i * size, size) for i in range(PIECES)])
    start()
    qkv.start()
    forget.start()
    share = Share(w, psize, own, g, spans)
    gain = gain_ref[0:1, :]
    for i, span in enumerate(spans):
        arrive(i)
        value = xin[span, :].astype(F32)
        own[span, :] = (value * inverse_rms(value) * gain).astype(BF16)
        share.send(i)
    close()
    for fetch in (qkv, forget, out_fetch):
        fetch.store()
    for i in range(3):
        qkv.relay(i)
    out_fetch.start()
    forget.relay(0)
    for i in range(3):
        qkv.relay_over(i)
        if i < PIECES:
            share.relay(i)
    forget.relay_over(0)
    out_fetch.relay(0)
    out_fetch.relay_over(0)
    share.wait()
    for fetch in (qkv, forget, out_fetch):
        fetch.wait()
    w.close()


def forward_exchange_kernel(
    psize, part, xin, gain_ref, gate_shard, gate_got, up_shard, up_got, down_shard, resid, g, gate, up, down,
    near, mid, far, own, gate_stage, gate_keep, up_stage, up_keep, down_stage, send_sem, recv_sem, local_sem,
):
    w = Wires(send_sem, recv_sem, local_sem)
    gate_fetch = Fetch(w, gate_shard, gate, gate_stage, 2, gate_got, gate_keep)
    up_fetch = Fetch(w, up_shard, up, up_stage, 2, up_got, up_keep)
    down_fetch = Fetch(w, down_shard, down, down_stage, 2)
    fetches = (gate_fetch, up_fetch, down_fetch)
    for fetch in fetches:
        fetch.load()
    w.greet(partners(w, psize, away=True, over_o=2))
    spans = row_spans(own.shape[0], PIECES)
    reduce = Reduce(w, psize, part, near, mid, far, spans)
    gate_fetch.start()
    reduce.start()
    up_fetch.start()
    down_fetch.start()
    for fetch in fetches:
        fetch.store()
    gate_fetch.relay_over(0)
    gate_fetch.relay_over(1)
    share = Share(w, psize, own, g, spans)
    gain = gain_ref[1:2, :]
    for i, span in enumerate(spans):
        value = reduce.rows(i) + xin[span, :].astype(F32)
        resid[span, :] = value
        own[span, :] = (value * inverse_rms(value) * gain).astype(BF16)
        share.send(i)
    for i in range(2):
        up_fetch.relay_over(i)
        down_fetch.relay(i)
    for i in range(PIECES):
        share.relay(i)
    for i in range(2):
        down_fetch.relay_over(i)
    share.wait()
    for fetch in fetches:
        fetch.wait()
    w.close()


class EarlySum:
    def __init__(self, wires, part, value, over, across, result, pieces):
        w = self.wires = wires
        self.part, self.value, self.over, self.across, self.result = part, value, over, across, result
        self.count, self.half_rows = pieces, value.shape[1]
        self.size = self.half_rows // pieces
        self.over_slots = [[w.slot() for _ in range(pieces)] for _ in range(2)]
        self.across_slots = [w.slot() for _ in range(pieces)]
        self.local_slot = w.local_used
        w.local_used += 2 + pieces

    def span(self, i):
        return pl.ds(i * self.size, self.size)

    def load_copy(self, half):
        start = pl.multiple_of((self.wires.o % 2) * self.half_rows, 16)
        return pltpu.make_async_copy(
            self.part.at[half, pl.ds(start, self.half_rows)],
            self.value.at[half],
            self.wires.local_sem.at[self.local_slot + half],
        )

    def load(self):
        for half in range(2):
            self.load_copy(half).start()

    def over_copy(self, half, i):
        w = self.wires
        start = pl.multiple_of((1 - w.o % 2) * self.half_rows + i * self.size, 16)
        return w.copy(
            self.part.at[half, pl.ds(start, self.size)],
            self.over.at[half, self.span(i)],
            {"o": w.o ^ 1},
            self.over_slots[half][i],
        )

    def across_copy(self, i):
        w = self.wires
        return w.copy(
            self.value.at[1, self.span(i)], self.across.at[self.span(i)], {"x": 1 - w.x}, self.across_slots[i]
        )

    def keep_copy(self, i):
        return pltpu.make_async_copy(
            self.value.at[0, self.span(i)],
            self.result.at[self.span(i)],
            self.wires.local_sem.at[self.local_slot + 2 + i],
        )

    def start(self, half):
        for i in range(self.count):
            self.over_copy(half, i).start()

    def pass_on(self, i):
        if i == 0:
            self.load_copy(1).wait()
        self.over_copy(1, i).wait_recv()
        span = self.span(i)
        self.value[1, span] = (
            self.value[1, span].astype(F32) + self.over[1, span].astype(F32)
        ).astype(BF16)
        self.across_copy(i).start()

    def finish(self, i):
        if i == 0:
            self.load_copy(0).wait()
        self.over_copy(0, i).wait_recv()
        self.across_copy(i).wait_recv()
        span = self.span(i)
        total = self.value[0, span].astype(F32) + self.over[0, span].astype(F32)
        self.value[0, span] = (total + self.across[span].astype(F32)).astype(BF16)
        self.keep_copy(i).start()

    def close(self):
        for i in range(self.count):
            for half in range(2):
                self.over_copy(half, i).wait_send()
            self.across_copy(i).wait_send()
            self.keep_copy(i).wait()


def backward_exchange_kernel(
    psize, part, resid, cot, gain_ref, down_own, down_other, gate_part, up_part,
    grad_resid, g, gain_grad, down_sum, gate_sum, up_sum,
    near, mid, far, own, down_across, gate_val, gate_over, gate_across, up_val, up_over, up_across,
    send_sem, recv_sem, local_sem,
):
    w = Wires(send_sem, recv_sem, local_sem)
    gate = EarlySum(w, gate_part, gate_val, gate_over, gate_across, gate_sum, 2)
    up = EarlySum(w, up_part, up_val, up_over, up_across, up_sum, 2)
    gate.load()
    up.load()
    w.greet(partners(w, psize, over_o=2))
    spans = row_spans(own.shape[0], PIECES)
    reduce = Reduce(w, psize, part, near, mid, far, spans)
    down_copy = w.send(down_other, down_across, {"x": 1 - w.x})
    gate.start(1)
    up.start(1)
    reduce.start()
    gate.start(0)
    up.start(0)
    for i in range(2):
        gate.pass_on(i)
    share = Share(w, psize, own, g, spans)
    gain = gain_ref[1:2, :]
    gain_sum = jnp.zeros((1, D), F32)
    for i, span in enumerate(spans):
        grad, gain_part = norm_back(reduce.rows(i), resid[span, :], cot[span, :].astype(F32), gain)
        grad_resid[span, :] = grad
        own[span, :] = grad.astype(BF16)
        gain_sum = gain_sum + gain_part
        share.send(i)
    gain_grad[...] = jnp.broadcast_to(gain_sum, gain_grad.shape)
    for i in range(2):
        up.pass_on(i)
    down_copy.wait_recv()
    down_sum[...] = (down_own[...].astype(F32) + down_across[...].astype(F32)).astype(BF16)
    share.relay(0)
    for i in range(2):
        gate.finish(i)
    for i in range(1, PIECES):
        share.relay(i)
    for i in range(2):
        up.finish(i)
    share.wait()
    gate.close()
    up.close()
    w.close()


class Spread:
    def __init__(self, wires, value, result):
        w = self.wires = wires
        self.value, self.result = value, result
        self.over_slot, self.near_slot, self.pass_slot = w.slot(), w.slot(), w.slot()
        self.local_slot = w.local_used
        w.local_used += 1

    def rows(self, mine):
        bit = self.wires.o % 2
        return self.result.at[bit if mine else 1 - bit]

    def over_copy(self):
        w = self.wires
        return w.copy(self.value, self.rows(True), {"o": w.o ^ 1}, self.over_slot)

    def near_copy(self):
        return self.wires.copy(self.value, self.rows(True), {"k": 1 - self.wires.k}, self.near_slot)

    def pass_copy(self):
        return self.wires.copy(self.rows(False), self.rows(False), {"k": 1 - self.wires.k}, self.pass_slot)

    def keep_copy(self):
        return pltpu.make_async_copy(
            self.value, self.rows(True), self.wires.local_sem.at[self.local_slot]
        )

    def start(self):
        @pl.when(self.wires.home)
        def _():
            self.over_copy().start()
            self.near_copy().start()
            self.keep_copy().start()

    def relay(self):
        @pl.when(self.wires.home)
        def _():
            self.over_copy().wait_recv()
            self.pass_copy().start()

    def wait(self):
        @pl.when(self.wires.home)
        def _():
            self.over_copy().wait_send()
            self.near_copy().wait_send()
            self.pass_copy().wait_send()
            self.keep_copy().wait()

        @pl.when(jnp.logical_not(self.wires.home))
        def _():
            self.near_copy().wait_recv()
            self.pass_copy().wait_recv()


class SmallSum:
    def __init__(self, wires, psize, osize, value, other, buffers):
        w = self.wires = wires
        self.value, self.other, self.buffers = value, other, buffers
        self.devices = [{"x": 1 - w.x}, {"k": 1 - w.k}]
        self.devices += [{"p": w.p ^ bit} for bit in bits_of(psize)]
        self.devices += [{"h": 1 - w.h}]
        self.devices += [{"o": w.o ^ bit} for bit in bits_of(osize)]
        self.slots = [w.slot() for _ in self.devices]

    def copy(self, step):
        source = self.other if step == 0 else self.value
        return self.wires.copy(source, self.buffers.at[step], self.devices[step], self.slots[step])

    def start(self):
        self.copy(0).start()

    def step(self, step):
        self.copy(step).wait()
        self.value[...] = self.value[...] + self.buffers[step]
        if step + 1 < len(self.devices):
            self.copy(step + 1).start()


class Chain:
    def __init__(self, wires, osize, value, stages, buffers, result, pieces):
        self.wires, self.value, self.stages, self.result = wires, value, stages, result
        self.buffers = buffers
        self.spans = row_spans(value.shape[0], pieces)
        self.slots = [[wires.slot() for _ in self.spans] for _ in stages]
        self.kept = [wires.local_used + i for i in range(pieces)]
        wires.local_used += pieces
        self.other = None

    def copy(self, stage, i):
        w, span = self.wires, self.spans[i]
        kind, slot = self.stages[stage], self.slots[stage][i]
        if kind == "x":
            return w.copy(self.other.at[span], self.buffers[stage].at[span], {"x": 1 - w.x}, slot)
        if kind == "h":
            return w.copy(self.value.at[span], self.buffers[stage].at[span], {"h": 1 - w.h}, slot)
        if kind == "k":
            return w.copy(self.value.at[span], self.result.at[span], {"k": 1 - w.k}, slot)
        return w.copy(self.value.at[span], self.buffers[stage].at[span], {"o": w.o ^ kind}, slot)

    def keep(self, i):
        span = self.spans[i]
        return pltpu.make_async_copy(
            self.value.at[span], self.result.at[span], self.wires.local_sem.at[self.kept[i]]
        )

    def start(self, stage, i):
        w, kind = self.wires, self.stages[stage]
        if kind == "x":
            self.copy(stage, i).start()
        elif kind == "h":
            @pl.when(jnp.logical_not(w.home))
            def _():
                self.copy(stage, i).start()
        else:
            @pl.when(w.home)
            def _():
                self.copy(stage, i).start()
                if kind == "k":
                    self.keep(i).start()

    def add(self, stage, i):
        span = self.spans[i]
        self.value[span, :] = (
            self.value[span, :].astype(F32) + self.buffers[stage][span, :].astype(F32)
        ).astype(BF16)

    def end(self, stage, i):
        w, kind = self.wires, self.stages[stage]
        if kind == "x":
            self.copy(stage, i).wait_recv()
            self.add(stage, i)
        elif kind == "h":
            @pl.when(w.home)
            def _():
                self.copy(stage, i).wait_recv()
                self.add(stage, i)
        elif kind == "k":
            @pl.when(w.home)
            def _():
                self.copy(stage, i).wait_send()
                self.keep(i).wait()

            @pl.when(jnp.logical_not(w.home))
            def _():
                self.copy(stage, i).wait_recv()
        else:
            @pl.when(w.home)
            def _():
                self.copy(stage, i).wait()
                self.add(stage, i)

    def close(self):
        w = self.wires
        for stage, kind in enumerate(self.stages):
            for i in range(len(self.spans)):
                if kind == "x":
                    self.copy(stage, i).wait_send()
                elif kind == "h":
                    @pl.when(jnp.logical_not(w.home))
                    def _():
                        self.copy(stage, i).wait_send()

    def step(self, stage, i):
        self.end(stage, i)
        if stage + 1 < len(self.stages):
            self.start(stage + 1, i)

    def order(self, first=0):
        return [(stage, i) for stage in range(first, len(self.stages)) for i in range(len(self.spans))]

    def run(self, first=0):
        for stage, i in self.order(first):
            self.step(stage, i)


def leave_kernel(
    psize, osize, proj_pieces, part, stream, base, gain_ref, small_in, proj_own, proj_other, out_own, out_other,
    up_in, gate_in, down_in, block, small, proj_sum, out_sum, up_sum, gate_sum, down_sum,
    near, mid, far, kept, proj_val, out_val, up_val, gate_val, down_val, proj_bufs, out_bufs, small_other, small_bufs,
    send_sem, recv_sem, local_sem,
):
    w = Wires(send_sem, recv_sem, local_sem)
    loads = [
        w.local(source, target)
        for source, target in (
            (up_in, up_val), (gate_in, gate_val), (down_in, down_val), (out_own, out_val), (proj_own, proj_val)
        )
    ]
    w.greet(partners(w, psize, away=True, over_o=osize))
    rows, half = kept.shape[1], kept.shape[2]
    spans = row_spans(rows, PIECES)
    size = rows // PIECES
    bits = bits_of(osize)

    proj = Chain(
        w, osize, proj_val, ["x", "h"] + bits + ["k"], [proj_bufs.at[i] for i in range(2 + len(bits))],
        proj_sum, proj_pieces,
    )
    proj.other = proj_other
    out = Chain(w, osize, out_val, ["x", "h"] + bits[1:], [out_bufs.at[i] for i in range(1 + len(bits))], None, 1)
    out.other = out_other
    out_spread = Spread(w, out_val, out_sum)
    spreads = [Spread(w, up_val, up_sum), Spread(w, gate_val, gate_sum), Spread(w, down_val, down_sum)]
    reduce = Reduce(w, psize, part, near, mid, far, spans)
    out.start(0, 0)
    for i in range(proj_pieces):
        proj.start(0, i)
    for load in loads:
        load.wait()
    for spread in spreads:
        spread.start()
    reduce.start()

    near_slots = [w.slot() for _ in spans]
    far_slots = [w.slot() for _ in spans]
    keep_slots = [w.local_used + i for i in range(PIECES)]
    w.local_used += PIECES

    def target(i):
        return block.at[pl.ds(pl.multiple_of(w.k * rows + i * size, 8), size)]

    def same_keep(i):
        return pltpu.make_async_copy(kept.at[0, spans[i]], target(i), local_sem.at[keep_slots[i]])

    def same_send(i):
        return w.copy(kept.at[1, spans[i]], target(i), {"x": 1 - w.x}, near_slots[i])

    def cross_near(i):
        return w.copy(kept.at[0, spans[i]], target(i), {"k": 1 - w.k}, near_slots[i])

    def cross_far(i):
        return w.copy(kept.at[1, spans[i]], target(i), {"k": 1 - w.k, "x": 1 - w.x}, far_slots[i])

    out.step(0, 0)
    for i in range(proj_pieces):
        proj.step(0, i)
    gain = gain_ref[0:1, :]
    gain_sum = jnp.zeros((1, D), F32)
    for i, span in enumerate(spans):
        grad, gain_part = norm_back(reduce.rows(i), stream[span, :].astype(F32), base[span, :], gain)
        gain_sum = gain_sum + gain_part
        kept[0, span, :] = grad[:, :half].astype(BF16)
        kept[1, span, :] = grad[:, half:].astype(BF16)

        @pl.when(w.same)
        def _():
            same_send(i).start()
            same_keep(i).start()

        @pl.when(jnp.logical_not(w.same))
        def _():
            cross_near(i).start()
            cross_far(i).start()

    row = lax.broadcasted_iota(jnp.int32, (8, half), 0)
    small[...] = jnp.where(row == 0, gain_sum[:, :half], small_in[:, :half])
    small_other[...] = jnp.where(row == 0, gain_sum[:, half:], small_in[:, half:])
    total = SmallSum(w, psize, osize, small, small_other, small_bufs)
    total.start()
    out.run(1)
    out_spread.start()
    for spread in spreads:
        spread.relay()
    smalls = list(range(len(total.devices)))
    for n, (stage, i) in enumerate(proj.order(1)):
        proj.step(stage, i)
        if n % 2 and smalls:
            total.step(smalls.pop(0))
    for step in smalls:
        total.step(step)
    out_spread.relay()
    for spread in spreads + [out_spread]:
        spread.wait()
    for i in range(PIECES):
        @pl.when(w.same)
        def _():
            same_keep(i).wait()
            same_send(i).wait_send()
            cross_near(i).wait_recv()

        @pl.when(jnp.logical_not(w.same))
        def _():
            cross_near(i).wait_send()
            cross_far(i).wait()
            same_send(i).wait_recv()

    proj.close()
    out.close()
    w.close()


ANY = pl.BlockSpec(memory_space=pl.ANY)
VMEM = pl.BlockSpec(memory_space=pltpu.VMEM)
SLOTS = 128


def exchange_call(kernel, name, collective_id, outs, out_specs, in_specs, scratch, args):
    return pl.pallas_call(
        kernel,
        out_shape=outs,
        in_specs=in_specs,
        out_specs=out_specs,
        scratch_shapes=scratch
        + [
            pltpu.SemaphoreType.DMA((SLOTS,)),
            pltpu.SemaphoreType.DMA((SLOTS,)),
            pltpu.SemaphoreType.DMA((SLOTS // 2,)),
        ],
        compiler_params=pltpu.CompilerParams(
            collective_id=collective_id, has_side_effects=True, vmem_limit_bytes=56 << 20
        ),
        name=name,
    )(*args)


def sds(shape, dtype):
    return jax.ShapeDtypeStruct(shape, dtype)


def sum_scratch(psize, rows):
    far = max(psize - 1, 1)
    return [
        pltpu.VMEM((psize, rows, D), BF16),
        pltpu.VMEM((far, rows, D), BF16),
        pltpu.VMEM((far, rows, D), BF16),
    ]


def enter(psize, layer_input, gains, qkv_weight, forget_weight, out_weight):
    rows = layer_input.shape[0] // 2
    half, width = qkv_weight.shape
    columns = width + forget_weight.shape[1]
    return exchange_call(
        functools.partial(enter_kernel, psize),
        "enter",
        1,
        (
            sds((rows, D), BF16),
            sds((2 * psize, rows, D), BF16),
            sds((2, half, columns), BF16),
            sds((out_weight.shape[0], 2 * half), BF16),
        ),
        (VMEM, ANY, ANY, ANY),
        [ANY, VMEM, ANY, ANY, ANY],
        [pltpu.VMEM((rows, D), BF16)]
        + [pltpu.VMEM(value.shape, BF16) for value in (qkv_weight, forget_weight, out_weight)],
        (layer_input, gains, qkv_weight, forget_weight, out_weight),
    )


def forward_exchange(psize, part, xin, gains, gate_weight, gate_got, up_weight, up_got, down_weight):
    rows = xin.shape[0]
    return exchange_call(
        functools.partial(forward_exchange_kernel, psize),
        "forward_exchange",
        2,
        (
            sds((rows, D), F32),
            sds((2 * psize, rows, D), BF16),
            sds((2,) + gate_weight.shape, BF16),
            sds((2,) + up_weight.shape, BF16),
            sds((down_weight.shape[0], D), BF16),
        ),
        (VMEM, ANY, ANY, ANY, ANY),
        [VMEM, VMEM, VMEM, ANY, ANY, ANY, ANY, ANY],
        sum_scratch(psize, rows)
        + [pltpu.VMEM((rows, D), BF16)]
        + [
            pltpu.VMEM(value.shape, BF16)
            for value in (gate_weight, gate_got, up_weight, up_got, down_weight)
        ],
        (part, xin, gains, gate_weight, gate_got, up_weight, up_got, down_weight),
    )


def backward_exchange(psize, part, resid, cot, gains, down_own, down_other, gate_part, up_part):
    rows = resid.shape[0]

    def early(value):
        half_rows = value.shape[1] // 2
        shape = (half_rows, value.shape[2])
        return [
            pltpu.VMEM((2,) + shape, BF16),
            pltpu.VMEM((2,) + shape, BF16),
            pltpu.VMEM(shape, BF16),
        ]

    def kept(value):
        return sds((value.shape[1] // 2, value.shape[2]), BF16)

    return exchange_call(
        functools.partial(backward_exchange_kernel, psize),
        "backward_exchange",
        3,
        (
            sds((rows, D), F32),
            sds((2 * psize, rows, D), BF16),
            sds((8, D), F32),
            sds(down_own.shape, BF16),
            kept(gate_part),
            kept(up_part),
        ),
        (VMEM, ANY, VMEM, VMEM, ANY, ANY),
        [VMEM, VMEM, VMEM, VMEM, VMEM, ANY, ANY, ANY],
        sum_scratch(psize, rows)
        + [pltpu.VMEM((rows, D), BF16), pltpu.VMEM(down_own.shape, BF16)]
        + early(gate_part)
        + early(up_part),
        (part, resid, cot, gains, down_own, down_other, gate_part, up_part),
    )


def leave(psize, osize, part, stream, base, gains, small, proj_own, proj_other, out_own, out_other, up, gate, down):
    rows = stream.shape[0]
    bits = len(bits_of(osize))
    half = D // 2

    def buffers(count, value):
        return pltpu.VMEM((count,) + value.shape, BF16)

    def both(value):
        return sds((2,) + value.shape, BF16)

    return exchange_call(
        functools.partial(leave_kernel, psize, osize, 6),
        "leave",
        4,
        (
            sds((2 * rows, half), BF16),
            sds((8, half), F32),
            sds(proj_own.shape, BF16),
            both(out_own),
            both(up),
            both(gate),
            both(down),
        ),
        (ANY, VMEM, ANY, ANY, ANY, ANY, ANY),
        [VMEM] * 5 + [ANY] * 7,
        sum_scratch(psize, rows)
        + [pltpu.VMEM((2, rows, half), BF16)]
        + [pltpu.VMEM(value.shape, BF16) for value in (proj_own, out_own, up, gate, down)]
        + [buffers(2 + bits, proj_own), buffers(1 + bits, out_own)]
        + [pltpu.VMEM((8, half), F32), pltpu.VMEM((3 + len(bits_of(psize)) + bits, 8, half), F32)],
        (part, stream, base, gains, small, proj_own, proj_other, out_own, out_other, up, gate, down),
    )


def make_shards(osize, psize):
    count = 2 * psize
    obits = bits_of(osize)

    def shards(
        layer_input,
        attn_gain,
        qkv_weight,
        forget_weight,
        forget_bias,
        out_weight,
        ffn_gain,
        gate_weight,
        up_weight,
        down_weight,
        prompt_doc,
        branch_seg,
        branch_doc,
        out_cotangent,
    ):
        core, xpos = lax.axis_index("k"), lax.axis_index("x")
        hpos, ppos, opos = lax.axis_index("h"), lax.axis_index("p"), lax.axis_index("o")
        home = core == hpos
        same = core == xpos
        heads = forget_weight.shape[1]
        width = heads * 3 * DH
        lane_pad = LANES - heads
        feat = D // 2

        def far_blocks(block):
            return [xor_swap(block, "p", psize, bit) for bit in range(1, psize)]

        def all_blocks(block, far):
            blocks = []
            for near in [block] + far:
                blocks += [near, swap(near, "k")]
            return jnp.concatenate(blocks, axis=0)

        def near_sums(partial):
            size = partial.shape[0] // count
            parts = [partial[i * size : (i + 1) * size] for i in range(count)]
            moved = [swap(parts[i + 1], "k") for i in range(0, count, 2)]
            return [add_parts(parts[i], moved[i // 2]) for i in range(0, count, 2)]

        def far_sums(sums):
            return [xor_swap(sums[bit], "p", psize, bit) for bit in range(1, psize)]

        def total_of(near, far):
            total = near.astype(F32)
            for value in far:
                total = total + value.astype(F32)
            return total

        prompt_len, branch_len = prompt_doc.shape[1], branch_seg.shape[1]
        packed = jnp.concatenate([prompt_doc[0], branch_seg[0], branch_doc[0]])
        sibling = swap(packed, "k")
        of_x = jnp.where(core == xpos, packed, sibling)
        of_peer = jnp.where(core == xpos, sibling, packed)
        from_peer = swap(of_peer, "x")
        packed = jnp.where(hpos == xpos, of_x, from_peer)
        prompt_ids = packed[:prompt_len]
        branch_ids = packed[prompt_len : prompt_len + branch_len]
        branch_docs = packed[prompt_len + branch_len :]
        gains = jnp.stack([attn_gain, ffn_gain])
        gains = jnp.concatenate([gains, swap(gains, "x")], axis=1)
        gain_a, gain_b = gains[0], gains[1]
        bias = jnp.where(home, forget_bias, lax.ppermute(forget_bias, ("k", "h"), [(1, 2), (2, 1)]))
        bias = jnp.concatenate([bias, jnp.zeros((lane_pad,), F32)])
        kcol, qrow, flags = group_codes(prompt_ids, branch_ids, branch_docs)

        gains8 = jnp.concatenate([gains, jnp.zeros((6, D), F32)])
        forget_wide = jnp.concatenate(
            [forget_weight, jnp.zeros((forget_weight.shape[0], lane_pad), BF16)], axis=1
        )
        first_part, second_part = qkv_weight, forget_wide
        if width % LANES:
            spare = jnp.zeros((qkv_weight.shape[0], LANES - width % LANES), BF16)
            first_part = jnp.concatenate([qkv_weight, forget_wide, spare], axis=1)
        xin, normed_a_all, w_proj, w_out = enter(
            psize, layer_input, gains8, first_part, second_part, out_weight
        )
        normed_a_all = normed_a_all.reshape(-1, D)
        w_proj = w_proj.reshape(D, -1)[:, : width + LANES]

        projected = matmul(normed_a_all, w_proj)
        qkv = projected[:, :width].astype(BF16).reshape(count, -1, width)
        logit = (projected[:, width:] + bias).reshape(count, -1, LANES)
        qkv, logit = lax.optimization_barrier((qkv, logit))
        gate_got = fetch_home_away(tie(take_half(gate_weight, opos % 2), qkv))
        up_got = fetch_home_away(tie(take_half(up_weight, opos % 2), qkv))
        cot = spread_tokens(tie(out_cotangent, qkv), core, same)
        attended, *saved = attention_forward(qkv, logit, kcol, qrow, flags, heads, prompt_len)
        attended = tie(attended.reshape(-1, heads * DH), gate_got, up_got, cot)
        part = matmul(attended, w_out).astype(BF16).reshape(count, -1, D)
        resid, normed_b_all, w_gate, w_up, w_down = forward_exchange(
            psize, part, xin, gains8, gate_weight, gate_got, up_weight, up_got, down_weight
        )
        normed_b_all = normed_b_all.reshape(-1, D)
        w_gate, w_up = w_gate.reshape(D, -1), w_up.reshape(D, -1)
        cot_far = far_blocks(tie(cot, normed_b_all))
        gate_pre = matmul(normed_b_all, w_gate)
        up_pre = matmul(normed_b_all, w_up)
        gate_sig = jax.nn.sigmoid(gate_pre)
        gate_act = gate_pre * gate_sig
        hidden = (gate_act * up_pre).astype(BF16)
        hidden = tie(hidden, *cot_far)
        cot_all = all_blocks(cot, cot_far)

        def finish(total, axis_bits):
            for bit in axis_bits:
                total = add_parts(total, home_swap(total, osize, bit))
            return total

        high = opos % 2 == 1
        down_part = contract_rows(hidden, cot_all).astype(BF16)
        down_keep, down_give = split_rows(down_part, high)
        down_moved = xor_swap(down_give, "o", osize, 1)
        out_sums = near_sums(matmul(hidden, w_down).astype(BF16))
        out_far = far_sums(out_sums)
        grad_hidden = contract_cols(tie(cot_all, out_sums[0]), w_down)
        grad_gate = (grad_hidden * up_pre * gate_sig * (1.0 + gate_pre * (1.0 - gate_sig))).astype(BF16)
        grad_up = (grad_hidden * gate_act).astype(BF16)
        gate_part = contract_rows(normed_b_all, grad_gate).astype(BF16)
        up_part = contract_rows(normed_b_all, grad_up).astype(BF16)
        part = (contract_cols(grad_gate, w_gate) + contract_cols(grad_up, w_up)).astype(BF16)
        part = tie(part, *out_far)
        layer_output = (resid + total_of(out_sums[0], out_far)).astype(BF16)
        down_total = add_parts(down_keep, down_moved)
        grad_resid, grad_branch_all, ffn_gain_part, down_total, gate_total, up_total = backward_exchange(
            psize,
            part.reshape(count, -1, D),
            resid,
            cot,
            gains8,
            down_total[:, :feat],
            down_total[:, feat:],
            gate_part.reshape(2, feat, -1),
            up_part.reshape(2, feat, -1),
        )
        grad_branch_all = grad_branch_all.reshape(-1, D)
        grad_attended = contract_cols(grad_branch_all, w_out).astype(BF16)
        out_part = contract_rows(attended, grad_branch_all).astype(BF16)
        out_keep, out_give = split_rows(out_part, high)
        grad_attended, out_keep, out_give, *totals = lax.optimization_barrier(
            (grad_attended, out_keep, out_give, down_total, gate_total, up_total) + unspread_parts(layer_output, same)
        )
        totals, (own_part, near_part, far_part) = totals[:3], totals[3:]
        moved = [to_home(value) for value in totals]
        out_moved = xor_swap(out_give, "o", osize, 1)
        near_moved, far_moved = unspread_moves(near_part, far_part)
        grad_proj, bias_sums = attention_backward(
            grad_attended.reshape(count, -1, heads * DH), saved, logit, kcol, qrow, flags, heads, prompt_len
        )
        grad_proj, bias_sums, out_moved, near_moved, far_moved, *moved = lax.optimization_barrier(
            (grad_proj, bias_sums, out_moved, near_moved, far_moved, *moved)
        )
        layer_output = unspread_join(own_part, near_moved, far_moved, core, same)
        grad_proj = grad_proj.reshape(-1, width + LANES)
        proj_part = contract_rows(normed_a_all, grad_proj).astype(BF16)
        part = contract_cols(grad_proj, w_proj).astype(BF16).reshape(count, -1, D)
        down_total, gate_total, up_total = (
            finish(add_parts(value, other), obits[1:]) for value, other in zip(totals, moved)
        )
        out_total = add_parts(out_keep, out_moved)

        slots = jnp.where(
            (jnp.arange(2 * psize) == core * psize + ppos)[:, None], bias_sums[:1, :heads], 0.0
        ).reshape(-1)
        slots = jnp.concatenate([slots, jnp.zeros((feat - slots.shape[0],), F32)])
        small = jnp.stack([jnp.zeros((D,), F32), ffn_gain_part[0], jnp.concatenate([slots, slots])])
        small = jnp.concatenate([small, jnp.zeros((5, D), F32)])
        input_grad, small, proj_grad, out_both, up_both, gate_both, down_both = leave(
            psize,
            osize,
            part,
            xin,
            grad_resid,
            gains8,
            small,
            proj_part[:feat],
            proj_part[feat:],
            out_total[:, :feat],
            out_total[:, feat:],
            up_total,
            gate_total,
            down_total,
        )
        proj_grad = proj_grad.astype(F32)
        qkv_grad, forget_grad = proj_grad[:, :width], proj_grad[:, width : width + heads]
        bias_all = small[2, : 2 * psize * heads].reshape(2 * psize, heads)
        forget_bias_grad = lax.dynamic_index_in_dim(bias_all, hpos * psize + ppos, 0, keepdims=False)

        def whole(halves):
            return halves.reshape(-1, halves.shape[2]).astype(F32)

        return (
            layer_output,
            input_grad,
            small[0],
            qkv_grad,
            forget_grad,
            forget_bias_grad,
            whole(out_both),
            small[1],
            whole(gate_both),
            whole(up_both),
            whole(down_both),
        )

    return shards


def solution(mesh):
    dp, row, col = mesh.shape["dp"], mesh.shape["row"], mesh.shape["col"]
    osize, psize = dp // 2, col // 2
    assert row == 2
    split = Mesh(mesh.devices.reshape(osize, 2, row, 2, psize), ("o", "k", "x", "h", "p"))
    tokens = P(("o", "k", "h", "p"), "x")
    rows_first = P("x", ("h", "p"))
    cols_first = P(("h", "p"), "x")
    groups = P(("o", "k", "x"), None)
    in_specs = (
        tokens,
        P("x"),
        rows_first,
        rows_first,
        P(("h", "p")),
        cols_first,
        P("x"),
        rows_first,
        rows_first,
        cols_first,
        groups,
        groups,
        groups,
        tokens,
    )
    out_specs = (
        tokens,
        tokens,
        P("x"),
        rows_first,
        rows_first,
        P(("h", "p")),
        cols_first,
        P("x"),
        rows_first,
        rows_first,
        cols_first,
    )
    return jax.shard_map(
        make_shards(osize, psize), mesh=split, in_specs=in_specs, out_specs=out_specs, check_vma=False
    )
```

```python
import functools

import jax
import jax.numpy as jnp
from jax import lax
from jax.experimental import pallas as pl
from jax.experimental.pallas import tpu as pltpu
from jax.sharding import Mesh, PartitionSpec as P

D = 1536
DH = 64
DOCS = 4
TILE = 256
EPS = 1e-06
MASKED = -1e30
LANES = 128
BF16 = jnp.bfloat16
F32 = jnp.float32


def swap(value, axis):
    return lax.ppermute(value, axis, [(0, 1), (1, 0)])


def xor_swap(value, axis, size, bit):
    return lax.ppermute(value, axis, [(i, i ^ bit) for i in range(size)])


def kxh(k, x, h):
    return (k * 2 + x) * 2 + h


def fetch_home_away(value):
    pairs = []
    for k in range(2):
        for x in range(2):
            for h in range(2):
                target = (k, 1 - x, h) if k == h else (1 - k, x, 1 - h)
                pairs.append((kxh(k, x, h), kxh(*target)))
    return lax.ppermute(value, ("k", "x", "h"), pairs)


def fetch_away(value):
    pairs = [
        (kxh(k, x, 1 - k), kxh(k, 1 - x, 1 - k)) for k in range(2) for x in range(2)
    ]
    return lax.ppermute(value, ("k", "x", "h"), pairs)


def tie(value, *others):
    return lax.optimization_barrier((value,) + others)[0]


def join_weight(shard, first, second, home, axis):
    mine = jnp.where(home, shard, first)
    other = jnp.where(home, first, second)
    return jnp.concatenate([mine, other], axis=axis)


def add_parts(kept, moved):
    return (kept.astype(F32) + moved.astype(F32)).astype(BF16)


def to_home(value):
    return lax.ppermute(value, ("k", "h"), [(1, 0), (2, 3)])


def from_home(value):
    return lax.ppermute(value, ("k", "h"), [(0, 2), (3, 1)])


def home_swap(value, size, bit):
    pairs = []
    for o in range(size):
        for k in range(2):
            pairs.append(((o * 2 + k) * 2 + k, ((o ^ bit) * 2 + k) * 2 + k))
    return lax.ppermute(value, ("o", "k", "h"), pairs)


def bits_of(size):
    return [1 << i for i in range(size.bit_length() - 1)]


def split_rows(value, high):
    half = value.shape[0] // 2
    low_rows, high_rows = value[:half], value[half:]
    return jnp.where(high, high_rows, low_rows), jnp.where(high, low_rows, high_rows)


def merge_rows(kept, moved, high):
    return jnp.concatenate([jnp.where(high, moved, kept), jnp.where(high, kept, moved)], axis=0)


def take_half(value, index):
    half = value.shape[0] // 2
    return lax.dynamic_slice_in_dim(value, index * half, half, 0)


def kx(k, x):
    return k * 2 + x


SPREAD_A = []
SPREAD_B = []
for _k in range(2):
    for _x in range(2):
        if _k == _x:
            SPREAD_A.append((kx(_k, _x), kx(1 - _k, _x)))
        else:
            SPREAD_A.append((kx(_k, _x), kx(_k, 1 - _x)))
            SPREAD_B.append((kx(_k, _x), kx(1 - _k, 1 - _x)))


def spread_tokens(block, core, same):
    near = take_half(block, core)
    far = take_half(block, 1 - core)
    first = lax.ppermute(jnp.where(same, far, near), ("k", "x"), SPREAD_A)
    second = lax.ppermute(far, ("k", "x"), SPREAD_B)
    own = jnp.where(same, near, first)
    other = jnp.where(same, first, second)
    return jnp.concatenate([own, other], axis=1)


def unspread_parts(rows, same):
    half = rows.shape[1] // 2
    own, other = rows[:, :half], rows[:, half:]
    return own, jnp.where(same, other, own), other


def unspread_moves(near, far):
    first = lax.ppermute(near, ("k", "x"), [(b, a) for a, b in SPREAD_A])
    second = lax.ppermute(far, ("k", "x"), [(b, a) for a, b in SPREAD_B])
    return first, second


def unspread_join(own, first, second, core, same):
    near = jnp.where(same, own, first)
    far = jnp.where(same, first, second)
    low = jnp.where(core == 0, near, far)
    high = jnp.where(core == 0, far, near)
    return jnp.concatenate([low, high], axis=0)


def contract_rows(left, right):
    return lax.dot_general(
        left, right, (((0,), (0,)), ((), ())), preferred_element_type=F32
    )


def contract_cols(left, right):
    return lax.dot_general(
        left, right, (((1,), (1,)), ((), ())), preferred_element_type=F32
    )


def matmul(left, right):
    return jnp.dot(left, right, preferred_element_type=F32)


def dot_nn(left, right):
    return lax.dot_general(left, right, (((1,), (0,)), ((), ())), preferred_element_type=F32)


def dot_nt(left, right):
    return lax.dot_general(left, right, (((1,), (1,)), ((), ())), preferred_element_type=F32)


def tile_mask(qrow, kcol, rows, cols, i, j):
    key_pos = j * TILE + lax.broadcasted_iota(jnp.int32, (TILE, TILE), 0)
    query_pos = i * TILE + lax.broadcasted_iota(jnp.int32, (TILE, TILE), 1)
    code = kcol[pl.ds(pl.multiple_of(j * TILE, TILE), TILE), 0:1]
    first = qrow[0:1, pl.ds(pl.multiple_of(i * TILE, TILE), TILE)]
    second = qrow[1:2, pl.ds(pl.multiple_of(i * TILE, TILE), TILE)]
    seen = (key_pos <= query_pos) & ((code == first) | (code == second))
    return jnp.where(seen, 0.0, MASKED)


def split_parts(value):
    high = value.astype(BF16)
    rest = value - high.astype(F32)
    mid = rest.astype(BF16)
    low = (rest - mid.astype(F32)).astype(BF16)
    return high, mid, low


def lane(shape):
    return lax.broadcasted_iota(jnp.int32, shape, 1)


def decay_map(pos_a, tag_a, limit_a, pos_b, tag_b, doc_b):
    adds = ((pos_b <= pos_a) & (tag_a == tag_b)) | (doc_b <= limit_a)
    return jnp.where(adds, 1.0, 0.0).astype(BF16)


def forward_kernel(
    heads, count, prompt_len, flags, qkv_hbm, logit_hbm, kcol, qrow, att_hbm, ot_hbm, lse_ref,
    qp_hbm, kp_hbm, vp_hbm, qkv, logit, qp, kp, vp, vt, rates, attended, ot, mask, m_ref, l_ref,
    in_sem, out_sem, keep_sem,
):
    me = lax.axis_index("p") * 2 + lax.axis_index("k")
    total = qkv.shape[0]
    size = total // count
    tiles = total // TILE
    loads = []
    for b in range(count):
        rows = pl.ds(b * size, size)
        loads.append(pltpu.make_async_copy(logit_hbm.at[b ^ me], logit.at[rows], in_sem.at[b]))
        loads.append(pltpu.make_async_copy(qkv_hbm.at[b ^ me], qkv.at[rows], in_sem.at[count + b]))
    for load in loads:
        load.start()
    for load in loads[::2]:
        load.wait()
    value = logit[...]
    rate = jnp.minimum(value, 0.0) - jnp.log1p(jnp.exp(-jnp.abs(value)))
    rate = jnp.where(lane(rate.shape) < heads, rate, 0.0)
    high, mid, low = split_parts(rate)
    packed = high.astype(F32) + pltpu.roll(mid.astype(F32), 8, 1) + pltpu.roll(low.astype(F32), 16, 1)
    rates[...] = packed.astype(BF16)
    for load in loads[1::2]:
        load.wait()
    place_row = lax.broadcasted_iota(jnp.int32, (LANES, LANES), 0)
    place_col = lax.broadcasted_iota(jnp.int32, (LANES, LANES), 1)

    def prepare(t, carry):
        rows = pl.ds(pl.multiple_of(t * TILE, TILE), TILE)

        def add_rates(u, acc):
            others = pl.ds(pl.multiple_of(u * TILE, TILE), TILE)
            pos_a = t * TILE + lax.broadcasted_iota(jnp.int32, (TILE, TILE), 0)
            pos_b = u * TILE + lax.broadcasted_iota(jnp.int32, (TILE, TILE), 1)
            adds = decay_map(
                pos_a, kcol[rows, 1:2], kcol[rows, 2:3], pos_b, qrow[2:3, others], qrow[3:4, others]
            )
            return acc + dot_nn(adds, rates[others, :])

        sums = lax.fori_loop(0, t + 1, add_rates, jnp.zeros((TILE, LANES), F32))
        decay = sums + pltpu.roll(sums, LANES - 8, 1) + pltpu.roll(sums, LANES - 16, 1)
        decay = jnp.where(lane(decay.shape) < heads, -decay, 0.0)
        high, mid, low = split_parts(decay)
        parts = (
            high.astype(F32) + pltpu.roll(mid.astype(F32), 8, 1) + pltpu.roll(low.astype(F32), 16, 1)
        ).astype(BF16)
        lanes = lane((TILE, LANES))
        for h in range(heads):
            base = 3 * DH * h
            query = qkv[rows, base : base + DH].astype(F32) * DH ** (-0.5)
            key = qkv[rows, base + DH : base + 2 * DH]
            worth = qkv[rows, base + 2 * DH : base + 3 * DH]
            ones = jnp.where((lanes >= DH) & (lanes < DH + 3), 1.0, 0.0)[:, :DH]
            ones = jnp.where(lane((TILE, DH)) < 3, 1.0, 0.0)
            qp[h, rows, :] = jnp.concatenate([query, ones], axis=1).astype(BF16)
            spread = jnp.where(
                (place_col >= DH) & (place_col < DH + 3) & (place_row == 8 * (place_col - DH) + h), 1.0, 0.0
            ).astype(BF16)
            extra = dot_nn(parts, spread)
            extra = jnp.where(lanes == DH + 3, 1.0, extra)
            key_wide = jnp.concatenate([key.astype(F32), extra[:, DH:]], axis=1)
            kp[h, rows, :] = key_wide.astype(BF16)
            vp[h, rows, :] = worth
            vt[h, :, rows] = worth.astype(F32).T.astype(BF16)
        return carry

    lax.fori_loop(0, tiles, prepare, 0)
    keeps = [
        pltpu.make_async_copy(qp, qp_hbm, keep_sem.at[0]),
        pltpu.make_async_copy(kp, kp_hbm, keep_sem.at[1]),
        pltpu.make_async_copy(vp, vp_hbm, keep_sem.at[2]),
    ]
    for keep in keeps:
        keep.start()

    def query_tile(i, carry):
        cols = pl.ds(pl.multiple_of(i * TILE, TILE), TILE)
        m_ref[...] = jnp.full(m_ref.shape, MASKED, F32)
        l_ref[...] = jnp.zeros(l_ref.shape, F32)
        ot[:, cols] = jnp.zeros((heads * DH, TILE), F32)

        def key_tile(j, inner):
            @pl.when(flags[i * tiles + j] > 0)
            def _():
                rows = pl.ds(pl.multiple_of(j * TILE, TILE), TILE)
                mask[...] = tile_mask(qrow, kcol, None, None, i, j)
                for h in range(heads):
                    scores = dot_nt(kp[h, rows, :], qp[h, cols, :]) + mask[...]
                    before = m_ref[h : h + 1, :]
                    top = jnp.maximum(before, jnp.max(scores, axis=0, keepdims=True))
                    expo = jnp.exp(scores - top)
                    shrink = jnp.exp(before - top)
                    m_ref[h : h + 1, :] = top
                    l_ref[h : h + 1, :] = l_ref[h : h + 1, :] * shrink + jnp.sum(expo, axis=0, keepdims=True)
                    part = dot_nn(vt[h, :, rows], expo.astype(BF16))
                    span = pl.ds(h * DH, DH)
                    ot[span, cols] = ot[span, cols] * shrink + part

            return inner

        lax.fori_loop(0, i + 1, key_tile, 0)
        for h in range(heads):
            span = pl.ds(h * DH, DH)
            ot[span, cols] = ot[span, cols] / l_ref[h : h + 1, :]
        lse_ref[:, cols] = m_ref[...] + jnp.log(l_ref[...])
        attended[cols, :] = ot[:, cols].T.astype(BF16)
        return carry

    lse_ref[...] = jnp.zeros(lse_ref.shape, F32)
    lax.fori_loop(0, tiles, query_tile, 0)
    stores = [pltpu.make_async_copy(ot, ot_hbm, keep_sem.at[3])]
    for b in range(count):
        stores.append(
            pltpu.make_async_copy(attended.at[pl.ds(b * size, size)], att_hbm.at[b ^ me], out_sem.at[b])
        )
    for store in stores:
        store.start()
    for copy in keeps + stores:
        copy.wait()


def attention_forward(qkv, logit, kcol, qrow, flags, heads, prompt_len):
    count, size, width = qkv.shape
    total = count * size
    any_spec = pl.BlockSpec(memory_space=pl.ANY)
    vmem = pl.BlockSpec(memory_space=pltpu.VMEM)
    shape = jax.ShapeDtypeStruct
    return pl.pallas_call(
        functools.partial(forward_kernel, heads, count, prompt_len),
        out_shape=(
            shape((count, size, heads * DH), BF16),
            shape((heads * DH, total), F32),
            shape((8, total), F32),
            shape((heads, total, LANES), BF16),
            shape((heads, total, LANES), BF16),
            shape((heads, total, DH), BF16),
        ),
        in_specs=[pl.BlockSpec(memory_space=pltpu.SMEM), any_spec, any_spec, vmem, vmem],
        out_specs=(any_spec, any_spec, vmem, any_spec, any_spec, any_spec),
        scratch_shapes=[
            pltpu.VMEM((total, width), BF16),
            pltpu.VMEM((total, LANES), F32),
            pltpu.VMEM((heads, total, LANES), BF16),
            pltpu.VMEM((heads, total, LANES), BF16),
            pltpu.VMEM((heads, total, DH), BF16),
            pltpu.VMEM((heads, DH, total), BF16),
            pltpu.VMEM((total, LANES), BF16),
            pltpu.VMEM((total, heads * DH), BF16),
            pltpu.VMEM((heads * DH, total), F32),
            pltpu.VMEM((TILE, TILE), F32),
            pltpu.VMEM((8, TILE), F32),
            pltpu.VMEM((8, TILE), F32),
            pltpu.SemaphoreType.DMA((2 * count,)),
            pltpu.SemaphoreType.DMA((count,)),
            pltpu.SemaphoreType.DMA((4,)),
        ],
        compiler_params=pltpu.CompilerParams(vmem_limit_bytes=48 << 20),
        cost_estimate=pl.CostEstimate(flops=20_000_000_000, bytes_accessed=30_000_000, transcendentals=0),
        name="attention_forward",
    )(flags, qkv, logit, kcol, qrow)


def backward_kernel(
    heads, count, prompt_len, flags, gatt_hbm, ot_ref, lse_ref, qp, kp, vp, logit_hbm, kcol, qrow,
    grad_hbm, bias_ref, gatt, logit, gout, kt, delta, dqt, dk, dv, mask, decay, grad, in_sem, out_sem,
):
    me = lax.axis_index("p") * 2 + lax.axis_index("k")
    total = gatt.shape[0]
    size = total // count
    tiles = total // TILE
    loads = []
    for b in range(count):
        rows = pl.ds(b * size, size)
        loads.append(pltpu.make_async_copy(gatt_hbm.at[b ^ me], gatt.at[rows], in_sem.at[b]))
        loads.append(pltpu.make_async_copy(logit_hbm.at[b ^ me], logit.at[rows], in_sem.at[count + b]))
    for load in loads:
        load.start()
    for load in loads:
        load.wait()
    dqt[...] = jnp.zeros(dqt.shape, F32)
    delta[...] = jnp.zeros(delta.shape, F32)

    def prepare(t, carry):
        rows = pl.ds(pl.multiple_of(t * TILE, TILE), TILE)
        turned = gatt[rows, :].astype(F32).T * ot_ref[:, rows]
        for h in range(heads):
            gout[h, rows, :] = gatt[rows, h * DH : (h + 1) * DH]
            kt[h, :, rows] = kp[h, rows, :].astype(F32).T[: DH + 8].astype(BF16)
            delta[h : h + 1, rows] = jnp.sum(turned[h * DH : (h + 1) * DH], axis=0, keepdims=True)
        return carry

    lax.fori_loop(0, tiles, prepare, 0)
    lanes = lane((TILE, LANES))

    def key_tile(j, carry):
        rows = pl.ds(pl.multiple_of(j * TILE, TILE), TILE)
        dk[...] = jnp.zeros(dk.shape, F32)
        dv[...] = jnp.zeros(dv.shape, F32)

        def query_tile(i, inner):
            @pl.when(flags[i * tiles + j] > 0)
            def _():
                cols = pl.ds(pl.multiple_of(i * TILE, TILE), TILE)
                mask[...] = tile_mask(qrow, kcol, None, None, i, j)
                for h in range(heads):
                    scores = dot_nt(kp[h, rows, :], qp[h, cols, :]) + mask[...]
                    probs = jnp.exp(scores - lse_ref[h : h + 1, cols])
                    grad_probs = dot_nt(vp[h, rows, :], gout[h, cols, :])
                    grad_scores = (probs * (grad_probs - delta[h : h + 1, cols])).astype(BF16)
                    dv[h] += dot_nn(probs.astype(BF16), gout[h, cols, :])
                    dk[h] += dot_nn(grad_scores, qp[h, cols, :])
                    dqt[h, :, cols] += dot_nn(kt[h, :, rows], grad_scores)

            return inner

        lax.fori_loop(j, tiles, query_tile, 0)
        keys = jnp.zeros((TILE, LANES), F32)
        for h in range(heads):
            grad_key = dk[h]
            keys += jnp.where(lanes == h, pltpu.roll(grad_key, LANES - DH + h, 1), 0.0)
            grad[rows, (3 * h + 1) * DH : (3 * h + 3) * DH] = jnp.concatenate(
                [grad_key[:, :DH], dv[h]], axis=1
            ).astype(BF16)
        decay[rows, :] = -keys
        return carry

    lax.fori_loop(0, tiles, key_tile, 0)

    def finish(t, carry):
        rows = pl.ds(pl.multiple_of(t * TILE, TILE), TILE)
        queries = jnp.zeros((TILE, LANES), F32)
        for h in range(heads):
            turned = jnp.concatenate([dqt[h, :, rows], jnp.zeros((LANES - DH - 8, TILE), F32)], axis=0).T
            queries += jnp.where(lanes == h, pltpu.roll(turned, LANES - DH - 3 + h, 1), 0.0)
            grad[rows, 3 * h * DH : (3 * h + 1) * DH] = (turned[:, :DH] * DH ** (-0.5)).astype(BF16)
        whole = decay[rows, :] + queries
        high, mid, low = split_parts(whole)
        decay[rows, :] = (
            high.astype(F32) + pltpu.roll(mid.astype(F32), 8, 1) + pltpu.roll(low.astype(F32), 16, 1)
        )
        return carry

    lax.fori_loop(0, tiles, finish, 0)

    def rates(t, bias):
        rows = pl.ds(pl.multiple_of(t * TILE, TILE), TILE)

        def add_decays(u, acc):
            others = pl.ds(pl.multiple_of(u * TILE, TILE), TILE)
            pos_b = t * TILE + lax.broadcasted_iota(jnp.int32, (TILE, TILE), 0)
            pos_a = u * TILE + lax.broadcasted_iota(jnp.int32, (TILE, TILE), 1)
            adds = decay_map(
                pos_a, qrow[2:3, others], qrow[4:5, others], pos_b, kcol[rows, 1:2], kcol[rows, 3:4]
            )
            return acc + dot_nn(adds, decay[others, :].astype(BF16))

        sums = lax.fori_loop(t, tiles, add_decays, jnp.zeros((TILE, LANES), F32))
        grad_rate = sums + pltpu.roll(sums, LANES - 8, 1) + pltpu.roll(sums, LANES - 16, 1)
        value = logit[rows, :]
        grad_forget = grad_rate / (1.0 + jnp.exp(value))
        grad_forget = jnp.where(lanes < heads, grad_forget, 0.0).astype(BF16)
        grad[rows, 3 * DH * heads :] = grad_forget
        return bias + jnp.sum(grad_forget.astype(F32), axis=0, keepdims=True)

    bias_ref[...] = jnp.broadcast_to(
        lax.fori_loop(0, tiles, rates, jnp.zeros((1, LANES), F32)), bias_ref.shape
    )
    stores = []
    for b in range(count):
        stores.append(
            pltpu.make_async_copy(grad.at[pl.ds(b * size, size)], grad_hbm.at[b ^ me], out_sem.at[b])
        )
    for store in stores:
        store.start()
    for store in stores:
        store.wait()


def attention_backward(grad_attended, saved, logit, kcol, qrow, flags, heads, prompt_len):
    ot, lse, qp, kp, vp = saved
    count, size, width = grad_attended.shape
    total = count * size
    any_spec = pl.BlockSpec(memory_space=pl.ANY)
    vmem = pl.BlockSpec(memory_space=pltpu.VMEM)
    shape = jax.ShapeDtypeStruct
    out_width = 3 * DH * heads + LANES
    return pl.pallas_call(
        functools.partial(backward_kernel, heads, count, prompt_len),
        out_shape=(shape((count, size, out_width), BF16), shape((8, LANES), F32)),
        in_specs=[pl.BlockSpec(memory_space=pltpu.SMEM), any_spec]
        + [vmem] * 5
        + [any_spec, vmem, vmem],
        out_specs=(any_spec, vmem),
        scratch_shapes=[
            pltpu.VMEM((total, width), BF16),
            pltpu.VMEM((total, LANES), F32),
            pltpu.VMEM((heads, total, DH), BF16),
            pltpu.VMEM((heads, DH + 8, total), BF16),
            pltpu.VMEM((8, total), F32),
            pltpu.VMEM((heads, DH + 8, total), F32),
            pltpu.VMEM((heads, TILE, LANES), F32),
            pltpu.VMEM((heads, TILE, DH), F32),
            pltpu.VMEM((TILE, TILE), F32),
            pltpu.VMEM((total, LANES), F32),
            pltpu.VMEM((total, out_width), BF16),
            pltpu.SemaphoreType.DMA((2 * count,)),
            pltpu.SemaphoreType.DMA((count,)),
        ],
        compiler_params=pltpu.CompilerParams(vmem_limit_bytes=56 << 20),
        cost_estimate=pl.CostEstimate(flops=50_000_000_000, bytes_accessed=30_000_000, transcendentals=0),
        name="attention_backward",
    )(flags, grad_attended, ot, lse, qp, kp, vp, logit, kcol, qrow)


def group_codes(prompt_ids, branch_ids, branch_docs):
    prompt_len = prompt_ids.shape[0]
    member = branch_ids[:, None] == jnp.arange(branch_docs.shape[0])[None, :]
    branch_doc_ids = jnp.sum(jnp.where(member, branch_docs[None, :], 0), axis=1)
    key_code = jnp.concatenate([prompt_ids, DOCS + branch_ids])
    first = jnp.concatenate([prompt_ids, branch_doc_ids])
    tag = jnp.concatenate([jnp.full_like(prompt_ids, -1), branch_ids])
    limit = jnp.concatenate([jnp.full_like(prompt_ids, -1), branch_doc_ids])
    prompt_code = jnp.concatenate([prompt_ids, jnp.full_like(branch_ids, DOCS)])
    total = key_code.shape[0]
    none = jnp.zeros_like(tag)
    kcol = jnp.stack([key_code, tag, limit, prompt_code] + [none] * 4, axis=1)
    qrow = jnp.stack([first, key_code, tag, prompt_code, limit] + [none] * 3, axis=0)
    tiles = total // TILE
    kinds = jnp.arange(2 * DOCS)
    key_bits = jnp.any(key_code.reshape(tiles, TILE, 1) == kinds, axis=1)
    query_bits = key_bits | jnp.any(first.reshape(tiles, TILE, 1) == kinds, axis=1)
    order = jnp.arange(tiles)
    meets = jnp.any(query_bits[:, None, :] & key_bits[None, :, :], axis=2)
    flags = (meets & (order[None, :] <= order[:, None])).astype(jnp.int32).reshape(-1)
    return kcol, qrow, flags


class Wires:
    def __init__(self, send_sem, recv_sem, local_sem):
        self.send_sem, self.recv_sem, self.local_sem = send_sem, recv_sem, local_sem
        self.used, self.local_used = 0, 0
        self.k, self.x = lax.axis_index("k"), lax.axis_index("x")
        self.h, self.p, self.o = lax.axis_index("h"), lax.axis_index("p"), lax.axis_index("o")
        self.home = self.k == self.h
        self.same = self.k == self.x
        self.pending = []

    def slot(self):
        self.used += 1
        return self.used - 1

    def copy(self, source, target, device, slot):
        return pltpu.make_async_remote_copy(
            src_ref=source,
            dst_ref=target,
            send_sem=self.send_sem.at[slot],
            recv_sem=self.recv_sem.at[slot],
            device_id=device,
            device_id_type=pl.DeviceIdType.MESH,
        )

    def send(self, source, target, device):
        copy = self.copy(source, target, device, self.slot())
        copy.start()
        self.pending.append(copy.wait_send)
        return copy

    def local(self, source, target):
        copy = pltpu.make_async_copy(source, target, self.local_sem.at[self.local_used])
        self.local_used += 1
        copy.start()
        return copy

    def greet(self, devices):
        barrier = pltpu.get_barrier_semaphore()
        for device in devices:
            pl.semaphore_signal(
                barrier, inc=1, device_id=device, device_id_type=pl.DeviceIdType.MESH
            )
        pl.semaphore_wait(barrier, len(devices))

    def close(self):
        for wait in self.pending:
            wait()


def row_spans(total, pieces):
    size = total // pieces
    return [pl.ds(i * size, size) for i in range(pieces)]


class Fetch:
    def __init__(self, wires, shard, target, stage, pieces, got=None, keep=None):
        w = self.wires = wires
        self.shard, self.target, self.stage, self.got, self.keep = shard, target, stage, got, keep
        self.count = pieces
        self.half_rows = shard.shape[0] // 2
        self.size = self.half_rows // pieces
        self.by_columns = len(target.shape) == 2
        self.first = [w.slot() for _ in range(pieces)]
        self.over = [w.slot() for _ in range(pieces)]
        self.second = [w.slot() for _ in range(2 * pieces)]
        self.local_slot = w.local_used
        w.local_used += 2

    def rows(self, i, mine=True):
        bit = self.wires.o % 2
        bit = bit if mine else 1 - bit
        return pl.ds(pl.multiple_of(bit * self.half_rows + i * self.size, 16), self.size)

    def place(self, half, span):
        if self.by_columns:
            width = self.shard.shape[1]
            return self.target.at[span, pl.ds(half * width, width)]
        return self.target.at[half, span]

    def first_copy(self, i, home):
        w, span = self.wires, self.rows(i)
        if home:
            return w.copy(self.shard.at[span], self.place(1, span), {"x": 1 - w.x}, self.first[i])
        device = {"k": 1 - w.k, "h": 1 - w.h}
        return w.copy(self.shard.at[span], self.place(0, span), device, self.first[i])

    def have(self, i, half):
        if self.got is None:
            return self.place(half, self.rows(i))
        return self.got.at[pl.ds(i * self.size, self.size)]

    def over_copy(self, i, home):
        w, half = self.wires, 1 if home else 0
        return w.copy(self.have(i, half), self.place(half, self.rows(i)), {"o": w.o ^ 1}, self.over[i])

    def second_copy(self, i, mine):
        w, span = self.wires, self.rows(i, mine)
        source = self.have(i, 0) if mine else self.place(0, span)
        slot = self.second[i if mine else self.count + i]
        return w.copy(source, self.place(1, span), {"x": 1 - w.x}, slot)

    def shard_load(self):
        return pltpu.make_async_copy(self.shard, self.stage, self.wires.local_sem.at[self.local_slot])

    def shard_store(self):
        whole = pl.ds(0, self.shard.shape[0])
        return pltpu.make_async_copy(
            self.stage, self.place(0, whole), self.wires.local_sem.at[self.local_slot]
        )

    def got_load(self):
        return pltpu.make_async_copy(self.got, self.keep, self.wires.local_sem.at[self.local_slot + 1])

    def got_store(self, half):
        bit = self.wires.o % 2
        span = pl.ds(pl.multiple_of(bit * self.half_rows, 16), self.half_rows)
        return pltpu.make_async_copy(
            self.keep, self.place(half, span), self.wires.local_sem.at[self.local_slot + 1]
        )

    def either(self, at_home, away):
        pl.when(self.wires.home)(at_home)
        pl.when(jnp.logical_not(self.wires.home))(away)

    def load(self):
        pl.when(self.wires.home)(lambda: self.shard_load().start())
        if self.got is not None:
            self.got_load().start()

    def start(self):
        if self.got is not None:
            for i in range(self.count):
                self.relay(i)
            return

        def go(home):
            for i in range(self.count):
                self.first_copy(i, home).start()

        self.either(lambda: go(True), lambda: go(False))

    def store(self):
        def at_home():
            self.shard_load().wait()
            self.shard_store().start()
            if self.got is not None:
                self.got_load().wait()
                self.got_store(1).start()

        def away():
            if self.got is not None:
                self.got_load().wait()
                self.got_store(0).start()

        self.either(at_home, away)

    def relay(self, i):
        def at_home():
            if self.got is None:
                self.first_copy(i, True).wait_recv()
            self.over_copy(i, True).start()

        def away():
            if self.got is None:
                self.first_copy(i, False).wait_recv()
            self.over_copy(i, False).start()
            self.second_copy(i, True).start()

        self.either(at_home, away)

    def relay_over(self, i):
        def away():
            self.over_copy(i, False).wait_recv()
            self.second_copy(i, False).start()

        pl.when(jnp.logical_not(self.wires.home))(away)

    def wait(self):
        def at_home():
            for i in range(self.count):
                if self.got is None:
                    self.first_copy(i, True).wait_send()
                self.over_copy(i, True).wait()
            self.shard_store().wait()
            if self.got is not None:
                self.got_store(1).wait()

        def away():
            for i in range(self.count):
                if self.got is None:
                    self.first_copy(i, False).wait_send()
                self.over_copy(i, False).wait_send()
                self.second_copy(i, True).wait()
                self.second_copy(i, False).wait()
            if self.got is not None:
                self.got_store(0).wait()

        self.either(at_home, away)


def partners(wires, psize, away=False, peers=True, over_o=0):
    devices = [{"k": 1 - wires.k}]
    if peers:
        devices += [{"p": wires.p ^ bit} for bit in range(1, psize)]
    devices += [{"x": 1 - wires.x}]
    devices += [{"k": 1 - wires.k, "x": 1 - wires.x}]
    if away:
        devices += [{"k": 1 - wires.k, "h": 1 - wires.h}, {"h": 1 - wires.h}]
    bit = 1
    while bit < over_o:
        devices += [{"o": wires.o ^ bit}]
        bit *= 2
    return devices


class Share:
    def __init__(self, wires, psize, own, g, spans):
        self.wires, self.psize, self.own, self.g, self.spans = wires, psize, own, g, spans
        self.near, self.far, self.kept, self.passed = [], {}, [], []

    def send(self, i):
        w, span = self.wires, self.spans[i]
        for bit in range(1, self.psize):
            self.far[bit, i] = w.send(self.own.at[span], self.g.at[2 * bit, span], {"p": w.p ^ bit})
        self.near.append(w.send(self.own.at[span], self.g.at[1, span], {"k": 1 - w.k}))
        self.kept.append(w.local(self.own.at[span], self.g.at[0, span]))

    def relay(self, i):
        w, span = self.wires, self.spans[i]
        for bit in range(1, self.psize):
            self.far[bit, i].wait_recv()
            self.passed.append(
                w.send(self.g.at[2 * bit, span], self.g.at[2 * bit + 1, span], {"k": 1 - w.k})
            )

    def wait(self):
        for copy in self.near + self.passed:
            copy.wait_recv()
        for copy in self.kept:
            copy.wait()


def by_chunks(span, body):
    def run(n, carry):
        body(pl.ds(pl.multiple_of(span.start + n * CHUNK, CHUNK), CHUNK))
        return carry

    lax.fori_loop(0, span.size // CHUNK, run, 0)


def add_into(value, *others):
    def body(rows):
        total = value[rows, :].astype(F32)
        for other in others:
            total = total + other[rows, :].astype(F32)
        value[rows, :] = total.astype(BF16)

    by_chunks(pl.ds(0, value.shape[0]), body)


class Reduce:
    def __init__(self, wires, psize, part, near, mid, far, spans):
        self.wires, self.psize, self.part = wires, psize, part
        self.near, self.mid, self.far, self.spans = near, mid, far, spans
        self.near_copies, self.far_copies = {}, {}

    def start(self):
        w = self.wires
        for bit in reversed(range(self.psize)):
            for i, span in enumerate(self.spans):
                self.near_copies[bit, i] = w.send(
                    self.part.at[2 * bit + 1, span], self.near.at[bit, span], {"k": 1 - w.k}
                )
        for bit in reversed(range(1, self.psize)):
            for i, span in enumerate(self.spans):
                self.near_copies[bit, i].wait_recv()

                def add(rows, bit=bit):
                    self.mid[bit - 1, rows] = (
                        self.part[2 * bit, rows].astype(F32) + self.near[bit, rows].astype(F32)
                    ).astype(BF16)

                by_chunks(span, add)
                self.far_copies[bit, i] = w.send(
                    self.mid.at[bit - 1, span], self.far.at[bit - 1, span], {"p": w.p ^ bit}
                )

    def each(self, i, body):
        span = self.spans[i]
        self.near_copies[0, i].wait_recv()
        for bit in range(1, self.psize):
            self.far_copies[bit, i].wait_recv()

        def run(rows):
            total = self.part[0, rows].astype(F32) + self.near[0, rows].astype(F32)
            for bit in range(1, self.psize):
                total = total + self.far[bit - 1, rows].astype(F32)
            body(rows, total)

        by_chunks(span, run)


CHUNK = 32
PIECES = 3


def inverse_rms(value):
    return lax.rsqrt(jnp.sum(value * value, axis=1, keepdims=True) / D + EPS)


def norm_back(grad, value, base, gain):
    rms = inverse_rms(value)
    gained = gain * grad
    inner = jnp.sum(value * gained, axis=1, keepdims=True)
    result = base + rms * gained - value * (rms * rms * rms) * inner / D
    parts = grad * value * rms
    return result, sum(parts[n : n + 8] for n in range(0, parts.shape[0], 8))


def enter_kernel(
    psize, x_ref, gain_own, codes_own, qkv_shard, forget_shard, out_shard, xin, g, proj, out, gain_ref, codes,
    own, qkv_stage, forget_stage, out_stage, send_sem, recv_sem, local_sem,
):
    w = Wires(send_sem, recv_sem, local_sem)
    width = qkv_shard.shape[1]
    qkv = Fetch(w, qkv_shard, proj.at[:, :, pl.ds(0, width)], qkv_stage, 3)
    forget = Fetch(
        w, forget_shard, proj.at[:, :, pl.ds(width, forget_shard.shape[1])], forget_stage, 1
    )
    out_fetch = Fetch(w, out_shard, out, out_stage, 1)
    for fetch in (qkv, forget, out_fetch):
        fetch.load()
    w.greet(partners(w, psize, away=True, over_o=2))
    rows, half = own.shape[0], x_ref.shape[1]
    spans = row_spans(rows, PIECES)
    size = rows // PIECES
    def spread(source, target, pieces):
        count = len(pieces)
        to_near = [w.slot() for _ in pieces]
        to_far = [w.slot() for _ in pieces]
        kept = [w.local_used + i for i in range(count)]
        w.local_used += count

        def piece(base, i):
            start, length = pieces[i]
            return source.at[pl.ds(pl.multiple_of(base * rows + start, 8), length)]

        def span(i):
            return pl.ds(pieces[i][0], pieces[i][1])

        left, right = pl.ds(0, half), pl.ds(half, half)

        def same_keep(i):
            return pltpu.make_async_copy(piece(w.k, i), target.at[span(i), left], local_sem.at[kept[i]])

        def same_send(i):
            return w.copy(piece(1 - w.k, i), target.at[span(i), left], {"k": 1 - w.k}, to_near[i])

        def cross_near(i):
            return w.copy(piece(w.k, i), target.at[span(i), right], {"x": 1 - w.x}, to_near[i])

        def cross_far(i):
            return w.copy(
                piece(1 - w.k, i), target.at[span(i), right], {"k": 1 - w.k, "x": 1 - w.x}, to_far[i]
            )

        def start():
            @pl.when(w.same)
            def _():
                for i in range(count):
                    same_send(i).start()
                    same_keep(i).start()

            @pl.when(jnp.logical_not(w.same))
            def _():
                for i in range(count):
                    cross_near(i).start()
                    cross_far(i).start()

        def arrive(i):
            @pl.when(w.same)
            def _():
                same_keep(i).wait()
                same_send(i).wait_recv()

            @pl.when(jnp.logical_not(w.same))
            def _():
                cross_near(i).wait_recv()
                cross_far(i).wait_recv()

        def close():
            @pl.when(w.same)
            def _():
                for i in range(count):
                    same_send(i).wait_send()

            @pl.when(jnp.logical_not(w.same))
            def _():
                for i in range(count):
                    cross_near(i).wait_send()
                    cross_far(i).wait_send()

        return start, arrive, close

    gain_copy = w.send(gain_own, gain_ref.at[:, pl.ds(half, half)], {"x": 1 - w.x})
    code_copies = [
        w.send(codes_own, codes.at[1], {"x": 1 - w.x}),
        w.send(codes_own, codes.at[2], {"k": 1 - w.k}),
        w.send(codes_own, codes.at[3], {"k": 1 - w.k, "x": 1 - w.x}),
    ]
    codes[0] = codes_own[...]
    start, arrive, close = spread(x_ref, xin, [(i * size, size) for i in range(PIECES)])
    start()
    qkv.start()
    forget.start()
    share = Share(w, psize, own, g, spans)
    gain_ref[:, pl.ds(0, half)] = gain_own[...]
    gain_copy.wait_recv()
    for i, span in enumerate(spans):
        arrive(i)

        def norm(rows):
            value = xin[rows, :].astype(F32)
            own[rows, :] = (value * inverse_rms(value) * gain_ref[0:1, :]).astype(BF16)

        by_chunks(span, norm)
        share.send(i)
    close()
    for fetch in (qkv, forget, out_fetch):
        fetch.store()
    for i in range(3):
        qkv.relay(i)
    out_fetch.start()
    forget.relay(0)
    for i in range(3):
        qkv.relay_over(i)
        if i < PIECES:
            share.relay(i)
    forget.relay_over(0)
    out_fetch.relay(0)
    out_fetch.relay_over(0)
    share.wait()
    for fetch in (qkv, forget, out_fetch):
        fetch.wait()
    for copy in code_copies:
        copy.wait_recv()
    w.close()


def forward_exchange_kernel(
    psize, part, xin, gain_ref, gate_shard, gate_got, up_shard, up_got, down_shard, resid, g, gate, up, down,
    near, mid, far, own, gate_stage, gate_keep, up_stage, up_keep, down_stage, send_sem, recv_sem, local_sem,
):
    w = Wires(send_sem, recv_sem, local_sem)
    gate_fetch = Fetch(w, gate_shard, gate, gate_stage, 2, gate_got, gate_keep)
    up_fetch = Fetch(w, up_shard, up, up_stage, 2, up_got, up_keep)
    down_fetch = Fetch(w, down_shard, down, down_stage, 2)
    fetches = (gate_fetch, up_fetch, down_fetch)
    for fetch in fetches:
        fetch.load()
    w.greet(partners(w, psize, away=True, over_o=2))
    spans = row_spans(own.shape[0], PIECES)
    reduce = Reduce(w, psize, part, near, mid, far, spans)
    gate_fetch.start()
    reduce.start()
    up_fetch.start()
    down_fetch.start()
    for fetch in fetches:
        fetch.store()
    for i in range(2):
        gate_fetch.relay_over(i)
    for i in range(2):
        down_fetch.relay(i)
    for i in range(2):
        up_fetch.relay_over(i)
    share = Share(w, psize, own, g, spans)
    for i in range(PIECES):

        def norm(rows, total):
            value = total + xin[rows, :].astype(F32)
            resid[rows, :] = value
            own[rows, :] = (value * inverse_rms(value) * gain_ref[1:2, :]).astype(BF16)

        reduce.each(i, norm)
        share.send(i)
    for i in range(2):
        down_fetch.relay_over(i)
    for i in range(PIECES):
        share.relay(i)
    share.wait()
    for fetch in fetches:
        fetch.wait()
    w.close()


class EarlySum:
    def __init__(self, wires, part, value, over, across, result, pieces, offset=0, got=None):
        w = self.wires = wires
        self.offset, self.got = offset, got
        self.part, self.value, self.over, self.across, self.result = part, value, over, across, result
        self.count, self.half_rows = pieces, value.shape[1]
        self.size = self.half_rows // pieces
        self.over_slots = [[w.slot() for _ in range(pieces)] for _ in range(2)]
        self.across_slots = [w.slot() for _ in range(pieces)]
        self.local_slot = w.local_used
        w.local_used += 2 + pieces

    def span(self, i):
        return pl.ds(i * self.size, self.size)

    def load_copy(self, half):
        start = pl.multiple_of(self.offset + (self.wires.o % 2) * self.half_rows, 16)
        return pltpu.make_async_copy(
            self.part.at[half, pl.ds(start, self.half_rows)],
            self.value.at[half],
            self.wires.local_sem.at[self.local_slot + half],
        )

    def load(self):
        for half in range(2):
            self.load_copy(half).start()

    def over_copy(self, half, i):
        w = self.wires
        start = pl.multiple_of(self.offset + (1 - w.o % 2) * self.half_rows + i * self.size, 16)
        return w.copy(
            self.part.at[half, pl.ds(start, self.size)],
            self.over.at[half, self.span(i)],
            {"o": w.o ^ 1},
            self.over_slots[half][i],
        )

    def across_copy(self, i):
        w = self.wires
        return w.copy(
            self.value.at[1, self.span(i)], self.across.at[self.span(i)], {"x": 1 - w.x}, self.across_slots[i]
        )

    def keep_copy(self, i):
        return pltpu.make_async_copy(
            self.value.at[0, self.span(i)],
            self.result.at[self.span(i)],
            self.wires.local_sem.at[self.local_slot + 2 + i],
        )

    def start(self, half):
        for i in range(self.count):
            self.over_copy(half, i).start()

    def pass_on(self, i):
        if i == 0:
            self.load_copy(1).wait()
        span = self.span(i)
        if self.got is None:
            self.over_copy(1, i).wait_recv()
            add_into(self.value.at[1, span], self.over.at[1, span])
        else:
            add_into(self.value.at[1, span], self.got.at[span])
        self.across_copy(i).start()

    def finish(self, i):
        if i == 0:
            self.load_copy(0).wait()
        self.over_copy(0, i).wait_recv()
        self.across_copy(i).wait_recv()
        span = self.span(i)
        add_into(self.value.at[0, span], self.over.at[0, span], self.across.at[span])
        if self.result is not None:
            self.keep_copy(i).start()

    def close(self):
        for i in range(self.count):
            for half in range(2):
                if half == 0 or self.got is None:
                    self.over_copy(half, i).wait_send()
            self.across_copy(i).wait_send()
            if self.result is not None:
                self.keep_copy(i).wait()


def backward_exchange_kernel(
    psize, part, resid, cot, gain_ref, down_own, down_other, gate_part, gate_got, up_part,
    grad_resid, g, gain_grad, down_sum, pair_sum,
    near, mid, far, own, down_across, gate_val, gate_over, gate_across, up_val, up_over, up_across,
    send_sem, recv_sem, local_sem,
):
    w = Wires(send_sem, recv_sem, local_sem)
    gate = EarlySum(w, gate_part, gate_val, gate_over, gate_across, pair_sum.at[0], 2, got=gate_got)
    up = EarlySum(w, up_part, up_val, up_over, up_across, pair_sum.at[1], 2)
    gate.load()
    up.load()
    w.greet(partners(w, psize, over_o=2))
    spans = row_spans(own.shape[0], PIECES)
    reduce = Reduce(w, psize, part, near, mid, far, spans)
    down_copy = w.send(down_other, down_across, {"x": 1 - w.x})
    gate.start(0)
    up.start(1)
    up.start(0)
    for i in range(2):
        gate.pass_on(i)
    reduce.start()
    share = Share(w, psize, own, g, spans)
    gain_grad[...] = jnp.zeros(gain_grad.shape, F32)

    def back(rows, total):
        grad, gain_part = norm_back(total, resid[rows, :], cot[rows, :].astype(F32), gain_ref[1:2, :])
        grad_resid[rows, :] = grad
        own[rows, :] = grad.astype(BF16)
        gain_grad[...] += gain_part

    for i in range(PIECES):
        reduce.each(i, back)
        share.send(i)
    for i in range(2):
        up.pass_on(i)
    share.relay(0)
    for i in range(2):
        gate.finish(i)
    down_copy.wait_recv()

    def add_down(rows):
        down_sum[rows, :] = (
            down_own[rows, :].astype(F32) + down_across[rows, :].astype(F32)
        ).astype(BF16)

    by_chunks(pl.ds(0, down_sum.shape[0]), add_down)
    for i in range(1, PIECES):
        share.relay(i)
    for i in range(2):
        up.finish(i)
    share.wait()
    gate.close()
    up.close()
    w.close()


class Spread:
    def __init__(self, wires, value, result):
        w = self.wires = wires
        self.value, self.result = value, result
        self.over_slot, self.near_slot, self.pass_slot = w.slot(), w.slot(), w.slot()
        self.local_slot = w.local_used
        w.local_used += 1

    def rows(self, mine):
        bit = self.wires.o % 2
        return self.result.at[bit if mine else 1 - bit]

    def over_copy(self):
        w = self.wires
        return w.copy(self.value, self.rows(True), {"o": w.o ^ 1}, self.over_slot)

    def near_copy(self):
        return self.wires.copy(self.value, self.rows(True), {"k": 1 - self.wires.k}, self.near_slot)

    def pass_copy(self):
        return self.wires.copy(self.rows(False), self.rows(False), {"k": 1 - self.wires.k}, self.pass_slot)

    def keep_copy(self):
        return pltpu.make_async_copy(
            self.value, self.rows(True), self.wires.local_sem.at[self.local_slot]
        )

    def start(self):
        @pl.when(self.wires.home)
        def _():
            self.over_copy().start()
            self.near_copy().start()
            self.keep_copy().start()

    def relay(self):
        @pl.when(self.wires.home)
        def _():
            self.over_copy().wait_recv()
            self.pass_copy().start()

    def wait(self):
        @pl.when(self.wires.home)
        def _():
            self.over_copy().wait_send()
            self.near_copy().wait_send()
            self.pass_copy().wait_send()
            self.keep_copy().wait()

        @pl.when(jnp.logical_not(self.wires.home))
        def _():
            self.near_copy().wait_recv()
            self.pass_copy().wait_recv()


class SmallSum:
    def __init__(self, wires, psize, osize, value, other, buffers):
        w = self.wires = wires
        self.value, self.other, self.buffers = value, other, buffers
        self.devices = [{"x": 1 - w.x}, {"k": 1 - w.k}]
        self.devices += [{"p": w.p ^ bit} for bit in bits_of(psize)]
        self.devices += [{"h": 1 - w.h}]
        self.devices += [{"o": w.o ^ bit} for bit in bits_of(osize)]
        self.slots = [w.slot() for _ in self.devices]

    def copy(self, step):
        source = self.other if step == 0 else self.value
        return self.wires.copy(source, self.buffers.at[step], self.devices[step], self.slots[step])

    def start(self):
        self.copy(0).start()

    def step(self, step):
        self.copy(step).wait()
        self.value[...] = self.value[...] + self.buffers[step]
        if step + 1 < len(self.devices):
            self.copy(step + 1).start()


class Chain:
    def __init__(self, wires, osize, value, stages, buffers, result, pieces):
        self.wires, self.value, self.stages, self.result = wires, value, stages, result
        self.buffers = buffers
        self.spans = row_spans(value.shape[0], pieces)
        self.slots = [[wires.slot() for _ in self.spans] for _ in stages]
        self.kept = [wires.local_used + i for i in range(pieces)]
        wires.local_used += pieces
        self.other = None

    def copy(self, stage, i):
        w, span = self.wires, self.spans[i]
        kind, slot = self.stages[stage], self.slots[stage][i]
        if kind == "x":
            return w.copy(self.other.at[span], self.buffers[stage].at[span], {"x": 1 - w.x}, slot)
        if kind == "h":
            return w.copy(self.value.at[span], self.buffers[stage].at[span], {"h": 1 - w.h}, slot)
        if kind == "k":
            return w.copy(self.value.at[span], self.result.at[span], {"k": 1 - w.k}, slot)
        return w.copy(self.value.at[span], self.buffers[stage].at[span], {"o": w.o ^ kind}, slot)

    def keep(self, i):
        span = self.spans[i]
        return pltpu.make_async_copy(
            self.value.at[span], self.result.at[span], self.wires.local_sem.at[self.kept[i]]
        )

    def start(self, stage, i):
        w, kind = self.wires, self.stages[stage]
        if kind == "x":
            self.copy(stage, i).start()
        elif kind == "h":
            @pl.when(jnp.logical_not(w.home))
            def _():
                self.copy(stage, i).start()
        else:
            @pl.when(w.home)
            def _():
                self.copy(stage, i).start()
                if kind == "k":
                    self.keep(i).start()

    def add(self, stage, i):
        span = self.spans[i]
        add_into(self.value.at[span], self.buffers[stage].at[span])

    def end(self, stage, i):
        w, kind = self.wires, self.stages[stage]
        if kind == "x":
            self.copy(stage, i).wait_recv()
            self.add(stage, i)
        elif kind == "h":
            @pl.when(w.home)
            def _():
                self.copy(stage, i).wait_recv()
                self.add(stage, i)
        elif kind == "k":
            @pl.when(w.home)
            def _():
                self.copy(stage, i).wait_send()
                self.keep(i).wait()

            @pl.when(jnp.logical_not(w.home))
            def _():
                self.copy(stage, i).wait_recv()
        else:
            @pl.when(w.home)
            def _():
                self.copy(stage, i).wait()
                self.add(stage, i)

    def close(self):
        w = self.wires
        for stage, kind in enumerate(self.stages):
            for i in range(len(self.spans)):
                if kind == "x":
                    self.copy(stage, i).wait_send()
                elif kind == "h":
                    @pl.when(jnp.logical_not(w.home))
                    def _():
                        self.copy(stage, i).wait_send()

    def step(self, stage, i):
        self.end(stage, i)
        if stage + 1 < len(self.stages):
            self.start(stage + 1, i)

    def order(self, first=0):
        return [(stage, i) for stage in range(first, len(self.stages)) for i in range(len(self.spans))]

    def run(self, first=0):
        for stage, i in self.order(first):
            self.step(stage, i)


def leave_kernel(
    psize, osize, pieces, part, stream, base, gain_ref, small_in, proj_in, out_own, out_other,
    pair_in, down_in, block, small, first_sum, second_sum, out_sum, up_sum, gate_sum, down_sum,
    near, mid, far, kept, first_val, second_val, out_val, up_val, gate_val, down_val, first_bufs,
    second_over, second_across, second_bufs, out_bufs, small_other, small_bufs, gain_acc,
    send_sem, recv_sem, local_sem,
):
    w = Wires(send_sem, recv_sem, local_sem)
    split = first_val.shape[0]
    second = EarlySum(w, proj_in, second_val, second_over, second_across, None, 2, split)
    second.load()
    loads = [
        w.local(source, target)
        for source, target in (
            (pair_in.at[1], up_val), (pair_in.at[0], gate_val), (down_in, down_val), (out_own, out_val),
            (proj_in.at[0, pl.ds(0, split)], first_val),
        )
    ]
    w.greet(partners(w, psize, away=True, over_o=osize))
    rows, half = kept.shape[1], kept.shape[2]
    spans = row_spans(rows, PIECES)
    size = rows // PIECES
    bits = bits_of(osize)

    first = Chain(
        w, osize, first_val, ["x", "h"] + bits + ["k"], [first_bufs.at[i] for i in range(2 + len(bits))],
        first_sum, pieces,
    )
    first.other = proj_in.at[1, pl.ds(0, split)]
    late = Chain(
        w, osize, second_val.at[0], ["h"] + bits[1:], [second_bufs.at[i] for i in range(len(bits))], None, 2
    )
    out = Chain(w, osize, out_val, ["x", "h"] + bits[1:], [out_bufs.at[i] for i in range(1 + len(bits))], None, 1)
    out.other = out_other
    spreads = [Spread(w, up_val, up_sum), Spread(w, gate_val, gate_sum), Spread(w, down_val, down_sum)]
    last_spreads = [Spread(w, out_val, out_sum), Spread(w, second_val.at[0], second_sum)]
    reduce = Reduce(w, psize, part, near, mid, far, spans)
    second.start(1)
    for i in range(pieces):
        first.start(0, i)
    out.start(0, 0)
    second.start(0)
    for load in loads:
        load.wait()
    reduce.start()
    for spread in spreads:
        spread.start()

    near_slots = [w.slot() for _ in spans]
    far_slots = [w.slot() for _ in spans]
    keep_slots = [w.local_used + i for i in range(PIECES)]
    w.local_used += PIECES

    def target(i):
        return block.at[pl.ds(pl.multiple_of(w.k * rows + i * size, 8), size)]

    def same_keep(i):
        return pltpu.make_async_copy(kept.at[0, spans[i]], target(i), local_sem.at[keep_slots[i]])

    def same_send(i):
        return w.copy(kept.at[1, spans[i]], target(i), {"x": 1 - w.x}, near_slots[i])

    def cross_near(i):
        return w.copy(kept.at[0, spans[i]], target(i), {"k": 1 - w.k}, near_slots[i])

    def cross_far(i):
        return w.copy(kept.at[1, spans[i]], target(i), {"k": 1 - w.k, "x": 1 - w.x}, far_slots[i])

    for i in range(2):
        second.pass_on(i)
    first.step(0, 0)
    for i in range(1, pieces):
        first.step(0, i)
        first.step(1, i - 1)
    out.step(0, 0)
    second.finish(0)
    late.start(0, 0)
    first.step(1, pieces - 1)
    gain_acc[...] = jnp.zeros(gain_acc.shape, F32)

    def back(rows_, total):
        grad, gain_part = norm_back(total, stream[rows_, :].astype(F32), base[rows_, :], gain_ref[0:1, :])
        gain_acc[...] += gain_part
        kept[0, rows_, :] = grad[:, :half].astype(BF16)
        kept[1, rows_, :] = grad[:, half:].astype(BF16)

    for i in range(PIECES):
        reduce.each(i, back)

        @pl.when(w.same)
        def _():
            same_send(i).start()
            same_keep(i).start()

        @pl.when(jnp.logical_not(w.same))
        def _():
            cross_near(i).start()
            cross_far(i).start()

        if i == 0:
            second.finish(1)
            late.start(0, 1)

    gain_sum = jnp.sum(gain_acc[...], axis=0, keepdims=True)
    row = lax.broadcasted_iota(jnp.int32, (8, half), 0)
    small[...] = jnp.where(row == 0, gain_sum[:, :half], small_in[:, :half])
    small_other[...] = jnp.where(row == 0, gain_sum[:, half:], small_in[:, half:])
    total = SmallSum(w, psize, osize, small, small_other, small_bufs)
    total.start()
    out.run(1)
    last_spreads[0].start()
    steps = [lambda a=a: late.step(*a) for a in late.order(0)] + [last_spreads[1].start]
    steps += [spread.relay for spread in spreads] + [lambda a=a: first.step(*a) for a in first.order(2)]
    steps += [last_spreads[0].relay, last_spreads[1].relay]
    smalls = list(range(len(total.devices)))
    for n, step in enumerate(steps):
        step()
        if n % 2 == 0 and smalls:
            total.step(smalls.pop(0))
    for step in smalls:
        total.step(step)
    for spread in spreads + last_spreads:
        spread.wait()
    for i in range(PIECES):
        @pl.when(w.same)
        def _():
            same_keep(i).wait()
            same_send(i).wait_send()
            cross_near(i).wait_recv()

        @pl.when(jnp.logical_not(w.same))
        def _():
            cross_near(i).wait_send()
            cross_far(i).wait()
            same_send(i).wait_recv()

    for chain in (first, second, late, out):
        chain.close()
    w.close()


ANY = pl.BlockSpec(memory_space=pl.ANY)
VMEM = pl.BlockSpec(memory_space=pltpu.VMEM)
SLOTS = 128


def exchange_call(kernel, name, collective_id, outs, out_specs, in_specs, scratch, args):
    return pl.pallas_call(
        kernel,
        out_shape=outs,
        in_specs=in_specs,
        out_specs=out_specs,
        scratch_shapes=scratch
        + [
            pltpu.SemaphoreType.DMA((SLOTS,)),
            pltpu.SemaphoreType.DMA((SLOTS,)),
            pltpu.SemaphoreType.DMA((SLOTS // 2,)),
        ],
        compiler_params=pltpu.CompilerParams(
            collective_id=collective_id, has_side_effects=True, vmem_limit_bytes=56 << 20
        ),
        name=name,
    )(*args)


def sds(shape, dtype):
    return jax.ShapeDtypeStruct(shape, dtype)


def sum_scratch(psize, rows):
    far = max(psize - 1, 1)
    return [
        pltpu.VMEM((psize, rows, D), BF16),
        pltpu.VMEM((far, rows, D), BF16),
        pltpu.VMEM((far, rows, D), BF16),
    ]


def enter(psize, layer_input, gains, codes, qkv_weight, forget_weight, out_weight):
    rows = layer_input.shape[0] // 2
    half, width = qkv_weight.shape
    columns = width + forget_weight.shape[1]
    return exchange_call(
        functools.partial(enter_kernel, psize),
        "enter",
        1,
        (
            sds((rows, D), BF16),
            sds((2 * psize, rows, D), BF16),
            sds((2, half, columns), BF16),
            sds((out_weight.shape[0], 2 * half), BF16),
            sds((8, D), F32),
            sds((4,) + codes.shape, jnp.int32),
        ),
        (VMEM, ANY, ANY, ANY, VMEM, VMEM),
        [ANY, VMEM, VMEM, ANY, ANY, ANY],
        [pltpu.VMEM((rows, D), BF16)]
        + [pltpu.VMEM(value.shape, BF16) for value in (qkv_weight, forget_weight, out_weight)],
        (layer_input, gains, codes, qkv_weight, forget_weight, out_weight),
    )


def forward_exchange(psize, part, xin, gains, gate_weight, gate_got, up_weight, up_got, down_weight):
    rows = xin.shape[0]
    return exchange_call(
        functools.partial(forward_exchange_kernel, psize),
        "forward_exchange",
        2,
        (
            sds((rows, D), F32),
            sds((2 * psize, rows, D), BF16),
            sds((2,) + gate_weight.shape, BF16),
            sds((2,) + up_weight.shape, BF16),
            sds((down_weight.shape[0], D), BF16),
        ),
        (VMEM, ANY, ANY, ANY, ANY),
        [VMEM, VMEM, VMEM, ANY, ANY, ANY, ANY, ANY],
        sum_scratch(psize, rows)
        + [pltpu.VMEM((rows, D), BF16)]
        + [
            pltpu.VMEM(value.shape, BF16)
            for value in (gate_weight, gate_got, up_weight, up_got, down_weight)
        ],
        (part, xin, gains, gate_weight, gate_got, up_weight, up_got, down_weight),
    )


def backward_exchange(psize, part, resid, cot, gains, down_own, down_other, gate_part, gate_got, up_part):
    rows = resid.shape[0]

    def early(value):
        half_rows = value.shape[1] // 2
        shape = (half_rows, value.shape[2])
        return [
            pltpu.VMEM((2,) + shape, BF16),
            pltpu.VMEM((2,) + shape, BF16),
            pltpu.VMEM(shape, BF16),
        ]

    return exchange_call(
        functools.partial(backward_exchange_kernel, psize),
        "backward_exchange",
        3,
        (
            sds((rows, D), F32),
            sds((2 * psize, rows, D), BF16),
            sds((8, D), F32),
            sds(down_own.shape, BF16),
            sds((2, gate_part.shape[1] // 2, gate_part.shape[2]), BF16),
        ),
        (VMEM, ANY, VMEM, VMEM, ANY),
        [VMEM, VMEM, VMEM, VMEM, VMEM, ANY, ANY, VMEM, ANY],
        sum_scratch(psize, rows)
        + [pltpu.VMEM((rows, D), BF16), pltpu.VMEM(down_own.shape, BF16)]
        + early(gate_part)
        + early(up_part),
        (part, resid, cot, gains, down_own, down_other, gate_part, gate_got, up_part),
    )


def leave(psize, osize, part, stream, base, gains, small, proj, out_own, out_other, pair, down):
    rows = stream.shape[0]
    bits = len(bits_of(osize))
    half = D // 2
    columns = proj.shape[2]
    split = proj.shape[1] // 2

    def scratch(*shape):
        return pltpu.VMEM(shape, BF16)

    def both(shape):
        return sds((2,) + shape, BF16)

    return exchange_call(
        functools.partial(leave_kernel, psize, osize, 3),
        "leave",
        4,
        (
            sds((2 * rows, half), BF16),
            sds((8, half), F32),
            sds((split, columns), BF16),
            both((split // 2, columns)),
            both(out_own.shape),
            both(pair.shape[1:]),
            both(pair.shape[1:]),
            both(down.shape),
        ),
        (ANY, VMEM, ANY, ANY, ANY, ANY, ANY, ANY),
        [VMEM] * 5 + [ANY] * 5,
        sum_scratch(psize, rows)
        + [
            scratch(2, rows, half),
            scratch(split, columns),
            scratch(2, split // 2, columns),
            scratch(*out_own.shape),
            scratch(*pair.shape[1:]),
            scratch(*pair.shape[1:]),
            scratch(*down.shape),
            scratch(2 + bits, split, columns),
            scratch(2, split // 2, columns),
            scratch(split // 2, columns),
            scratch(bits, split // 2, columns),
            scratch(1 + bits, *out_own.shape),
            pltpu.VMEM((8, half), F32),
            pltpu.VMEM((3 + len(bits_of(psize)) + bits, 8, half), F32),
            pltpu.VMEM((8, D), F32),
        ],
        (part, stream, base, gains, small, proj, out_own, out_other, pair, down),
    )


def make_shards(osize, psize):
    count = 2 * psize
    obits = bits_of(osize)

    def shards(
        layer_input,
        attn_gain,
        qkv_weight,
        forget_weight,
        forget_bias,
        out_weight,
        ffn_gain,
        gate_weight,
        up_weight,
        down_weight,
        prompt_doc,
        branch_seg,
        branch_doc,
        out_cotangent,
    ):
        core, xpos = lax.axis_index("k"), lax.axis_index("x")
        hpos, ppos, opos = lax.axis_index("h"), lax.axis_index("p"), lax.axis_index("o")
        home = core == hpos
        same = core == xpos
        heads = forget_weight.shape[1]
        width = heads * 3 * DH
        lane_pad = LANES - heads
        feat = D // 2

        def far_blocks(block):
            return [xor_swap(block, "p", psize, bit) for bit in range(1, psize)]

        def all_blocks(block, far):
            blocks = []
            for near in [block] + far:
                blocks += [near, swap(near, "k")]
            return jnp.concatenate(blocks, axis=0)

        def near_sums(partial):
            size = partial.shape[0] // count
            parts = [partial[i * size : (i + 1) * size] for i in range(count)]
            moved = [swap(parts[i + 1], "k") for i in range(0, count, 2)]
            return [add_parts(parts[i], moved[i // 2]) for i in range(0, count, 2)]

        def far_sums(sums):
            return [xor_swap(sums[bit], "p", psize, bit) for bit in range(1, psize)]

        def total_of(near, far):
            total = near.astype(F32)
            for value in far:
                total = total + value.astype(F32)
            return total

        prompt_len, branch_len = prompt_doc.shape[1], branch_seg.shape[1]
        packed = jnp.concatenate([prompt_doc[0], branch_seg[0], branch_doc[0]])
        code_rows = -(-packed.shape[0] // (8 * LANES)) * 8
        packed = jnp.pad(packed, (0, code_rows * LANES - packed.shape[0])).reshape(code_rows, LANES)
        own_gains = jnp.concatenate([jnp.stack([attn_gain, ffn_gain]), jnp.zeros((6, feat), F32)])
        bias = jnp.where(home, forget_bias, lax.ppermute(forget_bias, ("k", "h"), [(1, 2), (2, 1)]))
        bias = jnp.concatenate([bias, jnp.zeros((lane_pad,), F32)])

        forget_wide = jnp.concatenate(
            [forget_weight, jnp.zeros((forget_weight.shape[0], lane_pad), BF16)], axis=1
        )
        first_part, second_part = qkv_weight, forget_wide
        if width % LANES:
            spare = jnp.zeros((qkv_weight.shape[0], LANES - width % LANES), BF16)
            first_part = jnp.concatenate([qkv_weight, forget_wide, spare], axis=1)
        xin, normed_a_all, w_proj, w_out, gains8, codes = enter(
            psize, layer_input, own_gains, packed, first_part, second_part, out_weight
        )
        packed = lax.dynamic_index_in_dim(
            codes, (core ^ xpos) * 2 + (xpos ^ hpos), 0, keepdims=False
        ).reshape(-1)
        prompt_ids = packed[:prompt_len]
        branch_ids = packed[prompt_len : prompt_len + branch_len]
        branch_docs = packed[prompt_len + branch_len : prompt_len + branch_len + branch_doc.shape[1]]
        kcol, qrow, flags = group_codes(prompt_ids, branch_ids, branch_docs)
        normed_a_all = normed_a_all.reshape(-1, D)
        w_proj = w_proj.reshape(D, -1)[:, : width + LANES]

        projected = matmul(normed_a_all, w_proj)
        qkv = projected[:, :width].astype(BF16).reshape(count, -1, width)
        logit = (projected[:, width:] + bias).reshape(count, -1, LANES)
        cot_near, cot_far = take_half(out_cotangent, core), take_half(out_cotangent, 1 - core)
        qkv, logit, kcol, qrow, flags, gate_half, up_half, cot_first, cot_near, cot_far = lax.optimization_barrier(
            (
                qkv,
                logit,
                kcol,
                qrow,
                flags,
                take_half(gate_weight, opos % 2),
                take_half(up_weight, opos % 2),
                jnp.where(same, cot_far, cot_near),
                cot_near,
                cot_far,
            )
        )
        gate_got, up_got = fetch_home_away(gate_half), fetch_home_away(up_half)
        cot_first = lax.ppermute(cot_first, ("k", "x"), SPREAD_A)
        cot_second = lax.ppermute(cot_far, ("k", "x"), SPREAD_B)
        attended, *saved = attention_forward(qkv, logit, kcol, qrow, flags, heads, prompt_len)
        attended, gate_got, up_got, cot_first, cot_second, *saved = lax.optimization_barrier(
            (attended, gate_got, up_got, cot_first, cot_second, *saved)
        )
        attended = attended.reshape(-1, heads * DH)
        cot = jnp.concatenate(
            [jnp.where(same, cot_near, cot_first), jnp.where(same, cot_first, cot_second)], axis=1
        )
        part = matmul(attended, w_out).astype(BF16).reshape(count, -1, D)
        resid, normed_b_all, w_gate, w_up, w_down = forward_exchange(
            psize, part, xin, gains8, gate_weight, gate_got, up_weight, up_got, down_weight
        )
        normed_b_all = normed_b_all.reshape(-1, D)
        w_gate, w_up = w_gate.reshape(D, -1), w_up.reshape(D, -1)
        cot_others = far_blocks(tie(cot, normed_b_all))
        gate_pre = matmul(normed_b_all, w_gate)
        up_pre = matmul(normed_b_all, w_up)
        gate_sig = jax.nn.sigmoid(gate_pre)
        gate_act = gate_pre * gate_sig
        hidden = (gate_act * up_pre).astype(BF16)
        hidden = tie(hidden, *cot_others)
        cot_all = all_blocks(cot, cot_others)

        def finish(total, axis_bits):
            for bit in axis_bits:
                total = add_parts(total, home_swap(total, osize, bit))
            return total

        high = opos % 2 == 1
        down_part = contract_rows(hidden, cot_all).astype(BF16)
        down_keep, down_give = split_rows(down_part, high)
        down_moved = xor_swap(down_give, "o", osize, 1)
        out_sums = near_sums(matmul(hidden, w_down).astype(BF16))
        out_far = far_sums(out_sums)
        grad_hidden = contract_cols(tie(cot_all, out_sums[0]), w_down)
        grad_gate = (grad_hidden * up_pre * gate_sig * (1.0 + gate_pre * (1.0 - gate_sig))).astype(BF16)
        grad_up = (grad_hidden * gate_act).astype(BF16)
        gate_part = contract_rows(normed_b_all, grad_gate).astype(BF16).reshape(2, feat, -1)
        gate_got = xor_swap(take_half(gate_part[1], 1 - opos % 2), "o", osize, 1)
        grad_gate, grad_up = lax.optimization_barrier((grad_gate, grad_up, gate_part))[:2]
        up_part = contract_rows(normed_b_all, grad_up).astype(BF16).reshape(2, feat, -1)
        part = (contract_cols(grad_gate, w_gate) + contract_cols(grad_up, w_up)).astype(BF16)
        part, up_part, gate_got, down_moved, *out_far = lax.optimization_barrier(
            (part, up_part, gate_got, down_moved, *out_far)
        )
        layer_output = (resid + total_of(out_sums[0], out_far)).astype(BF16)
        down_total = add_parts(down_keep, down_moved)
        grad_resid, grad_branch_all, ffn_gain_part, down_total, pair_total = backward_exchange(
            psize,
            part.reshape(count, -1, D),
            resid,
            cot,
            gains8,
            down_total[:, :feat],
            down_total[:, feat:],
            gate_part,
            gate_got,
            up_part,
        )
        grad_branch_all = grad_branch_all.reshape(-1, D)
        grad_attended = contract_cols(grad_branch_all, w_out).astype(BF16)
        out_part = contract_rows(attended, grad_branch_all).astype(BF16)
        out_keep, out_give = split_rows(out_part, high)
        grad_attended, out_keep, out_give, down_total, pair_total, *block_parts = lax.optimization_barrier(
            (grad_attended, out_keep, out_give, down_total, pair_total) + unspread_parts(layer_output, same)
        )
        own_part, near_part, far_part = block_parts
        moved = [to_home(down_total), to_home(pair_total)]
        out_moved = xor_swap(out_give, "o", osize, 1)
        near_moved, far_moved = unspread_moves(near_part, far_part)
        grad_proj, bias_sums = attention_backward(
            grad_attended.reshape(count, -1, heads * DH), saved, logit, kcol, qrow, flags, heads, prompt_len
        )
        grad_proj, bias_sums, out_moved, near_moved, far_moved, *moved = lax.optimization_barrier(
            (grad_proj, bias_sums, out_moved, near_moved, far_moved, *moved)
        )
        layer_output = unspread_join(own_part, near_moved, far_moved, core, same)
        grad_proj = grad_proj.reshape(-1, width + LANES)
        proj_part = contract_rows(normed_a_all, grad_proj).astype(BF16)
        part = contract_cols(grad_proj, w_proj).astype(BF16).reshape(count, -1, D)
        down_total, pair_total = (
            finish(add_parts(value, other), obits[1:])
            for value, other in zip((down_total, pair_total), moved)
        )
        out_total = add_parts(out_keep, out_moved)

        slots = jnp.where(
            (jnp.arange(2 * psize) == core * psize + ppos)[:, None], bias_sums[:1, :heads], 0.0
        ).reshape(-1)
        slots = jnp.concatenate([slots, jnp.zeros((feat - slots.shape[0],), F32)])
        small = jnp.stack([jnp.zeros((D,), F32), jnp.sum(ffn_gain_part, axis=0), jnp.concatenate([slots, slots])])
        small = jnp.concatenate([small, jnp.zeros((5, D), F32)])
        input_grad, small, first_rows, second_rows, out_both, up_both, gate_both, down_both = leave(
            psize,
            osize,
            part,
            xin,
            grad_resid,
            gains8,
            small,
            proj_part.reshape(2, feat, -1),
            out_total[:, :feat],
            out_total[:, feat:],
            pair_total,
            down_total,
        )
        proj_grad = jnp.concatenate([first_rows, second_rows.reshape(first_rows.shape)], axis=0)
        qkv_grad = proj_grad[:, :width].astype(F32)
        forget_grad = proj_grad[:, width : width + heads].astype(F32)
        bias_all = small[2, : 2 * psize * heads].reshape(2 * psize, heads)
        forget_bias_grad = lax.dynamic_index_in_dim(bias_all, hpos * psize + ppos, 0, keepdims=False)

        def whole(halves):
            return halves.reshape(-1, halves.shape[2]).astype(F32)

        return (
            layer_output,
            input_grad,
            small[0],
            qkv_grad,
            forget_grad,
            forget_bias_grad,
            whole(out_both),
            small[1],
            whole(gate_both),
            whole(up_both),
            whole(down_both),
        )

    return shards


def solution(mesh):
    dp, row, col = mesh.shape["dp"], mesh.shape["row"], mesh.shape["col"]
    osize, psize = dp // 2, col // 2
    assert row == 2
    split = Mesh(mesh.devices.reshape(osize, 2, row, 2, psize), ("o", "k", "x", "h", "p"))
    tokens = P(("o", "k", "h", "p"), "x")
    rows_first = P("x", ("h", "p"))
    cols_first = P(("h", "p"), "x")
    groups = P(("o", "k", "x"), None)
    in_specs = (
        tokens,
        P("x"),
        rows_first,
        rows_first,
        P(("h", "p")),
        cols_first,
        P("x"),
        rows_first,
        rows_first,
        cols_first,
        groups,
        groups,
        groups,
        tokens,
    )
    out_specs = (
        tokens,
        tokens,
        P("x"),
        rows_first,
        rows_first,
        P(("h", "p")),
        cols_first,
        P("x"),
        rows_first,
        rows_first,
        cols_first,
    )
    return jax.shard_map(
        make_shards(osize, psize), mesh=split, in_specs=in_specs, out_specs=out_specs, check_vma=False
    )
```

```python
import functools

import jax
import jax.numpy as jnp
from jax import lax
from jax.experimental import pallas as pl
from jax.experimental.pallas import tpu as pltpu
from jax.sharding import Mesh, PartitionSpec as P

D = 1536
DH = 64
DOCS = 4
TILE = 256
EPS = 1e-06
MASKED = -1e30
LANES = 128
BF16 = jnp.bfloat16
F32 = jnp.float32


def swap(value, axis):
    return lax.ppermute(value, axis, [(0, 1), (1, 0)])


def xor_swap(value, axis, size, bit):
    return lax.ppermute(value, axis, [(i, i ^ bit) for i in range(size)])


def kxh(k, x, h):
    return (k * 2 + x) * 2 + h


def fetch_home_away(value):
    pairs = []
    for k in range(2):
        for x in range(2):
            for h in range(2):
                target = (k, 1 - x, h) if k == h else (1 - k, x, 1 - h)
                pairs.append((kxh(k, x, h), kxh(*target)))
    return lax.ppermute(value, ("k", "x", "h"), pairs)


def fetch_away(value):
    pairs = [
        (kxh(k, x, 1 - k), kxh(k, 1 - x, 1 - k)) for k in range(2) for x in range(2)
    ]
    return lax.ppermute(value, ("k", "x", "h"), pairs)


def tie(value, *others):
    return lax.optimization_barrier((value,) + others)[0]


def join_weight(shard, first, second, home, axis):
    mine = jnp.where(home, shard, first)
    other = jnp.where(home, first, second)
    return jnp.concatenate([mine, other], axis=axis)


def add_parts(kept, moved):
    return (kept.astype(F32) + moved.astype(F32)).astype(BF16)


def to_home(value):
    return lax.ppermute(value, ("k", "h"), [(1, 0), (2, 3)])


def from_home(value):
    return lax.ppermute(value, ("k", "h"), [(0, 2), (3, 1)])


def home_swap(value, size, bit):
    pairs = []
    for o in range(size):
        for k in range(2):
            pairs.append(((o * 2 + k) * 2 + k, ((o ^ bit) * 2 + k) * 2 + k))
    return lax.ppermute(value, ("o", "k", "h"), pairs)


def bits_of(size):
    return [1 << i for i in range(size.bit_length() - 1)]


def split_rows(value, high):
    half = value.shape[0] // 2
    low_rows, high_rows = value[:half], value[half:]
    return jnp.where(high, high_rows, low_rows), jnp.where(high, low_rows, high_rows)


def merge_rows(kept, moved, high):
    return jnp.concatenate([jnp.where(high, moved, kept), jnp.where(high, kept, moved)], axis=0)


def take_half(value, index):
    half = value.shape[0] // 2
    return lax.dynamic_slice_in_dim(value, index * half, half, 0)


def kx(k, x):
    return k * 2 + x


SPREAD_A = []
SPREAD_B = []
for _k in range(2):
    for _x in range(2):
        if _k == _x:
            SPREAD_A.append((kx(_k, _x), kx(1 - _k, _x)))
        else:
            SPREAD_A.append((kx(_k, _x), kx(_k, 1 - _x)))
            SPREAD_B.append((kx(_k, _x), kx(1 - _k, 1 - _x)))


def spread_tokens(block, core, same):
    near = take_half(block, core)
    far = take_half(block, 1 - core)
    first = lax.ppermute(jnp.where(same, far, near), ("k", "x"), SPREAD_A)
    second = lax.ppermute(far, ("k", "x"), SPREAD_B)
    own = jnp.where(same, near, first)
    other = jnp.where(same, first, second)
    return jnp.concatenate([own, other], axis=1)


def unspread_parts(rows, same):
    half = rows.shape[1] // 2
    own, other = rows[:, :half], rows[:, half:]
    return own, jnp.where(same, other, own), other


def unspread_moves(near, far):
    first = lax.ppermute(near, ("k", "x"), [(b, a) for a, b in SPREAD_A])
    second = lax.ppermute(far, ("k", "x"), [(b, a) for a, b in SPREAD_B])
    return first, second


def unspread_join(own, first, second, core, same):
    near = jnp.where(same, own, first)
    far = jnp.where(same, first, second)
    low = jnp.where(core == 0, near, far)
    high = jnp.where(core == 0, far, near)
    return jnp.concatenate([low, high], axis=0)


def contract_rows(left, right):
    return lax.dot_general(
        left, right, (((0,), (0,)), ((), ())), preferred_element_type=F32
    )


def contract_cols(left, right):
    return lax.dot_general(
        left, right, (((1,), (1,)), ((), ())), preferred_element_type=F32
    )


def matmul(left, right):
    return jnp.dot(left, right, preferred_element_type=F32)


def dot_nn(left, right):
    return lax.dot_general(left, right, (((1,), (0,)), ((), ())), preferred_element_type=F32)


def dot_nt(left, right):
    return lax.dot_general(left, right, (((1,), (1,)), ((), ())), preferred_element_type=F32)


def tile_mask(qrow, kcol, rows, cols, i, j):
    key_pos = j * TILE + lax.broadcasted_iota(jnp.int32, (TILE, TILE), 0)
    query_pos = i * TILE + lax.broadcasted_iota(jnp.int32, (TILE, TILE), 1)
    code = kcol[pl.ds(pl.multiple_of(j * TILE, TILE), TILE), 0:1]
    first = qrow[0:1, pl.ds(pl.multiple_of(i * TILE, TILE), TILE)]
    second = qrow[1:2, pl.ds(pl.multiple_of(i * TILE, TILE), TILE)]
    seen = (key_pos <= query_pos) & ((code == first) | (code == second))
    return jnp.where(seen, 0.0, MASKED)


def split_parts(value):
    high = value.astype(BF16)
    rest = value - high.astype(F32)
    mid = rest.astype(BF16)
    low = (rest - mid.astype(F32)).astype(BF16)
    return high, mid, low


def lane(shape):
    return lax.broadcasted_iota(jnp.int32, shape, 1)


def forward_kernel(
    heads, count, prompt_len, flags, proj_hbm, bias_ref, kcol, qrow, att_hbm, ot_hbm, lse_ref,
    qp_hbm, kp_hbm, vp_hbm, logit, qkv, qp, kp, vp, vt, rates, sums_ref, attended, ot, mask,
    in_sem, out_sem, keep_sem, *per_head,
):
    me = lax.axis_index("p") * 2 + lax.axis_index("k")
    total = qkv.shape[0]
    size = total // count
    tiles = total // TILE
    loads = []
    for b in range(count):
        rows = pl.ds(b * size, size)
        loads.append(pltpu.make_async_copy(proj_hbm.at[b ^ me], qkv.at[rows], in_sem.at[b]))
    for load in loads:
        load.start()
    for load in loads:
        load.wait()
    logit[...] = qkv[:, 3 * DH * heads :] + bias_ref[...]
    value = logit[...]
    rate = jnp.minimum(value, 0.0) - jnp.log1p(jnp.exp(-jnp.abs(value)))
    rate = jnp.where(lane(rate.shape) < heads, rate, 0.0)
    high, mid, low = split_parts(rate)
    packed = high.astype(F32) + pltpu.roll(mid.astype(F32), 8, 1) + pltpu.roll(low.astype(F32), 16, 1)
    rates[...] = packed.astype(BF16)
    place_row = lax.broadcasted_iota(jnp.int32, (LANES, LANES), 0)
    place_col = lax.broadcasted_iota(jnp.int32, (LANES, LANES), 1)

    prompt_tiles = prompt_len // TILE
    wide = (TILE, TILE)
    row_pos, col_pos = lax.broadcasted_iota(jnp.int32, wide, 0), lax.broadcasted_iota(jnp.int32, wide, 1)
    below = jnp.where(col_pos <= row_pos, 1.0, 0.0).astype(BF16)

    def prompt_sums(t, before):
        rows = pl.ds(pl.multiple_of(t * TILE, TILE), TILE)
        prefix = dot_nn(below, rates[rows, :]) + before
        sums_ref[rows, :] = prefix
        return prefix[TILE - 1 : TILE, :]

    lax.fori_loop(0, prompt_tiles, prompt_sums, jnp.zeros((1, LANES), F32))
    doc_index = lax.broadcasted_iota(jnp.int32, (8, prompt_len), 0)
    within = jnp.where(qrow[3:4, 0:prompt_len] <= doc_index, 1.0, 0.0).astype(BF16)
    doc_sums = dot_nn(within, rates[0:prompt_len, :])

    def branch_sums(t, carry):
        rows = pl.ds(pl.multiple_of(t * TILE, TILE), TILE)
        limit = kcol[rows, 2:3]
        start = jnp.zeros((TILE, LANES), F32)
        for doc in range(DOCS):
            start = jnp.where(limit == doc, doc_sums[doc : doc + 1, :], start)

        def add_own(u, acc):
            others = pl.ds(pl.multiple_of(u * TILE, TILE), TILE)
            own = (u * TILE + col_pos <= t * TILE + row_pos) & (kcol[rows, 1:2] == qrow[2:3, others])
            return acc + dot_nn(jnp.where(own, 1.0, 0.0).astype(BF16), rates[others, :])

        sums_ref[rows, :] = lax.fori_loop(prompt_tiles, t + 1, add_own, start)
        return carry

    lax.fori_loop(prompt_tiles, tiles, branch_sums, 0)

    def prepare(t, carry):
        rows = pl.ds(pl.multiple_of(t * TILE, TILE), TILE)
        sums = sums_ref[rows, :]
        decay = sums + pltpu.roll(sums, LANES - 8, 1) + pltpu.roll(sums, LANES - 16, 1)
        decay = jnp.where(lane(decay.shape) < heads, -decay, 0.0)
        high, mid, low = split_parts(decay)
        parts = (
            high.astype(F32) + pltpu.roll(mid.astype(F32), 8, 1) + pltpu.roll(low.astype(F32), 16, 1)
        ).astype(BF16)
        lanes = lane((TILE, LANES))
        for h in range(heads):
            base = 3 * DH * h
            query = qkv[rows, base : base + DH].astype(BF16).astype(F32) * DH ** (-0.5)
            key = qkv[rows, base + DH : base + 2 * DH]
            worth = qkv[rows, base + 2 * DH : base + 3 * DH].astype(BF16)
            ones = jnp.where((lanes >= DH) & (lanes < DH + 3), 1.0, 0.0)[:, :DH]
            ones = jnp.where(lane((TILE, DH)) < 3, 1.0, 0.0)
            qp[h, rows, :] = jnp.concatenate([query, ones], axis=1).astype(BF16)
            spread = jnp.where(
                (place_col >= DH) & (place_col < DH + 3) & (place_row == 8 * (place_col - DH) + h), 1.0, 0.0
            ).astype(BF16)
            extra = dot_nn(parts, spread)
            extra = jnp.where(lanes == DH + 3, 1.0, extra)
            key_wide = jnp.concatenate([key, extra[:, DH:]], axis=1)
            kp[h, rows, :] = key_wide.astype(BF16)
            vp[h, rows, :] = worth
            vt[h, :, rows] = worth.astype(F32).T.astype(BF16)
        return carry

    lax.fori_loop(0, tiles, prepare, 0)
    keeps = [
        pltpu.make_async_copy(qp, qp_hbm, keep_sem.at[0]),
        pltpu.make_async_copy(kp, kp_hbm, keep_sem.at[1]),
        pltpu.make_async_copy(vp, vp_hbm, keep_sem.at[2]),
    ]
    for keep in keeps:
        keep.start()

    acc, top_refs, total_refs, score_refs = (per_head[n * heads : (n + 1) * heads] for n in range(4))

    def query_tile(i, carry):
        cols = pl.ds(pl.multiple_of(i * TILE, TILE), TILE)
        for h in range(heads):
            top_refs[h][...] = jnp.full(top_refs[h].shape, MASKED, F32)
            total_refs[h][...] = jnp.zeros(total_refs[h].shape, F32)
            acc[h][...] = jnp.zeros(acc[h].shape, F32)

        def key_tile(j, inner):
            @pl.when(flags[i * tiles + j] > 0)
            def _():
                rows = pl.ds(pl.multiple_of(j * TILE, TILE), TILE)
                mask[...] = tile_mask(qrow, kcol, None, None, i, j)
                tops = []
                for h in range(heads):
                    scores = dot_nt(kp[h, rows, :], qp[h, cols, :]) + mask[...]
                    score_refs[h][...] = scores
                    tops.append(jnp.maximum(top_refs[h][0:1, :], jnp.max(scores, axis=0, keepdims=True)))
                for h, top in enumerate(tops):
                    expo = jnp.exp(score_refs[h][...] - top)
                    shrink = jnp.exp(top_refs[h][0:1, :] - top)
                    top_refs[h][0:1, :] = top
                    total_refs[h][0:1, :] = total_refs[h][0:1, :] * shrink + jnp.sum(expo, axis=0, keepdims=True)
                    acc[h][...] = acc[h][...] * shrink + dot_nn(vt[h, :, rows], expo.astype(BF16))

            return inner

        lax.fori_loop(0, i + 1, key_tile, 0)
        for h in range(heads):
            total = total_refs[h][0:1, :]
            ot[pl.ds(h * DH, DH), cols] = acc[h][...] / total
            lse_ref[h : h + 1, cols] = top_refs[h][0:1, :] + jnp.log(total)
        attended[cols, :] = ot[:, cols].T.astype(BF16)
        return carry

    lse_ref[...] = jnp.zeros(lse_ref.shape, F32)
    lax.fori_loop(0, tiles, query_tile, 0)
    stores = [pltpu.make_async_copy(ot, ot_hbm, keep_sem.at[3])]
    for b in range(count):
        stores.append(
            pltpu.make_async_copy(attended.at[pl.ds(b * size, size)], att_hbm.at[b ^ me], out_sem.at[b])
        )
    for store in stores:
        store.start()
    for copy in keeps + stores:
        copy.wait()


def attention_forward(projected, bias, kcol, qrow, flags, heads, prompt_len):
    count, size, width = projected.shape
    total = count * size
    any_spec = pl.BlockSpec(memory_space=pl.ANY)
    vmem = pl.BlockSpec(memory_space=pltpu.VMEM)
    shape = jax.ShapeDtypeStruct
    return pl.pallas_call(
        functools.partial(forward_kernel, heads, count, prompt_len),
        out_shape=(
            shape((count, size, heads * DH), BF16),
            shape((heads * DH, total), F32),
            shape((8, total), F32),
            shape((heads, total, LANES), BF16),
            shape((heads, total, LANES), BF16),
            shape((heads, total, DH), BF16),
            shape((total, LANES), F32),
        ),
        in_specs=[pl.BlockSpec(memory_space=pltpu.SMEM), any_spec, vmem, vmem, vmem],
        out_specs=(any_spec, any_spec, vmem, any_spec, any_spec, any_spec, vmem),
        scratch_shapes=[
            pltpu.VMEM((total, width), F32),
            pltpu.VMEM((heads, total, LANES), BF16),
            pltpu.VMEM((heads, total, LANES), BF16),
            pltpu.VMEM((heads, total, DH), BF16),
            pltpu.VMEM((heads, DH, total), BF16),
            pltpu.VMEM((total, LANES), BF16),
            pltpu.VMEM((total, LANES), F32),
            pltpu.VMEM((total, heads * DH), BF16),
            pltpu.VMEM((heads * DH, total), F32),
            pltpu.VMEM((TILE, TILE), F32),
            pltpu.SemaphoreType.DMA((count,)),
            pltpu.SemaphoreType.DMA((count,)),
            pltpu.SemaphoreType.DMA((4,)),
        ]
        + [pltpu.VMEM((DH, TILE), F32)] * heads
        + [pltpu.VMEM((8, TILE), F32)] * (2 * heads)
        + [pltpu.VMEM((TILE, TILE), F32)] * heads,
        compiler_params=pltpu.CompilerParams(vmem_limit_bytes=48 << 20),
        cost_estimate=pl.CostEstimate(flops=20_000_000_000, bytes_accessed=30_000_000, transcendentals=0),
        name="attention_forward",
    )(flags, projected, bias, kcol, qrow)


def backward_kernel(
    heads, count, prompt_len, flags, gatt_hbm, ot_ref, lse_ref, qp, kp, vp, logit, kcol, qrow,
    grad_hbm, bias_ref, gatt, gout, kt, delta, mask, decay, grad, in_sem, out_sem, *per_head,
):
    dqt, dk, dv, prob_refs, score_refs = (per_head[n * heads : (n + 1) * heads] for n in range(5))
    me = lax.axis_index("p") * 2 + lax.axis_index("k")
    total = gatt.shape[0]
    size = total // count
    tiles = total // TILE
    loads = []
    for b in range(count):
        rows = pl.ds(b * size, size)
        loads.append(pltpu.make_async_copy(gatt_hbm.at[b ^ me], gatt.at[rows], in_sem.at[b]))
    for load in loads:
        load.start()
    for load in loads:
        load.wait()
    for h in range(heads):
        dqt[h][...] = jnp.zeros(dqt[h].shape, F32)
    delta[...] = jnp.zeros(delta.shape, F32)

    def prepare(t, carry):
        rows = pl.ds(pl.multiple_of(t * TILE, TILE), TILE)
        turned = gatt[rows, :].astype(F32).T * ot_ref[:, rows]
        for h in range(heads):
            gout[h, rows, :] = gatt[rows, h * DH : (h + 1) * DH]
            kt[h, :, rows] = kp[h, rows, :].astype(F32).T[: DH + 8].astype(BF16)
            delta[h : h + 1, rows] = jnp.sum(turned[h * DH : (h + 1) * DH], axis=0, keepdims=True)
        return carry

    lax.fori_loop(0, tiles, prepare, 0)
    lanes = lane((TILE, LANES))

    def key_tile(j, carry):
        rows = pl.ds(pl.multiple_of(j * TILE, TILE), TILE)
        for h in range(heads):
            dk[h][...] = jnp.zeros(dk[h].shape, F32)
            dv[h][...] = jnp.zeros(dv[h].shape, F32)

        def query_tile(i, inner):
            @pl.when(flags[i * tiles + j] > 0)
            def _():
                cols = pl.ds(pl.multiple_of(i * TILE, TILE), TILE)
                mask[...] = tile_mask(qrow, kcol, None, None, i, j)
                for h in range(heads):
                    scores = dot_nt(kp[h, rows, :], qp[h, cols, :]) + mask[...]
                    prob_refs[h][...] = jnp.exp(scores - lse_ref[h : h + 1, cols])
                for h in range(heads):
                    probs = prob_refs[h][...]
                    grad_probs = dot_nt(vp[h, rows, :], gout[h, cols, :])
                    score_refs[h][...] = (probs * (grad_probs - delta[h : h + 1, cols])).astype(BF16)
                    dv[h][...] += dot_nn(probs.astype(BF16), gout[h, cols, :])
                for h in range(heads):
                    grad_scores = score_refs[h][...]
                    dk[h][...] += dot_nn(grad_scores, qp[h, cols, :])
                    dqt[h][:, cols] += dot_nn(kt[h, :, rows], grad_scores)

            return inner

        lax.fori_loop(j, tiles, query_tile, 0)
        keys = jnp.zeros((TILE, LANES), F32)
        for h in range(heads):
            grad_key = dk[h][...]
            keys += jnp.where(lanes == h, pltpu.roll(grad_key, LANES - DH + h, 1), 0.0)
            grad[rows, (3 * h + 1) * DH : (3 * h + 3) * DH] = jnp.concatenate(
                [grad_key[:, :DH], dv[h][...]], axis=1
            ).astype(BF16)
        decay[rows, :] = -keys
        return carry

    lax.fori_loop(0, tiles, key_tile, 0)

    def finish(t, carry):
        rows = pl.ds(pl.multiple_of(t * TILE, TILE), TILE)
        queries = jnp.zeros((TILE, LANES), F32)
        for h in range(heads):
            turned = jnp.concatenate([dqt[h][:, rows], jnp.zeros((LANES - DH - 8, TILE), F32)], axis=0).T
            queries += jnp.where(lanes == h, pltpu.roll(turned, LANES - DH - 3 + h, 1), 0.0)
            grad[rows, 3 * h * DH : (3 * h + 1) * DH] = (turned[:, :DH] * DH ** (-0.5)).astype(BF16)
        whole = decay[rows, :] + queries
        high, mid, low = split_parts(whole)
        decay[rows, :] = (
            high.astype(F32) + pltpu.roll(mid.astype(F32), 8, 1) + pltpu.roll(low.astype(F32), 16, 1)
        )
        return carry

    lax.fori_loop(0, tiles, finish, 0)

    prompt_tiles = prompt_len // TILE
    wide = (TILE, TILE)
    row_pos, col_pos = lax.broadcasted_iota(jnp.int32, wide, 0), lax.broadcasted_iota(jnp.int32, wide, 1)
    above = jnp.where(col_pos >= row_pos, 1.0, 0.0).astype(BF16)
    branch_len = total - prompt_len
    doc_index = lax.broadcasted_iota(jnp.int32, (8, branch_len), 0)
    chosen = jnp.where(qrow[4:5, prompt_len:total] == doc_index, 1.0, 0.0).astype(BF16)
    doc_sums = dot_nn(chosen, decay[prompt_len:total, :].astype(BF16))

    def prompt_sums(n, after):
        t = prompt_tiles - 1 - n
        rows = pl.ds(pl.multiple_of(t * TILE, TILE), TILE)
        suffix = dot_nn(above, decay[rows, :].astype(BF16)) + after
        doc = kcol[rows, 3:4]
        sums = suffix
        for d in range(DOCS):
            sums = sums + jnp.where(doc <= d, doc_sums[d : d + 1, :], 0.0)
        decay[rows, :] = sums
        return suffix[0:1, :]

    def branch_sums(t, carry):
        rows = pl.ds(pl.multiple_of(t * TILE, TILE), TILE)

        def add_own(u, acc):
            others = pl.ds(pl.multiple_of(u * TILE, TILE), TILE)
            own = (u * TILE + col_pos >= t * TILE + row_pos) & (kcol[rows, 1:2] == qrow[2:3, others])
            return acc + dot_nn(jnp.where(own, 1.0, 0.0).astype(BF16), decay[others, :].astype(BF16))

        decay[rows, :] = lax.fori_loop(t, tiles, add_own, jnp.zeros((TILE, LANES), F32))
        return carry

    lax.fori_loop(0, prompt_tiles, prompt_sums, jnp.zeros((1, LANES), F32))
    lax.fori_loop(prompt_tiles, tiles, branch_sums, 0)

    def rates(t, bias):
        rows = pl.ds(pl.multiple_of(t * TILE, TILE), TILE)
        sums = decay[rows, :]
        grad_rate = sums + pltpu.roll(sums, LANES - 8, 1) + pltpu.roll(sums, LANES - 16, 1)
        value = logit[rows, :]
        grad_forget = grad_rate / (1.0 + jnp.exp(value))
        grad_forget = jnp.where(lanes < heads, grad_forget, 0.0).astype(BF16)
        grad[rows, 3 * DH * heads :] = grad_forget
        return bias + jnp.sum(grad_forget.astype(F32), axis=0, keepdims=True)

    bias_ref[...] = jnp.broadcast_to(
        lax.fori_loop(0, tiles, rates, jnp.zeros((1, LANES), F32)), bias_ref.shape
    )
    stores = []
    for b in range(count):
        stores.append(
            pltpu.make_async_copy(grad.at[pl.ds(b * size, size)], grad_hbm.at[b ^ me], out_sem.at[b])
        )
    for store in stores:
        store.start()
    for store in stores:
        store.wait()


def attention_backward(grad_attended, saved, kcol, qrow, flags, heads, prompt_len):
    ot, lse, qp, kp, vp, logit = saved
    count, size, width = grad_attended.shape
    total = count * size
    any_spec = pl.BlockSpec(memory_space=pl.ANY)
    vmem = pl.BlockSpec(memory_space=pltpu.VMEM)
    shape = jax.ShapeDtypeStruct
    out_width = 3 * DH * heads + LANES
    return pl.pallas_call(
        functools.partial(backward_kernel, heads, count, prompt_len),
        out_shape=(shape((count, size, out_width), BF16), shape((8, LANES), F32)),
        in_specs=[pl.BlockSpec(memory_space=pltpu.SMEM), any_spec]
        + [vmem] * 8,
        out_specs=(any_spec, vmem),
        scratch_shapes=[
            pltpu.VMEM((total, width), BF16),
            pltpu.VMEM((heads, total, DH), BF16),
            pltpu.VMEM((heads, DH + 8, total), BF16),
            pltpu.VMEM((8, total), F32),
            pltpu.VMEM((TILE, TILE), F32),
            pltpu.VMEM((total, LANES), F32),
            pltpu.VMEM((total, out_width), BF16),
            pltpu.SemaphoreType.DMA((count,)),
            pltpu.SemaphoreType.DMA((count,)),
        ]
        + [pltpu.VMEM((DH + 8, total), F32)] * heads
        + [pltpu.VMEM((TILE, LANES), F32)] * heads
        + [pltpu.VMEM((TILE, DH), F32)] * heads
        + [pltpu.VMEM((TILE, TILE), F32)] * heads
        + [pltpu.VMEM((TILE, TILE), BF16)] * heads,
        compiler_params=pltpu.CompilerParams(vmem_limit_bytes=56 << 20),
        cost_estimate=pl.CostEstimate(flops=50_000_000_000, bytes_accessed=30_000_000, transcendentals=0),
        name="attention_backward",
    )(flags, grad_attended, ot, lse, qp, kp, vp, logit, kcol, qrow)


def group_codes(prompt_ids, branch_ids, branch_docs):
    prompt_len = prompt_ids.shape[0]
    member = branch_ids[:, None] == jnp.arange(branch_docs.shape[0])[None, :]
    branch_doc_ids = jnp.sum(jnp.where(member, branch_docs[None, :], 0), axis=1)
    key_code = jnp.concatenate([prompt_ids, DOCS + branch_ids])
    first = jnp.concatenate([prompt_ids, branch_doc_ids])
    tag = jnp.concatenate([jnp.full_like(prompt_ids, -1), branch_ids])
    limit = jnp.concatenate([jnp.full_like(prompt_ids, -1), branch_doc_ids])
    prompt_code = jnp.concatenate([prompt_ids, jnp.full_like(branch_ids, DOCS)])
    total = key_code.shape[0]
    none = jnp.zeros_like(tag)
    kcol = jnp.stack([key_code, tag, limit, prompt_code] + [none] * 4, axis=1)
    qrow = jnp.stack([first, key_code, tag, prompt_code, limit] + [none] * 3, axis=0)
    tiles = total // TILE
    kinds = jnp.arange(2 * DOCS)
    key_bits = jnp.any(key_code.reshape(tiles, TILE, 1) == kinds, axis=1)
    query_bits = key_bits | jnp.any(first.reshape(tiles, TILE, 1) == kinds, axis=1)
    order = jnp.arange(tiles)
    meets = jnp.any(query_bits[:, None, :] & key_bits[None, :, :], axis=2)
    flags = (meets & (order[None, :] <= order[:, None])).astype(jnp.int32).reshape(-1)
    return kcol, qrow, flags


class Wires:
    def __init__(self, send_sem, recv_sem, local_sem):
        self.send_sem, self.recv_sem, self.local_sem = send_sem, recv_sem, local_sem
        self.used, self.local_used = 0, 0
        self.k, self.x = lax.axis_index("k"), lax.axis_index("x")
        self.h, self.p, self.o = lax.axis_index("h"), lax.axis_index("p"), lax.axis_index("o")
        self.home = self.k == self.h
        self.same = self.k == self.x
        self.pending = []

    def slot(self):
        self.used += 1
        return self.used - 1

    def copy(self, source, target, device, slot):
        return pltpu.make_async_remote_copy(
            src_ref=source,
            dst_ref=target,
            send_sem=self.send_sem.at[slot],
            recv_sem=self.recv_sem.at[slot],
            device_id=device,
            device_id_type=pl.DeviceIdType.MESH,
        )

    def send(self, source, target, device):
        copy = self.copy(source, target, device, self.slot())
        copy.start()
        self.pending.append(copy.wait_send)
        return copy

    def local(self, source, target):
        copy = pltpu.make_async_copy(source, target, self.local_sem.at[self.local_used])
        self.local_used += 1
        copy.start()
        return copy

    def greet(self, devices):
        barrier = pltpu.get_barrier_semaphore()
        for device in devices:
            pl.semaphore_signal(
                barrier, inc=1, device_id=device, device_id_type=pl.DeviceIdType.MESH
            )
        pl.semaphore_wait(barrier, len(devices))

    def close(self):
        for wait in self.pending:
            wait()


def row_spans(total, pieces):
    size = total // pieces
    return [pl.ds(i * size, size) for i in range(pieces)]


class Fetch:
    def __init__(self, wires, shard, target, stage, pieces, got=None, keep=None):
        w = self.wires = wires
        self.shard, self.target, self.stage, self.got, self.keep = shard, target, stage, got, keep
        self.count = pieces
        self.half_rows = shard.shape[0] // 2
        self.size = self.half_rows // pieces
        self.by_columns = len(target.shape) == 2
        self.first = [w.slot() for _ in range(pieces)]
        self.over = [w.slot() for _ in range(pieces)]
        self.second = [w.slot() for _ in range(2 * pieces)]
        self.local_slot = w.local_used
        w.local_used += 2

    def rows(self, i, mine=True):
        bit = self.wires.o % 2
        bit = bit if mine else 1 - bit
        return pl.ds(pl.multiple_of(bit * self.half_rows + i * self.size, 16), self.size)

    def place(self, half, span):
        if self.by_columns:
            width = self.shard.shape[1]
            return self.target.at[span, pl.ds(half * width, width)]
        return self.target.at[half, span]

    def first_copy(self, i, home):
        w, span = self.wires, self.rows(i)
        if home:
            return w.copy(self.shard.at[span], self.place(1, span), {"x": 1 - w.x}, self.first[i])
        device = {"k": 1 - w.k, "h": 1 - w.h}
        return w.copy(self.shard.at[span], self.place(0, span), device, self.first[i])

    def have(self, i, half):
        if self.got is None:
            return self.place(half, self.rows(i))
        return self.got.at[pl.ds(i * self.size, self.size)]

    def over_copy(self, i, home):
        w, half = self.wires, 1 if home else 0
        return w.copy(self.have(i, half), self.place(half, self.rows(i)), {"o": w.o ^ 1}, self.over[i])

    def second_copy(self, i, mine):
        w, span = self.wires, self.rows(i, mine)
        source = self.have(i, 0) if mine else self.place(0, span)
        slot = self.second[i if mine else self.count + i]
        return w.copy(source, self.place(1, span), {"x": 1 - w.x}, slot)

    def shard_load(self):
        return pltpu.make_async_copy(self.shard, self.stage, self.wires.local_sem.at[self.local_slot])

    def shard_store(self):
        whole = pl.ds(0, self.shard.shape[0])
        return pltpu.make_async_copy(
            self.stage, self.place(0, whole), self.wires.local_sem.at[self.local_slot]
        )

    def got_load(self):
        return pltpu.make_async_copy(self.got, self.keep, self.wires.local_sem.at[self.local_slot + 1])

    def got_store(self, half):
        bit = self.wires.o % 2
        span = pl.ds(pl.multiple_of(bit * self.half_rows, 16), self.half_rows)
        return pltpu.make_async_copy(
            self.keep, self.place(half, span), self.wires.local_sem.at[self.local_slot + 1]
        )

    def either(self, at_home, away):
        pl.when(self.wires.home)(at_home)
        pl.when(jnp.logical_not(self.wires.home))(away)

    def load(self):
        pl.when(self.wires.home)(lambda: self.shard_load().start())
        if self.got is not None:
            self.got_load().start()

    def start(self):
        if self.got is not None:
            for i in range(self.count):
                self.relay(i)
            return

        def go(home):
            for i in range(self.count):
                self.first_copy(i, home).start()

        self.either(lambda: go(True), lambda: go(False))

    def store(self):
        def at_home():
            self.shard_load().wait()
            self.shard_store().start()
            if self.got is not None:
                self.got_load().wait()
                self.got_store(1).start()

        def away():
            if self.got is not None:
                self.got_load().wait()
                self.got_store(0).start()

        self.either(at_home, away)

    def relay(self, i):
        def at_home():
            if self.got is None:
                self.first_copy(i, True).wait_recv()
            self.over_copy(i, True).start()

        def away():
            if self.got is None:
                self.first_copy(i, False).wait_recv()
            self.over_copy(i, False).start()
            self.second_copy(i, True).start()

        self.either(at_home, away)

    def relay_over(self, i):
        def away():
            self.over_copy(i, False).wait_recv()
            self.second_copy(i, False).start()

        pl.when(jnp.logical_not(self.wires.home))(away)

    def wait(self):
        def at_home():
            for i in range(self.count):
                if self.got is None:
                    self.first_copy(i, True).wait_send()
                self.over_copy(i, True).wait()
            self.shard_store().wait()
            if self.got is not None:
                self.got_store(1).wait()

        def away():
            for i in range(self.count):
                if self.got is None:
                    self.first_copy(i, False).wait_send()
                self.over_copy(i, False).wait_send()
                self.second_copy(i, True).wait()
                self.second_copy(i, False).wait()
            if self.got is not None:
                self.got_store(0).wait()

        self.either(at_home, away)


def partners(wires, psize, away=False, peers=True, over_o=0):
    devices = [{"k": 1 - wires.k}]
    if peers:
        devices += [{"p": wires.p ^ bit} for bit in range(1, psize)]
    devices += [{"x": 1 - wires.x}]
    devices += [{"k": 1 - wires.k, "x": 1 - wires.x}]
    if away:
        devices += [{"k": 1 - wires.k, "h": 1 - wires.h}, {"h": 1 - wires.h}]
    bit = 1
    while bit < over_o:
        devices += [{"o": wires.o ^ bit}]
        bit *= 2
    return devices


class Share:
    def __init__(self, wires, psize, own, g, spans):
        self.wires, self.psize, self.own, self.g, self.spans = wires, psize, own, g, spans
        self.near, self.far, self.kept, self.passed = [], {}, [], []

    def send(self, i):
        w, span = self.wires, self.spans[i]
        for bit in range(1, self.psize):
            self.far[bit, i] = w.send(self.own.at[span], self.g.at[2 * bit, span], {"p": w.p ^ bit})
        self.near.append(w.send(self.own.at[span], self.g.at[1, span], {"k": 1 - w.k}))
        self.kept.append(w.local(self.own.at[span], self.g.at[0, span]))

    def relay(self, i):
        w, span = self.wires, self.spans[i]
        for bit in range(1, self.psize):
            self.far[bit, i].wait_recv()
            self.passed.append(
                w.send(self.g.at[2 * bit, span], self.g.at[2 * bit + 1, span], {"k": 1 - w.k})
            )

    def wait(self):
        for copy in self.near + self.passed:
            copy.wait_recv()
        for copy in self.kept:
            copy.wait()


def by_chunks(span, body):
    def run(n, carry):
        body(pl.ds(pl.multiple_of(span.start + n * CHUNK, CHUNK), CHUNK))
        return carry

    lax.fori_loop(0, span.size // CHUNK, run, 0)


def add_into(value, *others):
    def body(rows):
        total = value[rows, :].astype(F32)
        for other in others:
            total = total + other[rows, :].astype(F32)
        value[rows, :] = total.astype(BF16)

    by_chunks(pl.ds(0, value.shape[0]), body)


class Reduce:
    def __init__(self, wires, psize, part, near, mid, far, spans):
        self.wires, self.psize, self.part = wires, psize, part
        self.near, self.mid, self.far, self.spans = near, mid, far, spans
        self.near_copies, self.far_copies = {}, {}

    def start(self):
        w = self.wires
        for bit in reversed(range(self.psize)):
            for i, span in enumerate(self.spans):
                self.near_copies[bit, i] = w.send(
                    self.part.at[2 * bit + 1, span], self.near.at[bit, span], {"k": 1 - w.k}
                )
        for bit in reversed(range(1, self.psize)):
            for i, span in enumerate(self.spans):
                self.near_copies[bit, i].wait_recv()

                def add(rows, bit=bit):
                    self.mid[bit - 1, rows] = (
                        self.part[2 * bit, rows].astype(F32) + self.near[bit, rows].astype(F32)
                    ).astype(BF16)

                by_chunks(span, add)
                self.far_copies[bit, i] = w.send(
                    self.mid.at[bit - 1, span], self.far.at[bit - 1, span], {"p": w.p ^ bit}
                )

    def each(self, i, body):
        span = self.spans[i]
        self.near_copies[0, i].wait_recv()
        for bit in range(1, self.psize):
            self.far_copies[bit, i].wait_recv()

        def run(rows):
            total = self.part[0, rows].astype(F32) + self.near[0, rows].astype(F32)
            for bit in range(1, self.psize):
                total = total + self.far[bit - 1, rows].astype(F32)
            body(rows, total)

        by_chunks(span, run)


CHUNK = 32
PIECES = 3


def inverse_rms(value):
    return lax.rsqrt(jnp.sum(value * value, axis=1, keepdims=True) / D + EPS)


def norm_back(grad, value, base, gain):
    rms = inverse_rms(value)
    gained = gain * grad
    inner = jnp.sum(value * gained, axis=1, keepdims=True)
    result = base + rms * gained - value * (rms * rms * rms) * inner / D
    parts = grad * value * rms
    return result, sum(parts[n : n + 8] for n in range(0, parts.shape[0], 8))


def enter_kernel(
    psize, x_ref, gain_own, codes_own, qkv_shard, forget_shard, out_shard, xin, g, proj, out, gain_ref, codes,
    own, qkv_stage, forget_stage, out_stage, send_sem, recv_sem, local_sem,
):
    w = Wires(send_sem, recv_sem, local_sem)
    width = qkv_shard.shape[1]
    qkv = Fetch(w, qkv_shard, proj.at[:, :, pl.ds(0, width)], qkv_stage, 3)
    forget = Fetch(
        w, forget_shard, proj.at[:, :, pl.ds(width, forget_shard.shape[1])], forget_stage, 1
    )
    out_fetch = Fetch(w, out_shard, out, out_stage, 1)
    for fetch in (qkv, forget, out_fetch):
        fetch.load()
    w.greet(partners(w, psize, away=True, over_o=2))
    rows, half = own.shape[0], x_ref.shape[1]
    spans = row_spans(rows, PIECES)
    size = rows // PIECES
    def spread(source, target, pieces):
        count = len(pieces)
        to_near = [w.slot() for _ in pieces]
        to_far = [w.slot() for _ in pieces]
        kept = [w.local_used + i for i in range(count)]
        w.local_used += count

        def piece(base, i):
            start, length = pieces[i]
            return source.at[pl.ds(pl.multiple_of(base * rows + start, 8), length)]

        def span(i):
            return pl.ds(pieces[i][0], pieces[i][1])

        left, right = pl.ds(0, half), pl.ds(half, half)

        def same_keep(i):
            return pltpu.make_async_copy(piece(w.k, i), target.at[span(i), left], local_sem.at[kept[i]])

        def same_send(i):
            return w.copy(piece(1 - w.k, i), target.at[span(i), left], {"k": 1 - w.k}, to_near[i])

        def cross_near(i):
            return w.copy(piece(w.k, i), target.at[span(i), right], {"x": 1 - w.x}, to_near[i])

        def cross_far(i):
            return w.copy(
                piece(1 - w.k, i), target.at[span(i), right], {"k": 1 - w.k, "x": 1 - w.x}, to_far[i]
            )

        def start():
            @pl.when(w.same)
            def _():
                for i in range(count):
                    same_send(i).start()
                    same_keep(i).start()

            @pl.when(jnp.logical_not(w.same))
            def _():
                for i in range(count):
                    cross_near(i).start()
                    cross_far(i).start()

        def arrive(i):
            @pl.when(w.same)
            def _():
                same_keep(i).wait()
                same_send(i).wait_recv()

            @pl.when(jnp.logical_not(w.same))
            def _():
                cross_near(i).wait_recv()
                cross_far(i).wait_recv()

        def close():
            @pl.when(w.same)
            def _():
                for i in range(count):
                    same_send(i).wait_send()

            @pl.when(jnp.logical_not(w.same))
            def _():
                for i in range(count):
                    cross_near(i).wait_send()
                    cross_far(i).wait_send()

        return start, arrive, close

    gain_copy = w.send(gain_own, gain_ref.at[:, pl.ds(half, half)], {"x": 1 - w.x})
    code_copies = [
        w.send(codes_own, codes.at[1], {"x": 1 - w.x}),
        w.send(codes_own, codes.at[2], {"k": 1 - w.k}),
        w.send(codes_own, codes.at[3], {"k": 1 - w.k, "x": 1 - w.x}),
    ]
    codes[0] = codes_own[...]
    start, arrive, close = spread(x_ref, xin, [(i * size, size) for i in range(PIECES)])
    start()
    qkv.start()
    forget.start()
    share = Share(w, psize, own, g, spans)
    gain_ref[:, pl.ds(0, half)] = gain_own[...]
    gain_copy.wait_recv()
    for i, span in enumerate(spans):
        arrive(i)

        def norm(rows):
            value = xin[rows, :].astype(F32)
            own[rows, :] = (value * inverse_rms(value) * gain_ref[0:1, :]).astype(BF16)

        by_chunks(span, norm)
        share.send(i)
    close()
    for fetch in (qkv, forget, out_fetch):
        fetch.store()
    for i in range(3):
        qkv.relay(i)
    out_fetch.start()
    forget.relay(0)
    for i in range(3):
        qkv.relay_over(i)
        if i < PIECES:
            share.relay(i)
    forget.relay_over(0)
    out_fetch.relay(0)
    out_fetch.relay_over(0)
    share.wait()
    for fetch in (qkv, forget, out_fetch):
        fetch.wait()
    for copy in code_copies:
        copy.wait_recv()
    w.close()


def forward_exchange_kernel(
    psize, part, xin, gain_ref, gate_shard, gate_got, up_shard, up_got, down_shard, resid, g, gate, up, down,
    near, mid, far, own, gate_stage, gate_keep, up_stage, up_keep, down_stage, send_sem, recv_sem, local_sem,
):
    w = Wires(send_sem, recv_sem, local_sem)
    gate_fetch = Fetch(w, gate_shard, gate, gate_stage, 2, gate_got, gate_keep)
    up_fetch = Fetch(w, up_shard, up, up_stage, 2, up_got, up_keep)
    down_fetch = Fetch(w, down_shard, down, down_stage, 2)
    fetches = (gate_fetch, up_fetch, down_fetch)
    for fetch in fetches:
        fetch.load()
    w.greet(partners(w, psize, away=True, over_o=2))
    spans = row_spans(own.shape[0], PIECES)
    reduce = Reduce(w, psize, part, near, mid, far, spans)
    gate_fetch.start()
    reduce.start()
    up_fetch.start()
    down_fetch.start()
    for fetch in fetches:
        fetch.store()
    for i in range(2):
        gate_fetch.relay_over(i)
    for i in range(2):
        down_fetch.relay(i)
    for i in range(2):
        up_fetch.relay_over(i)
    share = Share(w, psize, own, g, spans)
    for i in range(PIECES):

        def norm(rows, total):
            value = total + xin[rows, :].astype(F32)
            resid[rows, :] = value
            own[rows, :] = (value * inverse_rms(value) * gain_ref[1:2, :]).astype(BF16)

        reduce.each(i, norm)
        share.send(i)
    for i in range(2):
        down_fetch.relay_over(i)
    for i in range(PIECES):
        share.relay(i)
    share.wait()
    for fetch in fetches:
        fetch.wait()
    w.close()


class EarlySum:
    def __init__(self, wires, part, value, over, across, result, pieces, offset=0, got=None):
        w = self.wires = wires
        self.offset, self.got = offset, got
        self.part, self.value, self.over, self.across, self.result = part, value, over, across, result
        self.count, self.half_rows = pieces, value.shape[1]
        self.size = self.half_rows // pieces
        self.over_slots = [[w.slot() for _ in range(pieces)] for _ in range(2)]
        self.across_slots = [w.slot() for _ in range(pieces)]
        self.local_slot = w.local_used
        w.local_used += 2 + pieces

    def span(self, i):
        return pl.ds(i * self.size, self.size)

    def load_copy(self, half):
        start = pl.multiple_of(self.offset + (self.wires.o % 2) * self.half_rows, 16)
        return pltpu.make_async_copy(
            self.part.at[half, pl.ds(start, self.half_rows)],
            self.value.at[half],
            self.wires.local_sem.at[self.local_slot + half],
        )

    def load(self):
        for half in range(2):
            self.load_copy(half).start()

    def over_copy(self, half, i):
        w = self.wires
        start = pl.multiple_of(self.offset + (1 - w.o % 2) * self.half_rows + i * self.size, 16)
        return w.copy(
            self.part.at[half, pl.ds(start, self.size)],
            self.over.at[half, self.span(i)],
            {"o": w.o ^ 1},
            self.over_slots[half][i],
        )

    def across_copy(self, i):
        w = self.wires
        return w.copy(
            self.value.at[1, self.span(i)], self.across.at[self.span(i)], {"x": 1 - w.x}, self.across_slots[i]
        )

    def keep_copy(self, i):
        return pltpu.make_async_copy(
            self.value.at[0, self.span(i)],
            self.result.at[self.span(i)],
            self.wires.local_sem.at[self.local_slot + 2 + i],
        )

    def start(self, half):
        for i in range(self.count):
            self.over_copy(half, i).start()

    def pass_on(self, i):
        if i == 0:
            self.load_copy(1).wait()
        span = self.span(i)
        if self.got is None:
            self.over_copy(1, i).wait_recv()
            add_into(self.value.at[1, span], self.over.at[1, span])
        else:
            add_into(self.value.at[1, span], self.got.at[span])
        self.across_copy(i).start()

    def finish(self, i):
        if i == 0:
            self.load_copy(0).wait()
        self.over_copy(0, i).wait_recv()
        self.across_copy(i).wait_recv()
        span = self.span(i)
        add_into(self.value.at[0, span], self.over.at[0, span], self.across.at[span])
        if self.result is not None:
            self.keep_copy(i).start()

    def close(self):
        for i in range(self.count):
            for half in range(2):
                if half == 0 or self.got is None:
                    self.over_copy(half, i).wait_send()
            self.across_copy(i).wait_send()
            if self.result is not None:
                self.keep_copy(i).wait()


def backward_exchange_kernel(
    psize, part, resid, cot, gain_ref, down_own, down_other, gate_part, gate_got, up_part,
    grad_resid, g, gain_grad, down_sum, pair_sum,
    near, mid, far, own, down_across, down_moved, gate_val, gate_over, gate_across, up_val, up_over, up_across,
    send_sem, recv_sem, local_sem,
):
    w = Wires(send_sem, recv_sem, local_sem)
    gate = EarlySum(w, gate_part, gate_val, gate_over, gate_across, pair_sum.at[0], 2, got=gate_got)
    up = EarlySum(w, up_part, up_val, up_over, up_across, pair_sum.at[1], 2)
    gate.load()
    up.load()
    w.greet(partners(w, psize, away=True, over_o=2))
    spans = row_spans(own.shape[0], PIECES)
    reduce = Reduce(w, psize, part, near, mid, far, spans)
    down_copy = w.send(down_other, down_across, {"x": 1 - w.x})
    gate.start(0)
    up.start(1)
    up.start(0)
    for i in range(2):
        gate.pass_on(i)
    reduce.start()
    down_home = w.copy(down_sum, down_moved, {"h": 1 - w.h}, w.slot())
    down_copy.wait_recv()

    def add_down(rows):
        down_sum[rows, :] = (
            down_own[rows, :].astype(F32) + down_across[rows, :].astype(F32)
        ).astype(BF16)

    by_chunks(pl.ds(0, down_sum.shape[0]), add_down)

    @pl.when(jnp.logical_not(w.home))
    def _():
        down_home.start()

    share = Share(w, psize, own, g, spans)
    gain_grad[...] = jnp.zeros(gain_grad.shape, F32)

    def back(rows, total):
        grad, gain_part = norm_back(total, resid[rows, :], cot[rows, :].astype(F32), gain_ref[1:2, :])
        grad_resid[rows, :] = grad
        own[rows, :] = grad.astype(BF16)
        gain_grad[...] += gain_part

    for i in range(PIECES):
        reduce.each(i, back)
        share.send(i)
    for i in range(2):
        up.pass_on(i)
    share.relay(0)
    for i in range(2):
        gate.finish(i)
    for i in range(1, PIECES):
        share.relay(i)
    for i in range(2):
        up.finish(i)
    share.wait()
    gate.close()
    up.close()

    @pl.when(jnp.logical_not(w.home))
    def _():
        down_home.wait_send()

    @pl.when(w.home)
    def _():
        down_home.wait_recv()
        add_into(down_sum, down_moved)

    w.close()


class Spread:
    def __init__(self, wires, value, result):
        w = self.wires = wires
        self.value, self.result = value, result
        self.over_slot, self.near_slot, self.pass_slot = w.slot(), w.slot(), w.slot()
        self.local_slot = w.local_used
        w.local_used += 1

    def rows(self, mine):
        bit = self.wires.o % 2
        return self.result.at[bit if mine else 1 - bit]

    def over_copy(self):
        w = self.wires
        return w.copy(self.value, self.rows(True), {"o": w.o ^ 1}, self.over_slot)

    def near_copy(self):
        return self.wires.copy(self.value, self.rows(True), {"k": 1 - self.wires.k}, self.near_slot)

    def pass_copy(self):
        return self.wires.copy(self.rows(False), self.rows(False), {"k": 1 - self.wires.k}, self.pass_slot)

    def keep_copy(self):
        return pltpu.make_async_copy(
            self.value, self.rows(True), self.wires.local_sem.at[self.local_slot]
        )

    def start(self):
        @pl.when(self.wires.home)
        def _():
            self.over_copy().start()
            self.near_copy().start()
            self.keep_copy().start()

    def relay(self):
        @pl.when(self.wires.home)
        def _():
            self.over_copy().wait_recv()
            self.pass_copy().start()

    def wait(self):
        @pl.when(self.wires.home)
        def _():
            self.over_copy().wait_send()
            self.near_copy().wait_send()
            self.pass_copy().wait_send()
            self.keep_copy().wait()

        @pl.when(jnp.logical_not(self.wires.home))
        def _():
            self.near_copy().wait_recv()
            self.pass_copy().wait_recv()


class SmallSum:
    def __init__(self, wires, psize, osize, value, other, buffers):
        w = self.wires = wires
        self.value, self.other, self.buffers = value, other, buffers
        self.devices = [{"x": 1 - w.x}, {"k": 1 - w.k}]
        self.devices += [{"p": w.p ^ bit} for bit in bits_of(psize)]
        self.devices += [{"h": 1 - w.h}]
        self.devices += [{"o": w.o ^ bit} for bit in bits_of(osize)]
        self.slots = [w.slot() for _ in self.devices]

    def copy(self, step):
        source = self.other if step == 0 else self.value
        return self.wires.copy(source, self.buffers.at[step], self.devices[step], self.slots[step])

    def start(self):
        self.copy(0).start()

    def step(self, step):
        self.copy(step).wait()
        self.value[...] = self.value[...] + self.buffers[step]
        if step + 1 < len(self.devices):
            self.copy(step + 1).start()


class Chain:
    def __init__(self, wires, osize, value, stages, buffers, result, pieces):
        self.wires, self.value, self.stages, self.result = wires, value, stages, result
        self.buffers = buffers
        self.spans = row_spans(value.shape[0], pieces)
        self.slots = [[wires.slot() for _ in self.spans] for _ in stages]
        self.kept = [wires.local_used + i for i in range(pieces)]
        wires.local_used += pieces
        self.other = None

    def copy(self, stage, i):
        w, span = self.wires, self.spans[i]
        kind, slot = self.stages[stage], self.slots[stage][i]
        if kind == "x":
            return w.copy(self.other.at[span], self.buffers[stage].at[span], {"x": 1 - w.x}, slot)
        if kind == "h":
            return w.copy(self.value.at[span], self.buffers[stage].at[span], {"h": 1 - w.h}, slot)
        if kind == "k":
            return w.copy(self.value.at[span], self.result.at[span], {"k": 1 - w.k}, slot)
        return w.copy(self.value.at[span], self.buffers[stage].at[span], {"o": w.o ^ kind}, slot)

    def keep(self, i):
        span = self.spans[i]
        return pltpu.make_async_copy(
            self.value.at[span], self.result.at[span], self.wires.local_sem.at[self.kept[i]]
        )

    def start(self, stage, i):
        w, kind = self.wires, self.stages[stage]
        if kind == "x":
            self.copy(stage, i).start()
        elif kind == "h":
            @pl.when(jnp.logical_not(w.home))
            def _():
                self.copy(stage, i).start()
        else:
            @pl.when(w.home)
            def _():
                self.copy(stage, i).start()
                if kind == "k":
                    self.keep(i).start()

    def add(self, stage, i):
        span = self.spans[i]
        add_into(self.value.at[span], self.buffers[stage].at[span])

    def end(self, stage, i):
        w, kind = self.wires, self.stages[stage]
        if kind == "x":
            self.copy(stage, i).wait_recv()
            self.add(stage, i)
        elif kind == "h":
            @pl.when(w.home)
            def _():
                self.copy(stage, i).wait_recv()
                self.add(stage, i)
        elif kind == "k":
            @pl.when(w.home)
            def _():
                self.copy(stage, i).wait_send()
                self.keep(i).wait()

            @pl.when(jnp.logical_not(w.home))
            def _():
                self.copy(stage, i).wait_recv()
        else:
            @pl.when(w.home)
            def _():
                self.copy(stage, i).wait()
                self.add(stage, i)

    def close(self):
        w = self.wires
        for stage, kind in enumerate(self.stages):
            for i in range(len(self.spans)):
                if kind == "x":
                    self.copy(stage, i).wait_send()
                elif kind == "h":
                    @pl.when(jnp.logical_not(w.home))
                    def _():
                        self.copy(stage, i).wait_send()

    def step(self, stage, i):
        self.end(stage, i)
        if stage + 1 < len(self.stages):
            self.start(stage + 1, i)

    def order(self, first=0):
        return [(stage, i) for stage in range(first, len(self.stages)) for i in range(len(self.spans))]

    def run(self, first=0):
        for stage, i in self.order(first):
            self.step(stage, i)


def leave_kernel(
    psize, osize, pieces, part, stream, base, gain_ref, small_in, proj_in, out_own, out_other,
    pair_in, down_in, block, small, first_sum, second_sum, out_sum, up_sum, gate_sum, down_sum,
    near, mid, far, kept, first_val, second_val, out_val, up_val, gate_val, down_val, first_bufs,
    second_over, second_across, second_bufs, out_bufs, small_other, small_bufs, gain_acc,
    send_sem, recv_sem, local_sem,
):
    w = Wires(send_sem, recv_sem, local_sem)
    split = first_val.shape[0]
    second = EarlySum(w, proj_in, second_val, second_over, second_across, None, 2, split)
    second.load()
    loads = [
        w.local(source, target)
        for source, target in (
            (pair_in.at[1], up_val), (pair_in.at[0], gate_val), (down_in, down_val), (out_own, out_val),
            (proj_in.at[0, pl.ds(0, split)], first_val),
        )
    ]
    w.greet(partners(w, psize, away=True, over_o=osize))
    rows, half = kept.shape[1], kept.shape[2]
    spans = row_spans(rows, PIECES)
    size = rows // PIECES
    bits = bits_of(osize)

    first = Chain(
        w, osize, first_val, ["x", "h"] + bits + ["k"], [first_bufs.at[i] for i in range(2 + len(bits))],
        first_sum, pieces,
    )
    first.other = proj_in.at[1, pl.ds(0, split)]
    late = Chain(
        w, osize, second_val.at[0], ["h"] + bits[1:], [second_bufs.at[i] for i in range(len(bits))], None, 2
    )
    out = Chain(w, osize, out_val, ["x", "h"] + bits[1:], [out_bufs.at[i] for i in range(1 + len(bits))], None, 1)
    out.other = out_other
    spreads = [Spread(w, up_val, up_sum), Spread(w, gate_val, gate_sum), Spread(w, down_val, down_sum)]
    last_spreads = [Spread(w, out_val, out_sum), Spread(w, second_val.at[0], second_sum)]
    reduce = Reduce(w, psize, part, near, mid, far, spans)
    second.start(1)
    for i in range(pieces):
        first.start(0, i)
    out.start(0, 0)
    second.start(0)
    for load in loads:
        load.wait()
    reduce.start()
    for spread in spreads:
        spread.start()

    near_slots = [w.slot() for _ in spans]
    far_slots = [w.slot() for _ in spans]
    keep_slots = [w.local_used + i for i in range(PIECES)]
    w.local_used += PIECES

    def target(i):
        return block.at[pl.ds(pl.multiple_of(w.k * rows + i * size, 8), size)]

    def same_keep(i):
        return pltpu.make_async_copy(kept.at[0, spans[i]], target(i), local_sem.at[keep_slots[i]])

    def same_send(i):
        return w.copy(kept.at[1, spans[i]], target(i), {"x": 1 - w.x}, near_slots[i])

    def cross_near(i):
        return w.copy(kept.at[0, spans[i]], target(i), {"k": 1 - w.k}, near_slots[i])

    def cross_far(i):
        return w.copy(kept.at[1, spans[i]], target(i), {"k": 1 - w.k, "x": 1 - w.x}, far_slots[i])

    for i in range(2):
        second.pass_on(i)
    first.step(0, 0)
    for i in range(1, pieces):
        first.step(0, i)
        first.step(1, i - 1)
    out.step(0, 0)
    second.finish(0)
    late.start(0, 0)
    first.step(1, pieces - 1)
    gain_acc[...] = jnp.zeros(gain_acc.shape, F32)

    def back(rows_, total):
        grad, gain_part = norm_back(total, stream[rows_, :].astype(F32), base[rows_, :], gain_ref[0:1, :])
        gain_acc[...] += gain_part
        kept[0, rows_, :] = grad[:, :half].astype(BF16)
        kept[1, rows_, :] = grad[:, half:].astype(BF16)

    for i in range(PIECES):
        reduce.each(i, back)

        @pl.when(w.same)
        def _():
            same_send(i).start()
            same_keep(i).start()

        @pl.when(jnp.logical_not(w.same))
        def _():
            cross_near(i).start()
            cross_far(i).start()

        if i == 0:
            second.finish(1)
            late.start(0, 1)

    gain_sum = jnp.sum(gain_acc[...], axis=0, keepdims=True)
    row = lax.broadcasted_iota(jnp.int32, (8, half), 0)
    small[...] = jnp.where(row == 0, gain_sum[:, :half], small_in[:, :half])
    small_other[...] = jnp.where(row == 0, gain_sum[:, half:], small_in[:, half:])
    total = SmallSum(w, psize, osize, small, small_other, small_bufs)
    total.start()
    out.run(1)
    last_spreads[0].start()
    steps = [lambda a=a: late.step(*a) for a in late.order(0)] + [last_spreads[1].start]
    steps += [spread.relay for spread in spreads] + [lambda a=a: first.step(*a) for a in first.order(2)]
    steps += [last_spreads[0].relay, last_spreads[1].relay]
    smalls = list(range(len(total.devices)))
    for n, step in enumerate(steps):
        step()
        if n % 2 == 0 and smalls:
            total.step(smalls.pop(0))
    for step in smalls:
        total.step(step)
    for spread in spreads + last_spreads:
        spread.wait()
    for i in range(PIECES):
        @pl.when(w.same)
        def _():
            same_keep(i).wait()
            same_send(i).wait_send()
            cross_near(i).wait_recv()

        @pl.when(jnp.logical_not(w.same))
        def _():
            cross_near(i).wait_send()
            cross_far(i).wait()
            same_send(i).wait_recv()

    for chain in (first, second, late, out):
        chain.close()
    w.close()


ANY = pl.BlockSpec(memory_space=pl.ANY)
VMEM = pl.BlockSpec(memory_space=pltpu.VMEM)
SLOTS = 128


def exchange_call(kernel, name, collective_id, outs, out_specs, in_specs, scratch, args):
    return pl.pallas_call(
        kernel,
        out_shape=outs,
        in_specs=in_specs,
        out_specs=out_specs,
        scratch_shapes=scratch
        + [
            pltpu.SemaphoreType.DMA((SLOTS,)),
            pltpu.SemaphoreType.DMA((SLOTS,)),
            pltpu.SemaphoreType.DMA((SLOTS // 2,)),
        ],
        compiler_params=pltpu.CompilerParams(
            collective_id=collective_id, has_side_effects=True, vmem_limit_bytes=56 << 20
        ),
        name=name,
    )(*args)


def sds(shape, dtype):
    return jax.ShapeDtypeStruct(shape, dtype)


def sum_scratch(psize, rows):
    far = max(psize - 1, 1)
    return [
        pltpu.VMEM((psize, rows, D), BF16),
        pltpu.VMEM((far, rows, D), BF16),
        pltpu.VMEM((far, rows, D), BF16),
    ]


def enter(psize, layer_input, gains, codes, qkv_weight, forget_weight, out_weight):
    rows = layer_input.shape[0] // 2
    half, width = qkv_weight.shape
    columns = width + forget_weight.shape[1]
    return exchange_call(
        functools.partial(enter_kernel, psize),
        "enter",
        1,
        (
            sds((rows, D), BF16),
            sds((2 * psize, rows, D), BF16),
            sds((2, half, columns), BF16),
            sds((out_weight.shape[0], 2 * half), BF16),
            sds((8, D), F32),
            sds((4,) + codes.shape, jnp.int32),
        ),
        (VMEM, ANY, ANY, ANY, VMEM, VMEM),
        [ANY, VMEM, VMEM, ANY, ANY, ANY],
        [pltpu.VMEM((rows, D), BF16)]
        + [pltpu.VMEM(value.shape, BF16) for value in (qkv_weight, forget_weight, out_weight)],
        (layer_input, gains, codes, qkv_weight, forget_weight, out_weight),
    )


def forward_exchange(psize, part, xin, gains, gate_weight, gate_got, up_weight, up_got, down_weight):
    rows = xin.shape[0]
    return exchange_call(
        functools.partial(forward_exchange_kernel, psize),
        "forward_exchange",
        2,
        (
            sds((rows, D), F32),
            sds((2 * psize, rows, D), BF16),
            sds((2,) + gate_weight.shape, BF16),
            sds((2,) + up_weight.shape, BF16),
            sds((down_weight.shape[0], D), BF16),
        ),
        (VMEM, ANY, ANY, ANY, ANY),
        [VMEM, VMEM, VMEM, ANY, ANY, ANY, ANY, ANY],
        sum_scratch(psize, rows)
        + [pltpu.VMEM((rows, D), BF16)]
        + [
            pltpu.VMEM(value.shape, BF16)
            for value in (gate_weight, gate_got, up_weight, up_got, down_weight)
        ],
        (part, xin, gains, gate_weight, gate_got, up_weight, up_got, down_weight),
    )


def backward_exchange(psize, part, resid, cot, gains, down_own, down_other, gate_part, gate_got, up_part):
    rows = resid.shape[0]

    def early(value):
        half_rows = value.shape[1] // 2
        shape = (half_rows, value.shape[2])
        return [
            pltpu.VMEM((2,) + shape, BF16),
            pltpu.VMEM((2,) + shape, BF16),
            pltpu.VMEM(shape, BF16),
        ]

    return exchange_call(
        functools.partial(backward_exchange_kernel, psize),
        "backward_exchange",
        3,
        (
            sds((rows, D), F32),
            sds((2 * psize, rows, D), BF16),
            sds((8, D), F32),
            sds(down_own.shape, BF16),
            sds((2, gate_part.shape[1] // 2, gate_part.shape[2]), BF16),
        ),
        (VMEM, ANY, VMEM, VMEM, ANY),
        [VMEM, VMEM, VMEM, VMEM, VMEM, ANY, ANY, VMEM, ANY],
        sum_scratch(psize, rows)
        + [pltpu.VMEM((rows, D), BF16)]
        + [pltpu.VMEM(down_own.shape, BF16)] * 2
        + early(gate_part)
        + early(up_part),
        (part, resid, cot, gains, down_own, down_other, gate_part, gate_got, up_part),
    )


def leave(psize, osize, part, stream, base, gains, small, proj, out_own, out_other, pair, down):
    rows = stream.shape[0]
    bits = len(bits_of(osize))
    half = D // 2
    columns = proj.shape[2]
    split = proj.shape[1] // 2

    def scratch(*shape):
        return pltpu.VMEM(shape, BF16)

    def both(shape):
        return sds((2,) + shape, BF16)

    return exchange_call(
        functools.partial(leave_kernel, psize, osize, 3),
        "leave",
        4,
        (
            sds((2 * rows, half), BF16),
            sds((8, half), F32),
            sds((split, columns), BF16),
            both((split // 2, columns)),
            both(out_own.shape),
            both(pair.shape[1:]),
            both(pair.shape[1:]),
            both(down.shape),
        ),
        (ANY, VMEM, ANY, ANY, ANY, ANY, ANY, ANY),
        [VMEM] * 5 + [ANY] * 5,
        sum_scratch(psize, rows)
        + [
            scratch(2, rows, half),
            scratch(split, columns),
            scratch(2, split // 2, columns),
            scratch(*out_own.shape),
            scratch(*pair.shape[1:]),
            scratch(*pair.shape[1:]),
            scratch(*down.shape),
            scratch(2 + bits, split, columns),
            scratch(2, split // 2, columns),
            scratch(split // 2, columns),
            scratch(bits, split // 2, columns),
            scratch(1 + bits, *out_own.shape),
            pltpu.VMEM((8, half), F32),
            pltpu.VMEM((3 + len(bits_of(psize)) + bits, 8, half), F32),
            pltpu.VMEM((8, D), F32),
        ],
        (part, stream, base, gains, small, proj, out_own, out_other, pair, down),
    )


def make_shards(osize, psize):
    count = 2 * psize
    obits = bits_of(osize)

    def shards(
        layer_input,
        attn_gain,
        qkv_weight,
        forget_weight,
        forget_bias,
        out_weight,
        ffn_gain,
        gate_weight,
        up_weight,
        down_weight,
        prompt_doc,
        branch_seg,
        branch_doc,
        out_cotangent,
    ):
        core, xpos = lax.axis_index("k"), lax.axis_index("x")
        hpos, ppos, opos = lax.axis_index("h"), lax.axis_index("p"), lax.axis_index("o")
        home = core == hpos
        same = core == xpos
        heads = forget_weight.shape[1]
        width = heads * 3 * DH
        lane_pad = LANES - heads
        feat = D // 2

        def far_blocks(block):
            return [xor_swap(block, "p", psize, bit) for bit in range(1, psize)]

        def all_blocks(block, far):
            blocks = []
            for near in [block] + far:
                blocks += [near, swap(near, "k")]
            return jnp.concatenate(blocks, axis=0)

        def near_sums(partial):
            size = partial.shape[0] // count
            parts = [partial[i * size : (i + 1) * size] for i in range(count)]
            moved = [swap(parts[i + 1], "k") for i in range(0, count, 2)]
            return [add_parts(parts[i], moved[i // 2]) for i in range(0, count, 2)]

        def far_sums(sums):
            return [xor_swap(sums[bit], "p", psize, bit) for bit in range(1, psize)]

        def total_of(near, far):
            total = near.astype(F32)
            for value in far:
                total = total + value.astype(F32)
            return total

        prompt_len, branch_len = prompt_doc.shape[1], branch_seg.shape[1]
        packed = jnp.concatenate([prompt_doc[0], branch_seg[0], branch_doc[0]])
        code_rows = -(-packed.shape[0] // (8 * LANES)) * 8
        packed = jnp.pad(packed, (0, code_rows * LANES - packed.shape[0])).reshape(code_rows, LANES)
        own_gains = jnp.concatenate([jnp.stack([attn_gain, ffn_gain]), jnp.zeros((6, feat), F32)])
        bias = jnp.where(home, forget_bias, lax.ppermute(forget_bias, ("k", "h"), [(1, 2), (2, 1)]))
        bias = jnp.concatenate([bias, jnp.zeros((lane_pad,), F32)])

        forget_wide = jnp.concatenate(
            [forget_weight, jnp.zeros((forget_weight.shape[0], lane_pad), BF16)], axis=1
        )
        first_part, second_part = qkv_weight, forget_wide
        if width % LANES:
            spare = jnp.zeros((qkv_weight.shape[0], LANES - width % LANES), BF16)
            first_part = jnp.concatenate([qkv_weight, forget_wide, spare], axis=1)
        xin, normed_a_all, w_proj, w_out, gains8, codes = enter(
            psize, layer_input, own_gains, packed, first_part, second_part, out_weight
        )
        packed = lax.dynamic_index_in_dim(
            codes, (core ^ xpos) * 2 + (xpos ^ hpos), 0, keepdims=False
        ).reshape(-1)
        prompt_ids = packed[:prompt_len]
        branch_ids = packed[prompt_len : prompt_len + branch_len]
        branch_docs = packed[prompt_len + branch_len : prompt_len + branch_len + branch_doc.shape[1]]
        kcol, qrow, flags = group_codes(prompt_ids, branch_ids, branch_docs)
        normed_a_all = normed_a_all.reshape(-1, D)
        w_proj = w_proj.reshape(D, -1)[:, : width + LANES]

        projected = matmul(normed_a_all, w_proj).reshape(count, -1, width + LANES)
        cot_near, cot_far = take_half(out_cotangent, core), take_half(out_cotangent, 1 - core)
        projected, kcol, qrow, flags, gate_half, up_half, cot_first, cot_near, cot_far = lax.optimization_barrier(
            (
                projected,
                kcol,
                qrow,
                flags,
                take_half(gate_weight, opos % 2),
                take_half(up_weight, opos % 2),
                jnp.where(same, cot_far, cot_near),
                cot_near,
                cot_far,
            )
        )
        gate_got, up_got = fetch_home_away(gate_half), fetch_home_away(up_half)
        cot_first = lax.ppermute(cot_first, ("k", "x"), SPREAD_A)
        cot_second = lax.ppermute(cot_far, ("k", "x"), SPREAD_B)
        attended, *saved = attention_forward(
            projected, bias[None], kcol, qrow, flags, heads, prompt_len
        )
        attended, gate_got, up_got, cot_first, cot_second, *saved = lax.optimization_barrier(
            (attended, gate_got, up_got, cot_first, cot_second, *saved)
        )
        attended = attended.reshape(-1, heads * DH)
        cot = jnp.concatenate(
            [jnp.where(same, cot_near, cot_first), jnp.where(same, cot_first, cot_second)], axis=1
        )
        part = matmul(attended, w_out).astype(BF16).reshape(count, -1, D)
        resid, normed_b_all, w_gate, w_up, w_down = forward_exchange(
            psize, part, xin, gains8, gate_weight, gate_got, up_weight, up_got, down_weight
        )
        normed_b_all = normed_b_all.reshape(-1, D)
        w_gate, w_up = w_gate.reshape(D, -1), w_up.reshape(D, -1)
        cot_others = far_blocks(tie(cot, normed_b_all))
        gate_pre = matmul(normed_b_all, w_gate)
        up_pre = matmul(normed_b_all, w_up)
        gate_sig = jax.nn.sigmoid(gate_pre)
        gate_act = gate_pre * gate_sig
        hidden = (gate_act * up_pre).astype(BF16)
        hidden = tie(hidden, *cot_others)
        cot_all = all_blocks(cot, cot_others)

        def finish(total, axis_bits):
            for bit in axis_bits:
                total = add_parts(total, home_swap(total, osize, bit))
            return total

        high = opos % 2 == 1
        down_part = contract_rows(hidden, cot_all).astype(BF16)
        down_keep, down_give = split_rows(down_part, high)
        down_moved = xor_swap(down_give, "o", osize, 1)
        out_sums = near_sums(matmul(hidden, w_down).astype(BF16))
        out_far = far_sums(out_sums)
        grad_hidden = contract_cols(tie(cot_all, out_sums[0]), w_down)
        grad_gate = (grad_hidden * up_pre * gate_sig * (1.0 + gate_pre * (1.0 - gate_sig))).astype(BF16)
        grad_up = (grad_hidden * gate_act).astype(BF16)
        gate_part = contract_rows(normed_b_all, grad_gate).astype(BF16).reshape(2, feat, -1)
        gate_got = xor_swap(take_half(gate_part[1], 1 - opos % 2), "o", osize, 1)
        grad_gate, grad_up = lax.optimization_barrier((grad_gate, grad_up, gate_part))[:2]
        up_part = contract_rows(normed_b_all, grad_up).astype(BF16).reshape(2, feat, -1)
        part = (contract_cols(grad_gate, w_gate) + contract_cols(grad_up, w_up)).astype(BF16)
        part, up_part, gate_got, down_moved, *out_far = lax.optimization_barrier(
            (part, up_part, gate_got, down_moved, *out_far)
        )
        layer_output = (resid + total_of(out_sums[0], out_far)).astype(BF16)
        down_total = add_parts(down_keep, down_moved)
        grad_resid, grad_branch_all, ffn_gain_part, down_total, pair_total = backward_exchange(
            psize,
            part.reshape(count, -1, D),
            resid,
            cot,
            gains8,
            down_total[:, :feat],
            down_total[:, feat:],
            gate_part,
            gate_got,
            up_part,
        )
        grad_branch_all = grad_branch_all.reshape(-1, D)
        grad_attended = contract_cols(grad_branch_all, w_out).astype(BF16)
        out_part = contract_rows(attended, grad_branch_all).astype(BF16)
        out_keep, out_give = split_rows(out_part, high)
        grad_attended, out_keep, out_give, down_total, pair_total, *block_parts = lax.optimization_barrier(
            (grad_attended, out_keep, out_give, down_total, pair_total) + unspread_parts(layer_output, same)
        )
        own_part, near_part, far_part = block_parts
        pair_moved = to_home(pair_total)
        out_moved = xor_swap(out_give, "o", osize, 1)
        near_moved, far_moved = unspread_moves(near_part, far_part)
        grad_proj, bias_sums = attention_backward(
            grad_attended.reshape(count, -1, heads * DH), saved, kcol, qrow, flags, heads, prompt_len
        )
        grad_proj, bias_sums, out_moved, near_moved, far_moved, pair_moved = lax.optimization_barrier(
            (grad_proj, bias_sums, out_moved, near_moved, far_moved, pair_moved)
        )
        layer_output = unspread_join(own_part, near_moved, far_moved, core, same)
        grad_proj = grad_proj.reshape(-1, width + LANES)
        proj_part = contract_rows(normed_a_all, grad_proj).astype(BF16)
        part = contract_cols(grad_proj, w_proj).astype(BF16).reshape(count, -1, D)
        down_total = finish(down_total, obits[1:])
        pair_total = finish(add_parts(pair_total, pair_moved), obits[1:])
        out_total = add_parts(out_keep, out_moved)

        slots = jnp.where(
            (jnp.arange(2 * psize) == core * psize + ppos)[:, None], bias_sums[:1, :heads], 0.0
        ).reshape(-1)
        slots = jnp.concatenate([slots, jnp.zeros((feat - slots.shape[0],), F32)])
        small = jnp.stack([jnp.zeros((D,), F32), jnp.sum(ffn_gain_part, axis=0), jnp.concatenate([slots, slots])])
        small = jnp.concatenate([small, jnp.zeros((5, D), F32)])
        input_grad, small, first_rows, second_rows, out_both, up_both, gate_both, down_both = leave(
            psize,
            osize,
            part,
            xin,
            grad_resid,
            gains8,
            small,
            proj_part.reshape(2, feat, -1),
            out_total[:, :feat],
            out_total[:, feat:],
            pair_total,
            down_total,
        )
        proj_grad = jnp.concatenate([first_rows, second_rows.reshape(first_rows.shape)], axis=0)
        qkv_grad = proj_grad[:, :width].astype(F32)
        forget_grad = proj_grad[:, width : width + heads].astype(F32)
        bias_all = small[2, : 2 * psize * heads].reshape(2 * psize, heads)
        forget_bias_grad = lax.dynamic_index_in_dim(bias_all, hpos * psize + ppos, 0, keepdims=False)

        def whole(halves):
            return halves.reshape(-1, halves.shape[2]).astype(F32)

        return (
            layer_output,
            input_grad,
            small[0],
            qkv_grad,
            forget_grad,
            forget_bias_grad,
            whole(out_both),
            small[1],
            whole(gate_both),
            whole(up_both),
            whole(down_both),
        )

    return shards


def solution(mesh):
    dp, row, col = mesh.shape["dp"], mesh.shape["row"], mesh.shape["col"]
    osize, psize = dp // 2, col // 2
    assert row == 2
    split = Mesh(mesh.devices.reshape(osize, 2, row, 2, psize), ("o", "k", "x", "h", "p"))
    tokens = P(("o", "k", "h", "p"), "x")
    rows_first = P("x", ("h", "p"))
    cols_first = P(("h", "p"), "x")
    groups = P(("o", "k", "x"), None)
    in_specs = (
        tokens,
        P("x"),
        rows_first,
        rows_first,
        P(("h", "p")),
        cols_first,
        P("x"),
        rows_first,
        rows_first,
        cols_first,
        groups,
        groups,
        groups,
        tokens,
    )
    out_specs = (
        tokens,
        tokens,
        P("x"),
        rows_first,
        rows_first,
        P(("h", "p")),
        cols_first,
        P("x"),
        rows_first,
        rows_first,
        cols_first,
    )
    return jax.shard_map(
        make_shards(osize, psize), mesh=split, in_specs=in_specs, out_specs=out_specs, check_vma=False
    )
```

```python
import functools

import jax
import jax.numpy as jnp
from jax import lax
from jax.experimental import pallas as pl
from jax.experimental.pallas import tpu as pltpu
from jax.sharding import Mesh, PartitionSpec as P

D = 1536
DH = 64
DOCS = 4
TILE = 256
EPS = 1e-06
MASKED = -1e30
LANES = 128
BF16 = jnp.bfloat16
F32 = jnp.float32


def swap(value, axis):
    return lax.ppermute(value, axis, [(0, 1), (1, 0)])


def xor_swap(value, axis, size, bit):
    return lax.ppermute(value, axis, [(i, i ^ bit) for i in range(size)])


def kxh(k, x, h):
    return (k * 2 + x) * 2 + h


def fetch_home_away(value):
    pairs = []
    for k in range(2):
        for x in range(2):
            for h in range(2):
                target = (k, 1 - x, h) if k == h else (1 - k, x, 1 - h)
                pairs.append((kxh(k, x, h), kxh(*target)))
    return lax.ppermute(value, ("k", "x", "h"), pairs)


def fetch_away(value):
    pairs = [
        (kxh(k, x, 1 - k), kxh(k, 1 - x, 1 - k)) for k in range(2) for x in range(2)
    ]
    return lax.ppermute(value, ("k", "x", "h"), pairs)


def tie(value, *others):
    return lax.optimization_barrier((value,) + others)[0]


def join_weight(shard, first, second, home, axis):
    mine = jnp.where(home, shard, first)
    other = jnp.where(home, first, second)
    return jnp.concatenate([mine, other], axis=axis)


def add_parts(kept, moved):
    return (kept.astype(F32) + moved.astype(F32)).astype(BF16)


def to_home(value):
    return lax.ppermute(value, ("k", "h"), [(1, 0), (2, 3)])


def from_home(value):
    return lax.ppermute(value, ("k", "h"), [(0, 2), (3, 1)])


def home_swap(value, size, bit):
    pairs = []
    for o in range(size):
        for k in range(2):
            pairs.append(((o * 2 + k) * 2 + k, ((o ^ bit) * 2 + k) * 2 + k))
    return lax.ppermute(value, ("o", "k", "h"), pairs)


def bits_of(size):
    return [1 << i for i in range(size.bit_length() - 1)]


def split_rows(value, high):
    half = value.shape[0] // 2
    low_rows, high_rows = value[:half], value[half:]
    return jnp.where(high, high_rows, low_rows), jnp.where(high, low_rows, high_rows)


def merge_rows(kept, moved, high):
    return jnp.concatenate([jnp.where(high, moved, kept), jnp.where(high, kept, moved)], axis=0)


def take_half(value, index):
    half = value.shape[0] // 2
    return lax.dynamic_slice_in_dim(value, index * half, half, 0)


def kx(k, x):
    return k * 2 + x


SPREAD_A = []
SPREAD_B = []
for _k in range(2):
    for _x in range(2):
        if _k == _x:
            SPREAD_A.append((kx(_k, _x), kx(1 - _k, _x)))
        else:
            SPREAD_A.append((kx(_k, _x), kx(_k, 1 - _x)))
            SPREAD_B.append((kx(_k, _x), kx(1 - _k, 1 - _x)))


def spread_tokens(block, core, same):
    near = take_half(block, core)
    far = take_half(block, 1 - core)
    first = lax.ppermute(jnp.where(same, far, near), ("k", "x"), SPREAD_A)
    second = lax.ppermute(far, ("k", "x"), SPREAD_B)
    own = jnp.where(same, near, first)
    other = jnp.where(same, first, second)
    return jnp.concatenate([own, other], axis=1)


def unspread_parts(rows, same):
    half = rows.shape[1] // 2
    own, other = rows[:, :half], rows[:, half:]
    return own, jnp.where(same, other, own), other


def unspread_moves(near, far):
    first = lax.ppermute(near, ("k", "x"), [(b, a) for a, b in SPREAD_A])
    second = lax.ppermute(far, ("k", "x"), [(b, a) for a, b in SPREAD_B])
    return first, second


def unspread_join(own, first, second, core, same):
    near = jnp.where(same, own, first)
    far = jnp.where(same, first, second)
    low = jnp.where(core == 0, near, far)
    high = jnp.where(core == 0, far, near)
    return jnp.concatenate([low, high], axis=0)


def contract_rows(left, right):
    return lax.dot_general(
        left, right, (((0,), (0,)), ((), ())), preferred_element_type=F32
    )


def contract_cols(left, right):
    return lax.dot_general(
        left, right, (((1,), (1,)), ((), ())), preferred_element_type=F32
    )


def matmul(left, right):
    return jnp.dot(left, right, preferred_element_type=F32)


def dot_nn(left, right):
    return lax.dot_general(left, right, (((1,), (0,)), ((), ())), preferred_element_type=F32)


def dot_nt(left, right):
    return lax.dot_general(left, right, (((1,), (1,)), ((), ())), preferred_element_type=F32)


def tile_mask(qrow, kcol, rows, cols, i, j):
    key_pos = j * TILE + lax.broadcasted_iota(jnp.int32, (TILE, TILE), 0)
    query_pos = i * TILE + lax.broadcasted_iota(jnp.int32, (TILE, TILE), 1)
    code = kcol[pl.ds(pl.multiple_of(j * TILE, TILE), TILE), 0:1]
    first = qrow[0:1, pl.ds(pl.multiple_of(i * TILE, TILE), TILE)]
    second = qrow[1:2, pl.ds(pl.multiple_of(i * TILE, TILE), TILE)]
    seen = (key_pos <= query_pos) & ((code == first) | (code == second))
    return jnp.where(seen, 0.0, MASKED)


def split_parts(value):
    high = value.astype(BF16)
    rest = value - high.astype(F32)
    mid = rest.astype(BF16)
    low = (rest - mid.astype(F32)).astype(BF16)
    return high, mid, low


def lane(shape):
    return lax.broadcasted_iota(jnp.int32, shape, 1)


def forward_kernel(
    heads, count, prompt_len, flags, proj_hbm, bias_ref, kcol, qrow, att_hbm, ot_hbm, lse_ref,
    qp_hbm, kp_hbm, vp_hbm, logit, qkv, qp, kp, vp, vt, rates, sums_ref, attended, ot, mask,
    in_sem, out_sem, keep_sem, *per_head,
):
    me = lax.axis_index("p") * 2 + lax.axis_index("k")
    total = qkv.shape[0]
    size = total // count
    tiles = total // TILE
    loads = []
    for b in range(count):
        rows = pl.ds(b * size, size)
        loads.append(pltpu.make_async_copy(proj_hbm.at[b ^ me], qkv.at[rows], in_sem.at[b]))
    for load in loads:
        load.start()
    for load in loads:
        load.wait()
    logit[...] = qkv[:, 3 * DH * heads :] + bias_ref[...]
    value = logit[...]
    rate = jnp.minimum(value, 0.0) - jnp.log1p(jnp.exp(-jnp.abs(value)))
    rate = jnp.where(lane(rate.shape) < heads, rate, 0.0)
    high, mid, low = split_parts(rate)
    packed = high.astype(F32) + pltpu.roll(mid.astype(F32), 8, 1) + pltpu.roll(low.astype(F32), 16, 1)
    rates[...] = packed.astype(BF16)
    place_row = lax.broadcasted_iota(jnp.int32, (LANES, LANES), 0)
    place_col = lax.broadcasted_iota(jnp.int32, (LANES, LANES), 1)

    prompt_tiles = prompt_len // TILE
    wide = (TILE, TILE)
    row_pos, col_pos = lax.broadcasted_iota(jnp.int32, wide, 0), lax.broadcasted_iota(jnp.int32, wide, 1)
    below = jnp.where(col_pos <= row_pos, 1.0, 0.0).astype(BF16)

    def prompt_sums(t, before):
        rows = pl.ds(pl.multiple_of(t * TILE, TILE), TILE)
        prefix = dot_nn(below, rates[rows, :]) + before
        sums_ref[rows, :] = prefix
        return prefix[TILE - 1 : TILE, :]

    lax.fori_loop(0, prompt_tiles, prompt_sums, jnp.zeros((1, LANES), F32))
    doc_index = lax.broadcasted_iota(jnp.int32, (8, prompt_len), 0)
    within = jnp.where(qrow[3:4, 0:prompt_len] <= doc_index, 1.0, 0.0).astype(BF16)
    doc_sums = dot_nn(within, rates[0:prompt_len, :])

    def branch_sums(t, carry):
        rows = pl.ds(pl.multiple_of(t * TILE, TILE), TILE)
        limit = kcol[rows, 2:3]
        start = jnp.zeros((TILE, LANES), F32)
        for doc in range(DOCS):
            start = jnp.where(limit == doc, doc_sums[doc : doc + 1, :], start)

        def add_own(u, acc):
            others = pl.ds(pl.multiple_of(u * TILE, TILE), TILE)
            own = (u * TILE + col_pos <= t * TILE + row_pos) & (kcol[rows, 1:2] == qrow[2:3, others])
            return acc + dot_nn(jnp.where(own, 1.0, 0.0).astype(BF16), rates[others, :])

        sums_ref[rows, :] = lax.fori_loop(prompt_tiles, t + 1, add_own, start)
        return carry

    lax.fori_loop(prompt_tiles, tiles, branch_sums, 0)

    def prepare(t, carry):
        rows = pl.ds(pl.multiple_of(t * TILE, TILE), TILE)
        sums = sums_ref[rows, :]
        decay = sums + pltpu.roll(sums, LANES - 8, 1) + pltpu.roll(sums, LANES - 16, 1)
        decay = jnp.where(lane(decay.shape) < heads, -decay, 0.0)
        high, mid, low = split_parts(decay)
        parts = (
            high.astype(F32) + pltpu.roll(mid.astype(F32), 8, 1) + pltpu.roll(low.astype(F32), 16, 1)
        ).astype(BF16)
        lanes = lane((TILE, LANES))
        for h in range(heads):
            base = 3 * DH * h
            query = qkv[rows, base : base + DH].astype(BF16).astype(F32) * DH ** (-0.5)
            key = qkv[rows, base + DH : base + 2 * DH]
            worth = qkv[rows, base + 2 * DH : base + 3 * DH].astype(BF16)
            ones = jnp.where((lanes >= DH) & (lanes < DH + 3), 1.0, 0.0)[:, :DH]
            ones = jnp.where(lane((TILE, DH)) < 3, 1.0, 0.0)
            qp[h, rows, :] = jnp.concatenate([query, ones], axis=1).astype(BF16)
            spread = jnp.where(
                (place_col >= DH) & (place_col < DH + 3) & (place_row == 8 * (place_col - DH) + h), 1.0, 0.0
            ).astype(BF16)
            extra = dot_nn(parts, spread)
            extra = jnp.where(lanes == DH + 3, 1.0, extra)
            key_wide = jnp.concatenate([key, extra[:, DH:]], axis=1)
            kp[h, rows, :] = key_wide.astype(BF16)
            vp[h, rows, :] = worth
            vt[h, :, rows] = worth.astype(F32).T.astype(BF16)
        return carry

    lax.fori_loop(0, tiles, prepare, 0)
    keeps = [
        pltpu.make_async_copy(qp, qp_hbm, keep_sem.at[0]),
        pltpu.make_async_copy(kp, kp_hbm, keep_sem.at[1]),
        pltpu.make_async_copy(vp, vp_hbm, keep_sem.at[2]),
    ]
    for keep in keeps:
        keep.start()

    acc, top_refs, total_refs, score_refs = (per_head[n * heads : (n + 1) * heads] for n in range(4))

    def query_tile(i, carry):
        cols = pl.ds(pl.multiple_of(i * TILE, TILE), TILE)
        for h in range(heads):
            top_refs[h][...] = jnp.full(top_refs[h].shape, MASKED, F32)
            total_refs[h][...] = jnp.zeros(total_refs[h].shape, F32)
            acc[h][...] = jnp.zeros(acc[h].shape, F32)

        def key_tile(j, inner):
            @pl.when(flags[i * tiles + j] > 0)
            def _():
                rows = pl.ds(pl.multiple_of(j * TILE, TILE), TILE)
                mask[...] = tile_mask(qrow, kcol, None, None, i, j)
                tops = []
                for h in range(heads):
                    scores = dot_nt(kp[h, rows, :], qp[h, cols, :]) + mask[...]
                    score_refs[h][...] = scores
                    tops.append(jnp.maximum(top_refs[h][0:1, :], jnp.max(scores, axis=0, keepdims=True)))
                for h, top in enumerate(tops):
                    expo = jnp.exp(score_refs[h][...] - top)
                    shrink = jnp.exp(top_refs[h][0:1, :] - top)
                    top_refs[h][0:1, :] = top
                    total_refs[h][0:1, :] = total_refs[h][0:1, :] * shrink + jnp.sum(expo, axis=0, keepdims=True)
                    acc[h][...] = acc[h][...] * shrink + dot_nn(vt[h, :, rows], expo.astype(BF16))

            return inner

        lax.fori_loop(0, i + 1, key_tile, 0)
        for h in range(heads):
            total = total_refs[h][0:1, :]
            ot[pl.ds(h * DH, DH), cols] = acc[h][...] / total
            lse_ref[h : h + 1, cols] = top_refs[h][0:1, :] + jnp.log(total)
        attended[cols, :] = ot[:, cols].T.astype(BF16)
        return carry

    lse_ref[...] = jnp.zeros(lse_ref.shape, F32)
    lax.fori_loop(0, tiles, query_tile, 0)
    stores = [pltpu.make_async_copy(ot, ot_hbm, keep_sem.at[3])]
    for b in range(count):
        stores.append(
            pltpu.make_async_copy(attended.at[pl.ds(b * size, size)], att_hbm.at[b ^ me], out_sem.at[b])
        )
    for store in stores:
        store.start()
    for copy in keeps + stores:
        copy.wait()


def attention_forward(projected, bias, kcol, qrow, flags, heads, prompt_len):
    count, size, width = projected.shape
    total = count * size
    any_spec = pl.BlockSpec(memory_space=pl.ANY)
    vmem = pl.BlockSpec(memory_space=pltpu.VMEM)
    shape = jax.ShapeDtypeStruct
    return pl.pallas_call(
        functools.partial(forward_kernel, heads, count, prompt_len),
        out_shape=(
            shape((count, size, heads * DH), BF16),
            shape((heads * DH, total), F32),
            shape((8, total), F32),
            shape((heads, total, LANES), BF16),
            shape((heads, total, LANES), BF16),
            shape((heads, total, DH), BF16),
            shape((total, LANES), F32),
        ),
        in_specs=[pl.BlockSpec(memory_space=pltpu.SMEM), any_spec, vmem, vmem, vmem],
        out_specs=(any_spec, any_spec, vmem, any_spec, any_spec, any_spec, vmem),
        scratch_shapes=[
            pltpu.VMEM((total, width), F32),
            pltpu.VMEM((heads, total, LANES), BF16),
            pltpu.VMEM((heads, total, LANES), BF16),
            pltpu.VMEM((heads, total, DH), BF16),
            pltpu.VMEM((heads, DH, total), BF16),
            pltpu.VMEM((total, LANES), BF16),
            pltpu.VMEM((total, LANES), F32),
            pltpu.VMEM((total, heads * DH), BF16),
            pltpu.VMEM((heads * DH, total), F32),
            pltpu.VMEM((TILE, TILE), F32),
            pltpu.SemaphoreType.DMA((count,)),
            pltpu.SemaphoreType.DMA((count,)),
            pltpu.SemaphoreType.DMA((4,)),
        ]
        + [pltpu.VMEM((DH, TILE), F32)] * heads
        + [pltpu.VMEM((8, TILE), F32)] * (2 * heads)
        + [pltpu.VMEM((TILE, TILE), F32)] * heads,
        compiler_params=pltpu.CompilerParams(vmem_limit_bytes=48 << 20),
        cost_estimate=pl.CostEstimate(flops=20_000_000_000, bytes_accessed=30_000_000, transcendentals=0),
        name="attention_forward",
    )(flags, projected, bias, kcol, qrow)


def backward_kernel(
    heads, count, prompt_len, flags, gatt_hbm, ot_ref, lse_ref, qp, kp, vp, logit, kcol, qrow,
    grad_hbm, bias_ref, gatt, gout, kt, delta, mask, decay, grad, in_sem, out_sem, *per_head,
):
    dqt, dk, dv, prob_refs, score_refs = (per_head[n * heads : (n + 1) * heads] for n in range(5))
    me = lax.axis_index("p") * 2 + lax.axis_index("k")
    total = gatt.shape[0]
    size = total // count
    tiles = total // TILE
    loads = []
    for b in range(count):
        rows = pl.ds(b * size, size)
        loads.append(pltpu.make_async_copy(gatt_hbm.at[b ^ me], gatt.at[rows], in_sem.at[b]))
    for load in loads:
        load.start()
    for load in loads:
        load.wait()
    for h in range(heads):
        dqt[h][...] = jnp.zeros(dqt[h].shape, F32)
    delta[...] = jnp.zeros(delta.shape, F32)

    def prepare(t, carry):
        rows = pl.ds(pl.multiple_of(t * TILE, TILE), TILE)
        turned = gatt[rows, :].astype(F32).T * ot_ref[:, rows]
        for h in range(heads):
            gout[h, rows, :] = gatt[rows, h * DH : (h + 1) * DH]
            kt[h, :, rows] = kp[h, rows, :].astype(F32).T[: DH + 8].astype(BF16)
            delta[h : h + 1, rows] = jnp.sum(turned[h * DH : (h + 1) * DH], axis=0, keepdims=True)
        return carry

    lax.fori_loop(0, tiles, prepare, 0)
    lanes = lane((TILE, LANES))

    def key_tile(j, carry):
        rows = pl.ds(pl.multiple_of(j * TILE, TILE), TILE)
        for h in range(heads):
            dk[h][...] = jnp.zeros(dk[h].shape, F32)
            dv[h][...] = jnp.zeros(dv[h].shape, F32)

        def query_tile(i, inner):
            @pl.when(flags[i * tiles + j] > 0)
            def _():
                cols = pl.ds(pl.multiple_of(i * TILE, TILE), TILE)
                mask[...] = tile_mask(qrow, kcol, None, None, i, j)
                for h in range(heads):
                    scores = dot_nt(kp[h, rows, :], qp[h, cols, :]) + mask[...]
                    prob_refs[h][...] = jnp.exp(scores - lse_ref[h : h + 1, cols])
                for h in range(heads):
                    probs = prob_refs[h][...]
                    grad_probs = dot_nt(vp[h, rows, :], gout[h, cols, :])
                    score_refs[h][...] = (probs * (grad_probs - delta[h : h + 1, cols])).astype(BF16)
                    dv[h][...] += dot_nn(probs.astype(BF16), gout[h, cols, :])
                for h in range(heads):
                    grad_scores = score_refs[h][...]
                    dk[h][...] += dot_nn(grad_scores, qp[h, cols, :])
                    dqt[h][:, cols] += dot_nn(kt[h, :, rows], grad_scores)

            return inner

        lax.fori_loop(j, tiles, query_tile, 0)
        keys = jnp.zeros((TILE, LANES), F32)
        for h in range(heads):
            grad_key = dk[h][...]
            keys += jnp.where(lanes == h, pltpu.roll(grad_key, LANES - DH + h, 1), 0.0)
            grad[rows, (3 * h + 1) * DH : (3 * h + 3) * DH] = jnp.concatenate(
                [grad_key[:, :DH], dv[h][...]], axis=1
            ).astype(BF16)
        decay[rows, :] = -keys
        return carry

    lax.fori_loop(0, tiles, key_tile, 0)

    def finish(t, carry):
        rows = pl.ds(pl.multiple_of(t * TILE, TILE), TILE)
        queries = jnp.zeros((TILE, LANES), F32)
        for h in range(heads):
            turned = jnp.concatenate([dqt[h][:, rows], jnp.zeros((LANES - DH - 8, TILE), F32)], axis=0).T
            queries += jnp.where(lanes == h, pltpu.roll(turned, LANES - DH - 3 + h, 1), 0.0)
            grad[rows, 3 * h * DH : (3 * h + 1) * DH] = (turned[:, :DH] * DH ** (-0.5)).astype(BF16)
        whole = decay[rows, :] + queries
        high, mid, low = split_parts(whole)
        decay[rows, :] = (
            high.astype(F32) + pltpu.roll(mid.astype(F32), 8, 1) + pltpu.roll(low.astype(F32), 16, 1)
        )
        return carry

    lax.fori_loop(0, tiles, finish, 0)

    prompt_tiles = prompt_len // TILE
    wide = (TILE, TILE)
    row_pos, col_pos = lax.broadcasted_iota(jnp.int32, wide, 0), lax.broadcasted_iota(jnp.int32, wide, 1)
    above = jnp.where(col_pos >= row_pos, 1.0, 0.0).astype(BF16)
    branch_len = total - prompt_len
    doc_index = lax.broadcasted_iota(jnp.int32, (8, branch_len), 0)
    chosen = jnp.where(qrow[4:5, prompt_len:total] == doc_index, 1.0, 0.0).astype(BF16)
    doc_sums = dot_nn(chosen, decay[prompt_len:total, :].astype(BF16))

    def prompt_sums(n, after):
        t = prompt_tiles - 1 - n
        rows = pl.ds(pl.multiple_of(t * TILE, TILE), TILE)
        suffix = dot_nn(above, decay[rows, :].astype(BF16)) + after
        doc = kcol[rows, 3:4]
        sums = suffix
        for d in range(DOCS):
            sums = sums + jnp.where(doc <= d, doc_sums[d : d + 1, :], 0.0)
        decay[rows, :] = sums
        return suffix[0:1, :]

    def branch_sums(t, carry):
        rows = pl.ds(pl.multiple_of(t * TILE, TILE), TILE)

        def add_own(u, acc):
            others = pl.ds(pl.multiple_of(u * TILE, TILE), TILE)
            own = (u * TILE + col_pos >= t * TILE + row_pos) & (kcol[rows, 1:2] == qrow[2:3, others])
            return acc + dot_nn(jnp.where(own, 1.0, 0.0).astype(BF16), decay[others, :].astype(BF16))

        decay[rows, :] = lax.fori_loop(t, tiles, add_own, jnp.zeros((TILE, LANES), F32))
        return carry

    lax.fori_loop(0, prompt_tiles, prompt_sums, jnp.zeros((1, LANES), F32))
    lax.fori_loop(prompt_tiles, tiles, branch_sums, 0)

    def rates(t, bias):
        rows = pl.ds(pl.multiple_of(t * TILE, TILE), TILE)
        sums = decay[rows, :]
        grad_rate = sums + pltpu.roll(sums, LANES - 8, 1) + pltpu.roll(sums, LANES - 16, 1)
        value = logit[rows, :]
        grad_forget = grad_rate / (1.0 + jnp.exp(value))
        grad_forget = jnp.where(lanes < heads, grad_forget, 0.0).astype(BF16)
        grad[rows, 3 * DH * heads :] = grad_forget
        return bias + jnp.sum(grad_forget.astype(F32), axis=0, keepdims=True)

    bias_ref[...] = jnp.broadcast_to(
        lax.fori_loop(0, tiles, rates, jnp.zeros((1, LANES), F32)), bias_ref.shape
    )
    stores = []
    for b in range(count):
        stores.append(
            pltpu.make_async_copy(grad.at[pl.ds(b * size, size)], grad_hbm.at[b ^ me], out_sem.at[b])
        )
    for store in stores:
        store.start()
    for store in stores:
        store.wait()


def attention_backward(grad_attended, saved, kcol, qrow, flags, heads, prompt_len):
    ot, lse, qp, kp, vp, logit = saved
    count, size, width = grad_attended.shape
    total = count * size
    any_spec = pl.BlockSpec(memory_space=pl.ANY)
    vmem = pl.BlockSpec(memory_space=pltpu.VMEM)
    shape = jax.ShapeDtypeStruct
    out_width = 3 * DH * heads + LANES
    return pl.pallas_call(
        functools.partial(backward_kernel, heads, count, prompt_len),
        out_shape=(shape((count, size, out_width), BF16), shape((8, LANES), F32)),
        in_specs=[pl.BlockSpec(memory_space=pltpu.SMEM), any_spec]
        + [vmem] * 8,
        out_specs=(any_spec, vmem),
        scratch_shapes=[
            pltpu.VMEM((total, width), BF16),
            pltpu.VMEM((heads, total, DH), BF16),
            pltpu.VMEM((heads, DH + 8, total), BF16),
            pltpu.VMEM((8, total), F32),
            pltpu.VMEM((TILE, TILE), F32),
            pltpu.VMEM((total, LANES), F32),
            pltpu.VMEM((total, out_width), BF16),
            pltpu.SemaphoreType.DMA((count,)),
            pltpu.SemaphoreType.DMA((count,)),
        ]
        + [pltpu.VMEM((DH + 8, total), F32)] * heads
        + [pltpu.VMEM((TILE, LANES), F32)] * heads
        + [pltpu.VMEM((TILE, DH), F32)] * heads
        + [pltpu.VMEM((TILE, TILE), F32)] * heads
        + [pltpu.VMEM((TILE, TILE), BF16)] * heads,
        compiler_params=pltpu.CompilerParams(vmem_limit_bytes=56 << 20),
        cost_estimate=pl.CostEstimate(flops=50_000_000_000, bytes_accessed=30_000_000, transcendentals=0),
        name="attention_backward",
    )(flags, grad_attended, ot, lse, qp, kp, vp, logit, kcol, qrow)


def group_codes(prompt_ids, branch_ids, branch_docs):
    prompt_len = prompt_ids.shape[0]
    member = branch_ids[:, None] == jnp.arange(branch_docs.shape[0])[None, :]
    branch_doc_ids = jnp.sum(jnp.where(member, branch_docs[None, :], 0), axis=1)
    key_code = jnp.concatenate([prompt_ids, DOCS + branch_ids])
    first = jnp.concatenate([prompt_ids, branch_doc_ids])
    tag = jnp.concatenate([jnp.full_like(prompt_ids, -1), branch_ids])
    limit = jnp.concatenate([jnp.full_like(prompt_ids, -1), branch_doc_ids])
    prompt_code = jnp.concatenate([prompt_ids, jnp.full_like(branch_ids, DOCS)])
    total = key_code.shape[0]
    none = jnp.zeros_like(tag)
    kcol = jnp.stack([key_code, tag, limit, prompt_code] + [none] * 4, axis=1)
    qrow = jnp.stack([first, key_code, tag, prompt_code, limit] + [none] * 3, axis=0)
    tiles = total // TILE
    kinds = jnp.arange(2 * DOCS)
    key_bits = jnp.any(key_code.reshape(tiles, TILE, 1) == kinds, axis=1)
    query_bits = key_bits | jnp.any(first.reshape(tiles, TILE, 1) == kinds, axis=1)
    order = jnp.arange(tiles)
    meets = jnp.any(query_bits[:, None, :] & key_bits[None, :, :], axis=2)
    flags = (meets & (order[None, :] <= order[:, None])).astype(jnp.int32).reshape(-1)
    return kcol, qrow, flags


class Wires:
    def __init__(self, send_sem, recv_sem, local_sem):
        self.send_sem, self.recv_sem, self.local_sem = send_sem, recv_sem, local_sem
        self.used, self.local_used = 0, 0
        self.k, self.x = lax.axis_index("k"), lax.axis_index("x")
        self.h, self.p, self.o = lax.axis_index("h"), lax.axis_index("p"), lax.axis_index("o")
        self.home = self.k == self.h
        self.same = self.k == self.x
        self.pending = []

    def slot(self):
        self.used += 1
        return self.used - 1

    def copy(self, source, target, device, slot):
        return pltpu.make_async_remote_copy(
            src_ref=source,
            dst_ref=target,
            send_sem=self.send_sem.at[slot],
            recv_sem=self.recv_sem.at[slot],
            device_id=device,
            device_id_type=pl.DeviceIdType.MESH,
        )

    def send(self, source, target, device):
        copy = self.copy(source, target, device, self.slot())
        copy.start()
        self.pending.append(copy.wait_send)
        return copy

    def local(self, source, target):
        copy = pltpu.make_async_copy(source, target, self.local_sem.at[self.local_used])
        self.local_used += 1
        copy.start()
        return copy

    def greet(self, devices):
        barrier = pltpu.get_barrier_semaphore()
        for device in devices:
            pl.semaphore_signal(
                barrier, inc=1, device_id=device, device_id_type=pl.DeviceIdType.MESH
            )
        pl.semaphore_wait(barrier, len(devices))

    def close(self):
        for wait in self.pending:
            wait()


def row_spans(total, pieces):
    size = total // pieces
    return [pl.ds(i * size, size) for i in range(pieces)]


class Fetch:
    def __init__(self, wires, shard, target, stage, pieces, got=None, keep=None):
        w = self.wires = wires
        self.shard, self.target, self.stage, self.got, self.keep = shard, target, stage, got, keep
        self.count = pieces
        self.half_rows = shard.shape[0] // 2
        self.size = self.half_rows // pieces
        self.by_columns = len(target.shape) == 2
        self.first = [w.slot() for _ in range(pieces)]
        self.over = [w.slot() for _ in range(pieces)]
        self.second = [w.slot() for _ in range(2 * pieces)]
        self.local_slot = w.local_used
        w.local_used += 2

    def rows(self, i, mine=True):
        bit = self.wires.o % 2
        bit = bit if mine else 1 - bit
        return pl.ds(pl.multiple_of(bit * self.half_rows + i * self.size, 16), self.size)

    def place(self, half, span):
        if self.by_columns:
            width = self.shard.shape[1]
            return self.target.at[span, pl.ds(half * width, width)]
        return self.target.at[half, span]

    def first_copy(self, i, home):
        w, span = self.wires, self.rows(i)
        if home:
            return w.copy(self.shard.at[span], self.place(1, span), {"x": 1 - w.x}, self.first[i])
        device = {"k": 1 - w.k, "h": 1 - w.h}
        return w.copy(self.shard.at[span], self.place(0, span), device, self.first[i])

    def have(self, i, half):
        if self.got is None:
            return self.place(half, self.rows(i))
        return self.got.at[pl.ds(i * self.size, self.size)]

    def over_copy(self, i, home):
        w, half = self.wires, 1 if home else 0
        return w.copy(self.have(i, half), self.place(half, self.rows(i)), {"o": w.o ^ 1}, self.over[i])

    def second_copy(self, i, mine):
        w, span = self.wires, self.rows(i, mine)
        source = self.have(i, 0) if mine else self.place(0, span)
        slot = self.second[i if mine else self.count + i]
        return w.copy(source, self.place(1, span), {"x": 1 - w.x}, slot)

    def shard_load(self):
        return pltpu.make_async_copy(self.shard, self.stage, self.wires.local_sem.at[self.local_slot])

    def shard_store(self):
        whole = pl.ds(0, self.shard.shape[0])
        return pltpu.make_async_copy(
            self.stage, self.place(0, whole), self.wires.local_sem.at[self.local_slot]
        )

    def got_load(self):
        return pltpu.make_async_copy(self.got, self.keep, self.wires.local_sem.at[self.local_slot + 1])

    def got_store(self, half):
        bit = self.wires.o % 2
        span = pl.ds(pl.multiple_of(bit * self.half_rows, 16), self.half_rows)
        return pltpu.make_async_copy(
            self.keep, self.place(half, span), self.wires.local_sem.at[self.local_slot + 1]
        )

    def either(self, at_home, away):
        pl.when(self.wires.home)(at_home)
        pl.when(jnp.logical_not(self.wires.home))(away)

    def load(self):
        pl.when(self.wires.home)(lambda: self.shard_load().start())
        if self.got is not None:
            self.got_load().start()

    def start(self):
        if self.got is not None:
            for i in range(self.count):
                self.relay(i)
            return

        def go(home):
            for i in range(self.count):
                self.first_copy(i, home).start()

        self.either(lambda: go(True), lambda: go(False))

    def store(self):
        def at_home():
            self.shard_load().wait()
            self.shard_store().start()
            if self.got is not None:
                self.got_load().wait()
                self.got_store(1).start()

        def away():
            if self.got is not None:
                self.got_load().wait()
                self.got_store(0).start()

        self.either(at_home, away)

    def relay(self, i):
        def at_home():
            if self.got is None:
                self.first_copy(i, True).wait_recv()
            self.over_copy(i, True).start()

        def away():
            if self.got is None:
                self.first_copy(i, False).wait_recv()
            self.over_copy(i, False).start()
            self.second_copy(i, True).start()

        self.either(at_home, away)

    def relay_over(self, i):
        def away():
            self.over_copy(i, False).wait_recv()
            self.second_copy(i, False).start()

        pl.when(jnp.logical_not(self.wires.home))(away)

    def wait(self):
        def at_home():
            for i in range(self.count):
                if self.got is None:
                    self.first_copy(i, True).wait_send()
                self.over_copy(i, True).wait()
            self.shard_store().wait()
            if self.got is not None:
                self.got_store(1).wait()

        def away():
            for i in range(self.count):
                if self.got is None:
                    self.first_copy(i, False).wait_send()
                self.over_copy(i, False).wait_send()
                self.second_copy(i, True).wait()
                self.second_copy(i, False).wait()
            if self.got is not None:
                self.got_store(0).wait()

        self.either(at_home, away)


def partners(wires, psize, away=False, peers=True, over_o=0):
    devices = [{"k": 1 - wires.k}]
    if peers:
        devices += [{"p": wires.p ^ bit} for bit in range(1, psize)]
    devices += [{"x": 1 - wires.x}]
    devices += [{"k": 1 - wires.k, "x": 1 - wires.x}]
    if away:
        devices += [{"k": 1 - wires.k, "h": 1 - wires.h}, {"h": 1 - wires.h}]
    bit = 1
    while bit < over_o:
        devices += [{"o": wires.o ^ bit}]
        bit *= 2
    return devices


class Share:
    def __init__(self, wires, psize, own, g, spans):
        self.wires, self.psize, self.own, self.g, self.spans = wires, psize, own, g, spans
        self.near, self.far, self.kept, self.passed = [], {}, [], []

    def send(self, i):
        w, span = self.wires, self.spans[i]
        for bit in range(1, self.psize):
            self.far[bit, i] = w.send(self.own.at[span], self.g.at[2 * bit, span], {"p": w.p ^ bit})
        self.near.append(w.send(self.own.at[span], self.g.at[1, span], {"k": 1 - w.k}))
        self.kept.append(w.local(self.own.at[span], self.g.at[0, span]))

    def relay(self, i):
        w, span = self.wires, self.spans[i]
        for bit in range(1, self.psize):
            self.far[bit, i].wait_recv()
            self.passed.append(
                w.send(self.g.at[2 * bit, span], self.g.at[2 * bit + 1, span], {"k": 1 - w.k})
            )

    def wait(self):
        for copy in self.near + self.passed:
            copy.wait_recv()
        for copy in self.kept:
            copy.wait()


def by_chunks(span, body):
    def run(n, carry):
        body(pl.ds(pl.multiple_of(span.start + n * CHUNK, CHUNK), CHUNK))
        return carry

    lax.fori_loop(0, span.size // CHUNK, run, 0)


def add_into(value, *others):
    def body(rows):
        total = value[rows, :].astype(F32)
        for other in others:
            total = total + other[rows, :].astype(F32)
        value[rows, :] = total.astype(BF16)

    by_chunks(pl.ds(0, value.shape[0]), body)


class Reduce:
    def __init__(self, wires, psize, part, near, mid, far, spans):
        self.wires, self.psize, self.part = wires, psize, part
        self.near, self.mid, self.far, self.spans = near, mid, far, spans
        self.near_copies, self.far_copies = {}, {}

    def start_near(self, bit):
        w = self.wires
        for i, span in enumerate(self.spans):
            self.near_copies[bit, i] = w.send(
                self.part.at[2 * bit + 1, span], self.near.at[bit, span], {"k": 1 - w.k}
            )

    def start_far(self, bit):
        w = self.wires
        for i, span in enumerate(self.spans):
            self.near_copies[bit, i].wait_recv()

            def add(rows, bit=bit):
                self.mid[bit - 1, rows] = (
                    self.part[2 * bit, rows].astype(F32) + self.near[bit, rows].astype(F32)
                ).astype(BF16)

            by_chunks(span, add)
            self.far_copies[bit, i] = w.send(
                self.mid.at[bit - 1, span], self.far.at[bit - 1, span], {"p": w.p ^ bit}
            )

    def start(self):
        for bit in reversed(range(self.psize)):
            self.start_near(bit)
        for bit in reversed(range(1, self.psize)):
            self.start_far(bit)

    def start_with(self, make):
        for bit in reversed(range(self.psize)):
            make(2 * bit + 1)
            self.start_near(bit)
            make(2 * bit)
            if bit:
                self.start_far(bit)

    def each(self, i, body):
        span = self.spans[i]
        self.near_copies[0, i].wait_recv()
        for bit in range(1, self.psize):
            self.far_copies[bit, i].wait_recv()

        def run(rows):
            total = self.part[0, rows].astype(F32) + self.near[0, rows].astype(F32)
            for bit in range(1, self.psize):
                total = total + self.far[bit - 1, rows].astype(F32)
            body(rows, total)

        by_chunks(span, run)


CHUNK = 32
PIECES = 3


def inverse_rms(value):
    return lax.rsqrt(jnp.sum(value * value, axis=1, keepdims=True) / D + EPS)


def norm_back(grad, value, base, gain):
    rms = inverse_rms(value)
    gained = gain * grad
    inner = jnp.sum(value * gained, axis=1, keepdims=True)
    result = base + rms * gained - value * (rms * rms * rms) * inner / D
    parts = grad * value * rms
    return result, sum(parts[n : n + 8] for n in range(0, parts.shape[0], 8))


def enter_kernel(
    psize, x_ref, gain_own, codes_own, qkv_shard, forget_shard, out_shard, xin, g, proj, out, gain_ref, codes, far_gains,
    own, qkv_stage, forget_stage, out_stage, send_sem, recv_sem, local_sem,
):
    w = Wires(send_sem, recv_sem, local_sem)
    width = qkv_shard.shape[1]
    qkv = Fetch(w, qkv_shard, proj.at[:, :, pl.ds(0, width)], qkv_stage, 3)
    forget = Fetch(
        w, forget_shard, proj.at[:, :, pl.ds(width, forget_shard.shape[1])], forget_stage, 1
    )
    out_fetch = Fetch(w, out_shard, out, out_stage, 1)
    for fetch in (qkv, forget, out_fetch):
        fetch.load()
    w.greet(partners(w, psize, away=True, over_o=2))
    rows, half = own.shape[0], x_ref.shape[1]
    spans = row_spans(rows, PIECES)
    size = rows // PIECES
    def spread(source, target, pieces):
        count = len(pieces)
        to_near = [w.slot() for _ in pieces]
        to_far = [w.slot() for _ in pieces]
        kept = [w.local_used + i for i in range(count)]
        w.local_used += count

        def piece(base, i):
            start, length = pieces[i]
            return source.at[pl.ds(pl.multiple_of(base * rows + start, 8), length)]

        def span(i):
            return pl.ds(pieces[i][0], pieces[i][1])

        left, right = pl.ds(0, half), pl.ds(half, half)

        def same_keep(i):
            return pltpu.make_async_copy(piece(w.k, i), target.at[span(i), left], local_sem.at[kept[i]])

        def same_send(i):
            return w.copy(piece(1 - w.k, i), target.at[span(i), left], {"k": 1 - w.k}, to_near[i])

        def cross_near(i):
            return w.copy(piece(w.k, i), target.at[span(i), right], {"x": 1 - w.x}, to_near[i])

        def cross_far(i):
            return w.copy(
                piece(1 - w.k, i), target.at[span(i), right], {"k": 1 - w.k, "x": 1 - w.x}, to_far[i]
            )

        def start():
            @pl.when(w.same)
            def _():
                for i in range(count):
                    same_send(i).start()
                    same_keep(i).start()

            @pl.when(jnp.logical_not(w.same))
            def _():
                for i in range(count):
                    cross_near(i).start()
                    cross_far(i).start()

        def arrive(i):
            @pl.when(w.same)
            def _():
                same_keep(i).wait()
                same_send(i).wait_recv()

            @pl.when(jnp.logical_not(w.same))
            def _():
                cross_near(i).wait_recv()
                cross_far(i).wait_recv()

        def close():
            @pl.when(w.same)
            def _():
                for i in range(count):
                    same_send(i).wait_send()

            @pl.when(jnp.logical_not(w.same))
            def _():
                for i in range(count):
                    cross_near(i).wait_send()
                    cross_far(i).wait_send()

        return start, arrive, close

    gain_copy = w.send(gain_own, gain_ref.at[:, pl.ds(half, half)], {"x": 1 - w.x})
    code_copies = [
        w.send(gain_own, far_gains, {"k": 1 - w.k, "h": 1 - w.h}),
        w.send(codes_own, codes.at[1], {"x": 1 - w.x}),
        w.send(codes_own, codes.at[2], {"k": 1 - w.k}),
        w.send(codes_own, codes.at[3], {"k": 1 - w.k, "x": 1 - w.x}),
    ]
    codes[0] = codes_own[...]
    start, arrive, close = spread(x_ref, xin, [(i * size, size) for i in range(PIECES)])
    start()
    qkv.start()
    forget.start()
    share = Share(w, psize, own, g, spans)
    gain_ref[:, pl.ds(0, half)] = gain_own[...]
    gain_copy.wait_recv()
    for i, span in enumerate(spans):
        arrive(i)

        def norm(rows):
            value = xin[rows, :].astype(F32)
            own[rows, :] = (value * inverse_rms(value) * gain_ref[0:1, :]).astype(BF16)

        by_chunks(span, norm)
        share.send(i)
    close()
    for fetch in (qkv, forget, out_fetch):
        fetch.store()
    for i in range(3):
        qkv.relay(i)
    out_fetch.start()
    forget.relay(0)
    for i in range(3):
        qkv.relay_over(i)
        if i < PIECES:
            share.relay(i)
    forget.relay_over(0)
    out_fetch.relay(0)
    out_fetch.relay_over(0)
    share.wait()
    for fetch in (qkv, forget, out_fetch):
        fetch.wait()
    for copy in code_copies:
        copy.wait_recv()
    w.close()


def forward_exchange_kernel(
    psize, part, xin, gain_ref, gate_shard, gate_got, up_shard, up_got, down_shard, resid, g, gate, up, down,
    near, mid, far, own, gate_stage, gate_keep, up_stage, up_keep, down_stage, send_sem, recv_sem, local_sem,
):
    w = Wires(send_sem, recv_sem, local_sem)
    gate_fetch = Fetch(w, gate_shard, gate, gate_stage, 2, gate_got, gate_keep)
    up_fetch = Fetch(w, up_shard, up, up_stage, 2, up_got, up_keep)
    down_fetch = Fetch(w, down_shard, down, down_stage, 2)
    fetches = (gate_fetch, up_fetch, down_fetch)
    for fetch in fetches:
        fetch.load()
    w.greet(partners(w, psize, away=True, over_o=2))
    spans = row_spans(own.shape[0], PIECES)
    reduce = Reduce(w, psize, part, near, mid, far, spans)
    gate_fetch.start()
    reduce.start()
    up_fetch.start()
    down_fetch.start()
    for fetch in fetches:
        fetch.store()
    for i in range(2):
        gate_fetch.relay_over(i)
    for i in range(2):
        down_fetch.relay(i)
    for i in range(2):
        up_fetch.relay_over(i)
    share = Share(w, psize, own, g, spans)
    for i in range(PIECES):

        def norm(rows, total):
            value = total + xin[rows, :].astype(F32)
            resid[rows, :] = value
            own[rows, :] = (value * inverse_rms(value) * gain_ref[1:2, :]).astype(BF16)

        reduce.each(i, norm)
        share.send(i)
    for i in range(2):
        down_fetch.relay_over(i)
    for i in range(PIECES):
        share.relay(i)
    share.wait()
    for fetch in fetches:
        fetch.wait()
    w.close()


class EarlySum:
    def __init__(self, wires, part, value, over, across, result, pieces, offset=0, got=None):
        w = self.wires = wires
        self.offset, self.got = offset, got
        self.part, self.value, self.over, self.across, self.result = part, value, over, across, result
        self.count, self.half_rows = pieces, value.shape[1]
        self.size = self.half_rows // pieces
        self.over_slots = [[w.slot() for _ in range(pieces)] for _ in range(2)]
        self.across_slots = [w.slot() for _ in range(pieces)]
        self.local_slot = w.local_used
        w.local_used += 2 + pieces

    def span(self, i):
        return pl.ds(i * self.size, self.size)

    def load_copy(self, half):
        start = pl.multiple_of(self.offset + (self.wires.o % 2) * self.half_rows, 16)
        return pltpu.make_async_copy(
            self.part.at[half, pl.ds(start, self.half_rows)],
            self.value.at[half],
            self.wires.local_sem.at[self.local_slot + half],
        )

    def load(self):
        for half in range(2):
            self.load_copy(half).start()

    def over_copy(self, half, i):
        w = self.wires
        start = pl.multiple_of(self.offset + (1 - w.o % 2) * self.half_rows + i * self.size, 16)
        return w.copy(
            self.part.at[half, pl.ds(start, self.size)],
            self.over.at[half, self.span(i)],
            {"o": w.o ^ 1},
            self.over_slots[half][i],
        )

    def across_copy(self, i):
        w = self.wires
        return w.copy(
            self.value.at[1, self.span(i)], self.across.at[self.span(i)], {"x": 1 - w.x}, self.across_slots[i]
        )

    def keep_copy(self, i):
        return pltpu.make_async_copy(
            self.value.at[0, self.span(i)],
            self.result.at[self.span(i)],
            self.wires.local_sem.at[self.local_slot + 2 + i],
        )

    def start(self, half):
        for i in range(self.count):
            self.over_copy(half, i).start()

    def pass_on(self, i):
        if i == 0:
            self.load_copy(1).wait()
        span = self.span(i)
        if self.got is None:
            self.over_copy(1, i).wait_recv()
            add_into(self.value.at[1, span], self.over.at[1, span])
        else:
            add_into(self.value.at[1, span], self.got.at[span])
        self.across_copy(i).start()

    def finish(self, i):
        if i == 0:
            self.load_copy(0).wait()
        self.over_copy(0, i).wait_recv()
        self.across_copy(i).wait_recv()
        span = self.span(i)
        add_into(self.value.at[0, span], self.over.at[0, span], self.across.at[span])
        if self.result is not None:
            self.keep_copy(i).start()

    def close(self):
        for i in range(self.count):
            for half in range(2):
                if half == 0 or self.got is None:
                    self.over_copy(half, i).wait_send()
            self.across_copy(i).wait_send()
            if self.result is not None:
                self.keep_copy(i).wait()


def backward_exchange_kernel(
    psize, part, resid, cot, gain_ref, down_own, down_other, gate_part, gate_got, up_part,
    grad_resid, g, gain_grad, down_sum, pair_sum,
    near, mid, far, own, down_across, down_moved, gate_val, gate_over, gate_across, up_val, up_over, up_across,
    send_sem, recv_sem, local_sem,
):
    w = Wires(send_sem, recv_sem, local_sem)
    gate = EarlySum(w, gate_part, gate_val, gate_over, gate_across, pair_sum.at[0], 2, got=gate_got)
    up = EarlySum(w, up_part, up_val, up_over, up_across, pair_sum.at[1], 2)
    gate.load()
    up.load()
    w.greet(partners(w, psize, away=True, over_o=2))
    spans = row_spans(own.shape[0], PIECES)
    reduce = Reduce(w, psize, part, near, mid, far, spans)
    down_copy = w.send(down_other, down_across, {"x": 1 - w.x})
    gate.start(0)
    up.start(1)
    up.start(0)
    for i in range(2):
        gate.pass_on(i)
    reduce.start()
    down_home = w.copy(down_sum, down_moved, {"h": 1 - w.h}, w.slot())
    down_copy.wait_recv()

    def add_down(rows):
        down_sum[rows, :] = (
            down_own[rows, :].astype(F32) + down_across[rows, :].astype(F32)
        ).astype(BF16)

    by_chunks(pl.ds(0, down_sum.shape[0]), add_down)

    @pl.when(jnp.logical_not(w.home))
    def _():
        down_home.start()

    share = Share(w, psize, own, g, spans)
    gain_grad[...] = jnp.zeros(gain_grad.shape, F32)

    def back(rows, total):
        grad, gain_part = norm_back(total, resid[rows, :], cot[rows, :].astype(F32), gain_ref[1:2, :])
        grad_resid[rows, :] = grad
        own[rows, :] = grad.astype(BF16)
        gain_grad[...] += gain_part

    for i in range(PIECES):
        reduce.each(i, back)
        share.send(i)
    for i in range(2):
        up.pass_on(i)
    share.relay(0)
    for i in range(2):
        gate.finish(i)
    for i in range(1, PIECES):
        share.relay(i)
    for i in range(2):
        up.finish(i)
    share.wait()
    gate.close()
    up.close()

    @pl.when(jnp.logical_not(w.home))
    def _():
        down_home.wait_send()

    @pl.when(w.home)
    def _():
        down_home.wait_recv()
        add_into(down_sum, down_moved)

    w.close()


class Spread:
    def __init__(self, wires, value, result):
        w = self.wires = wires
        self.value, self.result = value, result
        self.over_slot, self.near_slot, self.pass_slot = w.slot(), w.slot(), w.slot()
        self.local_slot = w.local_used
        w.local_used += 1

    def rows(self, mine):
        bit = self.wires.o % 2
        return self.result.at[bit if mine else 1 - bit]

    def over_copy(self):
        w = self.wires
        return w.copy(self.value, self.rows(True), {"o": w.o ^ 1}, self.over_slot)

    def near_copy(self):
        return self.wires.copy(self.value, self.rows(True), {"k": 1 - self.wires.k}, self.near_slot)

    def pass_copy(self):
        return self.wires.copy(self.rows(False), self.rows(False), {"k": 1 - self.wires.k}, self.pass_slot)

    def keep_copy(self):
        return pltpu.make_async_copy(
            self.value, self.rows(True), self.wires.local_sem.at[self.local_slot]
        )

    def start(self):
        @pl.when(self.wires.home)
        def _():
            self.over_copy().start()
            self.near_copy().start()
            self.keep_copy().start()

    def relay(self):
        @pl.when(self.wires.home)
        def _():
            self.over_copy().wait_recv()
            self.pass_copy().start()

    def wait(self):
        @pl.when(self.wires.home)
        def _():
            self.over_copy().wait_send()
            self.near_copy().wait_send()
            self.pass_copy().wait_send()
            self.keep_copy().wait()

        @pl.when(jnp.logical_not(self.wires.home))
        def _():
            self.near_copy().wait_recv()
            self.pass_copy().wait_recv()


class SmallSum:
    def __init__(self, wires, psize, osize, value, other, buffers):
        w = self.wires = wires
        self.value, self.other, self.buffers = value, other, buffers
        self.devices = [{"x": 1 - w.x}, {"k": 1 - w.k}]
        self.devices += [{"p": w.p ^ bit} for bit in bits_of(psize)]
        self.devices += [{"h": 1 - w.h}]
        self.devices += [{"o": w.o ^ bit} for bit in bits_of(osize)]
        self.slots = [w.slot() for _ in self.devices]

    def copy(self, step):
        source = self.other if step == 0 else self.value
        return self.wires.copy(source, self.buffers.at[step], self.devices[step], self.slots[step])

    def start(self):
        self.copy(0).start()

    def step(self, step):
        self.copy(step).wait()
        self.value[...] = self.value[...] + self.buffers[step]
        if step + 1 < len(self.devices):
            self.copy(step + 1).start()


class Chain:
    def __init__(self, wires, osize, value, stages, buffers, result, pieces):
        self.wires, self.value, self.stages, self.result = wires, value, stages, result
        self.buffers = buffers
        self.spans = row_spans(value.shape[0], pieces)
        self.slots = [[wires.slot() for _ in self.spans] for _ in stages]
        self.kept = [wires.local_used + i for i in range(pieces)]
        wires.local_used += pieces
        self.other = None

    def copy(self, stage, i):
        w, span = self.wires, self.spans[i]
        kind, slot = self.stages[stage], self.slots[stage][i]
        if kind == "x":
            return w.copy(self.other.at[span], self.buffers[stage].at[span], {"x": 1 - w.x}, slot)
        if kind == "h":
            return w.copy(self.value.at[span], self.buffers[stage].at[span], {"h": 1 - w.h}, slot)
        if kind == "k":
            return w.copy(self.value.at[span], self.result.at[span], {"k": 1 - w.k}, slot)
        return w.copy(self.value.at[span], self.buffers[stage].at[span], {"o": w.o ^ kind}, slot)

    def keep(self, i):
        span = self.spans[i]
        return pltpu.make_async_copy(
            self.value.at[span], self.result.at[span], self.wires.local_sem.at[self.kept[i]]
        )

    def start(self, stage, i):
        w, kind = self.wires, self.stages[stage]
        if kind == "x":
            self.copy(stage, i).start()
        elif kind == "h":
            @pl.when(jnp.logical_not(w.home))
            def _():
                self.copy(stage, i).start()
        else:
            @pl.when(w.home)
            def _():
                self.copy(stage, i).start()
                if kind == "k":
                    self.keep(i).start()

    def add(self, stage, i):
        span = self.spans[i]
        add_into(self.value.at[span], self.buffers[stage].at[span])

    def end(self, stage, i):
        w, kind = self.wires, self.stages[stage]
        if kind == "x":
            self.copy(stage, i).wait_recv()
            self.add(stage, i)
        elif kind == "h":
            @pl.when(w.home)
            def _():
                self.copy(stage, i).wait_recv()
                self.add(stage, i)
        elif kind == "k":
            @pl.when(w.home)
            def _():
                self.copy(stage, i).wait_send()
                self.keep(i).wait()

            @pl.when(jnp.logical_not(w.home))
            def _():
                self.copy(stage, i).wait_recv()
        else:
            @pl.when(w.home)
            def _():
                self.copy(stage, i).wait()
                self.add(stage, i)

    def close(self):
        w = self.wires
        for stage, kind in enumerate(self.stages):
            for i in range(len(self.spans)):
                if kind == "x":
                    self.copy(stage, i).wait_send()
                elif kind == "h":
                    @pl.when(jnp.logical_not(w.home))
                    def _():
                        self.copy(stage, i).wait_send()

    def step(self, stage, i):
        self.end(stage, i)
        if stage + 1 < len(self.stages):
            self.start(stage + 1, i)

    def order(self, first=0):
        return [(stage, i) for stage in range(first, len(self.stages)) for i in range(len(self.spans))]

    def run(self, first=0):
        for stage, i in self.order(first):
            self.step(stage, i)


def leave_kernel(
    psize, osize, pieces, grad_in, weight_in, stream, base, gain_ref, small_in, proj_in, out_own, out_other,
    pair_in, down_in, block, small, first_sum, second_sum, out_sum, up_sum, gate_sum, down_sum,
    near, mid, far, part, kept, first_val, second_val, out_val, up_val, gate_val, down_val, first_bufs,
    second_over, second_across, second_bufs, out_bufs, small_other, small_bufs, gain_acc,
    send_sem, recv_sem, local_sem,
):
    w = Wires(send_sem, recv_sem, local_sem)
    split = first_val.shape[0]
    second = EarlySum(w, proj_in, second_val, second_over, second_across, None, 2, split)
    second.load()
    loads = [
        w.local(source, target)
        for source, target in (
            (pair_in.at[1], up_val), (pair_in.at[0], gate_val), (down_in, down_val), (out_own, out_val),
            (proj_in.at[0, pl.ds(0, split)], first_val),
        )
    ]
    w.greet(partners(w, psize, away=True, over_o=osize))
    rows, half = kept.shape[1], kept.shape[2]
    spans = row_spans(rows, PIECES)
    size = rows // PIECES
    bits = bits_of(osize)

    first = Chain(
        w, osize, first_val, ["x", "h"] + bits + ["k"], [first_bufs.at[i] for i in range(2 + len(bits))],
        first_sum, pieces,
    )
    first.other = proj_in.at[1, pl.ds(0, split)]
    late = Chain(
        w, osize, second_val.at[0], ["h"] + bits[1:], [second_bufs.at[i] for i in range(len(bits))], None, 2
    )
    out = Chain(w, osize, out_val, ["x", "h"] + bits[1:], [out_bufs.at[i] for i in range(1 + len(bits))], None, 1)
    out.other = out_other
    spreads = [Spread(w, up_val, up_sum), Spread(w, gate_val, gate_sum), Spread(w, down_val, down_sum)]
    last_spreads = [Spread(w, out_val, out_sum), Spread(w, second_val.at[0], second_sum)]
    reduce = Reduce(w, psize, part, near, mid, far, spans)
    second.start(1)
    for i in range(pieces):
        first.start(0, i)
    out.start(0, 0)
    second.start(0)
    for load in loads:
        load.wait()
    for spread in spreads:
        spread.start()
    columns = D // TILE

    def multiply(block):
        def one(n, carry):
            span = pl.ds(pl.multiple_of(n * TILE, TILE), TILE)
            part[block, :, span] = dot_nt(grad_in[block], weight_in[span, :]).astype(BF16)
            return carry

        lax.fori_loop(0, columns, one, 0)

    reduce.start_with(multiply)

    near_slots = [w.slot() for _ in spans]
    far_slots = [w.slot() for _ in spans]
    keep_slots = [w.local_used + i for i in range(PIECES)]
    w.local_used += PIECES

    def target(i):
        return block.at[pl.ds(pl.multiple_of(w.k * rows + i * size, 8), size)]

    def same_keep(i):
        return pltpu.make_async_copy(kept.at[0, spans[i]], target(i), local_sem.at[keep_slots[i]])

    def same_send(i):
        return w.copy(kept.at[1, spans[i]], target(i), {"x": 1 - w.x}, near_slots[i])

    def cross_near(i):
        return w.copy(kept.at[0, spans[i]], target(i), {"k": 1 - w.k}, near_slots[i])

    def cross_far(i):
        return w.copy(kept.at[1, spans[i]], target(i), {"k": 1 - w.k, "x": 1 - w.x}, far_slots[i])

    for i in range(2):
        second.pass_on(i)
    first.step(0, 0)
    for i in range(1, pieces):
        first.step(0, i)
        first.step(1, i - 1)
    out.step(0, 0)
    second.finish(0)
    late.start(0, 0)
    first.step(1, pieces - 1)
    gain_acc[...] = jnp.zeros(gain_acc.shape, F32)

    def back(rows_, total):
        grad, gain_part = norm_back(total, stream[rows_, :].astype(F32), base[rows_, :], gain_ref[0:1, :])
        gain_acc[...] += gain_part
        kept[0, rows_, :] = grad[:, :half].astype(BF16)
        kept[1, rows_, :] = grad[:, half:].astype(BF16)

    for i in range(PIECES):
        reduce.each(i, back)

        @pl.when(w.same)
        def _():
            same_send(i).start()
            same_keep(i).start()

        @pl.when(jnp.logical_not(w.same))
        def _():
            cross_near(i).start()
            cross_far(i).start()

        if i == 0:
            second.finish(1)
            late.start(0, 1)

    gain_sum = jnp.sum(gain_acc[...], axis=0, keepdims=True)
    row = lax.broadcasted_iota(jnp.int32, (8, half), 0)
    small[...] = jnp.where(row == 0, gain_sum[:, :half], small_in[:, :half])
    small_other[...] = jnp.where(row == 0, gain_sum[:, half:], small_in[:, half:])
    total = SmallSum(w, psize, osize, small, small_other, small_bufs)
    total.start()
    out.run(1)
    last_spreads[0].start()
    steps = [lambda a=a: late.step(*a) for a in late.order(0)] + [last_spreads[1].start]
    steps += [spread.relay for spread in spreads] + [lambda a=a: first.step(*a) for a in first.order(2)]
    steps += [last_spreads[0].relay, last_spreads[1].relay]
    smalls = list(range(len(total.devices)))
    for n, step in enumerate(steps):
        step()
        if n % 2 == 0 and smalls:
            total.step(smalls.pop(0))
    for step in smalls:
        total.step(step)
    for spread in spreads + last_spreads:
        spread.wait()
    for i in range(PIECES):
        @pl.when(w.same)
        def _():
            same_keep(i).wait()
            same_send(i).wait_send()
            cross_near(i).wait_recv()

        @pl.when(jnp.logical_not(w.same))
        def _():
            cross_near(i).wait_send()
            cross_far(i).wait()
            same_send(i).wait_recv()

    for chain in (first, second, late, out):
        chain.close()
    w.close()


ANY = pl.BlockSpec(memory_space=pl.ANY)
VMEM = pl.BlockSpec(memory_space=pltpu.VMEM)
SLOTS = 128


def exchange_call(kernel, name, collective_id, outs, out_specs, in_specs, scratch, args):
    return pl.pallas_call(
        kernel,
        out_shape=outs,
        in_specs=in_specs,
        out_specs=out_specs,
        scratch_shapes=scratch
        + [
            pltpu.SemaphoreType.DMA((SLOTS,)),
            pltpu.SemaphoreType.DMA((SLOTS,)),
            pltpu.SemaphoreType.DMA((SLOTS // 2,)),
        ],
        compiler_params=pltpu.CompilerParams(
            collective_id=collective_id, has_side_effects=True, vmem_limit_bytes=56 << 20
        ),
        name=name,
    )(*args)


def sds(shape, dtype):
    return jax.ShapeDtypeStruct(shape, dtype)


def sum_scratch(psize, rows):
    far = max(psize - 1, 1)
    return [
        pltpu.VMEM((psize, rows, D), BF16),
        pltpu.VMEM((far, rows, D), BF16),
        pltpu.VMEM((far, rows, D), BF16),
    ]


def enter(psize, layer_input, gains, codes, qkv_weight, forget_weight, out_weight):
    rows = layer_input.shape[0] // 2
    half, width = qkv_weight.shape
    columns = width + forget_weight.shape[1]
    return exchange_call(
        functools.partial(enter_kernel, psize),
        "enter",
        1,
        (
            sds((rows, D), BF16),
            sds((2 * psize, rows, D), BF16),
            sds((2, half, columns), BF16),
            sds((out_weight.shape[0], 2 * half), BF16),
            sds((8, D), F32),
            sds((4,) + codes.shape, jnp.int32),
            sds(gains.shape, F32),
        ),
        (VMEM, ANY, ANY, ANY, VMEM, VMEM, VMEM),
        [ANY, VMEM, VMEM, ANY, ANY, ANY],
        [pltpu.VMEM((rows, D), BF16)]
        + [pltpu.VMEM(value.shape, BF16) for value in (qkv_weight, forget_weight, out_weight)],
        (layer_input, gains, codes, qkv_weight, forget_weight, out_weight),
    )


def forward_exchange(psize, part, xin, gains, gate_weight, gate_got, up_weight, up_got, down_weight):
    rows = xin.shape[0]
    return exchange_call(
        functools.partial(forward_exchange_kernel, psize),
        "forward_exchange",
        2,
        (
            sds((rows, D), F32),
            sds((2 * psize, rows, D), BF16),
            sds((2,) + gate_weight.shape, BF16),
            sds((2,) + up_weight.shape, BF16),
            sds((down_weight.shape[0], D), BF16),
        ),
        (VMEM, ANY, ANY, ANY, ANY),
        [VMEM, VMEM, VMEM, ANY, ANY, ANY, ANY, ANY],
        sum_scratch(psize, rows)
        + [pltpu.VMEM((rows, D), BF16)]
        + [
            pltpu.VMEM(value.shape, BF16)
            for value in (gate_weight, gate_got, up_weight, up_got, down_weight)
        ],
        (part, xin, gains, gate_weight, gate_got, up_weight, up_got, down_weight),
    )


def backward_exchange(psize, part, resid, cot, gains, down_own, down_other, gate_part, gate_got, up_part):
    rows = resid.shape[0]

    def early(value):
        half_rows = value.shape[1] // 2
        shape = (half_rows, value.shape[2])
        return [
            pltpu.VMEM((2,) + shape, BF16),
            pltpu.VMEM((2,) + shape, BF16),
            pltpu.VMEM(shape, BF16),
        ]

    return exchange_call(
        functools.partial(backward_exchange_kernel, psize),
        "backward_exchange",
        3,
        (
            sds((rows, D), F32),
            sds((2 * psize, rows, D), BF16),
            sds((8, D), F32),
            sds(down_own.shape, BF16),
            sds((2, gate_part.shape[1] // 2, gate_part.shape[2]), BF16),
        ),
        (VMEM, ANY, VMEM, VMEM, ANY),
        [VMEM, VMEM, VMEM, VMEM, VMEM, ANY, ANY, VMEM, ANY],
        sum_scratch(psize, rows)
        + [pltpu.VMEM((rows, D), BF16)]
        + [pltpu.VMEM(down_own.shape, BF16)] * 2
        + early(gate_part)
        + early(up_part),
        (part, resid, cot, gains, down_own, down_other, gate_part, gate_got, up_part),
    )


def leave(psize, osize, grad, weight, stream, base, gains, small, proj, out_own, out_other, pair, down):
    rows = stream.shape[0]
    bits = len(bits_of(osize))
    half = D // 2
    columns = proj.shape[2]
    split = proj.shape[1] // 2

    def scratch(*shape):
        return pltpu.VMEM(shape, BF16)

    def both(shape):
        return sds((2,) + shape, BF16)

    return exchange_call(
        functools.partial(leave_kernel, psize, osize, 3),
        "leave",
        4,
        (
            sds((2 * rows, half), BF16),
            sds((8, half), F32),
            sds((split, columns), BF16),
            both((split // 2, columns)),
            both(out_own.shape),
            both(pair.shape[1:]),
            both(pair.shape[1:]),
            both(down.shape),
        ),
        (ANY, VMEM, ANY, ANY, ANY, ANY, ANY, ANY),
        [VMEM] * 6 + [ANY] * 5,
        sum_scratch(psize, rows)
        + [
            scratch(2 * psize, rows, D),
            scratch(2, rows, half),
            scratch(split, columns),
            scratch(2, split // 2, columns),
            scratch(*out_own.shape),
            scratch(*pair.shape[1:]),
            scratch(*pair.shape[1:]),
            scratch(*down.shape),
            scratch(2 + bits, split, columns),
            scratch(2, split // 2, columns),
            scratch(split // 2, columns),
            scratch(bits, split // 2, columns),
            scratch(1 + bits, *out_own.shape),
            pltpu.VMEM((8, half), F32),
            pltpu.VMEM((3 + len(bits_of(psize)) + bits, 8, half), F32),
            pltpu.VMEM((8, D), F32),
        ],
        (grad, weight, stream, base, gains, small, proj, out_own, out_other, pair, down),
    )


def make_shards(osize, psize):
    count = 2 * psize
    obits = bits_of(osize)

    def shards(
        layer_input,
        attn_gain,
        qkv_weight,
        forget_weight,
        forget_bias,
        out_weight,
        ffn_gain,
        gate_weight,
        up_weight,
        down_weight,
        prompt_doc,
        branch_seg,
        branch_doc,
        out_cotangent,
    ):
        core, xpos = lax.axis_index("k"), lax.axis_index("x")
        hpos, ppos, opos = lax.axis_index("h"), lax.axis_index("p"), lax.axis_index("o")
        home = core == hpos
        same = core == xpos
        heads = forget_weight.shape[1]
        width = heads * 3 * DH
        lane_pad = LANES - heads
        feat = D // 2

        def far_blocks(block):
            return [xor_swap(block, "p", psize, bit) for bit in range(1, psize)]

        def all_blocks(block, far):
            blocks = []
            for near in [block] + far:
                blocks += [near, swap(near, "k")]
            return jnp.concatenate(blocks, axis=0)

        def near_sums(partial):
            size = partial.shape[0] // count
            parts = [partial[i * size : (i + 1) * size] for i in range(count)]
            moved = [swap(parts[i + 1], "k") for i in range(0, count, 2)]
            return [add_parts(parts[i], moved[i // 2]) for i in range(0, count, 2)]

        def far_sums(sums):
            return [xor_swap(sums[bit], "p", psize, bit) for bit in range(1, psize)]

        def total_of(near, far):
            total = near.astype(F32)
            for value in far:
                total = total + value.astype(F32)
            return total

        prompt_len, branch_len = prompt_doc.shape[1], branch_seg.shape[1]
        packed = jnp.concatenate([prompt_doc[0], branch_seg[0], branch_doc[0]])
        code_rows = -(-packed.shape[0] // (8 * LANES)) * 8
        packed = jnp.pad(packed, (0, code_rows * LANES - packed.shape[0])).reshape(code_rows, LANES)
        bias_row = jnp.pad(forget_bias, (0, feat - heads))
        own_gains = jnp.concatenate(
            [jnp.stack([attn_gain, ffn_gain, bias_row]), jnp.zeros((5, feat), F32)]
        )
        forget_wide = jnp.concatenate(
            [forget_weight, jnp.zeros((forget_weight.shape[0], lane_pad), BF16)], axis=1
        )
        first_part, second_part = qkv_weight, forget_wide
        if width % LANES:
            spare = jnp.zeros((qkv_weight.shape[0], LANES - width % LANES), BF16)
            first_part = jnp.concatenate([qkv_weight, forget_wide, spare], axis=1)
        xin, normed_a_all, w_proj, w_out, gains8, codes, far_gains = enter(
            psize, layer_input, own_gains, packed, first_part, second_part, out_weight
        )
        bias = jnp.where(home, own_gains[2, :LANES], far_gains[2, :LANES])
        packed = lax.dynamic_index_in_dim(
            codes, (core ^ xpos) * 2 + (xpos ^ hpos), 0, keepdims=False
        ).reshape(-1)
        prompt_ids = packed[:prompt_len]
        branch_ids = packed[prompt_len : prompt_len + branch_len]
        branch_docs = packed[prompt_len + branch_len : prompt_len + branch_len + branch_doc.shape[1]]
        kcol, qrow, flags = group_codes(prompt_ids, branch_ids, branch_docs)
        normed_a_all = normed_a_all.reshape(-1, D)
        w_proj = w_proj.reshape(D, -1)[:, : width + LANES]

        projected = matmul(normed_a_all, w_proj).reshape(count, -1, width + LANES)
        cot_near, cot_far = take_half(out_cotangent, core), take_half(out_cotangent, 1 - core)
        projected, kcol, qrow, flags, gate_half, up_half, cot_first, cot_near, cot_far = lax.optimization_barrier(
            (
                projected,
                kcol,
                qrow,
                flags,
                take_half(gate_weight, opos % 2),
                take_half(up_weight, opos % 2),
                jnp.where(same, cot_far, cot_near),
                cot_near,
                cot_far,
            )
        )
        gate_got, up_got = fetch_home_away(gate_half), fetch_home_away(up_half)
        cot_first = lax.ppermute(cot_first, ("k", "x"), SPREAD_A)
        cot_second = lax.ppermute(cot_far, ("k", "x"), SPREAD_B)
        attended, *saved = attention_forward(
            projected, bias[None], kcol, qrow, flags, heads, prompt_len
        )
        attended, gate_got, up_got, cot_first, cot_second, *saved = lax.optimization_barrier(
            (attended, gate_got, up_got, cot_first, cot_second, *saved)
        )
        attended = attended.reshape(-1, heads * DH)
        cot = jnp.concatenate(
            [jnp.where(same, cot_near, cot_first), jnp.where(same, cot_first, cot_second)], axis=1
        )
        part = matmul(attended, w_out).astype(BF16).reshape(count, -1, D)
        resid, normed_b_all, w_gate, w_up, w_down = forward_exchange(
            psize, part, xin, gains8, gate_weight, gate_got, up_weight, up_got, down_weight
        )
        normed_b_all = normed_b_all.reshape(-1, D)
        w_gate, w_up = w_gate.reshape(D, -1), w_up.reshape(D, -1)
        cot_others = far_blocks(tie(cot, normed_b_all))
        gate_pre = matmul(normed_b_all, w_gate)
        up_pre = matmul(normed_b_all, w_up)
        gate_sig = jax.nn.sigmoid(gate_pre)
        gate_act = gate_pre * gate_sig
        hidden = (gate_act * up_pre).astype(BF16)
        out_part = matmul(hidden, w_down).astype(BF16)
        out_part, *cot_others = lax.optimization_barrier((out_part, *cot_others))
        cot_all = all_blocks(cot, cot_others)

        def finish(total, axis_bits):
            for bit in axis_bits:
                total = add_parts(total, home_swap(total, osize, bit))
            return total

        high = opos % 2 == 1
        down_part = contract_rows(hidden, cot_all).astype(BF16)
        down_keep, down_give = split_rows(down_part, high)
        down_moved = xor_swap(down_give, "o", osize, 1)
        out_sums = near_sums(out_part)
        out_far = far_sums(out_sums)
        grad_hidden = contract_cols(tie(cot_all, out_sums[0]), w_down)
        grad_gate = (grad_hidden * up_pre * gate_sig * (1.0 + gate_pre * (1.0 - gate_sig))).astype(BF16)
        grad_up = (grad_hidden * gate_act).astype(BF16)
        gate_part = contract_rows(normed_b_all, grad_gate).astype(BF16).reshape(2, feat, -1)
        gate_got = xor_swap(take_half(gate_part[1], 1 - opos % 2), "o", osize, 1)
        grad_gate, grad_up, gate_part, *out_far = lax.optimization_barrier(
            (grad_gate, grad_up, gate_part, *out_far)
        )
        up_part = contract_rows(normed_b_all, grad_up).astype(BF16).reshape(2, feat, -1)
        part = (contract_cols(grad_gate, w_gate) + contract_cols(grad_up, w_up)).astype(BF16)
        part, up_part, gate_got, down_moved = lax.optimization_barrier(
            (part, up_part, gate_got, down_moved)
        )
        layer_output = (resid + total_of(out_sums[0], out_far)).astype(BF16)
        down_total = add_parts(down_keep, down_moved)
        grad_resid, grad_branch_all, ffn_gain_part, down_total, pair_total = backward_exchange(
            psize,
            part.reshape(count, -1, D),
            resid,
            cot,
            gains8,
            down_total[:, :feat],
            down_total[:, feat:],
            gate_part,
            gate_got,
            up_part,
        )
        grad_branch_all = grad_branch_all.reshape(-1, D)
        grad_attended = contract_cols(grad_branch_all, w_out).astype(BF16)
        out_part = contract_rows(attended, grad_branch_all).astype(BF16)
        out_keep, out_give = split_rows(out_part, high)
        grad_attended, out_keep, out_give, down_total, pair_total, *block_parts = lax.optimization_barrier(
            (grad_attended, out_keep, out_give, down_total, pair_total) + unspread_parts(layer_output, same)
        )
        own_part, near_part, far_part = block_parts
        pair_moved = to_home(pair_total)
        out_moved = xor_swap(out_give, "o", osize, 1)
        near_moved, far_moved = unspread_moves(near_part, far_part)
        grad_proj, bias_sums = attention_backward(
            grad_attended.reshape(count, -1, heads * DH), saved, kcol, qrow, flags, heads, prompt_len
        )
        grad_proj, bias_sums, out_moved, near_moved, far_moved, pair_moved = lax.optimization_barrier(
            (grad_proj, bias_sums, out_moved, near_moved, far_moved, pair_moved)
        )
        layer_output = unspread_join(own_part, near_moved, far_moved, core, same)
        grad_proj = grad_proj.reshape(-1, width + LANES)
        proj_part = contract_rows(normed_a_all, grad_proj).astype(BF16)
        down_total = finish(down_total, obits[1:])
        pair_total = finish(add_parts(pair_total, pair_moved), obits[1:])
        out_total = add_parts(out_keep, out_moved)

        slots = jnp.where(
            (jnp.arange(2 * psize) == core * psize + ppos)[:, None], bias_sums[:1, :heads], 0.0
        ).reshape(-1)
        slots = jnp.concatenate([slots, jnp.zeros((feat - slots.shape[0],), F32)])
        small = jnp.stack([jnp.zeros((D,), F32), jnp.sum(ffn_gain_part, axis=0), jnp.concatenate([slots, slots])])
        small = jnp.concatenate([small, jnp.zeros((5, D), F32)])
        input_grad, small, first_rows, second_rows, out_both, up_both, gate_both, down_both = leave(
            psize,
            osize,
            grad_proj.reshape(count, -1, width + LANES),
            w_proj,
            xin,
            grad_resid,
            gains8,
            small,
            proj_part.reshape(2, feat, -1),
            out_total[:, :feat],
            out_total[:, feat:],
            pair_total,
            down_total,
        )
        proj_grad = jnp.concatenate([first_rows, second_rows.reshape(first_rows.shape)], axis=0)
        qkv_grad = proj_grad[:, :width].astype(F32)
        forget_grad = proj_grad[:, width : width + heads].astype(F32)
        bias_all = small[2, : 2 * psize * heads].reshape(2 * psize, heads)
        forget_bias_grad = lax.dynamic_index_in_dim(bias_all, hpos * psize + ppos, 0, keepdims=False)

        def whole(halves):
            return halves.reshape(-1, halves.shape[2]).astype(F32)

        return (
            layer_output,
            input_grad,
            small[0],
            qkv_grad,
            forget_grad,
            forget_bias_grad,
            whole(out_both),
            small[1],
            whole(gate_both),
            whole(up_both),
            whole(down_both),
        )

    return shards


def solution(mesh):
    dp, row, col = mesh.shape["dp"], mesh.shape["row"], mesh.shape["col"]
    osize, psize = dp // 2, col // 2
    assert row == 2
    split = Mesh(mesh.devices.reshape(osize, 2, row, 2, psize), ("o", "k", "x", "h", "p"))
    tokens = P(("o", "k", "h", "p"), "x")
    rows_first = P("x", ("h", "p"))
    cols_first = P(("h", "p"), "x")
    groups = P(("o", "k", "x"), None)
    in_specs = (
        tokens,
        P("x"),
        rows_first,
        rows_first,
        P(("h", "p")),
        cols_first,
        P("x"),
        rows_first,
        rows_first,
        cols_first,
        groups,
        groups,
        groups,
        tokens,
    )
    out_specs = (
        tokens,
        tokens,
        P("x"),
        rows_first,
        rows_first,
        P(("h", "p")),
        cols_first,
        P("x"),
        rows_first,
        rows_first,
        cols_first,
    )
    return jax.shard_map(
        make_shards(osize, psize), mesh=split, in_specs=in_specs, out_specs=out_specs, check_vma=False
    )
```

```python
import functools

import jax
import jax.numpy as jnp
from jax import lax
from jax.experimental import pallas as pl
from jax.experimental.pallas import tpu as pltpu
from jax.sharding import Mesh, PartitionSpec as P

D = 1536
DH = 64
DOCS = 4
TILE = 256
EPS = 1e-06
MASKED = -1e30
LANES = 128
BF16 = jnp.bfloat16
F32 = jnp.float32


def swap(value, axis):
    return lax.ppermute(value, axis, [(0, 1), (1, 0)])


def xor_swap(value, axis, size, bit):
    return lax.ppermute(value, axis, [(i, i ^ bit) for i in range(size)])


def kxh(k, x, h):
    return (k * 2 + x) * 2 + h


def fetch_home_away(value):
    pairs = []
    for k in range(2):
        for x in range(2):
            for h in range(2):
                target = (k, 1 - x, h) if k == h else (1 - k, x, 1 - h)
                pairs.append((kxh(k, x, h), kxh(*target)))
    return lax.ppermute(value, ("k", "x", "h"), pairs)


def fetch_away(value):
    pairs = [
        (kxh(k, x, 1 - k), kxh(k, 1 - x, 1 - k)) for k in range(2) for x in range(2)
    ]
    return lax.ppermute(value, ("k", "x", "h"), pairs)


def tie(value, *others):
    return lax.optimization_barrier((value,) + others)[0]


def join_weight(shard, first, second, home, axis):
    mine = jnp.where(home, shard, first)
    other = jnp.where(home, first, second)
    return jnp.concatenate([mine, other], axis=axis)


def add_parts(kept, moved):
    return (kept.astype(F32) + moved.astype(F32)).astype(BF16)


def to_home(value):
    return lax.ppermute(value, ("k", "h"), [(1, 0), (2, 3)])


def from_home(value):
    return lax.ppermute(value, ("k", "h"), [(0, 2), (3, 1)])


def home_swap(value, size, bit):
    pairs = []
    for o in range(size):
        for k in range(2):
            pairs.append(((o * 2 + k) * 2 + k, ((o ^ bit) * 2 + k) * 2 + k))
    return lax.ppermute(value, ("o", "k", "h"), pairs)


def bits_of(size):
    return [1 << i for i in range(size.bit_length() - 1)]


def split_rows(value, high):
    half = value.shape[0] // 2
    low_rows, high_rows = value[:half], value[half:]
    return jnp.where(high, high_rows, low_rows), jnp.where(high, low_rows, high_rows)


def merge_rows(kept, moved, high):
    return jnp.concatenate([jnp.where(high, moved, kept), jnp.where(high, kept, moved)], axis=0)


def take_half(value, index):
    half = value.shape[0] // 2
    return lax.dynamic_slice_in_dim(value, index * half, half, 0)


def kx(k, x):
    return k * 2 + x


SPREAD_A = []
SPREAD_B = []
for _k in range(2):
    for _x in range(2):
        if _k == _x:
            SPREAD_A.append((kx(_k, _x), kx(1 - _k, _x)))
        else:
            SPREAD_A.append((kx(_k, _x), kx(_k, 1 - _x)))
            SPREAD_B.append((kx(_k, _x), kx(1 - _k, 1 - _x)))


def spread_tokens(block, core, same):
    near = take_half(block, core)
    far = take_half(block, 1 - core)
    first = lax.ppermute(jnp.where(same, far, near), ("k", "x"), SPREAD_A)
    second = lax.ppermute(far, ("k", "x"), SPREAD_B)
    own = jnp.where(same, near, first)
    other = jnp.where(same, first, second)
    return jnp.concatenate([own, other], axis=1)


def unspread_parts(rows, same):
    half = rows.shape[1] // 2
    own, other = rows[:, :half], rows[:, half:]
    return own, jnp.where(same, other, own), other


def unspread_moves(near, far):
    first = lax.ppermute(near, ("k", "x"), [(b, a) for a, b in SPREAD_A])
    second = lax.ppermute(far, ("k", "x"), [(b, a) for a, b in SPREAD_B])
    return first, second


def unspread_join(own, first, second, core, same):
    near = jnp.where(same, own, first)
    far = jnp.where(same, first, second)
    low = jnp.where(core == 0, near, far)
    high = jnp.where(core == 0, far, near)
    return jnp.concatenate([low, high], axis=0)


def contract_rows(left, right):
    return lax.dot_general(
        left, right, (((0,), (0,)), ((), ())), preferred_element_type=F32
    )


def contract_cols(left, right):
    return lax.dot_general(
        left, right, (((1,), (1,)), ((), ())), preferred_element_type=F32
    )


def matmul(left, right):
    return jnp.dot(left, right, preferred_element_type=F32)


def dot_nn(left, right):
    return lax.dot_general(left, right, (((1,), (0,)), ((), ())), preferred_element_type=F32)


def dot_nt(left, right):
    return lax.dot_general(left, right, (((1,), (1,)), ((), ())), preferred_element_type=F32)


def tile_mask(qrow, kcol, rows, cols, i, j):
    key_pos = j * TILE + lax.broadcasted_iota(jnp.int32, (TILE, TILE), 0)
    query_pos = i * TILE + lax.broadcasted_iota(jnp.int32, (TILE, TILE), 1)
    code = kcol[pl.ds(pl.multiple_of(j * TILE, TILE), TILE), 0:1]
    first = qrow[0:1, pl.ds(pl.multiple_of(i * TILE, TILE), TILE)]
    second = qrow[1:2, pl.ds(pl.multiple_of(i * TILE, TILE), TILE)]
    seen = (key_pos <= query_pos) & ((code == first) | (code == second))
    return jnp.where(seen, 0.0, MASKED)


def split_parts(value):
    high = value.astype(BF16)
    rest = value - high.astype(F32)
    mid = rest.astype(BF16)
    low = (rest - mid.astype(F32)).astype(BF16)
    return high, mid, low


def lane(shape):
    return lax.broadcasted_iota(jnp.int32, shape, 1)


def forward_kernel(
    heads, count, prompt_len, flags, proj_hbm, bias_ref, kcol, qrow, att_hbm, ot_hbm, lse_ref,
    qp_hbm, kp_hbm, vp_hbm, logit, qkv, qp, kp, vp, vt, rates, sums_ref, attended, ot, mask,
    in_sem, out_sem, keep_sem, *per_head,
):
    me = lax.axis_index("p") * 2 + lax.axis_index("k")
    total = qkv.shape[0]
    size = total // count
    tiles = total // TILE
    loads = []
    for b in range(count):
        rows = pl.ds(b * size, size)
        loads.append(pltpu.make_async_copy(proj_hbm.at[b ^ me], qkv.at[rows], in_sem.at[b]))
    for load in loads:
        load.start()
    for load in loads:
        load.wait()
    logit[...] = qkv[:, 3 * DH * heads :] + bias_ref[...]
    value = logit[...]
    rate = jnp.minimum(value, 0.0) - jnp.log1p(jnp.exp(-jnp.abs(value)))
    rate = jnp.where(lane(rate.shape) < heads, rate, 0.0)
    high, mid, low = split_parts(rate)
    packed = high.astype(F32) + pltpu.roll(mid.astype(F32), 8, 1) + pltpu.roll(low.astype(F32), 16, 1)
    rates[...] = packed.astype(BF16)
    place_row = lax.broadcasted_iota(jnp.int32, (LANES, LANES), 0)
    place_col = lax.broadcasted_iota(jnp.int32, (LANES, LANES), 1)

    prompt_tiles = prompt_len // TILE
    wide = (TILE, TILE)
    row_pos, col_pos = lax.broadcasted_iota(jnp.int32, wide, 0), lax.broadcasted_iota(jnp.int32, wide, 1)
    below = jnp.where(col_pos <= row_pos, 1.0, 0.0).astype(BF16)

    def prompt_sums(t, before):
        rows = pl.ds(pl.multiple_of(t * TILE, TILE), TILE)
        prefix = dot_nn(below, rates[rows, :]) + before
        sums_ref[rows, :] = prefix
        return prefix[TILE - 1 : TILE, :]

    lax.fori_loop(0, prompt_tiles, prompt_sums, jnp.zeros((1, LANES), F32))
    doc_index = lax.broadcasted_iota(jnp.int32, (8, prompt_len), 0)
    within = jnp.where(qrow[3:4, 0:prompt_len] <= doc_index, 1.0, 0.0).astype(BF16)
    doc_sums = dot_nn(within, rates[0:prompt_len, :])

    def branch_sums(t, carry):
        rows = pl.ds(pl.multiple_of(t * TILE, TILE), TILE)
        limit = kcol[rows, 2:3]
        start = jnp.zeros((TILE, LANES), F32)
        for doc in range(DOCS):
            start = jnp.where(limit == doc, doc_sums[doc : doc + 1, :], start)

        def add_own(u, acc):
            others = pl.ds(pl.multiple_of(u * TILE, TILE), TILE)
            own = (u * TILE + col_pos <= t * TILE + row_pos) & (kcol[rows, 1:2] == qrow[2:3, others])
            return acc + dot_nn(jnp.where(own, 1.0, 0.0).astype(BF16), rates[others, :])

        sums_ref[rows, :] = lax.fori_loop(prompt_tiles, t + 1, add_own, start)
        return carry

    lax.fori_loop(prompt_tiles, tiles, branch_sums, 0)

    def prepare(t, carry):
        rows = pl.ds(pl.multiple_of(t * TILE, TILE), TILE)
        sums = sums_ref[rows, :]
        decay = sums + pltpu.roll(sums, LANES - 8, 1) + pltpu.roll(sums, LANES - 16, 1)
        decay = jnp.where(lane(decay.shape) < heads, -decay, 0.0)
        high, mid, low = split_parts(decay)
        parts = (
            high.astype(F32) + pltpu.roll(mid.astype(F32), 8, 1) + pltpu.roll(low.astype(F32), 16, 1)
        ).astype(BF16)
        lanes = lane((TILE, LANES))
        for h in range(heads):
            base = 3 * DH * h
            query = qkv[rows, base : base + DH].astype(BF16).astype(F32) * DH ** (-0.5)
            key = qkv[rows, base + DH : base + 2 * DH]
            worth = qkv[rows, base + 2 * DH : base + 3 * DH].astype(BF16)
            ones = jnp.where((lanes >= DH) & (lanes < DH + 3), 1.0, 0.0)[:, :DH]
            ones = jnp.where(lane((TILE, DH)) < 3, 1.0, 0.0)
            qp[h, rows, :] = jnp.concatenate([query, ones], axis=1).astype(BF16)
            spread = jnp.where(
                (place_col >= DH) & (place_col < DH + 3) & (place_row == 8 * (place_col - DH) + h), 1.0, 0.0
            ).astype(BF16)
            extra = dot_nn(parts, spread)
            extra = jnp.where(lanes == DH + 3, 1.0, extra)
            key_wide = jnp.concatenate([key, extra[:, DH:]], axis=1)
            kp[h, rows, :] = key_wide.astype(BF16)
            vp[h, rows, :] = worth
            vt[h, :, rows] = worth.astype(F32).T.astype(BF16)
        return carry

    lax.fori_loop(0, tiles, prepare, 0)
    keeps = [
        pltpu.make_async_copy(qp, qp_hbm, keep_sem.at[0]),
        pltpu.make_async_copy(kp, kp_hbm, keep_sem.at[1]),
        pltpu.make_async_copy(vp, vp_hbm, keep_sem.at[2]),
    ]
    for keep in keeps:
        keep.start()

    acc, top_refs, total_refs, score_refs = (per_head[n * heads : (n + 1) * heads] for n in range(4))

    def query_tile(i, carry):
        cols = pl.ds(pl.multiple_of(i * TILE, TILE), TILE)
        for h in range(heads):
            top_refs[h][...] = jnp.full(top_refs[h].shape, MASKED, F32)
            total_refs[h][...] = jnp.zeros(total_refs[h].shape, F32)
            acc[h][...] = jnp.zeros(acc[h].shape, F32)

        def key_tile(j, inner):
            @pl.when(flags[i * tiles + j] > 0)
            def _():
                rows = pl.ds(pl.multiple_of(j * TILE, TILE), TILE)
                mask[...] = tile_mask(qrow, kcol, None, None, i, j)
                tops = []
                for h in range(heads):
                    scores = dot_nt(kp[h, rows, :], qp[h, cols, :]) + mask[...]
                    score_refs[h][...] = scores
                    tops.append(jnp.maximum(top_refs[h][0:1, :], jnp.max(scores, axis=0, keepdims=True)))
                for h, top in enumerate(tops):
                    expo = jnp.exp(score_refs[h][...] - top)
                    shrink = jnp.exp(top_refs[h][0:1, :] - top)
                    top_refs[h][0:1, :] = top
                    total_refs[h][0:1, :] = total_refs[h][0:1, :] * shrink + jnp.sum(expo, axis=0, keepdims=True)
                    acc[h][...] = acc[h][...] * shrink + dot_nn(vt[h, :, rows], expo.astype(BF16))

            return inner

        lax.fori_loop(0, i + 1, key_tile, 0)
        for h in range(heads):
            total = total_refs[h][0:1, :]
            ot[pl.ds(h * DH, DH), cols] = acc[h][...] / total
            lse_ref[h : h + 1, cols] = top_refs[h][0:1, :] + jnp.log(total)
        attended[cols, :] = ot[:, cols].T.astype(BF16)
        return carry

    lse_ref[...] = jnp.zeros(lse_ref.shape, F32)
    lax.fori_loop(0, tiles, query_tile, 0)
    stores = [pltpu.make_async_copy(ot, ot_hbm, keep_sem.at[3])]
    for b in range(count):
        stores.append(
            pltpu.make_async_copy(attended.at[pl.ds(b * size, size)], att_hbm.at[b ^ me], out_sem.at[b])
        )
    for store in stores:
        store.start()
    for copy in keeps + stores:
        copy.wait()


def attention_forward(projected, bias, kcol, qrow, flags, heads, prompt_len):
    count, size, width = projected.shape
    total = count * size
    any_spec = pl.BlockSpec(memory_space=pl.ANY)
    vmem = pl.BlockSpec(memory_space=pltpu.VMEM)
    shape = jax.ShapeDtypeStruct
    return pl.pallas_call(
        functools.partial(forward_kernel, heads, count, prompt_len),
        out_shape=(
            shape((count, size, heads * DH), BF16),
            shape((heads * DH, total), F32),
            shape((8, total), F32),
            shape((heads, total, LANES), BF16),
            shape((heads, total, LANES), BF16),
            shape((heads, total, DH), BF16),
            shape((total, LANES), F32),
        ),
        in_specs=[pl.BlockSpec(memory_space=pltpu.SMEM), any_spec, vmem, vmem, vmem],
        out_specs=(any_spec, any_spec, vmem, any_spec, any_spec, any_spec, vmem),
        scratch_shapes=[
            pltpu.VMEM((total, width), F32),
            pltpu.VMEM((heads, total, LANES), BF16),
            pltpu.VMEM((heads, total, LANES), BF16),
            pltpu.VMEM((heads, total, DH), BF16),
            pltpu.VMEM((heads, DH, total), BF16),
            pltpu.VMEM((total, LANES), BF16),
            pltpu.VMEM((total, LANES), F32),
            pltpu.VMEM((total, heads * DH), BF16),
            pltpu.VMEM((heads * DH, total), F32),
            pltpu.VMEM((TILE, TILE), F32),
            pltpu.SemaphoreType.DMA((count,)),
            pltpu.SemaphoreType.DMA((count,)),
            pltpu.SemaphoreType.DMA((4,)),
        ]
        + [pltpu.VMEM((DH, TILE), F32)] * heads
        + [pltpu.VMEM((8, TILE), F32)] * (2 * heads)
        + [pltpu.VMEM((TILE, TILE), F32)] * heads,
        compiler_params=pltpu.CompilerParams(vmem_limit_bytes=48 << 20),
        cost_estimate=pl.CostEstimate(flops=20_000_000_000, bytes_accessed=30_000_000, transcendentals=0),
        name="attention_forward",
    )(flags, projected, bias, kcol, qrow)


def backward_kernel(
    heads, count, prompt_len, flags, gatt_hbm, ot_ref, lse_ref, qp, kp, vp, logit, kcol, qrow,
    grad_hbm, bias_ref, gatt, gout, kt, delta, mask, decay, grad, in_sem, out_sem, *per_head,
):
    dqt, dk, dv, prob_refs, score_refs = (per_head[n * heads : (n + 1) * heads] for n in range(5))
    me = lax.axis_index("p") * 2 + lax.axis_index("k")
    total = gatt.shape[0]
    size = total // count
    tiles = total // TILE
    loads = []
    for b in range(count):
        rows = pl.ds(b * size, size)
        loads.append(pltpu.make_async_copy(gatt_hbm.at[b ^ me], gatt.at[rows], in_sem.at[b]))
    for load in loads:
        load.start()
    for load in loads:
        load.wait()
    for h in range(heads):
        dqt[h][...] = jnp.zeros(dqt[h].shape, F32)
    delta[...] = jnp.zeros(delta.shape, F32)

    def prepare(t, carry):
        rows = pl.ds(pl.multiple_of(t * TILE, TILE), TILE)
        turned = gatt[rows, :].astype(F32).T * ot_ref[:, rows]
        for h in range(heads):
            gout[h, rows, :] = gatt[rows, h * DH : (h + 1) * DH]
            kt[h, :, rows] = kp[h, rows, :].astype(F32).T[: DH + 8].astype(BF16)
            delta[h : h + 1, rows] = jnp.sum(turned[h * DH : (h + 1) * DH], axis=0, keepdims=True)
        return carry

    lax.fori_loop(0, tiles, prepare, 0)
    lanes = lane((TILE, LANES))

    def key_tile(j, carry):
        rows = pl.ds(pl.multiple_of(j * TILE, TILE), TILE)
        for h in range(heads):
            dk[h][...] = jnp.zeros(dk[h].shape, F32)
            dv[h][...] = jnp.zeros(dv[h].shape, F32)

        def query_tile(i, inner):
            @pl.when(flags[i * tiles + j] > 0)
            def _():
                cols = pl.ds(pl.multiple_of(i * TILE, TILE), TILE)
                mask[...] = tile_mask(qrow, kcol, None, None, i, j)
                for h in range(heads):
                    scores = dot_nt(kp[h, rows, :], qp[h, cols, :]) + mask[...]
                    prob_refs[h][...] = jnp.exp(scores - lse_ref[h : h + 1, cols])
                for h in range(heads):
                    probs = prob_refs[h][...]
                    grad_probs = dot_nt(vp[h, rows, :], gout[h, cols, :])
                    score_refs[h][...] = (probs * (grad_probs - delta[h : h + 1, cols])).astype(BF16)
                    dv[h][...] += dot_nn(probs.astype(BF16), gout[h, cols, :])
                for h in range(heads):
                    grad_scores = score_refs[h][...]
                    dk[h][...] += dot_nn(grad_scores, qp[h, cols, :])
                    dqt[h][:, cols] += dot_nn(kt[h, :, rows], grad_scores)

            return inner

        lax.fori_loop(j, tiles, query_tile, 0)
        keys = jnp.zeros((TILE, LANES), F32)
        for h in range(heads):
            grad_key = dk[h][...]
            keys += jnp.where(lanes == h, pltpu.roll(grad_key, LANES - DH + h, 1), 0.0)
            grad[rows, (3 * h + 1) * DH : (3 * h + 3) * DH] = jnp.concatenate(
                [grad_key[:, :DH], dv[h][...]], axis=1
            ).astype(BF16)
        decay[rows, :] = -keys
        return carry

    lax.fori_loop(0, tiles, key_tile, 0)

    def finish(t, carry):
        rows = pl.ds(pl.multiple_of(t * TILE, TILE), TILE)
        queries = jnp.zeros((TILE, LANES), F32)
        for h in range(heads):
            turned = jnp.concatenate([dqt[h][:, rows], jnp.zeros((LANES - DH - 8, TILE), F32)], axis=0).T
            queries += jnp.where(lanes == h, pltpu.roll(turned, LANES - DH - 3 + h, 1), 0.0)
            grad[rows, 3 * h * DH : (3 * h + 1) * DH] = (turned[:, :DH] * DH ** (-0.5)).astype(BF16)
        whole = decay[rows, :] + queries
        high, mid, low = split_parts(whole)
        decay[rows, :] = (
            high.astype(F32) + pltpu.roll(mid.astype(F32), 8, 1) + pltpu.roll(low.astype(F32), 16, 1)
        )
        return carry

    lax.fori_loop(0, tiles, finish, 0)

    prompt_tiles = prompt_len // TILE
    wide = (TILE, TILE)
    row_pos, col_pos = lax.broadcasted_iota(jnp.int32, wide, 0), lax.broadcasted_iota(jnp.int32, wide, 1)
    above = jnp.where(col_pos >= row_pos, 1.0, 0.0).astype(BF16)
    branch_len = total - prompt_len
    doc_index = lax.broadcasted_iota(jnp.int32, (8, branch_len), 0)
    chosen = jnp.where(qrow[4:5, prompt_len:total] == doc_index, 1.0, 0.0).astype(BF16)
    doc_sums = dot_nn(chosen, decay[prompt_len:total, :].astype(BF16))

    def prompt_sums(n, after):
        t = prompt_tiles - 1 - n
        rows = pl.ds(pl.multiple_of(t * TILE, TILE), TILE)
        suffix = dot_nn(above, decay[rows, :].astype(BF16)) + after
        doc = kcol[rows, 3:4]
        sums = suffix
        for d in range(DOCS):
            sums = sums + jnp.where(doc <= d, doc_sums[d : d + 1, :], 0.0)
        decay[rows, :] = sums
        return suffix[0:1, :]

    def branch_sums(t, carry):
        rows = pl.ds(pl.multiple_of(t * TILE, TILE), TILE)

        def add_own(u, acc):
            others = pl.ds(pl.multiple_of(u * TILE, TILE), TILE)
            own = (u * TILE + col_pos >= t * TILE + row_pos) & (kcol[rows, 1:2] == qrow[2:3, others])
            return acc + dot_nn(jnp.where(own, 1.0, 0.0).astype(BF16), decay[others, :].astype(BF16))

        decay[rows, :] = lax.fori_loop(t, tiles, add_own, jnp.zeros((TILE, LANES), F32))
        return carry

    lax.fori_loop(0, prompt_tiles, prompt_sums, jnp.zeros((1, LANES), F32))
    lax.fori_loop(prompt_tiles, tiles, branch_sums, 0)

    def rates(t, bias):
        rows = pl.ds(pl.multiple_of(t * TILE, TILE), TILE)
        sums = decay[rows, :]
        grad_rate = sums + pltpu.roll(sums, LANES - 8, 1) + pltpu.roll(sums, LANES - 16, 1)
        value = logit[rows, :]
        grad_forget = grad_rate / (1.0 + jnp.exp(value))
        grad_forget = jnp.where(lanes < heads, grad_forget, 0.0).astype(BF16)
        grad[rows, 3 * DH * heads :] = grad_forget
        return bias + jnp.sum(grad_forget.astype(F32), axis=0, keepdims=True)

    bias_ref[...] = jnp.broadcast_to(
        lax.fori_loop(0, tiles, rates, jnp.zeros((1, LANES), F32)), bias_ref.shape
    )
    stores = []
    for b in range(count):
        stores.append(
            pltpu.make_async_copy(grad.at[pl.ds(b * size, size)], grad_hbm.at[b ^ me], out_sem.at[b])
        )
    for store in stores:
        store.start()
    for store in stores:
        store.wait()


def attention_backward(grad_attended, saved, kcol, qrow, flags, heads, prompt_len):
    ot, lse, qp, kp, vp, logit = saved
    count, size, width = grad_attended.shape
    total = count * size
    any_spec = pl.BlockSpec(memory_space=pl.ANY)
    vmem = pl.BlockSpec(memory_space=pltpu.VMEM)
    shape = jax.ShapeDtypeStruct
    out_width = 3 * DH * heads + LANES
    return pl.pallas_call(
        functools.partial(backward_kernel, heads, count, prompt_len),
        out_shape=(shape((count, size, out_width), BF16), shape((8, LANES), F32)),
        in_specs=[pl.BlockSpec(memory_space=pltpu.SMEM), any_spec]
        + [vmem] * 8,
        out_specs=(any_spec, vmem),
        scratch_shapes=[
            pltpu.VMEM((total, width), BF16),
            pltpu.VMEM((heads, total, DH), BF16),
            pltpu.VMEM((heads, DH + 8, total), BF16),
            pltpu.VMEM((8, total), F32),
            pltpu.VMEM((TILE, TILE), F32),
            pltpu.VMEM((total, LANES), F32),
            pltpu.VMEM((total, out_width), BF16),
            pltpu.SemaphoreType.DMA((count,)),
            pltpu.SemaphoreType.DMA((count,)),
        ]
        + [pltpu.VMEM((DH + 8, total), F32)] * heads
        + [pltpu.VMEM((TILE, LANES), F32)] * heads
        + [pltpu.VMEM((TILE, DH), F32)] * heads
        + [pltpu.VMEM((TILE, TILE), F32)] * heads
        + [pltpu.VMEM((TILE, TILE), BF16)] * heads,
        compiler_params=pltpu.CompilerParams(vmem_limit_bytes=56 << 20),
        cost_estimate=pl.CostEstimate(flops=50_000_000_000, bytes_accessed=30_000_000, transcendentals=0),
        name="attention_backward",
    )(flags, grad_attended, ot, lse, qp, kp, vp, logit, kcol, qrow)


def group_codes(prompt_ids, branch_ids, branch_docs):
    prompt_len = prompt_ids.shape[0]
    member = branch_ids[:, None] == jnp.arange(branch_docs.shape[0])[None, :]
    branch_doc_ids = jnp.sum(jnp.where(member, branch_docs[None, :], 0), axis=1)
    key_code = jnp.concatenate([prompt_ids, DOCS + branch_ids])
    first = jnp.concatenate([prompt_ids, branch_doc_ids])
    tag = jnp.concatenate([jnp.full_like(prompt_ids, -1), branch_ids])
    limit = jnp.concatenate([jnp.full_like(prompt_ids, -1), branch_doc_ids])
    prompt_code = jnp.concatenate([prompt_ids, jnp.full_like(branch_ids, DOCS)])
    total = key_code.shape[0]
    none = jnp.zeros_like(tag)
    kcol = jnp.stack([key_code, tag, limit, prompt_code] + [none] * 4, axis=1)
    qrow = jnp.stack([first, key_code, tag, prompt_code, limit] + [none] * 3, axis=0)
    tiles = total // TILE
    kinds = jnp.arange(2 * DOCS)
    key_bits = jnp.any(key_code.reshape(tiles, TILE, 1) == kinds, axis=1)
    query_bits = key_bits | jnp.any(first.reshape(tiles, TILE, 1) == kinds, axis=1)
    order = jnp.arange(tiles)
    meets = jnp.any(query_bits[:, None, :] & key_bits[None, :, :], axis=2)
    flags = (meets & (order[None, :] <= order[:, None])).astype(jnp.int32).reshape(-1)
    return kcol, qrow, flags


class Wires:
    def __init__(self, send_sem, recv_sem, local_sem):
        self.send_sem, self.recv_sem, self.local_sem = send_sem, recv_sem, local_sem
        self.used, self.local_used = 0, 0
        self.k, self.x = lax.axis_index("k"), lax.axis_index("x")
        self.h, self.p, self.o = lax.axis_index("h"), lax.axis_index("p"), lax.axis_index("o")
        self.home = self.k == self.h
        self.same = self.k == self.x
        self.pending = []

    def slot(self):
        self.used += 1
        return self.used - 1

    def copy(self, source, target, device, slot):
        return pltpu.make_async_remote_copy(
            src_ref=source,
            dst_ref=target,
            send_sem=self.send_sem.at[slot],
            recv_sem=self.recv_sem.at[slot],
            device_id=device,
            device_id_type=pl.DeviceIdType.MESH,
        )

    def send(self, source, target, device):
        copy = self.copy(source, target, device, self.slot())
        copy.start()
        self.pending.append(copy.wait_send)
        return copy

    def local(self, source, target):
        copy = pltpu.make_async_copy(source, target, self.local_sem.at[self.local_used])
        self.local_used += 1
        copy.start()
        return copy

    def greet(self, devices):
        barrier = pltpu.get_barrier_semaphore()
        for device in devices:
            pl.semaphore_signal(
                barrier, inc=1, device_id=device, device_id_type=pl.DeviceIdType.MESH
            )
        pl.semaphore_wait(barrier, len(devices))

    def close(self):
        for wait in self.pending:
            wait()


def row_spans(total, pieces):
    size = total // pieces
    return [pl.ds(i * size, size) for i in range(pieces)]


class Fetch:
    def __init__(self, wires, shard, target, stage, pieces, got=None, keep=None):
        w = self.wires = wires
        self.shard, self.target, self.stage, self.got, self.keep = shard, target, stage, got, keep
        self.count = pieces
        self.half_rows = shard.shape[0] // 2
        self.size = self.half_rows // pieces
        self.by_columns = len(target.shape) == 2
        self.first = [w.slot() for _ in range(pieces)]
        self.over = [w.slot() for _ in range(pieces)]
        self.second = [w.slot() for _ in range(2 * pieces)]
        self.local_slot = w.local_used
        w.local_used += 2

    def rows(self, i, mine=True):
        bit = self.wires.o % 2
        bit = bit if mine else 1 - bit
        return pl.ds(pl.multiple_of(bit * self.half_rows + i * self.size, 16), self.size)

    def place(self, half, span):
        if self.by_columns:
            width = self.shard.shape[1]
            return self.target.at[span, pl.ds(half * width, width)]
        return self.target.at[half, span]

    def first_copy(self, i, home):
        w, span = self.wires, self.rows(i)
        if home:
            return w.copy(self.shard.at[span], self.place(1, span), {"x": 1 - w.x}, self.first[i])
        device = {"k": 1 - w.k, "h": 1 - w.h}
        return w.copy(self.shard.at[span], self.place(0, span), device, self.first[i])

    def have(self, i, half):
        if self.got is None:
            return self.place(half, self.rows(i))
        return self.got.at[pl.ds(i * self.size, self.size)]

    def over_copy(self, i, home):
        w, half = self.wires, 1 if home else 0
        return w.copy(self.have(i, half), self.place(half, self.rows(i)), {"o": w.o ^ 1}, self.over[i])

    def second_copy(self, i, mine):
        w, span = self.wires, self.rows(i, mine)
        source = self.have(i, 0) if mine else self.place(0, span)
        slot = self.second[i if mine else self.count + i]
        return w.copy(source, self.place(1, span), {"x": 1 - w.x}, slot)

    def shard_load(self):
        return pltpu.make_async_copy(self.shard, self.stage, self.wires.local_sem.at[self.local_slot])

    def shard_store(self):
        whole = pl.ds(0, self.shard.shape[0])
        return pltpu.make_async_copy(
            self.stage, self.place(0, whole), self.wires.local_sem.at[self.local_slot]
        )

    def got_load(self):
        return pltpu.make_async_copy(self.got, self.keep, self.wires.local_sem.at[self.local_slot + 1])

    def got_store(self, half):
        bit = self.wires.o % 2
        span = pl.ds(pl.multiple_of(bit * self.half_rows, 16), self.half_rows)
        return pltpu.make_async_copy(
            self.keep, self.place(half, span), self.wires.local_sem.at[self.local_slot + 1]
        )

    def either(self, at_home, away):
        pl.when(self.wires.home)(at_home)
        pl.when(jnp.logical_not(self.wires.home))(away)

    def load(self):
        pl.when(self.wires.home)(lambda: self.shard_load().start())
        if self.got is not None:
            self.got_load().start()

    def start(self):
        if self.got is not None:
            for i in range(self.count):
                self.relay(i)
            return

        def go(home):
            for i in range(self.count):
                self.first_copy(i, home).start()

        self.either(lambda: go(True), lambda: go(False))

    def store(self):
        def at_home():
            self.shard_load().wait()
            self.shard_store().start()
            if self.got is not None:
                self.got_load().wait()
                self.got_store(1).start()

        def away():
            if self.got is not None:
                self.got_load().wait()
                self.got_store(0).start()

        self.either(at_home, away)

    def relay(self, i):
        def at_home():
            if self.got is None:
                self.first_copy(i, True).wait_recv()
            self.over_copy(i, True).start()

        def away():
            if self.got is None:
                self.first_copy(i, False).wait_recv()
            self.over_copy(i, False).start()
            self.second_copy(i, True).start()

        self.either(at_home, away)

    def relay_over(self, i):
        def away():
            self.over_copy(i, False).wait_recv()
            self.second_copy(i, False).start()

        pl.when(jnp.logical_not(self.wires.home))(away)

    def wait(self):
        def at_home():
            for i in range(self.count):
                if self.got is None:
                    self.first_copy(i, True).wait_send()
                self.over_copy(i, True).wait()
            self.shard_store().wait()
            if self.got is not None:
                self.got_store(1).wait()

        def away():
            for i in range(self.count):
                if self.got is None:
                    self.first_copy(i, False).wait_send()
                self.over_copy(i, False).wait_send()
                self.second_copy(i, True).wait()
                self.second_copy(i, False).wait()
            if self.got is not None:
                self.got_store(0).wait()

        self.either(at_home, away)


def partners(wires, psize, away=False, peers=True, over_o=0):
    devices = [{"k": 1 - wires.k}]
    if peers:
        devices += [{"p": wires.p ^ bit} for bit in range(1, psize)]
    devices += [{"x": 1 - wires.x}]
    devices += [{"k": 1 - wires.k, "x": 1 - wires.x}]
    if away:
        devices += [{"k": 1 - wires.k, "h": 1 - wires.h}, {"h": 1 - wires.h}]
    bit = 1
    while bit < over_o:
        devices += [{"o": wires.o ^ bit}]
        bit *= 2
    return devices


class Share:
    def __init__(self, wires, psize, own, g, spans):
        self.wires, self.psize, self.own, self.g, self.spans = wires, psize, own, g, spans
        self.near, self.far, self.kept, self.passed = [], {}, [], []

    def send(self, i):
        w, span = self.wires, self.spans[i]
        for bit in range(1, self.psize):
            self.far[bit, i] = w.send(self.own.at[span], self.g.at[2 * bit, span], {"p": w.p ^ bit})
        self.near.append(w.send(self.own.at[span], self.g.at[1, span], {"k": 1 - w.k}))
        self.kept.append(w.local(self.own.at[span], self.g.at[0, span]))

    def relay(self, i):
        w, span = self.wires, self.spans[i]
        for bit in range(1, self.psize):
            self.far[bit, i].wait_recv()
            self.passed.append(
                w.send(self.g.at[2 * bit, span], self.g.at[2 * bit + 1, span], {"k": 1 - w.k})
            )

    def wait(self):
        for copy in self.near + self.passed:
            copy.wait_recv()
        for copy in self.kept:
            copy.wait()


def by_chunks(span, body):
    def run(n, carry):
        body(pl.ds(pl.multiple_of(span.start + n * CHUNK, CHUNK), CHUNK))
        return carry

    lax.fori_loop(0, span.size // CHUNK, run, 0)


def add_into(value, *others):
    def body(rows):
        total = value[rows, :].astype(F32)
        for other in others:
            total = total + other[rows, :].astype(F32)
        value[rows, :] = total.astype(BF16)

    by_chunks(pl.ds(0, value.shape[0]), body)


class Reduce:
    def __init__(self, wires, psize, part, near, mid, far, spans):
        self.wires, self.psize, self.part = wires, psize, part
        self.near, self.mid, self.far, self.spans = near, mid, far, spans
        self.near_copies, self.far_copies = {}, {}

    def start_near(self, bit):
        w = self.wires
        for i, span in enumerate(self.spans):
            self.near_copies[bit, i] = w.send(
                self.part.at[2 * bit + 1, span], self.near.at[bit, span], {"k": 1 - w.k}
            )

    def start_far(self, bit):
        w = self.wires
        for i, span in enumerate(self.spans):
            self.near_copies[bit, i].wait_recv()

            def add(rows, bit=bit):
                self.mid[bit - 1, rows] = (
                    self.part[2 * bit, rows].astype(F32) + self.near[bit, rows].astype(F32)
                ).astype(BF16)

            by_chunks(span, add)
            self.far_copies[bit, i] = w.send(
                self.mid.at[bit - 1, span], self.far.at[bit - 1, span], {"p": w.p ^ bit}
            )

    def start(self):
        for bit in reversed(range(self.psize)):
            self.start_near(bit)
        for bit in reversed(range(1, self.psize)):
            self.start_far(bit)

    def start_with(self, make):
        for bit in reversed(range(self.psize)):
            make(2 * bit + 1)
            self.start_near(bit)
            make(2 * bit)
            if bit:
                self.start_far(bit)

    def each(self, i, body):
        span = self.spans[i]
        self.near_copies[0, i].wait_recv()
        for bit in range(1, self.psize):
            self.far_copies[bit, i].wait_recv()

        def run(rows):
            total = self.part[0, rows].astype(F32) + self.near[0, rows].astype(F32)
            for bit in range(1, self.psize):
                total = total + self.far[bit - 1, rows].astype(F32)
            body(rows, total)

        by_chunks(span, run)


CHUNK = 32
PIECES = 3


def inverse_rms(value):
    return lax.rsqrt(jnp.sum(value * value, axis=1, keepdims=True) / D + EPS)


def norm_back(grad, value, base, gain):
    rms = inverse_rms(value)
    gained = gain * grad
    inner = jnp.sum(value * gained, axis=1, keepdims=True)
    result = base + rms * gained - value * (rms * rms * rms) * inner / D
    parts = grad * value * rms
    return result, sum(parts[n : n + 8] for n in range(0, parts.shape[0], 8))


def enter_kernel(
    psize, x_ref, gain_own, codes_own, qkv_shard, forget_shard, out_shard, xin, g, proj, out, gain_ref, codes, far_gains,
    own, qkv_stage, forget_stage, out_stage, send_sem, recv_sem, local_sem,
):
    w = Wires(send_sem, recv_sem, local_sem)
    width = qkv_shard.shape[1]
    qkv = Fetch(w, qkv_shard, proj.at[:, :, pl.ds(0, width)], qkv_stage, 3)
    forget = Fetch(
        w, forget_shard, proj.at[:, :, pl.ds(width, forget_shard.shape[1])], forget_stage, 1
    )
    out_fetch = Fetch(w, out_shard, out, out_stage, 1)
    for fetch in (qkv, forget, out_fetch):
        fetch.load()
    w.greet(partners(w, psize, away=True, over_o=2))
    rows, half = own.shape[0], x_ref.shape[1]
    spans = row_spans(rows, PIECES)
    size = rows // PIECES
    def spread(source, target, pieces):
        count = len(pieces)
        to_near = [w.slot() for _ in pieces]
        to_far = [w.slot() for _ in pieces]
        kept = [w.local_used + i for i in range(count)]
        w.local_used += count

        def piece(base, i):
            start, length = pieces[i]
            return source.at[pl.ds(pl.multiple_of(base * rows + start, 8), length)]

        def span(i):
            return pl.ds(pieces[i][0], pieces[i][1])

        left, right = pl.ds(0, half), pl.ds(half, half)

        def same_keep(i):
            return pltpu.make_async_copy(piece(w.k, i), target.at[span(i), left], local_sem.at[kept[i]])

        def same_send(i):
            return w.copy(piece(1 - w.k, i), target.at[span(i), left], {"k": 1 - w.k}, to_near[i])

        def cross_near(i):
            return w.copy(piece(w.k, i), target.at[span(i), right], {"x": 1 - w.x}, to_near[i])

        def cross_far(i):
            return w.copy(
                piece(1 - w.k, i), target.at[span(i), right], {"k": 1 - w.k, "x": 1 - w.x}, to_far[i]
            )

        def start():
            @pl.when(w.same)
            def _():
                for i in range(count):
                    same_send(i).start()
                    same_keep(i).start()

            @pl.when(jnp.logical_not(w.same))
            def _():
                for i in range(count):
                    cross_near(i).start()
                    cross_far(i).start()

        def arrive(i):
            @pl.when(w.same)
            def _():
                same_keep(i).wait()
                same_send(i).wait_recv()

            @pl.when(jnp.logical_not(w.same))
            def _():
                cross_near(i).wait_recv()
                cross_far(i).wait_recv()

        def close():
            @pl.when(w.same)
            def _():
                for i in range(count):
                    same_send(i).wait_send()

            @pl.when(jnp.logical_not(w.same))
            def _():
                for i in range(count):
                    cross_near(i).wait_send()
                    cross_far(i).wait_send()

        return start, arrive, close

    gain_copy = w.send(gain_own, gain_ref.at[:, pl.ds(half, half)], {"x": 1 - w.x})
    code_copies = [
        w.send(gain_own, far_gains, {"k": 1 - w.k, "h": 1 - w.h}),
        w.send(codes_own, codes.at[1], {"x": 1 - w.x}),
        w.send(codes_own, codes.at[2], {"k": 1 - w.k}),
        w.send(codes_own, codes.at[3], {"k": 1 - w.k, "x": 1 - w.x}),
    ]
    codes[0] = codes_own[...]
    start, arrive, close = spread(x_ref, xin, [(i * size, size) for i in range(PIECES)])
    start()
    qkv.start()
    forget.start()
    share = Share(w, psize, own, g, spans)
    gain_ref[:, pl.ds(0, half)] = gain_own[...]
    gain_copy.wait_recv()
    for i, span in enumerate(spans):
        arrive(i)

        def norm(rows):
            value = xin[rows, :].astype(F32)
            own[rows, :] = (value * inverse_rms(value) * gain_ref[0:1, :]).astype(BF16)

        by_chunks(span, norm)
        share.send(i)
    close()
    for fetch in (qkv, forget, out_fetch):
        fetch.store()
    for i in range(3):
        qkv.relay(i)
    out_fetch.start()
    forget.relay(0)
    for i in range(3):
        qkv.relay_over(i)
        if i < PIECES:
            share.relay(i)
    forget.relay_over(0)
    out_fetch.relay(0)
    out_fetch.relay_over(0)
    share.wait()
    for fetch in (qkv, forget, out_fetch):
        fetch.wait()
    for copy in code_copies:
        copy.wait_recv()
    w.close()


def forward_exchange_kernel(
    psize, part, xin, gain_ref, gate_shard, gate_got, up_shard, up_got, down_shard, resid, g, gate, up, down,
    near, mid, far, own, gate_stage, gate_keep, up_stage, up_keep, down_stage, send_sem, recv_sem, local_sem,
):
    w = Wires(send_sem, recv_sem, local_sem)
    gate_fetch = Fetch(w, gate_shard, gate, gate_stage, 2, gate_got, gate_keep)
    up_fetch = Fetch(w, up_shard, up, up_stage, 2, up_got, up_keep)
    down_fetch = Fetch(w, down_shard, down, down_stage, 2)
    fetches = (gate_fetch, up_fetch, down_fetch)
    for fetch in fetches:
        fetch.load()
    w.greet(partners(w, psize, away=True, over_o=2))
    spans = row_spans(own.shape[0], PIECES)
    reduce = Reduce(w, psize, part, near, mid, far, spans)
    gate_fetch.start()
    reduce.start()
    up_fetch.start()
    down_fetch.start()
    for fetch in fetches:
        fetch.store()
    for i in range(2):
        gate_fetch.relay_over(i)
    for i in range(2):
        down_fetch.relay(i)
    for i in range(2):
        up_fetch.relay_over(i)
    share = Share(w, psize, own, g, spans)
    for i in range(PIECES):

        def norm(rows, total):
            value = total + xin[rows, :].astype(F32)
            resid[rows, :] = value
            own[rows, :] = (value * inverse_rms(value) * gain_ref[1:2, :]).astype(BF16)

        reduce.each(i, norm)
        share.send(i)
    for i in range(2):
        down_fetch.relay_over(i)
    for i in range(PIECES):
        share.relay(i)
    share.wait()
    for fetch in fetches:
        fetch.wait()
    w.close()


class EarlySum:
    def __init__(self, wires, part, value, over, across, result, pieces, offset=0, got=None):
        w = self.wires = wires
        self.offset, self.got = offset, got
        self.part, self.value, self.over, self.across, self.result = part, value, over, across, result
        self.count, self.half_rows = pieces, value.shape[1]
        self.size = self.half_rows // pieces
        self.over_slots = [[w.slot() for _ in range(pieces)] for _ in range(2)]
        self.across_slots = [w.slot() for _ in range(pieces)]
        self.local_slot = w.local_used
        w.local_used += 2 + pieces

    def span(self, i):
        return pl.ds(i * self.size, self.size)

    def load_copy(self, half):
        start = pl.multiple_of(self.offset + (self.wires.o % 2) * self.half_rows, 16)
        return pltpu.make_async_copy(
            self.part.at[half, pl.ds(start, self.half_rows)],
            self.value.at[half],
            self.wires.local_sem.at[self.local_slot + half],
        )

    def load(self):
        for half in range(2):
            self.load_copy(half).start()

    def over_copy(self, half, i):
        w = self.wires
        start = pl.multiple_of(self.offset + (1 - w.o % 2) * self.half_rows + i * self.size, 16)
        return w.copy(
            self.part.at[half, pl.ds(start, self.size)],
            self.over.at[half, self.span(i)],
            {"o": w.o ^ 1},
            self.over_slots[half][i],
        )

    def across_copy(self, i):
        w = self.wires
        return w.copy(
            self.value.at[1, self.span(i)], self.across.at[self.span(i)], {"x": 1 - w.x}, self.across_slots[i]
        )

    def keep_copy(self, i):
        return pltpu.make_async_copy(
            self.value.at[0, self.span(i)],
            self.result.at[self.span(i)],
            self.wires.local_sem.at[self.local_slot + 2 + i],
        )

    def start(self, half):
        for i in range(self.count):
            self.over_copy(half, i).start()

    def pass_on(self, i):
        if i == 0:
            self.load_copy(1).wait()
        span = self.span(i)
        if self.got is None:
            self.over_copy(1, i).wait_recv()
            add_into(self.value.at[1, span], self.over.at[1, span])
        else:
            add_into(self.value.at[1, span], self.got.at[span])
        self.across_copy(i).start()

    def finish(self, i):
        if i == 0:
            self.load_copy(0).wait()
        self.over_copy(0, i).wait_recv()
        self.across_copy(i).wait_recv()
        span = self.span(i)
        add_into(self.value.at[0, span], self.over.at[0, span], self.across.at[span])
        if self.result is not None:
            self.keep_copy(i).start()

    def close(self):
        for i in range(self.count):
            for half in range(2):
                if half == 0 or self.got is None:
                    self.over_copy(half, i).wait_send()
            self.across_copy(i).wait_send()
            if self.result is not None:
                self.keep_copy(i).wait()


def backward_exchange_kernel(
    psize, grad_gate, grad_up, w_gate, w_up, resid, cot, gain_ref, down_own, down_other, gate_part, up_part,
    grad_resid, g, gain_grad, down_sum, pair_sum,
    near, mid, far, own, part, down_across, down_moved, gate_val, gate_over, gate_across, up_val, up_over, up_across,
    send_sem, recv_sem, local_sem,
):
    w = Wires(send_sem, recv_sem, local_sem)
    gate = EarlySum(w, gate_part, gate_val, gate_over, gate_across, pair_sum.at[0], 2)
    up = EarlySum(w, up_part, up_val, up_over, up_across, pair_sum.at[1], 2)
    gate.load()
    up.load()
    w.greet(partners(w, psize, away=True, over_o=2))
    spans = row_spans(own.shape[0], PIECES)
    reduce = Reduce(w, psize, part, near, mid, far, spans)
    down_copy = w.send(down_other, down_across, {"x": 1 - w.x})
    gate.start(1)
    up.start(1)
    gate.start(0)
    up.start(0)

    def multiply(block):
        def one(n, carry):
            span = pl.ds(pl.multiple_of(n * TILE, TILE), TILE)
            sums = dot_nt(grad_gate[block], w_gate[span, :]) + dot_nt(grad_up[block], w_up[span, :])
            part[block, :, span] = sums.astype(BF16)
            return carry

        lax.fori_loop(0, D // TILE, one, 0)

    reduce.start_with(multiply)
    for i in range(2):
        gate.pass_on(i)
    down_home = w.copy(down_sum, down_moved, {"h": 1 - w.h}, w.slot())
    down_copy.wait_recv()

    def add_down(rows):
        down_sum[rows, :] = (
            down_own[rows, :].astype(F32) + down_across[rows, :].astype(F32)
        ).astype(BF16)

    by_chunks(pl.ds(0, down_sum.shape[0]), add_down)

    @pl.when(jnp.logical_not(w.home))
    def _():
        down_home.start()

    share = Share(w, psize, own, g, spans)
    gain_grad[...] = jnp.zeros(gain_grad.shape, F32)

    def back(rows, total):
        grad, gain_part = norm_back(total, resid[rows, :], cot[rows, :].astype(F32), gain_ref[1:2, :])
        grad_resid[rows, :] = grad
        own[rows, :] = grad.astype(BF16)
        gain_grad[...] += gain_part

    for i in range(PIECES):
        reduce.each(i, back)
        share.send(i)
    for i in range(2):
        up.pass_on(i)
    share.relay(0)
    for i in range(2):
        gate.finish(i)
    for i in range(1, PIECES):
        share.relay(i)
    for i in range(2):
        up.finish(i)
    share.wait()
    gate.close()
    up.close()

    @pl.when(jnp.logical_not(w.home))
    def _():
        down_home.wait_send()

    @pl.when(w.home)
    def _():
        down_home.wait_recv()
        add_into(down_sum, down_moved)

    w.close()


class Spread:
    def __init__(self, wires, value, result):
        w = self.wires = wires
        self.value, self.result = value, result
        self.over_slot, self.near_slot, self.pass_slot = w.slot(), w.slot(), w.slot()
        self.local_slot = w.local_used
        w.local_used += 1

    def rows(self, mine):
        bit = self.wires.o % 2
        return self.result.at[bit if mine else 1 - bit]

    def over_copy(self):
        w = self.wires
        return w.copy(self.value, self.rows(True), {"o": w.o ^ 1}, self.over_slot)

    def near_copy(self):
        return self.wires.copy(self.value, self.rows(True), {"k": 1 - self.wires.k}, self.near_slot)

    def pass_copy(self):
        return self.wires.copy(self.rows(False), self.rows(False), {"k": 1 - self.wires.k}, self.pass_slot)

    def keep_copy(self):
        return pltpu.make_async_copy(
            self.value, self.rows(True), self.wires.local_sem.at[self.local_slot]
        )

    def start(self):
        @pl.when(self.wires.home)
        def _():
            self.over_copy().start()
            self.near_copy().start()
            self.keep_copy().start()

    def relay(self):
        @pl.when(self.wires.home)
        def _():
            self.over_copy().wait_recv()
            self.pass_copy().start()

    def wait(self):
        @pl.when(self.wires.home)
        def _():
            self.over_copy().wait_send()
            self.near_copy().wait_send()
            self.pass_copy().wait_send()
            self.keep_copy().wait()

        @pl.when(jnp.logical_not(self.wires.home))
        def _():
            self.near_copy().wait_recv()
            self.pass_copy().wait_recv()


class SmallSum:
    def __init__(self, wires, psize, osize, value, other, buffers):
        w = self.wires = wires
        self.value, self.other, self.buffers = value, other, buffers
        self.devices = [{"x": 1 - w.x}, {"k": 1 - w.k}]
        self.devices += [{"p": w.p ^ bit} for bit in bits_of(psize)]
        self.devices += [{"h": 1 - w.h}]
        self.devices += [{"o": w.o ^ bit} for bit in bits_of(osize)]
        self.slots = [w.slot() for _ in self.devices]

    def copy(self, step):
        source = self.other if step == 0 else self.value
        return self.wires.copy(source, self.buffers.at[step], self.devices[step], self.slots[step])

    def start(self):
        self.copy(0).start()

    def step(self, step):
        self.copy(step).wait()
        self.value[...] = self.value[...] + self.buffers[step]
        if step + 1 < len(self.devices):
            self.copy(step + 1).start()


class Chain:
    def __init__(self, wires, osize, value, stages, buffers, result, pieces):
        self.wires, self.value, self.stages, self.result = wires, value, stages, result
        self.buffers = buffers
        self.spans = row_spans(value.shape[0], pieces)
        self.slots = [[wires.slot() for _ in self.spans] for _ in stages]
        self.kept = [wires.local_used + i for i in range(pieces)]
        wires.local_used += pieces
        self.other = None

    def copy(self, stage, i):
        w, span = self.wires, self.spans[i]
        kind, slot = self.stages[stage], self.slots[stage][i]
        if kind == "x":
            return w.copy(self.other.at[span], self.buffers[stage].at[span], {"x": 1 - w.x}, slot)
        if kind == "h":
            return w.copy(self.value.at[span], self.buffers[stage].at[span], {"h": 1 - w.h}, slot)
        if kind == "k":
            return w.copy(self.value.at[span], self.result.at[span], {"k": 1 - w.k}, slot)
        return w.copy(self.value.at[span], self.buffers[stage].at[span], {"o": w.o ^ kind}, slot)

    def keep(self, i):
        span = self.spans[i]
        return pltpu.make_async_copy(
            self.value.at[span], self.result.at[span], self.wires.local_sem.at[self.kept[i]]
        )

    def start(self, stage, i):
        w, kind = self.wires, self.stages[stage]
        if kind == "x":
            self.copy(stage, i).start()
        elif kind == "h":
            @pl.when(jnp.logical_not(w.home))
            def _():
                self.copy(stage, i).start()
        else:
            @pl.when(w.home)
            def _():
                self.copy(stage, i).start()
                if kind == "k":
                    self.keep(i).start()

    def add(self, stage, i):
        span = self.spans[i]
        add_into(self.value.at[span], self.buffers[stage].at[span])

    def end(self, stage, i):
        w, kind = self.wires, self.stages[stage]
        if kind == "x":
            self.copy(stage, i).wait_recv()
            self.add(stage, i)
        elif kind == "h":
            @pl.when(w.home)
            def _():
                self.copy(stage, i).wait_recv()
                self.add(stage, i)
        elif kind == "k":
            @pl.when(w.home)
            def _():
                self.copy(stage, i).wait_send()
                self.keep(i).wait()

            @pl.when(jnp.logical_not(w.home))
            def _():
                self.copy(stage, i).wait_recv()
        else:
            @pl.when(w.home)
            def _():
                self.copy(stage, i).wait()
                self.add(stage, i)

    def close(self):
        w = self.wires
        for stage, kind in enumerate(self.stages):
            for i in range(len(self.spans)):
                if kind == "x":
                    self.copy(stage, i).wait_send()
                elif kind == "h":
                    @pl.when(jnp.logical_not(w.home))
                    def _():
                        self.copy(stage, i).wait_send()

    def step(self, stage, i):
        self.end(stage, i)
        if stage + 1 < len(self.stages):
            self.start(stage + 1, i)

    def order(self, first=0):
        return [(stage, i) for stage in range(first, len(self.stages)) for i in range(len(self.spans))]

    def run(self, first=0):
        for stage, i in self.order(first):
            self.step(stage, i)


def leave_kernel(
    psize, osize, pieces, grad_in, weight_in, stream, base, gain_ref, small_in, proj_in, out_own, out_other,
    pair_in, down_in, block, small, first_sum, second_sum, out_sum, up_sum, gate_sum, down_sum,
    near, mid, far, part, kept, first_val, second_val, out_val, up_val, gate_val, down_val, first_bufs,
    second_over, second_across, second_bufs, out_bufs, small_other, small_bufs, gain_acc,
    send_sem, recv_sem, local_sem,
):
    w = Wires(send_sem, recv_sem, local_sem)
    split = first_val.shape[0]
    second = EarlySum(w, proj_in, second_val, second_over, second_across, None, 2, split)
    second.load()
    loads = [
        w.local(source, target)
        for source, target in (
            (pair_in.at[1], up_val), (pair_in.at[0], gate_val), (down_in, down_val), (out_own, out_val),
            (proj_in.at[0, pl.ds(0, split)], first_val),
        )
    ]
    w.greet(partners(w, psize, away=True, over_o=osize))
    rows, half = kept.shape[1], kept.shape[2]
    spans = row_spans(rows, PIECES)
    size = rows // PIECES
    bits = bits_of(osize)

    first = Chain(
        w, osize, first_val, ["x", "h"] + bits + ["k"], [first_bufs.at[i] for i in range(2 + len(bits))],
        first_sum, pieces,
    )
    first.other = proj_in.at[1, pl.ds(0, split)]
    late = Chain(
        w, osize, second_val.at[0], ["h"] + bits[1:], [second_bufs.at[i] for i in range(len(bits))], None, 2
    )
    out = Chain(w, osize, out_val, ["x", "h"] + bits[1:], [out_bufs.at[i] for i in range(1 + len(bits))], None, 1)
    out.other = out_other
    spreads = [Spread(w, up_val, up_sum), Spread(w, gate_val, gate_sum), Spread(w, down_val, down_sum)]
    last_spreads = [Spread(w, out_val, out_sum), Spread(w, second_val.at[0], second_sum)]
    reduce = Reduce(w, psize, part, near, mid, far, spans)
    second.start(1)
    for i in range(pieces):
        first.start(0, i)
    out.start(0, 0)
    second.start(0)
    for load in loads:
        load.wait()
    for spread in spreads:
        spread.start()
    columns = D // TILE

    def multiply(block):
        def one(n, carry):
            span = pl.ds(pl.multiple_of(n * TILE, TILE), TILE)
            part[block, :, span] = dot_nt(grad_in[block], weight_in[span, :]).astype(BF16)
            return carry

        lax.fori_loop(0, columns, one, 0)

    reduce.start_with(multiply)

    near_slots = [w.slot() for _ in spans]
    far_slots = [w.slot() for _ in spans]
    keep_slots = [w.local_used + i for i in range(PIECES)]
    w.local_used += PIECES

    def target(i):
        return block.at[pl.ds(pl.multiple_of(w.k * rows + i * size, 8), size)]

    def same_keep(i):
        return pltpu.make_async_copy(kept.at[0, spans[i]], target(i), local_sem.at[keep_slots[i]])

    def same_send(i):
        return w.copy(kept.at[1, spans[i]], target(i), {"x": 1 - w.x}, near_slots[i])

    def cross_near(i):
        return w.copy(kept.at[0, spans[i]], target(i), {"k": 1 - w.k}, near_slots[i])

    def cross_far(i):
        return w.copy(kept.at[1, spans[i]], target(i), {"k": 1 - w.k, "x": 1 - w.x}, far_slots[i])

    for i in range(2):
        second.pass_on(i)
    first.step(0, 0)
    for i in range(1, pieces):
        first.step(0, i)
        first.step(1, i - 1)
    out.step(0, 0)
    second.finish(0)
    late.start(0, 0)
    first.step(1, pieces - 1)
    gain_acc[...] = jnp.zeros(gain_acc.shape, F32)

    def back(rows_, total):
        grad, gain_part = norm_back(total, stream[rows_, :].astype(F32), base[rows_, :], gain_ref[0:1, :])
        gain_acc[...] += gain_part
        kept[0, rows_, :] = grad[:, :half].astype(BF16)
        kept[1, rows_, :] = grad[:, half:].astype(BF16)

    for i in range(PIECES):
        reduce.each(i, back)

        @pl.when(w.same)
        def _():
            same_send(i).start()
            same_keep(i).start()

        @pl.when(jnp.logical_not(w.same))
        def _():
            cross_near(i).start()
            cross_far(i).start()

        if i == 0:
            second.finish(1)
            late.start(0, 1)

    gain_sum = jnp.sum(gain_acc[...], axis=0, keepdims=True)
    row = lax.broadcasted_iota(jnp.int32, (8, half), 0)
    small[...] = jnp.where(row == 0, gain_sum[:, :half], small_in[:, :half])
    small_other[...] = jnp.where(row == 0, gain_sum[:, half:], small_in[:, half:])
    total = SmallSum(w, psize, osize, small, small_other, small_bufs)
    total.start()
    out.run(1)
    last_spreads[0].start()
    steps = [lambda a=a: late.step(*a) for a in late.order(0)] + [last_spreads[1].start]
    steps += [spread.relay for spread in spreads] + [lambda a=a: first.step(*a) for a in first.order(2)]
    steps += [last_spreads[0].relay, last_spreads[1].relay]
    smalls = list(range(len(total.devices)))
    for n, step in enumerate(steps):
        step()
        if n % 2 == 0 and smalls:
            total.step(smalls.pop(0))
    for step in smalls:
        total.step(step)
    for spread in spreads + last_spreads:
        spread.wait()
    for i in range(PIECES):
        @pl.when(w.same)
        def _():
            same_keep(i).wait()
            same_send(i).wait_send()
            cross_near(i).wait_recv()

        @pl.when(jnp.logical_not(w.same))
        def _():
            cross_near(i).wait_send()
            cross_far(i).wait()
            same_send(i).wait_recv()

    for chain in (first, second, late, out):
        chain.close()
    w.close()


ANY = pl.BlockSpec(memory_space=pl.ANY)
VMEM = pl.BlockSpec(memory_space=pltpu.VMEM)
SLOTS = 128


def exchange_call(kernel, name, collective_id, outs, out_specs, in_specs, scratch, args):
    return pl.pallas_call(
        kernel,
        out_shape=outs,
        in_specs=in_specs,
        out_specs=out_specs,
        scratch_shapes=scratch
        + [
            pltpu.SemaphoreType.DMA((SLOTS,)),
            pltpu.SemaphoreType.DMA((SLOTS,)),
            pltpu.SemaphoreType.DMA((SLOTS // 2,)),
        ],
        compiler_params=pltpu.CompilerParams(
            collective_id=collective_id, has_side_effects=True, vmem_limit_bytes=56 << 20
        ),
        name=name,
    )(*args)


def sds(shape, dtype):
    return jax.ShapeDtypeStruct(shape, dtype)


def sum_scratch(psize, rows):
    far = max(psize - 1, 1)
    return [
        pltpu.VMEM((psize, rows, D), BF16),
        pltpu.VMEM((far, rows, D), BF16),
        pltpu.VMEM((far, rows, D), BF16),
    ]


def enter(psize, layer_input, gains, codes, qkv_weight, forget_weight, out_weight):
    rows = layer_input.shape[0] // 2
    half, width = qkv_weight.shape
    columns = width + forget_weight.shape[1]
    return exchange_call(
        functools.partial(enter_kernel, psize),
        "enter",
        1,
        (
            sds((rows, D), BF16),
            sds((2 * psize, rows, D), BF16),
            sds((2, half, columns), BF16),
            sds((out_weight.shape[0], 2 * half), BF16),
            sds((8, D), F32),
            sds((4,) + codes.shape, jnp.int32),
            sds(gains.shape, F32),
        ),
        (VMEM, ANY, ANY, ANY, VMEM, VMEM, VMEM),
        [ANY, VMEM, VMEM, ANY, ANY, ANY],
        [pltpu.VMEM((rows, D), BF16)]
        + [pltpu.VMEM(value.shape, BF16) for value in (qkv_weight, forget_weight, out_weight)],
        (layer_input, gains, codes, qkv_weight, forget_weight, out_weight),
    )


def forward_exchange(psize, part, xin, gains, gate_weight, gate_got, up_weight, up_got, down_weight):
    rows = xin.shape[0]
    return exchange_call(
        functools.partial(forward_exchange_kernel, psize),
        "forward_exchange",
        2,
        (
            sds((rows, D), F32),
            sds((2 * psize, rows, D), BF16),
            sds((2,) + gate_weight.shape, BF16),
            sds((2,) + up_weight.shape, BF16),
            sds((down_weight.shape[0], D), BF16),
        ),
        (VMEM, ANY, ANY, ANY, ANY),
        [VMEM, VMEM, VMEM, ANY, ANY, ANY, ANY, ANY],
        sum_scratch(psize, rows)
        + [pltpu.VMEM((rows, D), BF16)]
        + [
            pltpu.VMEM(value.shape, BF16)
            for value in (gate_weight, gate_got, up_weight, up_got, down_weight)
        ],
        (part, xin, gains, gate_weight, gate_got, up_weight, up_got, down_weight),
    )


def backward_exchange(
    psize, grad_gate, grad_up, w_gate, w_up, resid, cot, gains, down_own, down_other, gate_part, up_part
):
    rows = resid.shape[0]

    def early(value):
        half_rows = value.shape[1] // 2
        shape = (half_rows, value.shape[2])
        return [
            pltpu.VMEM((2,) + shape, BF16),
            pltpu.VMEM((2,) + shape, BF16),
            pltpu.VMEM(shape, BF16),
        ]

    return exchange_call(
        functools.partial(backward_exchange_kernel, psize),
        "backward_exchange",
        3,
        (
            sds((rows, D), F32),
            sds((2 * psize, rows, D), BF16),
            sds((8, D), F32),
            sds(down_own.shape, BF16),
            sds((2, gate_part.shape[1] // 2, gate_part.shape[2]), BF16),
        ),
        (VMEM, ANY, VMEM, VMEM, ANY),
        [VMEM] * 8 + [ANY, ANY, ANY],
        sum_scratch(psize, rows)
        + [pltpu.VMEM((rows, D), BF16), pltpu.VMEM((2 * psize, rows, D), BF16)]
        + [pltpu.VMEM(down_own.shape, BF16)] * 2
        + early(gate_part)
        + early(up_part),
        (grad_gate, grad_up, w_gate, w_up, resid, cot, gains, down_own, down_other, gate_part, up_part),
    )


def leave(psize, osize, grad, weight, stream, base, gains, small, proj, out_own, out_other, pair, down):
    rows = stream.shape[0]
    bits = len(bits_of(osize))
    half = D // 2
    columns = proj.shape[2]
    split = proj.shape[1] // 2

    def scratch(*shape):
        return pltpu.VMEM(shape, BF16)

    def both(shape):
        return sds((2,) + shape, BF16)

    return exchange_call(
        functools.partial(leave_kernel, psize, osize, 3),
        "leave",
        4,
        (
            sds((2 * rows, half), BF16),
            sds((8, half), F32),
            sds((split, columns), BF16),
            both((split // 2, columns)),
            both(out_own.shape),
            both(pair.shape[1:]),
            both(pair.shape[1:]),
            both(down.shape),
        ),
        (ANY, VMEM, ANY, ANY, ANY, ANY, ANY, ANY),
        [VMEM] * 6 + [ANY] * 5,
        sum_scratch(psize, rows)
        + [
            scratch(2 * psize, rows, D),
            scratch(2, rows, half),
            scratch(split, columns),
            scratch(2, split // 2, columns),
            scratch(*out_own.shape),
            scratch(*pair.shape[1:]),
            scratch(*pair.shape[1:]),
            scratch(*down.shape),
            scratch(2 + bits, split, columns),
            scratch(2, split // 2, columns),
            scratch(split // 2, columns),
            scratch(bits, split // 2, columns),
            scratch(1 + bits, *out_own.shape),
            pltpu.VMEM((8, half), F32),
            pltpu.VMEM((3 + len(bits_of(psize)) + bits, 8, half), F32),
            pltpu.VMEM((8, D), F32),
        ],
        (grad, weight, stream, base, gains, small, proj, out_own, out_other, pair, down),
    )


def make_shards(osize, psize):
    count = 2 * psize
    obits = bits_of(osize)

    def shards(
        layer_input,
        attn_gain,
        qkv_weight,
        forget_weight,
        forget_bias,
        out_weight,
        ffn_gain,
        gate_weight,
        up_weight,
        down_weight,
        prompt_doc,
        branch_seg,
        branch_doc,
        out_cotangent,
    ):
        core, xpos = lax.axis_index("k"), lax.axis_index("x")
        hpos, ppos, opos = lax.axis_index("h"), lax.axis_index("p"), lax.axis_index("o")
        home = core == hpos
        same = core == xpos
        heads = forget_weight.shape[1]
        width = heads * 3 * DH
        lane_pad = LANES - heads
        feat = D // 2

        def far_blocks(block):
            return [xor_swap(block, "p", psize, bit) for bit in range(1, psize)]

        def all_blocks(block, far):
            blocks = []
            for near in [block] + far:
                blocks += [near, swap(near, "k")]
            return jnp.concatenate(blocks, axis=0)

        def near_sums(partial):
            size = partial.shape[0] // count
            parts = [partial[i * size : (i + 1) * size] for i in range(count)]
            moved = [swap(parts[i + 1], "k") for i in range(0, count, 2)]
            return [add_parts(parts[i], moved[i // 2]) for i in range(0, count, 2)]

        def far_sums(sums):
            return [xor_swap(sums[bit], "p", psize, bit) for bit in range(1, psize)]

        def total_of(near, far):
            total = near.astype(F32)
            for value in far:
                total = total + value.astype(F32)
            return total

        prompt_len, branch_len = prompt_doc.shape[1], branch_seg.shape[1]
        packed = jnp.concatenate([prompt_doc[0], branch_seg[0], branch_doc[0]])
        code_rows = -(-packed.shape[0] // (8 * LANES)) * 8
        packed = jnp.pad(packed, (0, code_rows * LANES - packed.shape[0])).reshape(code_rows, LANES)
        bias_row = jnp.pad(forget_bias, (0, feat - heads))
        own_gains = jnp.concatenate(
            [jnp.stack([attn_gain, ffn_gain, bias_row]), jnp.zeros((5, feat), F32)]
        )
        forget_wide = jnp.concatenate(
            [forget_weight, jnp.zeros((forget_weight.shape[0], lane_pad), BF16)], axis=1
        )
        first_part, second_part = qkv_weight, forget_wide
        if width % LANES:
            spare = jnp.zeros((qkv_weight.shape[0], LANES - width % LANES), BF16)
            first_part = jnp.concatenate([qkv_weight, forget_wide, spare], axis=1)
        xin, normed_a_all, w_proj, w_out, gains8, codes, far_gains = enter(
            psize, layer_input, own_gains, packed, first_part, second_part, out_weight
        )
        bias = jnp.where(home, own_gains[2, :LANES], far_gains[2, :LANES])
        packed = lax.dynamic_index_in_dim(
            codes, (core ^ xpos) * 2 + (xpos ^ hpos), 0, keepdims=False
        ).reshape(-1)
        prompt_ids = packed[:prompt_len]
        branch_ids = packed[prompt_len : prompt_len + branch_len]
        branch_docs = packed[prompt_len + branch_len : prompt_len + branch_len + branch_doc.shape[1]]
        kcol, qrow, flags = group_codes(prompt_ids, branch_ids, branch_docs)
        normed_a_all = normed_a_all.reshape(-1, D)
        w_proj = w_proj.reshape(D, -1)[:, : width + LANES]

        projected = matmul(normed_a_all, w_proj).reshape(count, -1, width + LANES)
        cot_near, cot_far = take_half(out_cotangent, core), take_half(out_cotangent, 1 - core)
        projected, kcol, qrow, flags, gate_half, up_half, cot_first, cot_near, cot_far = lax.optimization_barrier(
            (
                projected,
                kcol,
                qrow,
                flags,
                take_half(gate_weight, opos % 2),
                take_half(up_weight, opos % 2),
                jnp.where(same, cot_far, cot_near),
                cot_near,
                cot_far,
            )
        )
        gate_got, up_got = fetch_home_away(gate_half), fetch_home_away(up_half)
        cot_first = lax.ppermute(cot_first, ("k", "x"), SPREAD_A)
        cot_second = lax.ppermute(cot_far, ("k", "x"), SPREAD_B)
        attended, *saved = attention_forward(
            projected, bias[None], kcol, qrow, flags, heads, prompt_len
        )
        attended, gate_got, up_got, cot_first, cot_second, *saved = lax.optimization_barrier(
            (attended, gate_got, up_got, cot_first, cot_second, *saved)
        )
        attended = attended.reshape(-1, heads * DH)
        cot = jnp.concatenate(
            [jnp.where(same, cot_near, cot_first), jnp.where(same, cot_first, cot_second)], axis=1
        )
        part = matmul(attended, w_out).astype(BF16).reshape(count, -1, D)
        resid, normed_b_all, w_gate, w_up, w_down = forward_exchange(
            psize, part, xin, gains8, gate_weight, gate_got, up_weight, up_got, down_weight
        )
        normed_b_all = normed_b_all.reshape(-1, D)
        w_gate, w_up = w_gate.reshape(D, -1), w_up.reshape(D, -1)
        cot_others = far_blocks(tie(cot, normed_b_all))
        gate_pre = matmul(normed_b_all, w_gate)
        up_pre = matmul(normed_b_all, w_up)
        gate_sig = jax.nn.sigmoid(gate_pre)
        gate_act = gate_pre * gate_sig
        hidden = (gate_act * up_pre).astype(BF16)
        out_part = matmul(hidden, w_down).astype(BF16)
        out_part, *cot_others = lax.optimization_barrier((out_part, *cot_others))
        cot_all = all_blocks(cot, cot_others)

        def finish(total, axis_bits):
            for bit in axis_bits:
                total = add_parts(total, home_swap(total, osize, bit))
            return total

        high = opos % 2 == 1
        down_part = contract_rows(hidden, cot_all).astype(BF16)
        down_keep, down_give = split_rows(down_part, high)
        down_moved = xor_swap(down_give, "o", osize, 1)
        out_sums = near_sums(out_part)
        out_far = far_sums(out_sums)
        grad_hidden = contract_cols(tie(cot_all, out_sums[0]), w_down)
        grad_gate = (grad_hidden * up_pre * gate_sig * (1.0 + gate_pre * (1.0 - gate_sig))).astype(BF16)
        grad_up = (grad_hidden * gate_act).astype(BF16)
        gate_part = contract_rows(normed_b_all, grad_gate).astype(BF16).reshape(2, feat, -1)
        up_part = contract_rows(normed_b_all, grad_up).astype(BF16).reshape(2, feat, -1)
        up_part, gate_part, down_moved, *out_far = lax.optimization_barrier(
            (up_part, gate_part, down_moved, *out_far)
        )
        layer_output = (resid + total_of(out_sums[0], out_far)).astype(BF16)
        down_total = add_parts(down_keep, down_moved)
        grad_resid, grad_branch_all, ffn_gain_part, down_total, pair_total = backward_exchange(
            psize,
            grad_gate.reshape(count, -1, grad_gate.shape[1]),
            grad_up.reshape(count, -1, grad_up.shape[1]),
            w_gate,
            w_up,
            resid,
            cot,
            gains8,
            down_total[:, :feat],
            down_total[:, feat:],
            gate_part,
            up_part,
        )
        grad_branch_all = grad_branch_all.reshape(-1, D)
        grad_attended = contract_cols(grad_branch_all, w_out).astype(BF16)
        out_part = contract_rows(attended, grad_branch_all).astype(BF16)
        out_keep, out_give = split_rows(out_part, high)
        grad_attended, out_keep, out_give, down_total, pair_total, *block_parts = lax.optimization_barrier(
            (grad_attended, out_keep, out_give, down_total, pair_total) + unspread_parts(layer_output, same)
        )
        own_part, near_part, far_part = block_parts
        pair_moved = to_home(pair_total)
        out_moved = xor_swap(out_give, "o", osize, 1)
        near_moved, far_moved = unspread_moves(near_part, far_part)
        grad_proj, bias_sums = attention_backward(
            grad_attended.reshape(count, -1, heads * DH), saved, kcol, qrow, flags, heads, prompt_len
        )
        grad_proj, bias_sums, out_moved, near_moved, far_moved, pair_moved = lax.optimization_barrier(
            (grad_proj, bias_sums, out_moved, near_moved, far_moved, pair_moved)
        )
        layer_output = unspread_join(own_part, near_moved, far_moved, core, same)
        grad_proj = grad_proj.reshape(-1, width + LANES)
        proj_part = contract_rows(normed_a_all, grad_proj).astype(BF16)
        down_total = finish(down_total, obits[1:])
        pair_total = finish(add_parts(pair_total, pair_moved), obits[1:])
        out_total = add_parts(out_keep, out_moved)

        slots = jnp.where(
            (jnp.arange(2 * psize) == core * psize + ppos)[:, None], bias_sums[:1, :heads], 0.0
        ).reshape(-1)
        slots = jnp.concatenate([slots, jnp.zeros((feat - slots.shape[0],), F32)])
        small = jnp.stack([jnp.zeros((D,), F32), jnp.sum(ffn_gain_part, axis=0), jnp.concatenate([slots, slots])])
        small = jnp.concatenate([small, jnp.zeros((5, D), F32)])
        input_grad, small, first_rows, second_rows, out_both, up_both, gate_both, down_both = leave(
            psize,
            osize,
            grad_proj.reshape(count, -1, width + LANES),
            w_proj,
            xin,
            grad_resid,
            gains8,
            small,
            proj_part.reshape(2, feat, -1),
            out_total[:, :feat],
            out_total[:, feat:],
            pair_total,
            down_total,
        )
        proj_grad = jnp.concatenate([first_rows, second_rows.reshape(first_rows.shape)], axis=0)
        qkv_grad = proj_grad[:, :width].astype(F32)
        forget_grad = proj_grad[:, width : width + heads].astype(F32)
        bias_all = small[2, : 2 * psize * heads].reshape(2 * psize, heads)
        forget_bias_grad = lax.dynamic_index_in_dim(bias_all, hpos * psize + ppos, 0, keepdims=False)

        def whole(halves):
            return halves.reshape(-1, halves.shape[2]).astype(F32)

        return (
            layer_output,
            input_grad,
            small[0],
            qkv_grad,
            forget_grad,
            forget_bias_grad,
            whole(out_both),
            small[1],
            whole(gate_both),
            whole(up_both),
            whole(down_both),
        )

    return shards


def solution(mesh):
    dp, row, col = mesh.shape["dp"], mesh.shape["row"], mesh.shape["col"]
    osize, psize = dp // 2, col // 2
    assert row == 2
    split = Mesh(mesh.devices.reshape(osize, 2, row, 2, psize), ("o", "k", "x", "h", "p"))
    tokens = P(("o", "k", "h", "p"), "x")
    rows_first = P("x", ("h", "p"))
    cols_first = P(("h", "p"), "x")
    groups = P(("o", "k", "x"), None)
    in_specs = (
        tokens,
        P("x"),
        rows_first,
        rows_first,
        P(("h", "p")),
        cols_first,
        P("x"),
        rows_first,
        rows_first,
        cols_first,
        groups,
        groups,
        groups,
        tokens,
    )
    out_specs = (
        tokens,
        tokens,
        P("x"),
        rows_first,
        rows_first,
        P(("h", "p")),
        cols_first,
        P("x"),
        rows_first,
        rows_first,
        cols_first,
    )
    return jax.shard_map(
        make_shards(osize, psize), mesh=split, in_specs=in_specs, out_specs=out_specs, check_vma=False
    )
```

```python
import functools

import jax
import jax.numpy as jnp
from jax import lax
from jax.experimental import pallas as pl
from jax.experimental.pallas import tpu as pltpu
from jax.sharding import Mesh, PartitionSpec as P

D = 1536
DH = 64
DOCS = 4
TILE = 256
EPS = 1e-06
MASKED = -1e30
LANES = 128
BF16 = jnp.bfloat16
F32 = jnp.float32


def swap(value, axis):
    return lax.ppermute(value, axis, [(0, 1), (1, 0)])


def xor_swap(value, axis, size, bit):
    return lax.ppermute(value, axis, [(i, i ^ bit) for i in range(size)])


def kxh(k, x, h):
    return (k * 2 + x) * 2 + h


def fetch_home_away(value):
    pairs = []
    for k in range(2):
        for x in range(2):
            for h in range(2):
                target = (k, 1 - x, h) if k == h else (1 - k, x, 1 - h)
                pairs.append((kxh(k, x, h), kxh(*target)))
    return lax.ppermute(value, ("k", "x", "h"), pairs)


def fetch_away(value):
    pairs = [
        (kxh(k, x, 1 - k), kxh(k, 1 - x, 1 - k)) for k in range(2) for x in range(2)
    ]
    return lax.ppermute(value, ("k", "x", "h"), pairs)


def tie(value, *others):
    return lax.optimization_barrier((value,) + others)[0]


def join_weight(shard, first, second, home, axis):
    mine = jnp.where(home, shard, first)
    other = jnp.where(home, first, second)
    return jnp.concatenate([mine, other], axis=axis)


def add_parts(kept, moved):
    return (kept.astype(F32) + moved.astype(F32)).astype(BF16)


def to_home(value):
    return lax.ppermute(value, ("k", "h"), [(1, 0), (2, 3)])


def from_home(value):
    return lax.ppermute(value, ("k", "h"), [(0, 2), (3, 1)])


def home_swap(value, size, bit):
    pairs = []
    for o in range(size):
        for k in range(2):
            pairs.append(((o * 2 + k) * 2 + k, ((o ^ bit) * 2 + k) * 2 + k))
    return lax.ppermute(value, ("o", "k", "h"), pairs)


def bits_of(size):
    return [1 << i for i in range(size.bit_length() - 1)]


def split_rows(value, high):
    half = value.shape[0] // 2
    low_rows, high_rows = value[:half], value[half:]
    return jnp.where(high, high_rows, low_rows), jnp.where(high, low_rows, high_rows)


def merge_rows(kept, moved, high):
    return jnp.concatenate([jnp.where(high, moved, kept), jnp.where(high, kept, moved)], axis=0)


def take_half(value, index):
    half = value.shape[0] // 2
    return lax.dynamic_slice_in_dim(value, index * half, half, 0)


def kx(k, x):
    return k * 2 + x


SPREAD_A = []
SPREAD_B = []
for _k in range(2):
    for _x in range(2):
        if _k == _x:
            SPREAD_A.append((kx(_k, _x), kx(1 - _k, _x)))
        else:
            SPREAD_A.append((kx(_k, _x), kx(_k, 1 - _x)))
            SPREAD_B.append((kx(_k, _x), kx(1 - _k, 1 - _x)))


def spread_tokens(block, core, same):
    near = take_half(block, core)
    far = take_half(block, 1 - core)
    first = lax.ppermute(jnp.where(same, far, near), ("k", "x"), SPREAD_A)
    second = lax.ppermute(far, ("k", "x"), SPREAD_B)
    own = jnp.where(same, near, first)
    other = jnp.where(same, first, second)
    return jnp.concatenate([own, other], axis=1)


def unspread_parts(rows, same):
    half = rows.shape[1] // 2
    own, other = rows[:, :half], rows[:, half:]
    return own, jnp.where(same, other, own), other


def unspread_moves(near, far):
    first = lax.ppermute(near, ("k", "x"), [(b, a) for a, b in SPREAD_A])
    second = lax.ppermute(far, ("k", "x"), [(b, a) for a, b in SPREAD_B])
    return first, second


def unspread_join(own, first, second, core, same):
    near = jnp.where(same, own, first)
    far = jnp.where(same, first, second)
    low = jnp.where(core == 0, near, far)
    high = jnp.where(core == 0, far, near)
    return jnp.concatenate([low, high], axis=0)


def contract_rows(left, right):
    return lax.dot_general(
        left, right, (((0,), (0,)), ((), ())), preferred_element_type=F32
    )


def contract_cols(left, right):
    return lax.dot_general(
        left, right, (((1,), (1,)), ((), ())), preferred_element_type=F32
    )


def matmul(left, right):
    return jnp.dot(left, right, preferred_element_type=F32)


def dot_nn(left, right):
    return lax.dot_general(left, right, (((1,), (0,)), ((), ())), preferred_element_type=F32)


def dot_nt(left, right):
    return lax.dot_general(left, right, (((1,), (1,)), ((), ())), preferred_element_type=F32)


def tile_mask(qrow, kcol, rows, cols, i, j):
    key_pos = j * TILE + lax.broadcasted_iota(jnp.int32, (TILE, TILE), 0)
    query_pos = i * TILE + lax.broadcasted_iota(jnp.int32, (TILE, TILE), 1)
    code = kcol[pl.ds(pl.multiple_of(j * TILE, TILE), TILE), 0:1]
    first = qrow[0:1, pl.ds(pl.multiple_of(i * TILE, TILE), TILE)]
    second = qrow[1:2, pl.ds(pl.multiple_of(i * TILE, TILE), TILE)]
    seen = (key_pos <= query_pos) & ((code == first) | (code == second))
    return jnp.where(seen, 0.0, MASKED)


def split_parts(value):
    high = value.astype(BF16)
    rest = value - high.astype(F32)
    mid = rest.astype(BF16)
    low = (rest - mid.astype(F32)).astype(BF16)
    return high, mid, low


def lane(shape):
    return lax.broadcasted_iota(jnp.int32, shape, 1)


def forward_kernel(
    heads, count, prompt_len, flags, proj_hbm, bias_ref, kcol, qrow, att_hbm, ot_hbm, lse_ref,
    qp_hbm, kp_hbm, vp_hbm, logit, qkv, qp, kp, vp, vt, rates, sums_ref, attended, ot, mask,
    in_sem, out_sem, keep_sem, *per_head,
):
    me = lax.axis_index("p") * 2 + lax.axis_index("k")
    total = qkv.shape[0]
    size = total // count
    tiles = total // TILE
    loads = []
    for b in range(count):
        rows = pl.ds(b * size, size)
        loads.append(pltpu.make_async_copy(proj_hbm.at[b ^ me], qkv.at[rows], in_sem.at[b]))
    for load in loads:
        load.start()
    for load in loads:
        load.wait()
    logit[...] = qkv[:, 3 * DH * heads :] + bias_ref[...]
    value = logit[...]
    rate = jnp.minimum(value, 0.0) - jnp.log1p(jnp.exp(-jnp.abs(value)))
    rate = jnp.where(lane(rate.shape) < heads, rate, 0.0)
    high, mid, low = split_parts(rate)
    packed = high.astype(F32) + pltpu.roll(mid.astype(F32), 8, 1) + pltpu.roll(low.astype(F32), 16, 1)
    rates[...] = packed.astype(BF16)
    place_row = lax.broadcasted_iota(jnp.int32, (LANES, LANES), 0)
    place_col = lax.broadcasted_iota(jnp.int32, (LANES, LANES), 1)

    prompt_tiles = prompt_len // TILE
    wide = (TILE, TILE)
    row_pos, col_pos = lax.broadcasted_iota(jnp.int32, wide, 0), lax.broadcasted_iota(jnp.int32, wide, 1)
    below = jnp.where(col_pos <= row_pos, 1.0, 0.0).astype(BF16)

    def prompt_sums(t, before):
        rows = pl.ds(pl.multiple_of(t * TILE, TILE), TILE)
        prefix = dot_nn(below, rates[rows, :]) + before
        sums_ref[rows, :] = prefix
        return prefix[TILE - 1 : TILE, :]

    lax.fori_loop(0, prompt_tiles, prompt_sums, jnp.zeros((1, LANES), F32))
    doc_index = lax.broadcasted_iota(jnp.int32, (8, prompt_len), 0)
    within = jnp.where(qrow[3:4, 0:prompt_len] <= doc_index, 1.0, 0.0).astype(BF16)
    doc_sums = dot_nn(within, rates[0:prompt_len, :])

    def branch_sums(t, carry):
        rows = pl.ds(pl.multiple_of(t * TILE, TILE), TILE)
        limit = kcol[rows, 2:3]
        start = jnp.zeros((TILE, LANES), F32)
        for doc in range(DOCS):
            start = jnp.where(limit == doc, doc_sums[doc : doc + 1, :], start)

        def add_own(u, acc):
            others = pl.ds(pl.multiple_of(u * TILE, TILE), TILE)
            own = (u * TILE + col_pos <= t * TILE + row_pos) & (kcol[rows, 1:2] == qrow[2:3, others])
            return acc + dot_nn(jnp.where(own, 1.0, 0.0).astype(BF16), rates[others, :])

        sums_ref[rows, :] = lax.fori_loop(prompt_tiles, t + 1, add_own, start)
        return carry

    lax.fori_loop(prompt_tiles, tiles, branch_sums, 0)

    def prepare(t, carry):
        rows = pl.ds(pl.multiple_of(t * TILE, TILE), TILE)
        sums = sums_ref[rows, :]
        decay = sums + pltpu.roll(sums, LANES - 8, 1) + pltpu.roll(sums, LANES - 16, 1)
        decay = jnp.where(lane(decay.shape) < heads, -decay, 0.0)
        high, mid, low = split_parts(decay)
        parts = (
            high.astype(F32) + pltpu.roll(mid.astype(F32), 8, 1) + pltpu.roll(low.astype(F32), 16, 1)
        ).astype(BF16)
        lanes = lane((TILE, LANES))
        for h in range(heads):
            base = 3 * DH * h
            query = qkv[rows, base : base + DH].astype(BF16).astype(F32) * DH ** (-0.5)
            key = qkv[rows, base + DH : base + 2 * DH]
            worth = qkv[rows, base + 2 * DH : base + 3 * DH].astype(BF16)
            ones = jnp.where((lanes >= DH) & (lanes < DH + 3), 1.0, 0.0)[:, :DH]
            ones = jnp.where(lane((TILE, DH)) < 3, 1.0, 0.0)
            qp[h, rows, :] = jnp.concatenate([query, ones], axis=1).astype(BF16)
            spread = jnp.where(
                (place_col >= DH) & (place_col < DH + 3) & (place_row == 8 * (place_col - DH) + h), 1.0, 0.0
            ).astype(BF16)
            extra = dot_nn(parts, spread)
            extra = jnp.where(lanes == DH + 3, 1.0, extra)
            key_wide = jnp.concatenate([key, extra[:, DH:]], axis=1)
            kp[h, rows, :] = key_wide.astype(BF16)
            vp[h, rows, :] = worth
            vt[h, :, rows] = worth.astype(F32).T.astype(BF16)
        return carry

    lax.fori_loop(0, tiles, prepare, 0)
    keeps = [
        pltpu.make_async_copy(qp, qp_hbm, keep_sem.at[0]),
        pltpu.make_async_copy(kp, kp_hbm, keep_sem.at[1]),
        pltpu.make_async_copy(vp, vp_hbm, keep_sem.at[2]),
    ]
    for keep in keeps:
        keep.start()

    acc, top_refs, total_refs, score_refs = (per_head[n * heads : (n + 1) * heads] for n in range(4))

    def query_tile(i, carry):
        cols = pl.ds(pl.multiple_of(i * TILE, TILE), TILE)
        for h in range(heads):
            top_refs[h][...] = jnp.full(top_refs[h].shape, MASKED, F32)
            total_refs[h][...] = jnp.zeros(total_refs[h].shape, F32)
            acc[h][...] = jnp.zeros(acc[h].shape, F32)

        def key_tile(j, inner):
            @pl.when(flags[i * tiles + j] > 0)
            def _():
                rows = pl.ds(pl.multiple_of(j * TILE, TILE), TILE)
                mask[...] = tile_mask(qrow, kcol, None, None, i, j)
                tops = []
                for h in range(heads):
                    scores = dot_nt(kp[h, rows, :], qp[h, cols, :]) + mask[...]
                    score_refs[h][...] = scores
                    tops.append(jnp.maximum(top_refs[h][0:1, :], jnp.max(scores, axis=0, keepdims=True)))
                for h, top in enumerate(tops):
                    expo = jnp.exp(score_refs[h][...] - top)
                    shrink = jnp.exp(top_refs[h][0:1, :] - top)
                    top_refs[h][0:1, :] = top
                    total_refs[h][0:1, :] = total_refs[h][0:1, :] * shrink + jnp.sum(expo, axis=0, keepdims=True)
                    acc[h][...] = acc[h][...] * shrink + dot_nn(vt[h, :, rows], expo.astype(BF16))

            return inner

        lax.fori_loop(0, i + 1, key_tile, 0)
        for h in range(heads):
            total = total_refs[h][0:1, :]
            ot[pl.ds(h * DH, DH), cols] = acc[h][...] / total
            lse_ref[h : h + 1, cols] = top_refs[h][0:1, :] + jnp.log(total)
        attended[cols, :] = ot[:, cols].T.astype(BF16)
        return carry

    lse_ref[...] = jnp.zeros(lse_ref.shape, F32)
    lax.fori_loop(0, tiles, query_tile, 0)
    stores = [pltpu.make_async_copy(ot, ot_hbm, keep_sem.at[3])]
    for b in range(count):
        stores.append(
            pltpu.make_async_copy(attended.at[pl.ds(b * size, size)], att_hbm.at[b ^ me], out_sem.at[b])
        )
    for store in stores:
        store.start()
    for copy in keeps + stores:
        copy.wait()


def attention_forward(projected, bias, kcol, qrow, flags, heads, prompt_len):
    count, size, width = projected.shape
    total = count * size
    any_spec = pl.BlockSpec(memory_space=pl.ANY)
    vmem = pl.BlockSpec(memory_space=pltpu.VMEM)
    shape = jax.ShapeDtypeStruct
    return pl.pallas_call(
        functools.partial(forward_kernel, heads, count, prompt_len),
        out_shape=(
            shape((count, size, heads * DH), BF16),
            shape((heads * DH, total), F32),
            shape((8, total), F32),
            shape((heads, total, LANES), BF16),
            shape((heads, total, LANES), BF16),
            shape((heads, total, DH), BF16),
            shape((total, LANES), F32),
        ),
        in_specs=[pl.BlockSpec(memory_space=pltpu.SMEM), any_spec, vmem, vmem, vmem],
        out_specs=(any_spec, any_spec, vmem, any_spec, any_spec, any_spec, vmem),
        scratch_shapes=[
            pltpu.VMEM((total, width), F32),
            pltpu.VMEM((heads, total, LANES), BF16),
            pltpu.VMEM((heads, total, LANES), BF16),
            pltpu.VMEM((heads, total, DH), BF16),
            pltpu.VMEM((heads, DH, total), BF16),
            pltpu.VMEM((total, LANES), BF16),
            pltpu.VMEM((total, LANES), F32),
            pltpu.VMEM((total, heads * DH), BF16),
            pltpu.VMEM((heads * DH, total), F32),
            pltpu.VMEM((TILE, TILE), F32),
            pltpu.SemaphoreType.DMA((count,)),
            pltpu.SemaphoreType.DMA((count,)),
            pltpu.SemaphoreType.DMA((4,)),
        ]
        + [pltpu.VMEM((DH, TILE), F32)] * heads
        + [pltpu.VMEM((8, TILE), F32)] * (2 * heads)
        + [pltpu.VMEM((TILE, TILE), F32)] * heads,
        compiler_params=pltpu.CompilerParams(vmem_limit_bytes=48 << 20),
        cost_estimate=pl.CostEstimate(flops=20_000_000_000, bytes_accessed=30_000_000, transcendentals=0),
        name="attention_forward",
    )(flags, projected, bias, kcol, qrow)


def backward_kernel(
    heads, count, prompt_len, flags, gatt_hbm, ot_ref, lse_ref, qp, kp, vp, logit, kcol, qrow,
    grad_hbm, bias_ref, gatt, gout, kt, delta, mask, decay, grad, in_sem, out_sem, *per_head,
):
    dqt, dk, dv, prob_refs, score_refs = (per_head[n * heads : (n + 1) * heads] for n in range(5))
    me = lax.axis_index("p") * 2 + lax.axis_index("k")
    total = gatt.shape[0]
    size = total // count
    tiles = total // TILE
    loads = []
    for b in range(count):
        rows = pl.ds(b * size, size)
        loads.append(pltpu.make_async_copy(gatt_hbm.at[b ^ me], gatt.at[rows], in_sem.at[b]))
    for load in loads:
        load.start()
    for load in loads:
        load.wait()
    for h in range(heads):
        dqt[h][...] = jnp.zeros(dqt[h].shape, F32)
    delta[...] = jnp.zeros(delta.shape, F32)

    def prepare(t, carry):
        rows = pl.ds(pl.multiple_of(t * TILE, TILE), TILE)
        turned = gatt[rows, :].astype(F32).T * ot_ref[:, rows]
        for h in range(heads):
            gout[h, rows, :] = gatt[rows, h * DH : (h + 1) * DH]
            kt[h, :, rows] = kp[h, rows, :].astype(F32).T[: DH + 8].astype(BF16)
            delta[h : h + 1, rows] = jnp.sum(turned[h * DH : (h + 1) * DH], axis=0, keepdims=True)
        return carry

    lax.fori_loop(0, tiles, prepare, 0)
    lanes = lane((TILE, LANES))

    def key_tile(j, carry):
        rows = pl.ds(pl.multiple_of(j * TILE, TILE), TILE)
        for h in range(heads):
            dk[h][...] = jnp.zeros(dk[h].shape, F32)
            dv[h][...] = jnp.zeros(dv[h].shape, F32)

        def query_tile(i, inner):
            @pl.when(flags[i * tiles + j] > 0)
            def _():
                cols = pl.ds(pl.multiple_of(i * TILE, TILE), TILE)
                mask[...] = tile_mask(qrow, kcol, None, None, i, j)
                for h in range(heads):
                    scores = dot_nt(kp[h, rows, :], qp[h, cols, :]) + mask[...]
                    prob_refs[h][...] = jnp.exp(scores - lse_ref[h : h + 1, cols])
                for h in range(heads):
                    probs = prob_refs[h][...]
                    grad_probs = dot_nt(vp[h, rows, :], gout[h, cols, :])
                    score_refs[h][...] = (probs * (grad_probs - delta[h : h + 1, cols])).astype(BF16)
                    dv[h][...] += dot_nn(probs.astype(BF16), gout[h, cols, :])
                for h in range(heads):
                    grad_scores = score_refs[h][...]
                    dk[h][...] += dot_nn(grad_scores, qp[h, cols, :])
                    dqt[h][:, cols] += dot_nn(kt[h, :, rows], grad_scores)

            return inner

        lax.fori_loop(j, tiles, query_tile, 0)
        keys = jnp.zeros((TILE, LANES), F32)
        for h in range(heads):
            grad_key = dk[h][...]
            keys += jnp.where(lanes == h, pltpu.roll(grad_key, LANES - DH + h, 1), 0.0)
            grad[rows, (3 * h + 1) * DH : (3 * h + 3) * DH] = jnp.concatenate(
                [grad_key[:, :DH], dv[h][...]], axis=1
            ).astype(BF16)
        decay[rows, :] = -keys
        return carry

    lax.fori_loop(0, tiles, key_tile, 0)

    def finish(t, carry):
        rows = pl.ds(pl.multiple_of(t * TILE, TILE), TILE)
        queries = jnp.zeros((TILE, LANES), F32)
        for h in range(heads):
            turned = jnp.concatenate([dqt[h][:, rows], jnp.zeros((LANES - DH - 8, TILE), F32)], axis=0).T
            queries += jnp.where(lanes == h, pltpu.roll(turned, LANES - DH - 3 + h, 1), 0.0)
            grad[rows, 3 * h * DH : (3 * h + 1) * DH] = (turned[:, :DH] * DH ** (-0.5)).astype(BF16)
        whole = decay[rows, :] + queries
        high, mid, low = split_parts(whole)
        decay[rows, :] = (
            high.astype(F32) + pltpu.roll(mid.astype(F32), 8, 1) + pltpu.roll(low.astype(F32), 16, 1)
        )
        return carry

    lax.fori_loop(0, tiles, finish, 0)

    prompt_tiles = prompt_len // TILE
    wide = (TILE, TILE)
    row_pos, col_pos = lax.broadcasted_iota(jnp.int32, wide, 0), lax.broadcasted_iota(jnp.int32, wide, 1)
    above = jnp.where(col_pos >= row_pos, 1.0, 0.0).astype(BF16)
    branch_len = total - prompt_len
    doc_index = lax.broadcasted_iota(jnp.int32, (8, branch_len), 0)
    chosen = jnp.where(qrow[4:5, prompt_len:total] == doc_index, 1.0, 0.0).astype(BF16)
    doc_sums = dot_nn(chosen, decay[prompt_len:total, :].astype(BF16))

    def prompt_sums(n, after):
        t = prompt_tiles - 1 - n
        rows = pl.ds(pl.multiple_of(t * TILE, TILE), TILE)
        suffix = dot_nn(above, decay[rows, :].astype(BF16)) + after
        doc = kcol[rows, 3:4]
        sums = suffix
        for d in range(DOCS):
            sums = sums + jnp.where(doc <= d, doc_sums[d : d + 1, :], 0.0)
        decay[rows, :] = sums
        return suffix[0:1, :]

    def branch_sums(t, carry):
        rows = pl.ds(pl.multiple_of(t * TILE, TILE), TILE)

        def add_own(u, acc):
            others = pl.ds(pl.multiple_of(u * TILE, TILE), TILE)
            own = (u * TILE + col_pos >= t * TILE + row_pos) & (kcol[rows, 1:2] == qrow[2:3, others])
            return acc + dot_nn(jnp.where(own, 1.0, 0.0).astype(BF16), decay[others, :].astype(BF16))

        decay[rows, :] = lax.fori_loop(t, tiles, add_own, jnp.zeros((TILE, LANES), F32))
        return carry

    lax.fori_loop(0, prompt_tiles, prompt_sums, jnp.zeros((1, LANES), F32))
    lax.fori_loop(prompt_tiles, tiles, branch_sums, 0)

    def rates(t, bias):
        rows = pl.ds(pl.multiple_of(t * TILE, TILE), TILE)
        sums = decay[rows, :]
        grad_rate = sums + pltpu.roll(sums, LANES - 8, 1) + pltpu.roll(sums, LANES - 16, 1)
        value = logit[rows, :]
        grad_forget = grad_rate / (1.0 + jnp.exp(value))
        grad_forget = jnp.where(lanes < heads, grad_forget, 0.0).astype(BF16)
        grad[rows, 3 * DH * heads :] = grad_forget
        return bias + jnp.sum(grad_forget.astype(F32), axis=0, keepdims=True)

    bias_ref[...] = jnp.broadcast_to(
        lax.fori_loop(0, tiles, rates, jnp.zeros((1, LANES), F32)), bias_ref.shape
    )
    stores = []
    for b in range(count):
        stores.append(
            pltpu.make_async_copy(grad.at[pl.ds(b * size, size)], grad_hbm.at[b ^ me], out_sem.at[b])
        )
    for store in stores:
        store.start()
    for store in stores:
        store.wait()


def attention_backward(grad_attended, saved, kcol, qrow, flags, heads, prompt_len):
    ot, lse, qp, kp, vp, logit = saved
    count, size, width = grad_attended.shape
    total = count * size
    any_spec = pl.BlockSpec(memory_space=pl.ANY)
    vmem = pl.BlockSpec(memory_space=pltpu.VMEM)
    shape = jax.ShapeDtypeStruct
    out_width = 3 * DH * heads + LANES
    return pl.pallas_call(
        functools.partial(backward_kernel, heads, count, prompt_len),
        out_shape=(shape((count, size, out_width), BF16), shape((8, LANES), F32)),
        in_specs=[pl.BlockSpec(memory_space=pltpu.SMEM), any_spec]
        + [vmem] * 8,
        out_specs=(any_spec, vmem),
        scratch_shapes=[
            pltpu.VMEM((total, width), BF16),
            pltpu.VMEM((heads, total, DH), BF16),
            pltpu.VMEM((heads, DH + 8, total), BF16),
            pltpu.VMEM((8, total), F32),
            pltpu.VMEM((TILE, TILE), F32),
            pltpu.VMEM((total, LANES), F32),
            pltpu.VMEM((total, out_width), BF16),
            pltpu.SemaphoreType.DMA((count,)),
            pltpu.SemaphoreType.DMA((count,)),
        ]
        + [pltpu.VMEM((DH + 8, total), F32)] * heads
        + [pltpu.VMEM((TILE, LANES), F32)] * heads
        + [pltpu.VMEM((TILE, DH), F32)] * heads
        + [pltpu.VMEM((TILE, TILE), F32)] * heads
        + [pltpu.VMEM((TILE, TILE), BF16)] * heads,
        compiler_params=pltpu.CompilerParams(vmem_limit_bytes=56 << 20),
        cost_estimate=pl.CostEstimate(flops=50_000_000_000, bytes_accessed=30_000_000, transcendentals=0),
        name="attention_backward",
    )(flags, grad_attended, ot, lse, qp, kp, vp, logit, kcol, qrow)


def group_codes(prompt_ids, branch_ids, branch_docs):
    prompt_len = prompt_ids.shape[0]
    member = branch_ids[:, None] == jnp.arange(branch_docs.shape[0])[None, :]
    branch_doc_ids = jnp.sum(jnp.where(member, branch_docs[None, :], 0), axis=1)
    key_code = jnp.concatenate([prompt_ids, DOCS + branch_ids])
    first = jnp.concatenate([prompt_ids, branch_doc_ids])
    tag = jnp.concatenate([jnp.full_like(prompt_ids, -1), branch_ids])
    limit = jnp.concatenate([jnp.full_like(prompt_ids, -1), branch_doc_ids])
    prompt_code = jnp.concatenate([prompt_ids, jnp.full_like(branch_ids, DOCS)])
    total = key_code.shape[0]
    none = jnp.zeros_like(tag)
    kcol = jnp.stack([key_code, tag, limit, prompt_code] + [none] * 4, axis=1)
    qrow = jnp.stack([first, key_code, tag, prompt_code, limit] + [none] * 3, axis=0)
    tiles = total // TILE
    kinds = jnp.arange(2 * DOCS)
    key_bits = jnp.any(key_code.reshape(tiles, TILE, 1) == kinds, axis=1)
    query_bits = key_bits | jnp.any(first.reshape(tiles, TILE, 1) == kinds, axis=1)
    order = jnp.arange(tiles)
    meets = jnp.any(query_bits[:, None, :] & key_bits[None, :, :], axis=2)
    flags = (meets & (order[None, :] <= order[:, None])).astype(jnp.int32).reshape(-1)
    return kcol, qrow, flags


class Wires:
    def __init__(self, send_sem, recv_sem, local_sem):
        self.send_sem, self.recv_sem, self.local_sem = send_sem, recv_sem, local_sem
        self.used, self.local_used = 0, 0
        self.k, self.x = lax.axis_index("k"), lax.axis_index("x")
        self.h, self.p, self.o = lax.axis_index("h"), lax.axis_index("p"), lax.axis_index("o")
        self.home = self.k == self.h
        self.same = self.k == self.x
        self.pending = []

    def slot(self):
        self.used += 1
        return self.used - 1

    def copy(self, source, target, device, slot):
        return pltpu.make_async_remote_copy(
            src_ref=source,
            dst_ref=target,
            send_sem=self.send_sem.at[slot],
            recv_sem=self.recv_sem.at[slot],
            device_id=device,
            device_id_type=pl.DeviceIdType.MESH,
        )

    def send(self, source, target, device):
        copy = self.copy(source, target, device, self.slot())
        copy.start()
        self.pending.append(copy.wait_send)
        return copy

    def local(self, source, target):
        copy = pltpu.make_async_copy(source, target, self.local_sem.at[self.local_used])
        self.local_used += 1
        copy.start()
        return copy

    def greet(self, devices):
        barrier = pltpu.get_barrier_semaphore()
        for device in devices:
            pl.semaphore_signal(
                barrier, inc=1, device_id=device, device_id_type=pl.DeviceIdType.MESH
            )
        pl.semaphore_wait(barrier, len(devices))

    def close(self):
        for wait in self.pending:
            wait()


def row_spans(total, pieces):
    size = total // pieces
    return [pl.ds(i * size, size) for i in range(pieces)]


class Fetch:
    def __init__(self, wires, shard, target, stage, pieces, got=None, keep=None):
        w = self.wires = wires
        self.shard, self.target, self.stage, self.got, self.keep = shard, target, stage, got, keep
        self.count = pieces
        self.half_rows = shard.shape[0] // 2
        self.size = self.half_rows // pieces
        self.by_columns = len(target.shape) == 2
        self.first = [w.slot() for _ in range(pieces)]
        self.over = [w.slot() for _ in range(pieces)]
        self.second = [w.slot() for _ in range(2 * pieces)]
        self.local_slot = w.local_used
        w.local_used += 2

    def rows(self, i, mine=True):
        bit = self.wires.o % 2
        bit = bit if mine else 1 - bit
        return pl.ds(pl.multiple_of(bit * self.half_rows + i * self.size, 16), self.size)

    def place(self, half, span):
        if self.by_columns:
            width = self.shard.shape[1]
            return self.target.at[span, pl.ds(half * width, width)]
        return self.target.at[half, span]

    def first_copy(self, i, home):
        w, span = self.wires, self.rows(i)
        if home:
            return w.copy(self.shard.at[span], self.place(1, span), {"x": 1 - w.x}, self.first[i])
        device = {"k": 1 - w.k, "h": 1 - w.h}
        return w.copy(self.shard.at[span], self.place(0, span), device, self.first[i])

    def have(self, i, half):
        if self.got is None:
            return self.place(half, self.rows(i))
        return self.got.at[pl.ds(i * self.size, self.size)]

    def over_copy(self, i, home):
        w, half = self.wires, 1 if home else 0
        return w.copy(self.have(i, half), self.place(half, self.rows(i)), {"o": w.o ^ 1}, self.over[i])

    def second_copy(self, i, mine):
        w, span = self.wires, self.rows(i, mine)
        source = self.have(i, 0) if mine else self.place(0, span)
        slot = self.second[i if mine else self.count + i]
        return w.copy(source, self.place(1, span), {"x": 1 - w.x}, slot)

    def shard_load(self):
        return pltpu.make_async_copy(self.shard, self.stage, self.wires.local_sem.at[self.local_slot])

    def shard_store(self):
        whole = pl.ds(0, self.shard.shape[0])
        return pltpu.make_async_copy(
            self.stage, self.place(0, whole), self.wires.local_sem.at[self.local_slot]
        )

    def got_load(self):
        return pltpu.make_async_copy(self.got, self.keep, self.wires.local_sem.at[self.local_slot + 1])

    def got_store(self, half):
        bit = self.wires.o % 2
        span = pl.ds(pl.multiple_of(bit * self.half_rows, 16), self.half_rows)
        return pltpu.make_async_copy(
            self.keep, self.place(half, span), self.wires.local_sem.at[self.local_slot + 1]
        )

    def either(self, at_home, away):
        pl.when(self.wires.home)(at_home)
        pl.when(jnp.logical_not(self.wires.home))(away)

    def load(self):
        pl.when(self.wires.home)(lambda: self.shard_load().start())
        if self.got is not None:
            self.got_load().start()

    def start(self):
        if self.got is not None:
            for i in range(self.count):
                self.relay(i)
            return

        def go(home):
            for i in range(self.count):
                self.first_copy(i, home).start()

        self.either(lambda: go(True), lambda: go(False))

    def store(self):
        def at_home():
            self.shard_load().wait()
            self.shard_store().start()
            if self.got is not None:
                self.got_load().wait()
                self.got_store(1).start()

        def away():
            if self.got is not None:
                self.got_load().wait()
                self.got_store(0).start()

        self.either(at_home, away)

    def relay(self, i):
        def at_home():
            if self.got is None:
                self.first_copy(i, True).wait_recv()
            self.over_copy(i, True).start()

        def away():
            if self.got is None:
                self.first_copy(i, False).wait_recv()
            self.over_copy(i, False).start()
            self.second_copy(i, True).start()

        self.either(at_home, away)

    def relay_over(self, i):
        def away():
            self.over_copy(i, False).wait_recv()
            self.second_copy(i, False).start()

        pl.when(jnp.logical_not(self.wires.home))(away)

    def wait(self):
        def at_home():
            for i in range(self.count):
                if self.got is None:
                    self.first_copy(i, True).wait_send()
                self.over_copy(i, True).wait()
            self.shard_store().wait()
            if self.got is not None:
                self.got_store(1).wait()

        def away():
            for i in range(self.count):
                if self.got is None:
                    self.first_copy(i, False).wait_send()
                self.over_copy(i, False).wait_send()
                self.second_copy(i, True).wait()
                self.second_copy(i, False).wait()
            if self.got is not None:
                self.got_store(0).wait()

        self.either(at_home, away)


def partners(wires, psize, away=False, peers=True, over_o=0):
    devices = [{"k": 1 - wires.k}]
    if peers:
        devices += [{"p": wires.p ^ bit} for bit in range(1, psize)]
    devices += [{"x": 1 - wires.x}]
    devices += [{"k": 1 - wires.k, "x": 1 - wires.x}]
    if away:
        devices += [{"k": 1 - wires.k, "h": 1 - wires.h}, {"h": 1 - wires.h}]
    bit = 1
    while bit < over_o:
        devices += [{"o": wires.o ^ bit}]
        bit *= 2
    return devices


class Share:
    def __init__(self, wires, psize, own, g, spans):
        self.wires, self.psize, self.own, self.g, self.spans = wires, psize, own, g, spans
        self.near, self.far, self.kept, self.passed = [], {}, [], []

    def send(self, i):
        w, span = self.wires, self.spans[i]
        for bit in range(1, self.psize):
            self.far[bit, i] = w.send(self.own.at[span], self.g.at[2 * bit, span], {"p": w.p ^ bit})
        self.near.append(w.send(self.own.at[span], self.g.at[1, span], {"k": 1 - w.k}))
        self.kept.append(w.local(self.own.at[span], self.g.at[0, span]))

    def relay(self, i):
        w, span = self.wires, self.spans[i]
        for bit in range(1, self.psize):
            self.far[bit, i].wait_recv()
            self.passed.append(
                w.send(self.g.at[2 * bit, span], self.g.at[2 * bit + 1, span], {"k": 1 - w.k})
            )

    def wait(self):
        for copy in self.near + self.passed:
            copy.wait_recv()
        for copy in self.kept:
            copy.wait()


def by_chunks(span, body):
    def run(n, carry):
        body(pl.ds(pl.multiple_of(span.start + n * CHUNK, CHUNK), CHUNK))
        return carry

    lax.fori_loop(0, span.size // CHUNK, run, 0)


def add_into(value, *others):
    def body(rows):
        total = value[rows, :].astype(F32)
        for other in others:
            total = total + other[rows, :].astype(F32)
        value[rows, :] = total.astype(BF16)

    by_chunks(pl.ds(0, value.shape[0]), body)


class Reduce:
    def __init__(self, wires, psize, part, near, mid, far, spans):
        self.wires, self.psize, self.part = wires, psize, part
        self.near, self.mid, self.far, self.spans = near, mid, far, spans
        self.near_copies, self.far_copies = {}, {}

    def start_near(self, bit):
        w = self.wires
        for i, span in enumerate(self.spans):
            self.near_copies[bit, i] = w.send(
                self.part.at[2 * bit + 1, span], self.near.at[bit, span], {"k": 1 - w.k}
            )

    def start_far(self, bit):
        w = self.wires
        for i, span in enumerate(self.spans):
            self.near_copies[bit, i].wait_recv()

            def add(rows, bit=bit):
                self.mid[bit - 1, rows] = (
                    self.part[2 * bit, rows].astype(F32) + self.near[bit, rows].astype(F32)
                ).astype(BF16)

            by_chunks(span, add)
            self.far_copies[bit, i] = w.send(
                self.mid.at[bit - 1, span], self.far.at[bit - 1, span], {"p": w.p ^ bit}
            )

    def start(self):
        for bit in reversed(range(self.psize)):
            self.start_near(bit)
        for bit in reversed(range(1, self.psize)):
            self.start_far(bit)

    def start_with(self, make):
        for bit in reversed(range(self.psize)):
            make(2 * bit + 1)
            self.start_near(bit)
            make(2 * bit)
            if bit:
                self.start_far(bit)

    def each(self, i, body):
        span = self.spans[i]
        self.near_copies[0, i].wait_recv()
        for bit in range(1, self.psize):
            self.far_copies[bit, i].wait_recv()

        def run(rows):
            total = self.part[0, rows].astype(F32) + self.near[0, rows].astype(F32)
            for bit in range(1, self.psize):
                total = total + self.far[bit - 1, rows].astype(F32)
            body(rows, total)

        by_chunks(span, run)


CHUNK = 32
PIECES = 3


def inverse_rms(value):
    return lax.rsqrt(jnp.sum(value * value, axis=1, keepdims=True) / D + EPS)


def norm_back(grad, value, base, gain):
    rms = inverse_rms(value)
    gained = gain * grad
    inner = jnp.sum(value * gained, axis=1, keepdims=True)
    result = base + rms * gained - value * (rms * rms * rms) * inner / D
    parts = grad * value * rms
    return result, sum(parts[n : n + 8] for n in range(0, parts.shape[0], 8))


def enter_kernel(
    psize, x_ref, gain_own, codes_own, qkv_shard, forget_shard, out_shard, xin, g, proj, out, gain_ref, codes, far_gains,
    own, qkv_stage, forget_stage, out_stage, send_sem, recv_sem, local_sem,
):
    w = Wires(send_sem, recv_sem, local_sem)
    width = qkv_shard.shape[1]
    qkv = Fetch(w, qkv_shard, proj.at[:, :, pl.ds(0, width)], qkv_stage, 3)
    forget = Fetch(
        w, forget_shard, proj.at[:, :, pl.ds(width, forget_shard.shape[1])], forget_stage, 1
    )
    out_fetch = Fetch(w, out_shard, out, out_stage, 1)
    for fetch in (qkv, forget, out_fetch):
        fetch.load()
    w.greet(partners(w, psize, away=True, over_o=2))
    rows, half = own.shape[0], x_ref.shape[1]
    spans = row_spans(rows, PIECES)
    size = rows // PIECES
    def spread(source, target, pieces):
        count = len(pieces)
        to_near = [w.slot() for _ in pieces]
        to_far = [w.slot() for _ in pieces]
        kept = [w.local_used + i for i in range(count)]
        w.local_used += count

        def piece(base, i):
            start, length = pieces[i]
            return source.at[pl.ds(pl.multiple_of(base * rows + start, 8), length)]

        def span(i):
            return pl.ds(pieces[i][0], pieces[i][1])

        left, right = pl.ds(0, half), pl.ds(half, half)

        def same_keep(i):
            return pltpu.make_async_copy(piece(w.k, i), target.at[span(i), left], local_sem.at[kept[i]])

        def same_send(i):
            return w.copy(piece(1 - w.k, i), target.at[span(i), left], {"k": 1 - w.k}, to_near[i])

        def cross_near(i):
            return w.copy(piece(w.k, i), target.at[span(i), right], {"x": 1 - w.x}, to_near[i])

        def cross_far(i):
            return w.copy(
                piece(1 - w.k, i), target.at[span(i), right], {"k": 1 - w.k, "x": 1 - w.x}, to_far[i]
            )

        def start():
            @pl.when(w.same)
            def _():
                for i in range(count):
                    same_send(i).start()
                    same_keep(i).start()

            @pl.when(jnp.logical_not(w.same))
            def _():
                for i in range(count):
                    cross_near(i).start()
                    cross_far(i).start()

        def arrive(i):
            @pl.when(w.same)
            def _():
                same_keep(i).wait()
                same_send(i).wait_recv()

            @pl.when(jnp.logical_not(w.same))
            def _():
                cross_near(i).wait_recv()
                cross_far(i).wait_recv()

        def close():
            @pl.when(w.same)
            def _():
                for i in range(count):
                    same_send(i).wait_send()

            @pl.when(jnp.logical_not(w.same))
            def _():
                for i in range(count):
                    cross_near(i).wait_send()
                    cross_far(i).wait_send()

        return start, arrive, close

    gain_copy = w.send(gain_own, gain_ref.at[:, pl.ds(half, half)], {"x": 1 - w.x})
    code_copies = [
        w.send(gain_own, far_gains, {"k": 1 - w.k, "h": 1 - w.h}),
        w.send(codes_own, codes.at[1], {"x": 1 - w.x}),
        w.send(codes_own, codes.at[2], {"k": 1 - w.k}),
        w.send(codes_own, codes.at[3], {"k": 1 - w.k, "x": 1 - w.x}),
    ]
    codes[0] = codes_own[...]
    start, arrive, close = spread(x_ref, xin, [(i * size, size) for i in range(PIECES)])
    start()
    qkv.start()
    forget.start()
    share = Share(w, psize, own, g, spans)
    gain_ref[:, pl.ds(0, half)] = gain_own[...]
    gain_copy.wait_recv()
    for i, span in enumerate(spans):
        arrive(i)

        def norm(rows):
            value = xin[rows, :].astype(F32)
            own[rows, :] = (value * inverse_rms(value) * gain_ref[0:1, :]).astype(BF16)

        by_chunks(span, norm)
        share.send(i)
    close()
    for fetch in (qkv, forget, out_fetch):
        fetch.store()
    for i in range(3):
        qkv.relay(i)
    out_fetch.start()
    forget.relay(0)
    for i in range(3):
        qkv.relay_over(i)
        if i < PIECES:
            share.relay(i)
    for i in range(3, PIECES):
        share.relay(i)
    forget.relay_over(0)
    out_fetch.relay(0)
    out_fetch.relay_over(0)
    share.wait()
    for fetch in (qkv, forget, out_fetch):
        fetch.wait()
    for copy in code_copies:
        copy.wait_recv()
    w.close()


def forward_exchange_kernel(
    psize, attended, w_out, xin, gain_ref, gate_shard, gate_got, up_shard, up_got, down_shard, resid, g, gate, up, down,
    near, mid, far, own, part, gate_stage, gate_keep, up_stage, up_keep, down_stage, send_sem, recv_sem, local_sem,
):
    w = Wires(send_sem, recv_sem, local_sem)
    gate_fetch = Fetch(w, gate_shard, gate, gate_stage, 2, gate_got, gate_keep)
    up_fetch = Fetch(w, up_shard, up, up_stage, 2, up_got, up_keep)
    down_fetch = Fetch(w, down_shard, down, down_stage, 2)
    fetches = (gate_fetch, up_fetch, down_fetch)
    for fetch in fetches:
        fetch.load()
    w.greet(partners(w, psize, away=True, over_o=2))
    spans = row_spans(own.shape[0], PIECES)
    reduce = Reduce(w, psize, part, near, mid, far, spans)
    gate_fetch.start()

    def multiply(block):
        def one(n, carry):
            span = pl.ds(pl.multiple_of(n * TILE, TILE), TILE)
            part[block, :, span] = dot_nn(attended[block], w_out[:, span]).astype(BF16)
            return carry

        lax.fori_loop(0, D // TILE, one, 0)

    reduce.start_with(multiply)
    up_fetch.start()
    down_fetch.start()
    for fetch in fetches:
        fetch.store()
    for i in range(2):
        gate_fetch.relay_over(i)
    for i in range(2):
        down_fetch.relay(i)
    for i in range(2):
        up_fetch.relay_over(i)
    share = Share(w, psize, own, g, spans)
    for i in range(PIECES):

        def norm(rows, total):
            value = total + xin[rows, :].astype(F32)
            resid[rows, :] = value
            own[rows, :] = (value * inverse_rms(value) * gain_ref[1:2, :]).astype(BF16)

        reduce.each(i, norm)
        share.send(i)
    for i in range(2):
        down_fetch.relay_over(i)
    for i in range(PIECES):
        share.relay(i)
    share.wait()
    for fetch in fetches:
        fetch.wait()
    w.close()


class EarlySum:
    def __init__(self, wires, part, value, over, across, result, pieces, offset=0, got=None):
        w = self.wires = wires
        self.offset, self.got = offset, got
        self.part, self.value, self.over, self.across, self.result = part, value, over, across, result
        self.count, self.half_rows = pieces, value.shape[1]
        self.size = self.half_rows // pieces
        self.over_slots = [[w.slot() for _ in range(pieces)] for _ in range(2)]
        self.across_slots = [w.slot() for _ in range(pieces)]
        self.local_slot = w.local_used
        w.local_used += 2 + pieces

    def span(self, i):
        return pl.ds(i * self.size, self.size)

    def load_copy(self, half):
        start = pl.multiple_of(self.offset + (self.wires.o % 2) * self.half_rows, 16)
        return pltpu.make_async_copy(
            self.part.at[half, pl.ds(start, self.half_rows)],
            self.value.at[half],
            self.wires.local_sem.at[self.local_slot + half],
        )

    def load(self):
        for half in range(2):
            self.load_copy(half).start()

    def over_copy(self, half, i):
        w = self.wires
        start = pl.multiple_of(self.offset + (1 - w.o % 2) * self.half_rows + i * self.size, 16)
        return w.copy(
            self.part.at[half, pl.ds(start, self.size)],
            self.over.at[half, self.span(i)],
            {"o": w.o ^ 1},
            self.over_slots[half][i],
        )

    def across_copy(self, i):
        w = self.wires
        return w.copy(
            self.value.at[1, self.span(i)], self.across.at[self.span(i)], {"x": 1 - w.x}, self.across_slots[i]
        )

    def keep_copy(self, i):
        return pltpu.make_async_copy(
            self.value.at[0, self.span(i)],
            self.result.at[self.span(i)],
            self.wires.local_sem.at[self.local_slot + 2 + i],
        )

    def start(self, half):
        for i in range(self.count):
            self.over_copy(half, i).start()

    def pass_on(self, i):
        if i == 0:
            self.load_copy(1).wait()
        span = self.span(i)
        if self.got is None:
            self.over_copy(1, i).wait_recv()
            add_into(self.value.at[1, span], self.over.at[1, span])
        else:
            add_into(self.value.at[1, span], self.got.at[span])
        self.across_copy(i).start()

    def finish(self, i):
        if i == 0:
            self.load_copy(0).wait()
        self.over_copy(0, i).wait_recv()
        self.across_copy(i).wait_recv()
        span = self.span(i)
        add_into(self.value.at[0, span], self.over.at[0, span], self.across.at[span])
        if self.result is not None:
            self.keep_copy(i).start()

    def close(self):
        for i in range(self.count):
            for half in range(2):
                if half == 0 or self.got is None:
                    self.over_copy(half, i).wait_send()
            self.across_copy(i).wait_send()
            if self.result is not None:
                self.keep_copy(i).wait()


def backward_exchange_kernel(
    psize, grad_gate, grad_up, w_gate, w_up, resid, cot, gain_ref, down_own, down_other, gate_part, up_part,
    grad_resid, g, gain_grad, down_sum, pair_sum,
    near, mid, far, own, part, down_across, down_moved, gate_val, gate_over, gate_across, up_val, up_over, up_across,
    send_sem, recv_sem, local_sem,
):
    w = Wires(send_sem, recv_sem, local_sem)
    gate = EarlySum(w, gate_part, gate_val, gate_over, gate_across, pair_sum.at[0], 2)
    up = EarlySum(w, up_part, up_val, up_over, up_across, pair_sum.at[1], 2)
    gate.load()
    up.load()
    w.greet(partners(w, psize, away=True, over_o=2))
    spans = row_spans(own.shape[0], PIECES)
    reduce = Reduce(w, psize, part, near, mid, far, spans)
    down_copy = w.send(down_other, down_across, {"x": 1 - w.x})
    gate.start(1)
    up.start(1)
    gate.start(0)
    up.start(0)

    def multiply(block):
        def one(n, carry):
            span = pl.ds(pl.multiple_of(n * TILE, TILE), TILE)
            sums = dot_nt(grad_gate[block], w_gate[span, :]) + dot_nt(grad_up[block], w_up[span, :])
            part[block, :, span] = sums.astype(BF16)
            return carry

        lax.fori_loop(0, D // TILE, one, 0)

    reduce.start_with(multiply)
    for i in range(2):
        gate.pass_on(i)
    down_home = w.copy(down_sum, down_moved, {"h": 1 - w.h}, w.slot())
    down_copy.wait_recv()

    def add_down(rows):
        down_sum[rows, :] = (
            down_own[rows, :].astype(F32) + down_across[rows, :].astype(F32)
        ).astype(BF16)

    by_chunks(pl.ds(0, down_sum.shape[0]), add_down)

    @pl.when(jnp.logical_not(w.home))
    def _():
        down_home.start()

    share = Share(w, psize, own, g, spans)
    gain_grad[...] = jnp.zeros(gain_grad.shape, F32)

    def back(rows, total):
        grad, gain_part = norm_back(total, resid[rows, :], cot[rows, :].astype(F32), gain_ref[1:2, :])
        grad_resid[rows, :] = grad
        own[rows, :] = grad.astype(BF16)
        gain_grad[...] += gain_part

    for i in range(PIECES):
        reduce.each(i, back)
        share.send(i)
    for i in range(2):
        up.pass_on(i)
    share.relay(0)
    for i in range(2):
        gate.finish(i)
    for i in range(1, PIECES):
        share.relay(i)
    for i in range(2):
        up.finish(i)
    share.wait()
    gate.close()
    up.close()

    @pl.when(jnp.logical_not(w.home))
    def _():
        down_home.wait_send()

    @pl.when(w.home)
    def _():
        down_home.wait_recv()
        add_into(down_sum, down_moved)

    w.close()


class Spread:
    def __init__(self, wires, value, result):
        w = self.wires = wires
        self.value, self.result = value, result
        self.over_slot, self.near_slot, self.pass_slot = w.slot(), w.slot(), w.slot()
        self.local_slot = w.local_used
        w.local_used += 1

    def rows(self, mine):
        bit = self.wires.o % 2
        return self.result.at[bit if mine else 1 - bit]

    def over_copy(self):
        w = self.wires
        return w.copy(self.value, self.rows(True), {"o": w.o ^ 1}, self.over_slot)

    def near_copy(self):
        return self.wires.copy(self.value, self.rows(True), {"k": 1 - self.wires.k}, self.near_slot)

    def pass_copy(self):
        return self.wires.copy(self.rows(False), self.rows(False), {"k": 1 - self.wires.k}, self.pass_slot)

    def keep_copy(self):
        return pltpu.make_async_copy(
            self.value, self.rows(True), self.wires.local_sem.at[self.local_slot]
        )

    def start(self):
        @pl.when(self.wires.home)
        def _():
            self.over_copy().start()
            self.near_copy().start()
            self.keep_copy().start()

    def relay(self):
        @pl.when(self.wires.home)
        def _():
            self.over_copy().wait_recv()
            self.pass_copy().start()

    def wait(self):
        @pl.when(self.wires.home)
        def _():
            self.over_copy().wait_send()
            self.near_copy().wait_send()
            self.pass_copy().wait_send()
            self.keep_copy().wait()

        @pl.when(jnp.logical_not(self.wires.home))
        def _():
            self.near_copy().wait_recv()
            self.pass_copy().wait_recv()


class SmallSum:
    def __init__(self, wires, psize, osize, value, other, buffers):
        w = self.wires = wires
        self.value, self.other, self.buffers = value, other, buffers
        self.devices = [{"x": 1 - w.x}, {"k": 1 - w.k}]
        self.devices += [{"p": w.p ^ bit} for bit in bits_of(psize)]
        self.devices += [{"h": 1 - w.h}]
        self.devices += [{"o": w.o ^ bit} for bit in bits_of(osize)]
        self.slots = [w.slot() for _ in self.devices]

    def copy(self, step):
        source = self.other if step == 0 else self.value
        return self.wires.copy(source, self.buffers.at[step], self.devices[step], self.slots[step])

    def start(self):
        self.copy(0).start()

    def step(self, step):
        self.copy(step).wait()
        self.value[...] = self.value[...] + self.buffers[step]
        if step + 1 < len(self.devices):
            self.copy(step + 1).start()


class Chain:
    def __init__(self, wires, osize, value, stages, buffers, result, pieces):
        self.wires, self.value, self.stages, self.result = wires, value, stages, result
        self.buffers = buffers
        self.spans = row_spans(value.shape[0], pieces)
        self.slots = [[wires.slot() for _ in self.spans] for _ in stages]
        self.kept = [wires.local_used + i for i in range(pieces)]
        wires.local_used += pieces
        self.other = None

    def copy(self, stage, i):
        w, span = self.wires, self.spans[i]
        kind, slot = self.stages[stage], self.slots[stage][i]
        if kind == "x":
            return w.copy(self.other.at[span], self.buffers[stage].at[span], {"x": 1 - w.x}, slot)
        if kind == "h":
            return w.copy(self.value.at[span], self.buffers[stage].at[span], {"h": 1 - w.h}, slot)
        if kind == "k":
            return w.copy(self.value.at[span], self.result.at[span], {"k": 1 - w.k}, slot)
        return w.copy(self.value.at[span], self.buffers[stage].at[span], {"o": w.o ^ kind}, slot)

    def keep(self, i):
        span = self.spans[i]
        return pltpu.make_async_copy(
            self.value.at[span], self.result.at[span], self.wires.local_sem.at[self.kept[i]]
        )

    def start(self, stage, i):
        w, kind = self.wires, self.stages[stage]
        if kind == "x":
            self.copy(stage, i).start()
        elif kind == "h":
            @pl.when(jnp.logical_not(w.home))
            def _():
                self.copy(stage, i).start()
        else:
            @pl.when(w.home)
            def _():
                self.copy(stage, i).start()
                if kind == "k":
                    self.keep(i).start()

    def add(self, stage, i):
        span = self.spans[i]
        add_into(self.value.at[span], self.buffers[stage].at[span])

    def end(self, stage, i):
        w, kind = self.wires, self.stages[stage]
        if kind == "x":
            self.copy(stage, i).wait_recv()
            self.add(stage, i)
        elif kind == "h":
            @pl.when(w.home)
            def _():
                self.copy(stage, i).wait_recv()
                self.add(stage, i)
        elif kind == "k":
            @pl.when(w.home)
            def _():
                self.copy(stage, i).wait_send()
                self.keep(i).wait()

            @pl.when(jnp.logical_not(w.home))
            def _():
                self.copy(stage, i).wait_recv()
        else:
            @pl.when(w.home)
            def _():
                self.copy(stage, i).wait()
                self.add(stage, i)

    def close(self):
        w = self.wires
        for stage, kind in enumerate(self.stages):
            for i in range(len(self.spans)):
                if kind == "x":
                    self.copy(stage, i).wait_send()
                elif kind == "h":
                    @pl.when(jnp.logical_not(w.home))
                    def _():
                        self.copy(stage, i).wait_send()

    def step(self, stage, i):
        self.end(stage, i)
        if stage + 1 < len(self.stages):
            self.start(stage + 1, i)

    def order(self, first=0):
        return [(stage, i) for stage in range(first, len(self.stages)) for i in range(len(self.spans))]

    def run(self, first=0):
        for stage, i in self.order(first):
            self.step(stage, i)


def leave_kernel(
    psize, osize, pieces, grad_in, weight_in, stream, base, gain_ref, small_in, proj_in, out_own, out_other,
    pair_in, down_in, block, small, first_sum, second_sum, out_sum, up_sum, gate_sum, down_sum,
    near, mid, far, part, kept, first_val, second_val, out_val, up_val, gate_val, down_val, first_bufs,
    second_over, second_across, second_bufs, out_bufs, small_other, small_bufs, gain_acc,
    send_sem, recv_sem, local_sem,
):
    w = Wires(send_sem, recv_sem, local_sem)
    split = first_val.shape[0]
    second = EarlySum(w, proj_in, second_val, second_over, second_across, None, 2, split)
    second.load()
    loads = [
        w.local(source, target)
        for source, target in (
            (pair_in.at[1], up_val), (pair_in.at[0], gate_val), (down_in, down_val), (out_own, out_val),
            (proj_in.at[0, pl.ds(0, split)], first_val),
        )
    ]
    w.greet(partners(w, psize, away=True, over_o=osize))
    rows, half = kept.shape[1], kept.shape[2]
    spans = row_spans(rows, PIECES)
    size = rows // PIECES
    bits = bits_of(osize)

    first = Chain(
        w, osize, first_val, ["x", "h"] + bits + ["k"], [first_bufs.at[i] for i in range(2 + len(bits))],
        first_sum, pieces,
    )
    first.other = proj_in.at[1, pl.ds(0, split)]
    late = Chain(
        w, osize, second_val.at[0], ["h"] + bits[1:], [second_bufs.at[i] for i in range(len(bits))], None, 2
    )
    out = Chain(w, osize, out_val, ["x", "h"] + bits[1:], [out_bufs.at[i] for i in range(1 + len(bits))], None, 1)
    out.other = out_other
    spreads = [Spread(w, up_val, up_sum), Spread(w, gate_val, gate_sum), Spread(w, down_val, down_sum)]
    last_spreads = [Spread(w, out_val, out_sum), Spread(w, second_val.at[0], second_sum)]
    reduce = Reduce(w, psize, part, near, mid, far, spans)
    second.start(1)
    for i in range(pieces):
        first.start(0, i)
    out.start(0, 0)
    second.start(0)
    for load in loads:
        load.wait()
    for spread in spreads:
        spread.start()
    columns = D // TILE

    def multiply(block):
        def one(n, carry):
            span = pl.ds(pl.multiple_of(n * TILE, TILE), TILE)
            part[block, :, span] = dot_nt(grad_in[block], weight_in[span, :]).astype(BF16)
            return carry

        lax.fori_loop(0, columns, one, 0)

    reduce.start_with(multiply)

    near_slots = [w.slot() for _ in spans]
    far_slots = [w.slot() for _ in spans]
    keep_slots = [w.local_used + i for i in range(PIECES)]
    w.local_used += PIECES

    def target(i):
        return block.at[pl.ds(pl.multiple_of(w.k * rows + i * size, 8), size)]

    def same_keep(i):
        return pltpu.make_async_copy(kept.at[0, spans[i]], target(i), local_sem.at[keep_slots[i]])

    def same_send(i):
        return w.copy(kept.at[1, spans[i]], target(i), {"x": 1 - w.x}, near_slots[i])

    def cross_near(i):
        return w.copy(kept.at[0, spans[i]], target(i), {"k": 1 - w.k}, near_slots[i])

    def cross_far(i):
        return w.copy(kept.at[1, spans[i]], target(i), {"k": 1 - w.k, "x": 1 - w.x}, far_slots[i])

    for i in range(2):
        second.pass_on(i)
    first.step(0, 0)
    for i in range(1, pieces):
        first.step(0, i)
        first.step(1, i - 1)
    out.step(0, 0)
    second.finish(0)
    late.start(0, 0)
    first.step(1, pieces - 1)
    gain_acc[...] = jnp.zeros(gain_acc.shape, F32)

    def back(rows_, total):
        grad, gain_part = norm_back(total, stream[rows_, :].astype(F32), base[rows_, :], gain_ref[0:1, :])
        gain_acc[...] += gain_part
        kept[0, rows_, :] = grad[:, :half].astype(BF16)
        kept[1, rows_, :] = grad[:, half:].astype(BF16)

    for i in range(PIECES):
        reduce.each(i, back)

        @pl.when(w.same)
        def _():
            same_send(i).start()
            same_keep(i).start()

        @pl.when(jnp.logical_not(w.same))
        def _():
            cross_near(i).start()
            cross_far(i).start()

        if i == 0:
            second.finish(1)
            late.start(0, 1)

    gain_sum = jnp.sum(gain_acc[...], axis=0, keepdims=True)
    row = lax.broadcasted_iota(jnp.int32, (8, half), 0)
    small[...] = jnp.where(row == 0, gain_sum[:, :half], small_in[:, :half])
    small_other[...] = jnp.where(row == 0, gain_sum[:, half:], small_in[:, half:])
    total = SmallSum(w, psize, osize, small, small_other, small_bufs)
    total.start()
    out.run(1)
    last_spreads[0].start()
    steps = [lambda a=a: late.step(*a) for a in late.order(0)] + [last_spreads[1].start]
    steps += [spread.relay for spread in spreads] + [lambda a=a: first.step(*a) for a in first.order(2)]
    steps += [last_spreads[0].relay, last_spreads[1].relay]
    smalls = list(range(len(total.devices)))
    for n, step in enumerate(steps):
        step()
        if n % 2 == 0 and smalls:
            total.step(smalls.pop(0))
    for step in smalls:
        total.step(step)
    for spread in spreads + last_spreads:
        spread.wait()
    for i in range(PIECES):
        @pl.when(w.same)
        def _():
            same_keep(i).wait()
            same_send(i).wait_send()
            cross_near(i).wait_recv()

        @pl.when(jnp.logical_not(w.same))
        def _():
            cross_near(i).wait_send()
            cross_far(i).wait()
            same_send(i).wait_recv()

    for chain in (first, second, late, out):
        chain.close()
    w.close()


ANY = pl.BlockSpec(memory_space=pl.ANY)
VMEM = pl.BlockSpec(memory_space=pltpu.VMEM)
SLOTS = 128


def exchange_call(kernel, name, collective_id, outs, out_specs, in_specs, scratch, args):
    return pl.pallas_call(
        kernel,
        out_shape=outs,
        in_specs=in_specs,
        out_specs=out_specs,
        scratch_shapes=scratch
        + [
            pltpu.SemaphoreType.DMA((SLOTS,)),
            pltpu.SemaphoreType.DMA((SLOTS,)),
            pltpu.SemaphoreType.DMA((SLOTS // 2,)),
        ],
        compiler_params=pltpu.CompilerParams(
            collective_id=collective_id, has_side_effects=True, vmem_limit_bytes=56 << 20
        ),
        name=name,
    )(*args)


def sds(shape, dtype):
    return jax.ShapeDtypeStruct(shape, dtype)


def sum_scratch(psize, rows):
    far = max(psize - 1, 1)
    return [
        pltpu.VMEM((psize, rows, D), BF16),
        pltpu.VMEM((far, rows, D), BF16),
        pltpu.VMEM((far, rows, D), BF16),
    ]


def enter(psize, layer_input, gains, codes, qkv_weight, forget_weight, out_weight):
    rows = layer_input.shape[0] // 2
    half, width = qkv_weight.shape
    columns = width + forget_weight.shape[1]
    return exchange_call(
        functools.partial(enter_kernel, psize),
        "enter",
        1,
        (
            sds((rows, D), BF16),
            sds((2 * psize, rows, D), BF16),
            sds((2, half, columns), BF16),
            sds((out_weight.shape[0], 2 * half), BF16),
            sds((8, D), F32),
            sds((4,) + codes.shape, jnp.int32),
            sds(gains.shape, F32),
        ),
        (VMEM, ANY, ANY, ANY, VMEM, VMEM, VMEM),
        [ANY, VMEM, VMEM, ANY, ANY, ANY],
        [pltpu.VMEM((rows, D), BF16)]
        + [pltpu.VMEM(value.shape, BF16) for value in (qkv_weight, forget_weight, out_weight)],
        (layer_input, gains, codes, qkv_weight, forget_weight, out_weight),
    )


def forward_exchange(psize, attended, w_out, xin, gains, gate_weight, gate_got, up_weight, up_got, down_weight):
    rows = xin.shape[0]
    return exchange_call(
        functools.partial(forward_exchange_kernel, psize),
        "forward_exchange",
        2,
        (
            sds((rows, D), F32),
            sds((2 * psize, rows, D), BF16),
            sds((2,) + gate_weight.shape, BF16),
            sds((2,) + up_weight.shape, BF16),
            sds((down_weight.shape[0], D), BF16),
        ),
        (VMEM, ANY, ANY, ANY, ANY),
        [VMEM, VMEM, VMEM, VMEM, ANY, ANY, ANY, ANY, ANY],
        sum_scratch(psize, rows)
        + [pltpu.VMEM((rows, D), BF16), pltpu.VMEM((2 * psize, rows, D), BF16)]
        + [
            pltpu.VMEM(value.shape, BF16)
            for value in (gate_weight, gate_got, up_weight, up_got, down_weight)
        ],
        (attended, w_out, xin, gains, gate_weight, gate_got, up_weight, up_got, down_weight),
    )


def backward_exchange(
    psize, grad_gate, grad_up, w_gate, w_up, resid, cot, gains, down_own, down_other, gate_part, up_part
):
    rows = resid.shape[0]

    def early(value):
        half_rows = value.shape[1] // 2
        shape = (half_rows, value.shape[2])
        return [
            pltpu.VMEM((2,) + shape, BF16),
            pltpu.VMEM((2,) + shape, BF16),
            pltpu.VMEM(shape, BF16),
        ]

    return exchange_call(
        functools.partial(backward_exchange_kernel, psize),
        "backward_exchange",
        3,
        (
            sds((rows, D), F32),
            sds((2 * psize, rows, D), BF16),
            sds((8, D), F32),
            sds(down_own.shape, BF16),
            sds((2, gate_part.shape[1] // 2, gate_part.shape[2]), BF16),
        ),
        (VMEM, ANY, VMEM, VMEM, ANY),
        [VMEM] * 8 + [ANY, ANY, ANY],
        sum_scratch(psize, rows)
        + [pltpu.VMEM((rows, D), BF16), pltpu.VMEM((2 * psize, rows, D), BF16)]
        + [pltpu.VMEM(down_own.shape, BF16)] * 2
        + early(gate_part)
        + early(up_part),
        (grad_gate, grad_up, w_gate, w_up, resid, cot, gains, down_own, down_other, gate_part, up_part),
    )


def leave(psize, osize, grad, weight, stream, base, gains, small, proj, out_own, out_other, pair, down):
    rows = stream.shape[0]
    bits = len(bits_of(osize))
    half = D // 2
    columns = proj.shape[2]
    split = proj.shape[1] // 2

    def scratch(*shape):
        return pltpu.VMEM(shape, BF16)

    def both(shape):
        return sds((2,) + shape, BF16)

    return exchange_call(
        functools.partial(leave_kernel, psize, osize, 3),
        "leave",
        4,
        (
            sds((2 * rows, half), BF16),
            sds((8, half), F32),
            sds((split, columns), BF16),
            both((split // 2, columns)),
            both(out_own.shape),
            both(pair.shape[1:]),
            both(pair.shape[1:]),
            both(down.shape),
        ),
        (ANY, VMEM, ANY, ANY, ANY, ANY, ANY, ANY),
        [VMEM] * 6 + [ANY] * 5,
        sum_scratch(psize, rows)
        + [
            scratch(2 * psize, rows, D),
            scratch(2, rows, half),
            scratch(split, columns),
            scratch(2, split // 2, columns),
            scratch(*out_own.shape),
            scratch(*pair.shape[1:]),
            scratch(*pair.shape[1:]),
            scratch(*down.shape),
            scratch(2 + bits, split, columns),
            scratch(2, split // 2, columns),
            scratch(split // 2, columns),
            scratch(bits, split // 2, columns),
            scratch(1 + bits, *out_own.shape),
            pltpu.VMEM((8, half), F32),
            pltpu.VMEM((3 + len(bits_of(psize)) + bits, 8, half), F32),
            pltpu.VMEM((8, D), F32),
        ],
        (grad, weight, stream, base, gains, small, proj, out_own, out_other, pair, down),
    )


def make_shards(osize, psize):
    count = 2 * psize
    obits = bits_of(osize)

    def shards(
        layer_input,
        attn_gain,
        qkv_weight,
        forget_weight,
        forget_bias,
        out_weight,
        ffn_gain,
        gate_weight,
        up_weight,
        down_weight,
        prompt_doc,
        branch_seg,
        branch_doc,
        out_cotangent,
    ):
        core, xpos = lax.axis_index("k"), lax.axis_index("x")
        hpos, ppos, opos = lax.axis_index("h"), lax.axis_index("p"), lax.axis_index("o")
        home = core == hpos
        same = core == xpos
        heads = forget_weight.shape[1]
        width = heads * 3 * DH
        lane_pad = LANES - heads
        feat = D // 2

        def far_blocks(block):
            return [xor_swap(block, "p", psize, bit) for bit in range(1, psize)]

        def all_blocks(block, far):
            blocks = []
            for near in [block] + far:
                blocks += [near, swap(near, "k")]
            return jnp.concatenate(blocks, axis=0)

        def near_sums(partial):
            size = partial.shape[0] // count
            parts = [partial[i * size : (i + 1) * size] for i in range(count)]
            moved = [swap(parts[i + 1], "k") for i in range(0, count, 2)]
            return [add_parts(parts[i], moved[i // 2]) for i in range(0, count, 2)]

        def far_sums(sums):
            return [xor_swap(sums[bit], "p", psize, bit) for bit in range(1, psize)]

        def total_of(near, far):
            total = near.astype(F32)
            for value in far:
                total = total + value.astype(F32)
            return total

        prompt_len, branch_len = prompt_doc.shape[1], branch_seg.shape[1]
        packed = jnp.concatenate([prompt_doc[0], branch_seg[0], branch_doc[0]])
        code_rows = -(-packed.shape[0] // (8 * LANES)) * 8
        packed = jnp.pad(packed, (0, code_rows * LANES - packed.shape[0])).reshape(code_rows, LANES)
        bias_row = jnp.pad(forget_bias, (0, feat - heads))
        own_gains = jnp.concatenate(
            [jnp.stack([attn_gain, ffn_gain, bias_row]), jnp.zeros((5, feat), F32)]
        )
        forget_wide = jnp.concatenate(
            [forget_weight, jnp.zeros((forget_weight.shape[0], lane_pad), BF16)], axis=1
        )
        first_part, second_part = qkv_weight, forget_wide
        if width % LANES:
            spare = jnp.zeros((qkv_weight.shape[0], LANES - width % LANES), BF16)
            first_part = jnp.concatenate([qkv_weight, forget_wide, spare], axis=1)
        xin, normed_a_all, w_proj, w_out, gains8, codes, far_gains = enter(
            psize, layer_input, own_gains, packed, first_part, second_part, out_weight
        )
        bias = jnp.where(home, own_gains[2, :LANES], far_gains[2, :LANES])
        packed = lax.dynamic_index_in_dim(
            codes, (core ^ xpos) * 2 + (xpos ^ hpos), 0, keepdims=False
        ).reshape(-1)
        prompt_ids = packed[:prompt_len]
        branch_ids = packed[prompt_len : prompt_len + branch_len]
        branch_docs = packed[prompt_len + branch_len : prompt_len + branch_len + branch_doc.shape[1]]
        kcol, qrow, flags = group_codes(prompt_ids, branch_ids, branch_docs)
        normed_a_all = normed_a_all.reshape(-1, D)
        w_proj = w_proj.reshape(D, -1)[:, : width + LANES]

        projected = matmul(normed_a_all, w_proj).reshape(count, -1, width + LANES)
        cot_near, cot_far = take_half(out_cotangent, core), take_half(out_cotangent, 1 - core)
        projected, kcol, qrow, flags, gate_half, up_half, cot_first, cot_near, cot_far = lax.optimization_barrier(
            (
                projected,
                kcol,
                qrow,
                flags,
                take_half(gate_weight, opos % 2),
                take_half(up_weight, opos % 2),
                jnp.where(same, cot_far, cot_near),
                cot_near,
                cot_far,
            )
        )
        gate_got, up_got = fetch_home_away(gate_half), fetch_home_away(up_half)
        cot_first = lax.ppermute(cot_first, ("k", "x"), SPREAD_A)
        cot_second = lax.ppermute(cot_far, ("k", "x"), SPREAD_B)
        attended, *saved = attention_forward(
            projected, bias[None], kcol, qrow, flags, heads, prompt_len
        )
        attended, gate_got, up_got, cot_first, cot_second, *saved = lax.optimization_barrier(
            (attended, gate_got, up_got, cot_first, cot_second, *saved)
        )
        attended = attended.reshape(-1, heads * DH)
        cot = jnp.concatenate(
            [jnp.where(same, cot_near, cot_first), jnp.where(same, cot_first, cot_second)], axis=1
        )
        resid, normed_b_all, w_gate, w_up, w_down = forward_exchange(
            psize, attended.reshape(count, -1, heads * DH), w_out, xin, gains8, gate_weight, gate_got, up_weight, up_got, down_weight
        )
        normed_b_all = normed_b_all.reshape(-1, D)
        w_gate, w_up = w_gate.reshape(D, -1), w_up.reshape(D, -1)
        cot_others = far_blocks(tie(cot, normed_b_all))
        gate_pre = matmul(normed_b_all, w_gate)
        up_pre = matmul(normed_b_all, w_up)
        gate_sig = jax.nn.sigmoid(gate_pre)
        gate_act = gate_pre * gate_sig
        hidden = (gate_act * up_pre).astype(BF16)
        out_part = matmul(hidden, w_down).astype(BF16)
        out_part, *cot_others = lax.optimization_barrier((out_part, *cot_others))
        cot_all = all_blocks(cot, cot_others)

        def finish(total, axis_bits):
            for bit in axis_bits:
                total = add_parts(total, home_swap(total, osize, bit))
            return total

        high = opos % 2 == 1
        down_part = contract_rows(hidden, cot_all).astype(BF16)
        down_keep, down_give = split_rows(down_part, high)
        down_moved = xor_swap(down_give, "o", osize, 1)
        out_sums = near_sums(out_part)
        out_far = far_sums(out_sums)
        grad_hidden = contract_cols(tie(cot_all, out_sums[0]), w_down)
        grad_gate = (grad_hidden * up_pre * gate_sig * (1.0 + gate_pre * (1.0 - gate_sig))).astype(BF16)
        grad_up = (grad_hidden * gate_act).astype(BF16)
        gate_part = contract_rows(normed_b_all, grad_gate).astype(BF16).reshape(2, feat, -1)
        up_part = contract_rows(normed_b_all, grad_up).astype(BF16).reshape(2, feat, -1)
        up_part, gate_part, down_moved, *out_far = lax.optimization_barrier(
            (up_part, gate_part, down_moved, *out_far)
        )
        layer_output = (resid + total_of(out_sums[0], out_far)).astype(BF16)
        down_total = add_parts(down_keep, down_moved)
        grad_resid, grad_branch_all, ffn_gain_part, down_total, pair_total = backward_exchange(
            psize,
            grad_gate.reshape(count, -1, grad_gate.shape[1]),
            grad_up.reshape(count, -1, grad_up.shape[1]),
            w_gate,
            w_up,
            resid,
            cot,
            gains8,
            down_total[:, :feat],
            down_total[:, feat:],
            gate_part,
            up_part,
        )
        grad_branch_all = grad_branch_all.reshape(-1, D)
        grad_attended = contract_cols(grad_branch_all, w_out).astype(BF16)
        out_part = contract_rows(attended, grad_branch_all).astype(BF16)
        out_keep, out_give = split_rows(out_part, high)
        grad_attended, out_keep, out_give, down_total, pair_total, *block_parts = lax.optimization_barrier(
            (grad_attended, out_keep, out_give, down_total, pair_total) + unspread_parts(layer_output, same)
        )
        own_part, near_part, far_part = block_parts
        pair_moved = to_home(pair_total)
        out_moved = xor_swap(out_give, "o", osize, 1)
        near_moved, far_moved = unspread_moves(near_part, far_part)
        grad_proj, bias_sums = attention_backward(
            grad_attended.reshape(count, -1, heads * DH), saved, kcol, qrow, flags, heads, prompt_len
        )
        grad_proj, bias_sums, out_moved, near_moved, far_moved, pair_moved = lax.optimization_barrier(
            (grad_proj, bias_sums, out_moved, near_moved, far_moved, pair_moved)
        )
        layer_output = unspread_join(own_part, near_moved, far_moved, core, same)
        grad_proj = grad_proj.reshape(-1, width + LANES)
        proj_part = contract_rows(normed_a_all, grad_proj).astype(BF16)
        down_total = finish(down_total, obits[1:])
        pair_total = finish(add_parts(pair_total, pair_moved), obits[1:])
        out_total = add_parts(out_keep, out_moved)

        slots = jnp.where(
            (jnp.arange(2 * psize) == core * psize + ppos)[:, None], bias_sums[:1, :heads], 0.0
        ).reshape(-1)
        slots = jnp.concatenate([slots, jnp.zeros((feat - slots.shape[0],), F32)])
        small = jnp.stack([jnp.zeros((D,), F32), jnp.sum(ffn_gain_part, axis=0), jnp.concatenate([slots, slots])])
        small = jnp.concatenate([small, jnp.zeros((5, D), F32)])
        input_grad, small, first_rows, second_rows, out_both, up_both, gate_both, down_both = leave(
            psize,
            osize,
            grad_proj.reshape(count, -1, width + LANES),
            w_proj,
            xin,
            grad_resid,
            gains8,
            small,
            proj_part.reshape(2, feat, -1),
            out_total[:, :feat],
            out_total[:, feat:],
            pair_total,
            down_total,
        )
        proj_grad = jnp.concatenate([first_rows, second_rows.reshape(first_rows.shape)], axis=0)
        qkv_grad = proj_grad[:, :width].astype(F32)
        forget_grad = proj_grad[:, width : width + heads].astype(F32)
        bias_all = small[2, : 2 * psize * heads].reshape(2 * psize, heads)
        forget_bias_grad = lax.dynamic_index_in_dim(bias_all, hpos * psize + ppos, 0, keepdims=False)

        def whole(halves):
            return halves.reshape(-1, halves.shape[2]).astype(F32)

        return (
            layer_output,
            input_grad,
            small[0],
            qkv_grad,
            forget_grad,
            forget_bias_grad,
            whole(out_both),
            small[1],
            whole(gate_both),
            whole(up_both),
            whole(down_both),
        )

    return shards


def solution(mesh):
    dp, row, col = mesh.shape["dp"], mesh.shape["row"], mesh.shape["col"]
    osize, psize = dp // 2, col // 2
    assert row == 2
    split = Mesh(mesh.devices.reshape(osize, 2, row, 2, psize), ("o", "k", "x", "h", "p"))
    tokens = P(("o", "k", "h", "p"), "x")
    rows_first = P("x", ("h", "p"))
    cols_first = P(("h", "p"), "x")
    groups = P(("o", "k", "x"), None)
    in_specs = (
        tokens,
        P("x"),
        rows_first,
        rows_first,
        P(("h", "p")),
        cols_first,
        P("x"),
        rows_first,
        rows_first,
        cols_first,
        groups,
        groups,
        groups,
        tokens,
    )
    out_specs = (
        tokens,
        tokens,
        P("x"),
        rows_first,
        rows_first,
        P(("h", "p")),
        cols_first,
        P("x"),
        rows_first,
        rows_first,
        cols_first,
    )
    return jax.shard_map(
        make_shards(osize, psize), mesh=split, in_specs=in_specs, out_specs=out_specs, check_vma=False
    )
```

```python
import functools

import jax
import jax.numpy as jnp
from jax import lax
from jax.experimental import pallas as pl
from jax.experimental.pallas import tpu as pltpu
from jax.sharding import Mesh, PartitionSpec as P

D = 1536
DH = 64
DOCS = 4
TILE = 256
EPS = 1e-06
MASKED = -1e30
LANES = 128
BF16 = jnp.bfloat16
F32 = jnp.float32


def swap(value, axis):
    return lax.ppermute(value, axis, [(0, 1), (1, 0)])


def xor_swap(value, axis, size, bit):
    return lax.ppermute(value, axis, [(i, i ^ bit) for i in range(size)])


def kxh(k, x, h):
    return (k * 2 + x) * 2 + h


def fetch_home_away(value):
    pairs = []
    for k in range(2):
        for x in range(2):
            for h in range(2):
                target = (k, 1 - x, h) if k == h else (1 - k, x, 1 - h)
                pairs.append((kxh(k, x, h), kxh(*target)))
    return lax.ppermute(value, ("k", "x", "h"), pairs)


def fetch_away(value):
    pairs = [
        (kxh(k, x, 1 - k), kxh(k, 1 - x, 1 - k)) for k in range(2) for x in range(2)
    ]
    return lax.ppermute(value, ("k", "x", "h"), pairs)


def tie(value, *others):
    return lax.optimization_barrier((value,) + others)[0]


def join_weight(shard, first, second, home, axis):
    mine = jnp.where(home, shard, first)
    other = jnp.where(home, first, second)
    return jnp.concatenate([mine, other], axis=axis)


def add_parts(kept, moved):
    return (kept.astype(F32) + moved.astype(F32)).astype(BF16)


def to_home(value):
    return lax.ppermute(value, ("k", "h"), [(1, 0), (2, 3)])


def from_home(value):
    return lax.ppermute(value, ("k", "h"), [(0, 2), (3, 1)])


def home_swap(value, size, bit):
    pairs = []
    for o in range(size):
        for k in range(2):
            pairs.append(((o * 2 + k) * 2 + k, ((o ^ bit) * 2 + k) * 2 + k))
    return lax.ppermute(value, ("o", "k", "h"), pairs)


def bits_of(size):
    return [1 << i for i in range(size.bit_length() - 1)]


def split_rows(value, high):
    half = value.shape[0] // 2
    low_rows, high_rows = value[:half], value[half:]
    return jnp.where(high, high_rows, low_rows), jnp.where(high, low_rows, high_rows)


def merge_rows(kept, moved, high):
    return jnp.concatenate([jnp.where(high, moved, kept), jnp.where(high, kept, moved)], axis=0)


def take_half(value, index):
    half = value.shape[0] // 2
    return lax.dynamic_slice_in_dim(value, index * half, half, 0)


def kx(k, x):
    return k * 2 + x


SPREAD_A = []
SPREAD_B = []
for _k in range(2):
    for _x in range(2):
        if _k == _x:
            SPREAD_A.append((kx(_k, _x), kx(1 - _k, _x)))
        else:
            SPREAD_A.append((kx(_k, _x), kx(_k, 1 - _x)))
            SPREAD_B.append((kx(_k, _x), kx(1 - _k, 1 - _x)))


def spread_tokens(block, core, same):
    near = take_half(block, core)
    far = take_half(block, 1 - core)
    first = lax.ppermute(jnp.where(same, far, near), ("k", "x"), SPREAD_A)
    second = lax.ppermute(far, ("k", "x"), SPREAD_B)
    own = jnp.where(same, near, first)
    other = jnp.where(same, first, second)
    return jnp.concatenate([own, other], axis=1)


def unspread_parts(rows, same):
    half = rows.shape[1] // 2
    own, other = rows[:, :half], rows[:, half:]
    return own, jnp.where(same, other, own), other


def unspread_moves(near, far):
    first = lax.ppermute(near, ("k", "x"), [(b, a) for a, b in SPREAD_A])
    second = lax.ppermute(far, ("k", "x"), [(b, a) for a, b in SPREAD_B])
    return first, second


def unspread_join(own, first, second, core, same):
    near = jnp.where(same, own, first)
    far = jnp.where(same, first, second)
    low = jnp.where(core == 0, near, far)
    high = jnp.where(core == 0, far, near)
    return jnp.concatenate([low, high], axis=0)


def contract_rows(left, right):
    return lax.dot_general(
        left, right, (((0,), (0,)), ((), ())), preferred_element_type=F32
    )


def contract_cols(left, right):
    return lax.dot_general(
        left, right, (((1,), (1,)), ((), ())), preferred_element_type=F32
    )


def matmul(left, right):
    return jnp.dot(left, right, preferred_element_type=F32)


def dot_nn(left, right):
    return lax.dot_general(left, right, (((1,), (0,)), ((), ())), preferred_element_type=F32)


def dot_nt(left, right):
    return lax.dot_general(left, right, (((1,), (1,)), ((), ())), preferred_element_type=F32)


def tile_mask(qrow, kcol, rows, cols, i, j):
    key_pos = j * TILE + lax.broadcasted_iota(jnp.int32, (TILE, TILE), 0)
    query_pos = i * TILE + lax.broadcasted_iota(jnp.int32, (TILE, TILE), 1)
    code = kcol[pl.ds(pl.multiple_of(j * TILE, TILE), TILE), 0:1]
    first = qrow[0:1, pl.ds(pl.multiple_of(i * TILE, TILE), TILE)]
    second = qrow[1:2, pl.ds(pl.multiple_of(i * TILE, TILE), TILE)]
    seen = (key_pos <= query_pos) & ((code == first) | (code == second))
    return jnp.where(seen, 0.0, MASKED)


def split_parts(value):
    high = value.astype(BF16)
    rest = value - high.astype(F32)
    mid = rest.astype(BF16)
    low = (rest - mid.astype(F32)).astype(BF16)
    return high, mid, low


def lane(shape):
    return lax.broadcasted_iota(jnp.int32, shape, 1)


def forward_kernel(
    heads, count, prompt_len, flags, proj_hbm, bias_ref, kcol, qrow, att_hbm, ot_hbm, lse_ref,
    qp_hbm, kp_hbm, vp_hbm, logit, qkv, qp, kp, vp, vt, rates, sums_ref, attended, ot, mask,
    in_sem, out_sem, keep_sem, *per_head,
):
    me = lax.axis_index("p") * 2 + lax.axis_index("k")
    total = qkv.shape[0]
    size = total // count
    tiles = total // TILE
    loads = []
    for b in range(count):
        rows = pl.ds(b * size, size)
        loads.append(pltpu.make_async_copy(proj_hbm.at[b ^ me], qkv.at[rows], in_sem.at[b]))
    for load in loads:
        load.start()
    for load in loads:
        load.wait()
    logit[...] = qkv[:, 3 * DH * heads :] + bias_ref[...]
    value = logit[...]
    rate = jnp.minimum(value, 0.0) - jnp.log1p(jnp.exp(-jnp.abs(value)))
    rate = jnp.where(lane(rate.shape) < heads, rate, 0.0)
    high, mid, low = split_parts(rate)
    packed = high.astype(F32) + pltpu.roll(mid.astype(F32), 8, 1) + pltpu.roll(low.astype(F32), 16, 1)
    rates[...] = packed.astype(BF16)
    place_row = lax.broadcasted_iota(jnp.int32, (LANES, LANES), 0)
    place_col = lax.broadcasted_iota(jnp.int32, (LANES, LANES), 1)

    prompt_tiles = prompt_len // TILE
    wide = (TILE, TILE)
    row_pos, col_pos = lax.broadcasted_iota(jnp.int32, wide, 0), lax.broadcasted_iota(jnp.int32, wide, 1)
    below = jnp.where(col_pos <= row_pos, 1.0, 0.0).astype(BF16)

    def prompt_sums(t, before):
        rows = pl.ds(pl.multiple_of(t * TILE, TILE), TILE)
        prefix = dot_nn(below, rates[rows, :]) + before
        sums_ref[rows, :] = prefix
        return prefix[TILE - 1 : TILE, :]

    lax.fori_loop(0, prompt_tiles, prompt_sums, jnp.zeros((1, LANES), F32))
    doc_index = lax.broadcasted_iota(jnp.int32, (8, prompt_len), 0)
    within = jnp.where(qrow[3:4, 0:prompt_len] <= doc_index, 1.0, 0.0).astype(BF16)
    doc_sums = dot_nn(within, rates[0:prompt_len, :])

    def branch_sums(t, carry):
        rows = pl.ds(pl.multiple_of(t * TILE, TILE), TILE)
        limit = kcol[rows, 2:3]
        start = jnp.zeros((TILE, LANES), F32)
        for doc in range(DOCS):
            start = jnp.where(limit == doc, doc_sums[doc : doc + 1, :], start)

        def add_own(u, acc):
            others = pl.ds(pl.multiple_of(u * TILE, TILE), TILE)
            own = (u * TILE + col_pos <= t * TILE + row_pos) & (kcol[rows, 1:2] == qrow[2:3, others])
            return acc + dot_nn(jnp.where(own, 1.0, 0.0).astype(BF16), rates[others, :])

        sums_ref[rows, :] = lax.fori_loop(prompt_tiles, t + 1, add_own, start)
        return carry

    lax.fori_loop(prompt_tiles, tiles, branch_sums, 0)

    def prepare(t, carry):
        rows = pl.ds(pl.multiple_of(t * TILE, TILE), TILE)
        sums = sums_ref[rows, :]
        decay = sums + pltpu.roll(sums, LANES - 8, 1) + pltpu.roll(sums, LANES - 16, 1)
        decay = jnp.where(lane(decay.shape) < heads, -decay, 0.0)
        high, mid, low = split_parts(decay)
        parts = (
            high.astype(F32) + pltpu.roll(mid.astype(F32), 8, 1) + pltpu.roll(low.astype(F32), 16, 1)
        ).astype(BF16)
        lanes = lane((TILE, LANES))
        for h in range(heads):
            base = 3 * DH * h
            query = qkv[rows, base : base + DH].astype(BF16).astype(F32) * DH ** (-0.5)
            key = qkv[rows, base + DH : base + 2 * DH]
            worth = qkv[rows, base + 2 * DH : base + 3 * DH].astype(BF16)
            ones = jnp.where((lanes >= DH) & (lanes < DH + 3), 1.0, 0.0)[:, :DH]
            ones = jnp.where(lane((TILE, DH)) < 3, 1.0, 0.0)
            qp[h, rows, :] = jnp.concatenate([query, ones], axis=1).astype(BF16)
            spread = jnp.where(
                (place_col >= DH) & (place_col < DH + 3) & (place_row == 8 * (place_col - DH) + h), 1.0, 0.0
            ).astype(BF16)
            extra = dot_nn(parts, spread)
            extra = jnp.where(lanes == DH + 3, 1.0, extra)
            key_wide = jnp.concatenate([key, extra[:, DH:]], axis=1)
            kp[h, rows, :] = key_wide.astype(BF16)
            vp[h, rows, :] = worth
            vt[h, :, rows] = worth.astype(F32).T.astype(BF16)
        return carry

    lax.fori_loop(0, tiles, prepare, 0)
    keeps = [
        pltpu.make_async_copy(qp, qp_hbm, keep_sem.at[0]),
        pltpu.make_async_copy(kp, kp_hbm, keep_sem.at[1]),
        pltpu.make_async_copy(vp, vp_hbm, keep_sem.at[2]),
    ]
    for keep in keeps:
        keep.start()

    acc, top_refs, total_refs, score_refs = (per_head[n * heads : (n + 1) * heads] for n in range(4))

    def query_tile(i, carry):
        cols = pl.ds(pl.multiple_of(i * TILE, TILE), TILE)
        for h in range(heads):
            top_refs[h][...] = jnp.full(top_refs[h].shape, MASKED, F32)
            total_refs[h][...] = jnp.zeros(total_refs[h].shape, F32)
            acc[h][...] = jnp.zeros(acc[h].shape, F32)

        def key_tile(j, inner):
            @pl.when(flags[i * tiles + j] > 0)
            def _():
                rows = pl.ds(pl.multiple_of(j * TILE, TILE), TILE)
                mask[...] = tile_mask(qrow, kcol, None, None, i, j)
                tops = []
                for h in range(heads):
                    scores = dot_nt(kp[h, rows, :], qp[h, cols, :]) + mask[...]
                    score_refs[h][...] = scores
                    tops.append(jnp.maximum(top_refs[h][0:1, :], jnp.max(scores, axis=0, keepdims=True)))
                for h, top in enumerate(tops):
                    expo = jnp.exp(score_refs[h][...] - top)
                    shrink = jnp.exp(top_refs[h][0:1, :] - top)
                    top_refs[h][0:1, :] = top
                    total_refs[h][0:1, :] = total_refs[h][0:1, :] * shrink + jnp.sum(expo, axis=0, keepdims=True)
                    acc[h][...] = acc[h][...] * shrink + dot_nn(vt[h, :, rows], expo.astype(BF16))

            return inner

        lax.fori_loop(0, i + 1, key_tile, 0)
        for h in range(heads):
            total = total_refs[h][0:1, :]
            ot[pl.ds(h * DH, DH), cols] = acc[h][...] / total
            lse_ref[h : h + 1, cols] = top_refs[h][0:1, :] + jnp.log(total)
        attended[cols, :] = ot[:, cols].T.astype(BF16)
        return carry

    lse_ref[...] = jnp.zeros(lse_ref.shape, F32)
    lax.fori_loop(0, tiles, query_tile, 0)
    stores = [pltpu.make_async_copy(ot, ot_hbm, keep_sem.at[3])]
    for b in range(count):
        stores.append(
            pltpu.make_async_copy(attended.at[pl.ds(b * size, size)], att_hbm.at[b ^ me], out_sem.at[b])
        )
    for store in stores:
        store.start()
    for copy in keeps + stores:
        copy.wait()


def attention_forward(projected, bias, kcol, qrow, flags, heads, prompt_len):
    count, size, width = projected.shape
    total = count * size
    any_spec = pl.BlockSpec(memory_space=pl.ANY)
    vmem = pl.BlockSpec(memory_space=pltpu.VMEM)
    shape = jax.ShapeDtypeStruct
    return pl.pallas_call(
        functools.partial(forward_kernel, heads, count, prompt_len),
        out_shape=(
            shape((count, size, heads * DH), BF16),
            shape((heads * DH, total), F32),
            shape((8, total), F32),
            shape((heads, total, LANES), BF16),
            shape((heads, total, LANES), BF16),
            shape((heads, total, DH), BF16),
            shape((total, LANES), F32),
        ),
        in_specs=[pl.BlockSpec(memory_space=pltpu.SMEM), any_spec, vmem, vmem, vmem],
        out_specs=(any_spec, any_spec, vmem, any_spec, any_spec, any_spec, vmem),
        scratch_shapes=[
            pltpu.VMEM((total, width), F32),
            pltpu.VMEM((heads, total, LANES), BF16),
            pltpu.VMEM((heads, total, LANES), BF16),
            pltpu.VMEM((heads, total, DH), BF16),
            pltpu.VMEM((heads, DH, total), BF16),
            pltpu.VMEM((total, LANES), BF16),
            pltpu.VMEM((total, LANES), F32),
            pltpu.VMEM((total, heads * DH), BF16),
            pltpu.VMEM((heads * DH, total), F32),
            pltpu.VMEM((TILE, TILE), F32),
            pltpu.SemaphoreType.DMA((count,)),
            pltpu.SemaphoreType.DMA((count,)),
            pltpu.SemaphoreType.DMA((4,)),
        ]
        + [pltpu.VMEM((DH, TILE), F32)] * heads
        + [pltpu.VMEM((8, TILE), F32)] * (2 * heads)
        + [pltpu.VMEM((TILE, TILE), F32)] * heads,
        compiler_params=pltpu.CompilerParams(vmem_limit_bytes=48 << 20),
        cost_estimate=pl.CostEstimate(flops=20_000_000_000, bytes_accessed=30_000_000, transcendentals=0),
        name="attention_forward",
    )(flags, projected, bias, kcol, qrow)


def backward_kernel(
    heads, count, prompt_len, flags, gatt_hbm, ot_ref, lse_ref, qp, kp, vp, logit, kcol, qrow,
    grad_hbm, bias_ref, gatt, gout, kt, delta, mask, decay, grad, in_sem, out_sem, *per_head,
):
    dqt, dk, dv, prob_refs, score_refs = (per_head[n * heads : (n + 1) * heads] for n in range(5))
    me = lax.axis_index("p") * 2 + lax.axis_index("k")
    total = gatt.shape[0]
    size = total // count
    tiles = total // TILE
    loads = []
    for b in range(count):
        rows = pl.ds(b * size, size)
        loads.append(pltpu.make_async_copy(gatt_hbm.at[b ^ me], gatt.at[rows], in_sem.at[b]))
    for load in loads:
        load.start()
    for load in loads:
        load.wait()
    for h in range(heads):
        dqt[h][...] = jnp.zeros(dqt[h].shape, F32)
    delta[...] = jnp.zeros(delta.shape, F32)

    def prepare(t, carry):
        rows = pl.ds(pl.multiple_of(t * TILE, TILE), TILE)
        turned = gatt[rows, :].astype(F32).T * ot_ref[:, rows]
        for h in range(heads):
            gout[h, rows, :] = gatt[rows, h * DH : (h + 1) * DH]
            kt[h, :, rows] = kp[h, rows, :].astype(F32).T[: DH + 8].astype(BF16)
            delta[h : h + 1, rows] = jnp.sum(turned[h * DH : (h + 1) * DH], axis=0, keepdims=True)
        return carry

    lax.fori_loop(0, tiles, prepare, 0)
    lanes = lane((TILE, LANES))

    def key_tile(j, carry):
        rows = pl.ds(pl.multiple_of(j * TILE, TILE), TILE)
        for h in range(heads):
            dk[h][...] = jnp.zeros(dk[h].shape, F32)
            dv[h][...] = jnp.zeros(dv[h].shape, F32)

        def query_tile(i, inner):
            @pl.when(flags[i * tiles + j] > 0)
            def _():
                cols = pl.ds(pl.multiple_of(i * TILE, TILE), TILE)
                mask[...] = tile_mask(qrow, kcol, None, None, i, j)
                for h in range(heads):
                    scores = dot_nt(kp[h, rows, :], qp[h, cols, :]) + mask[...]
                    prob_refs[h][...] = jnp.exp(scores - lse_ref[h : h + 1, cols])
                for h in range(heads):
                    probs = prob_refs[h][...]
                    grad_probs = dot_nt(vp[h, rows, :], gout[h, cols, :])
                    score_refs[h][...] = (probs * (grad_probs - delta[h : h + 1, cols])).astype(BF16)
                    dv[h][...] += dot_nn(probs.astype(BF16), gout[h, cols, :])
                for h in range(heads):
                    grad_scores = score_refs[h][...]
                    dk[h][...] += dot_nn(grad_scores, qp[h, cols, :])
                    dqt[h][:, cols] += dot_nn(kt[h, :, rows], grad_scores)

            return inner

        lax.fori_loop(j, tiles, query_tile, 0)
        keys = jnp.zeros((TILE, LANES), F32)
        for h in range(heads):
            grad_key = dk[h][...]
            keys += jnp.where(lanes == h, pltpu.roll(grad_key, LANES - DH + h, 1), 0.0)
            grad[rows, (3 * h + 1) * DH : (3 * h + 3) * DH] = jnp.concatenate(
                [grad_key[:, :DH], dv[h][...]], axis=1
            ).astype(BF16)
        decay[rows, :] = -keys
        return carry

    lax.fori_loop(0, tiles, key_tile, 0)

    def finish(t, carry):
        rows = pl.ds(pl.multiple_of(t * TILE, TILE), TILE)
        queries = jnp.zeros((TILE, LANES), F32)
        for h in range(heads):
            turned = jnp.concatenate([dqt[h][:, rows], jnp.zeros((LANES - DH - 8, TILE), F32)], axis=0).T
            queries += jnp.where(lanes == h, pltpu.roll(turned, LANES - DH - 3 + h, 1), 0.0)
            grad[rows, 3 * h * DH : (3 * h + 1) * DH] = (turned[:, :DH] * DH ** (-0.5)).astype(BF16)
        whole = decay[rows, :] + queries
        high, mid, low = split_parts(whole)
        decay[rows, :] = (
            high.astype(F32) + pltpu.roll(mid.astype(F32), 8, 1) + pltpu.roll(low.astype(F32), 16, 1)
        )
        return carry

    lax.fori_loop(0, tiles, finish, 0)

    prompt_tiles = prompt_len // TILE
    wide = (TILE, TILE)
    row_pos, col_pos = lax.broadcasted_iota(jnp.int32, wide, 0), lax.broadcasted_iota(jnp.int32, wide, 1)
    above = jnp.where(col_pos >= row_pos, 1.0, 0.0).astype(BF16)
    branch_len = total - prompt_len
    doc_index = lax.broadcasted_iota(jnp.int32, (8, branch_len), 0)
    chosen = jnp.where(qrow[4:5, prompt_len:total] == doc_index, 1.0, 0.0).astype(BF16)
    doc_sums = dot_nn(chosen, decay[prompt_len:total, :].astype(BF16))

    def prompt_sums(n, after):
        t = prompt_tiles - 1 - n
        rows = pl.ds(pl.multiple_of(t * TILE, TILE), TILE)
        suffix = dot_nn(above, decay[rows, :].astype(BF16)) + after
        doc = kcol[rows, 3:4]
        sums = suffix
        for d in range(DOCS):
            sums = sums + jnp.where(doc <= d, doc_sums[d : d + 1, :], 0.0)
        decay[rows, :] = sums
        return suffix[0:1, :]

    def branch_sums(t, carry):
        rows = pl.ds(pl.multiple_of(t * TILE, TILE), TILE)

        def add_own(u, acc):
            others = pl.ds(pl.multiple_of(u * TILE, TILE), TILE)
            own = (u * TILE + col_pos >= t * TILE + row_pos) & (kcol[rows, 1:2] == qrow[2:3, others])
            return acc + dot_nn(jnp.where(own, 1.0, 0.0).astype(BF16), decay[others, :].astype(BF16))

        decay[rows, :] = lax.fori_loop(t, tiles, add_own, jnp.zeros((TILE, LANES), F32))
        return carry

    lax.fori_loop(0, prompt_tiles, prompt_sums, jnp.zeros((1, LANES), F32))
    lax.fori_loop(prompt_tiles, tiles, branch_sums, 0)

    def rates(t, bias):
        rows = pl.ds(pl.multiple_of(t * TILE, TILE), TILE)
        sums = decay[rows, :]
        grad_rate = sums + pltpu.roll(sums, LANES - 8, 1) + pltpu.roll(sums, LANES - 16, 1)
        value = logit[rows, :]
        grad_forget = grad_rate / (1.0 + jnp.exp(value))
        grad_forget = jnp.where(lanes < heads, grad_forget, 0.0).astype(BF16)
        grad[rows, 3 * DH * heads :] = grad_forget
        return bias + jnp.sum(grad_forget.astype(F32), axis=0, keepdims=True)

    bias_ref[...] = jnp.broadcast_to(
        lax.fori_loop(0, tiles, rates, jnp.zeros((1, LANES), F32)), bias_ref.shape
    )
    stores = []
    for b in range(count):
        stores.append(
            pltpu.make_async_copy(grad.at[pl.ds(b * size, size)], grad_hbm.at[b ^ me], out_sem.at[b])
        )
    for store in stores:
        store.start()
    for store in stores:
        store.wait()


def attention_backward(grad_attended, saved, kcol, qrow, flags, heads, prompt_len):
    ot, lse, qp, kp, vp, logit = saved
    count, size, width = grad_attended.shape
    total = count * size
    any_spec = pl.BlockSpec(memory_space=pl.ANY)
    vmem = pl.BlockSpec(memory_space=pltpu.VMEM)
    shape = jax.ShapeDtypeStruct
    out_width = 3 * DH * heads + LANES
    return pl.pallas_call(
        functools.partial(backward_kernel, heads, count, prompt_len),
        out_shape=(shape((count, size, out_width), BF16), shape((8, LANES), F32)),
        in_specs=[pl.BlockSpec(memory_space=pltpu.SMEM), any_spec]
        + [vmem] * 8,
        out_specs=(any_spec, vmem),
        scratch_shapes=[
            pltpu.VMEM((total, width), BF16),
            pltpu.VMEM((heads, total, DH), BF16),
            pltpu.VMEM((heads, DH + 8, total), BF16),
            pltpu.VMEM((8, total), F32),
            pltpu.VMEM((TILE, TILE), F32),
            pltpu.VMEM((total, LANES), F32),
            pltpu.VMEM((total, out_width), BF16),
            pltpu.SemaphoreType.DMA((count,)),
            pltpu.SemaphoreType.DMA((count,)),
        ]
        + [pltpu.VMEM((DH + 8, total), F32)] * heads
        + [pltpu.VMEM((TILE, LANES), F32)] * heads
        + [pltpu.VMEM((TILE, DH), F32)] * heads
        + [pltpu.VMEM((TILE, TILE), F32)] * heads
        + [pltpu.VMEM((TILE, TILE), BF16)] * heads,
        compiler_params=pltpu.CompilerParams(vmem_limit_bytes=56 << 20),
        cost_estimate=pl.CostEstimate(flops=50_000_000_000, bytes_accessed=30_000_000, transcendentals=0),
        name="attention_backward",
    )(flags, grad_attended, ot, lse, qp, kp, vp, logit, kcol, qrow)


def group_codes(prompt_ids, branch_ids, branch_docs):
    prompt_len = prompt_ids.shape[0]
    member = branch_ids[:, None] == jnp.arange(branch_docs.shape[0])[None, :]
    branch_doc_ids = jnp.sum(jnp.where(member, branch_docs[None, :], 0), axis=1)
    key_code = jnp.concatenate([prompt_ids, DOCS + branch_ids])
    first = jnp.concatenate([prompt_ids, branch_doc_ids])
    tag = jnp.concatenate([jnp.full_like(prompt_ids, -1), branch_ids])
    limit = jnp.concatenate([jnp.full_like(prompt_ids, -1), branch_doc_ids])
    prompt_code = jnp.concatenate([prompt_ids, jnp.full_like(branch_ids, DOCS)])
    total = key_code.shape[0]
    none = jnp.zeros_like(tag)
    kcol = jnp.stack([key_code, tag, limit, prompt_code] + [none] * 4, axis=1)
    qrow = jnp.stack([first, key_code, tag, prompt_code, limit] + [none] * 3, axis=0)
    tiles = total // TILE
    kinds = jnp.arange(2 * DOCS)
    key_bits = jnp.any(key_code.reshape(tiles, TILE, 1) == kinds, axis=1)
    query_bits = key_bits | jnp.any(first.reshape(tiles, TILE, 1) == kinds, axis=1)
    order = jnp.arange(tiles)
    meets = jnp.any(query_bits[:, None, :] & key_bits[None, :, :], axis=2)
    flags = (meets & (order[None, :] <= order[:, None])).astype(jnp.int32).reshape(-1)
    return kcol, qrow, flags


class Wires:
    def __init__(self, send_sem, recv_sem, local_sem):
        self.send_sem, self.recv_sem, self.local_sem = send_sem, recv_sem, local_sem
        self.used, self.local_used = 0, 0
        self.k, self.x = lax.axis_index("k"), lax.axis_index("x")
        self.h, self.p, self.o = lax.axis_index("h"), lax.axis_index("p"), lax.axis_index("o")
        self.home = self.k == self.h
        self.same = self.k == self.x
        self.pending = []

    def slot(self):
        self.used += 1
        return self.used - 1

    def copy(self, source, target, device, slot):
        return pltpu.make_async_remote_copy(
            src_ref=source,
            dst_ref=target,
            send_sem=self.send_sem.at[slot],
            recv_sem=self.recv_sem.at[slot],
            device_id=device,
            device_id_type=pl.DeviceIdType.MESH,
        )

    def send(self, source, target, device):
        copy = self.copy(source, target, device, self.slot())
        copy.start()
        self.pending.append(copy.wait_send)
        return copy

    def local(self, source, target):
        copy = pltpu.make_async_copy(source, target, self.local_sem.at[self.local_used])
        self.local_used += 1
        copy.start()
        return copy

    def greet(self, devices):
        barrier = pltpu.get_barrier_semaphore()
        for device in devices:
            pl.semaphore_signal(
                barrier, inc=1, device_id=device, device_id_type=pl.DeviceIdType.MESH
            )
        pl.semaphore_wait(barrier, len(devices))

    def close(self):
        for wait in self.pending:
            wait()


def row_spans(total, pieces):
    size = total // pieces
    return [pl.ds(i * size, size) for i in range(pieces)]


class Fetch:
    def __init__(self, wires, shard, target, stage, pieces, got=None, keep=None):
        w = self.wires = wires
        self.shard, self.target, self.stage, self.got, self.keep = shard, target, stage, got, keep
        self.count = pieces
        self.half_rows = shard.shape[0] // 2
        self.size = self.half_rows // pieces
        self.by_columns = len(target.shape) == 2
        self.first = [w.slot() for _ in range(pieces)]
        self.over = [w.slot() for _ in range(pieces)]
        self.second = [w.slot() for _ in range(2 * pieces)]
        self.local_slot = w.local_used
        w.local_used += 2

    def rows(self, i, mine=True):
        bit = self.wires.o % 2
        bit = bit if mine else 1 - bit
        return pl.ds(pl.multiple_of(bit * self.half_rows + i * self.size, 16), self.size)

    def place(self, half, span):
        if self.by_columns:
            width = self.shard.shape[1]
            return self.target.at[span, pl.ds(half * width, width)]
        return self.target.at[half, span]

    def first_copy(self, i, home):
        w, span = self.wires, self.rows(i)
        if home:
            return w.copy(self.shard.at[span], self.place(1, span), {"x": 1 - w.x}, self.first[i])
        device = {"k": 1 - w.k, "h": 1 - w.h}
        return w.copy(self.shard.at[span], self.place(0, span), device, self.first[i])

    def have(self, i, half):
        if self.got is None:
            return self.place(half, self.rows(i))
        return self.got.at[pl.ds(i * self.size, self.size)]

    def over_copy(self, i, home):
        w, half = self.wires, 1 if home else 0
        return w.copy(self.have(i, half), self.place(half, self.rows(i)), {"o": w.o ^ 1}, self.over[i])

    def second_copy(self, i, mine):
        w, span = self.wires, self.rows(i, mine)
        source = self.have(i, 0) if mine else self.place(0, span)
        slot = self.second[i if mine else self.count + i]
        return w.copy(source, self.place(1, span), {"x": 1 - w.x}, slot)

    def shard_load(self):
        return pltpu.make_async_copy(self.shard, self.stage, self.wires.local_sem.at[self.local_slot])

    def shard_store(self):
        whole = pl.ds(0, self.shard.shape[0])
        return pltpu.make_async_copy(
            self.stage, self.place(0, whole), self.wires.local_sem.at[self.local_slot]
        )

    def got_load(self):
        return pltpu.make_async_copy(self.got, self.keep, self.wires.local_sem.at[self.local_slot + 1])

    def got_store(self, half):
        bit = self.wires.o % 2
        span = pl.ds(pl.multiple_of(bit * self.half_rows, 16), self.half_rows)
        return pltpu.make_async_copy(
            self.keep, self.place(half, span), self.wires.local_sem.at[self.local_slot + 1]
        )

    def either(self, at_home, away):
        pl.when(self.wires.home)(at_home)
        pl.when(jnp.logical_not(self.wires.home))(away)

    def load(self):
        pl.when(self.wires.home)(lambda: self.shard_load().start())
        if self.got is not None:
            self.got_load().start()

    def start(self):
        if self.got is not None:
            for i in range(self.count):
                self.relay(i)
            return

        def go(home):
            for i in range(self.count):
                self.first_copy(i, home).start()

        self.either(lambda: go(True), lambda: go(False))

    def store(self):
        def at_home():
            self.shard_load().wait()
            self.shard_store().start()
            if self.got is not None:
                self.got_load().wait()
                self.got_store(1).start()

        def away():
            if self.got is not None:
                self.got_load().wait()
                self.got_store(0).start()

        self.either(at_home, away)

    def relay(self, i):
        def at_home():
            if self.got is None:
                self.first_copy(i, True).wait_recv()
            self.over_copy(i, True).start()

        def away():
            if self.got is None:
                self.first_copy(i, False).wait_recv()
            self.over_copy(i, False).start()
            self.second_copy(i, True).start()

        self.either(at_home, away)

    def relay_over(self, i):
        def away():
            self.over_copy(i, False).wait_recv()
            self.second_copy(i, False).start()

        pl.when(jnp.logical_not(self.wires.home))(away)

    def wait(self):
        def at_home():
            for i in range(self.count):
                if self.got is None:
                    self.first_copy(i, True).wait_send()
                self.over_copy(i, True).wait()
            self.shard_store().wait()
            if self.got is not None:
                self.got_store(1).wait()

        def away():
            for i in range(self.count):
                if self.got is None:
                    self.first_copy(i, False).wait_send()
                self.over_copy(i, False).wait_send()
                self.second_copy(i, True).wait()
                self.second_copy(i, False).wait()
            if self.got is not None:
                self.got_store(0).wait()

        self.either(at_home, away)


def partners(wires, psize, away=False, peers=True, over_o=0):
    devices = [{"k": 1 - wires.k}]
    if peers:
        devices += [{"p": wires.p ^ bit} for bit in range(1, psize)]
    devices += [{"x": 1 - wires.x}]
    devices += [{"k": 1 - wires.k, "x": 1 - wires.x}]
    if away:
        devices += [{"k": 1 - wires.k, "h": 1 - wires.h}, {"h": 1 - wires.h}]
    bit = 1
    while bit < over_o:
        devices += [{"o": wires.o ^ bit}]
        bit *= 2
    return devices


class Share:
    def __init__(self, wires, psize, own, g, spans):
        self.wires, self.psize, self.own, self.g, self.spans = wires, psize, own, g, spans
        self.near, self.far, self.kept, self.passed = [], {}, [], []

    def send(self, i):
        w, span = self.wires, self.spans[i]
        for bit in range(1, self.psize):
            self.far[bit, i] = w.send(self.own.at[span], self.g.at[2 * bit, span], {"p": w.p ^ bit})
        self.near.append(w.send(self.own.at[span], self.g.at[1, span], {"k": 1 - w.k}))
        self.kept.append(w.local(self.own.at[span], self.g.at[0, span]))

    def relay(self, i):
        w, span = self.wires, self.spans[i]
        for bit in range(1, self.psize):
            self.far[bit, i].wait_recv()
            self.passed.append(
                w.send(self.g.at[2 * bit, span], self.g.at[2 * bit + 1, span], {"k": 1 - w.k})
            )

    def wait(self):
        for copy in self.near + self.passed:
            copy.wait_recv()
        for copy in self.kept:
            copy.wait()


def by_chunks(span, body):
    def run(n, carry):
        body(pl.ds(pl.multiple_of(span.start + n * CHUNK, CHUNK), CHUNK))
        return carry

    lax.fori_loop(0, span.size // CHUNK, run, 0)


def add_into(value, *others):
    def body(rows):
        total = value[rows, :].astype(F32)
        for other in others:
            total = total + other[rows, :].astype(F32)
        value[rows, :] = total.astype(BF16)

    by_chunks(pl.ds(0, value.shape[0]), body)


class Reduce:
    def __init__(self, wires, psize, part, near, mid, far, spans):
        self.wires, self.psize, self.part = wires, psize, part
        self.near, self.mid, self.far, self.spans = near, mid, far, spans
        self.near_copies, self.far_copies = {}, {}

    def start_near(self, bit):
        w = self.wires
        for i, span in enumerate(self.spans):
            self.near_copies[bit, i] = w.send(
                self.part.at[2 * bit + 1, span], self.near.at[bit, span], {"k": 1 - w.k}
            )

    def start_far(self, bit):
        w = self.wires
        for i, span in enumerate(self.spans):
            self.near_copies[bit, i].wait_recv()

            def add(rows, bit=bit):
                self.mid[bit - 1, rows] = (
                    self.part[2 * bit, rows].astype(F32) + self.near[bit, rows].astype(F32)
                ).astype(BF16)

            by_chunks(span, add)
            self.far_copies[bit, i] = w.send(
                self.mid.at[bit - 1, span], self.far.at[bit - 1, span], {"p": w.p ^ bit}
            )

    def start(self):
        for bit in reversed(range(self.psize)):
            self.start_near(bit)
        for bit in reversed(range(1, self.psize)):
            self.start_far(bit)

    def start_with(self, make):
        for bit in reversed(range(self.psize)):
            make(2 * bit + 1)
            self.start_near(bit)
            make(2 * bit)
            if bit:
                self.start_far(bit)

    def each(self, i, body):
        span = self.spans[i]
        self.near_copies[0, i].wait_recv()
        for bit in range(1, self.psize):
            self.far_copies[bit, i].wait_recv()

        def run(rows):
            total = self.part[0, rows].astype(F32) + self.near[0, rows].astype(F32)
            for bit in range(1, self.psize):
                total = total + self.far[bit - 1, rows].astype(F32)
            body(rows, total)

        by_chunks(span, run)


CHUNK = 32
PIECES = 3


def inverse_rms(value):
    return lax.rsqrt(jnp.sum(value * value, axis=1, keepdims=True) / D + EPS)


def norm_back(grad, value, base, gain):
    rms = inverse_rms(value)
    gained = gain * grad
    inner = jnp.sum(value * gained, axis=1, keepdims=True)
    result = base + rms * gained - value * (rms * rms * rms) * inner / D
    parts = grad * value * rms
    return result, sum(parts[n : n + 8] for n in range(0, parts.shape[0], 8))


def enter_kernel(
    psize, x_ref, gain_own, codes_own, qkv_shard, forget_shard, out_shard, xin, g, proj, out, gain_ref, codes, far_gains,
    own, qkv_stage, forget_stage, out_stage, send_sem, recv_sem, local_sem,
):
    w = Wires(send_sem, recv_sem, local_sem)
    width = qkv_shard.shape[1]
    qkv = Fetch(w, qkv_shard, proj.at[:, :, pl.ds(0, width)], qkv_stage, 3)
    forget = Fetch(
        w, forget_shard, proj.at[:, :, pl.ds(width, forget_shard.shape[1])], forget_stage, 1
    )
    out_fetch = Fetch(w, out_shard, out, out_stage, 1)
    for fetch in (qkv, forget, out_fetch):
        fetch.load()
    w.greet(partners(w, psize, away=True, over_o=2))
    rows, half = own.shape[0], x_ref.shape[1]
    spans = row_spans(rows, PIECES)
    size = rows // PIECES
    def spread(source, target, pieces):
        count = len(pieces)
        to_near = [w.slot() for _ in pieces]
        to_far = [w.slot() for _ in pieces]
        kept = [w.local_used + i for i in range(count)]
        w.local_used += count

        def piece(base, i):
            start, length = pieces[i]
            return source.at[pl.ds(pl.multiple_of(base * rows + start, 8), length)]

        def span(i):
            return pl.ds(pieces[i][0], pieces[i][1])

        left, right = pl.ds(0, half), pl.ds(half, half)

        def same_keep(i):
            return pltpu.make_async_copy(piece(w.k, i), target.at[span(i), left], local_sem.at[kept[i]])

        def same_send(i):
            return w.copy(piece(1 - w.k, i), target.at[span(i), left], {"k": 1 - w.k}, to_near[i])

        def cross_near(i):
            return w.copy(piece(w.k, i), target.at[span(i), right], {"x": 1 - w.x}, to_near[i])

        def cross_far(i):
            return w.copy(
                piece(1 - w.k, i), target.at[span(i), right], {"k": 1 - w.k, "x": 1 - w.x}, to_far[i]
            )

        def start():
            @pl.when(w.same)
            def _():
                for i in range(count):
                    same_send(i).start()
                    same_keep(i).start()

            @pl.when(jnp.logical_not(w.same))
            def _():
                for i in range(count):
                    cross_near(i).start()
                    cross_far(i).start()

        def arrive(i):
            @pl.when(w.same)
            def _():
                same_keep(i).wait()
                same_send(i).wait_recv()

            @pl.when(jnp.logical_not(w.same))
            def _():
                cross_near(i).wait_recv()
                cross_far(i).wait_recv()

        def close():
            @pl.when(w.same)
            def _():
                for i in range(count):
                    same_send(i).wait_send()

            @pl.when(jnp.logical_not(w.same))
            def _():
                for i in range(count):
                    cross_near(i).wait_send()
                    cross_far(i).wait_send()

        return start, arrive, close

    gain_copy = w.send(gain_own, gain_ref.at[:, pl.ds(half, half)], {"x": 1 - w.x})
    code_copies = [
        w.send(gain_own, far_gains, {"k": 1 - w.k, "h": 1 - w.h}),
        w.send(codes_own, codes.at[1], {"x": 1 - w.x}),
        w.send(codes_own, codes.at[2], {"k": 1 - w.k}),
        w.send(codes_own, codes.at[3], {"k": 1 - w.k, "x": 1 - w.x}),
    ]
    codes[0] = codes_own[...]
    start, arrive, close = spread(x_ref, xin, [(i * size, size) for i in range(PIECES)])
    start()
    qkv.start()
    forget.start()
    share = Share(w, psize, own, g, spans)
    gain_ref[:, pl.ds(0, half)] = gain_own[...]
    gain_copy.wait_recv()
    for i, span in enumerate(spans):
        arrive(i)

        def norm(rows):
            value = xin[rows, :].astype(F32)
            own[rows, :] = (value * inverse_rms(value) * gain_ref[0:1, :]).astype(BF16)

        by_chunks(span, norm)
        share.send(i)
    close()
    for fetch in (qkv, forget, out_fetch):
        fetch.store()
    for i in range(3):
        qkv.relay(i)
    out_fetch.start()
    forget.relay(0)
    for i in range(3):
        qkv.relay_over(i)
        if i < PIECES:
            share.relay(i)
    for i in range(3, PIECES):
        share.relay(i)
    forget.relay_over(0)
    out_fetch.relay(0)
    out_fetch.relay_over(0)
    share.wait()
    for fetch in (qkv, forget, out_fetch):
        fetch.wait()
    for copy in code_copies:
        copy.wait_recv()
    w.close()


def forward_exchange_kernel(
    psize, attended, w_out, xin, gain_ref, gate_shard, gate_got, up_shard, up_got, down_shard, resid, g, gate, up, down,
    near, mid, far, own, part, gate_stage, gate_keep, up_stage, up_keep, down_stage, send_sem, recv_sem, local_sem,
):
    w = Wires(send_sem, recv_sem, local_sem)
    gate_fetch = Fetch(w, gate_shard, gate, gate_stage, 2, gate_got, gate_keep)
    up_fetch = Fetch(w, up_shard, up, up_stage, 2, up_got, up_keep)
    down_fetch = Fetch(w, down_shard, down, down_stage, 2)
    fetches = (gate_fetch, up_fetch, down_fetch)
    for fetch in fetches:
        fetch.load()
    w.greet(partners(w, psize, away=True, over_o=2))
    spans = row_spans(own.shape[0], PIECES)
    reduce = Reduce(w, psize, part, near, mid, far, spans)
    gate_fetch.start()

    def multiply(block):
        def one(n, carry):
            span = pl.ds(pl.multiple_of(n * TILE, TILE), TILE)
            part[block, :, span] = dot_nn(attended[block], w_out[:, span]).astype(BF16)
            return carry

        lax.fori_loop(0, D // TILE, one, 0)

    reduce.start_with(multiply)
    up_fetch.start()
    down_fetch.start()
    for fetch in fetches:
        fetch.store()
    for i in range(2):
        gate_fetch.relay_over(i)
    for i in range(2):
        down_fetch.relay(i)
    for i in range(2):
        up_fetch.relay_over(i)
    share = Share(w, psize, own, g, spans)
    for i in range(PIECES):

        def norm(rows, total):
            value = total + xin[rows, :].astype(F32)
            resid[rows, :] = value
            own[rows, :] = (value * inverse_rms(value) * gain_ref[1:2, :]).astype(BF16)

        reduce.each(i, norm)
        share.send(i)
    for i in range(2):
        down_fetch.relay_over(i)
    for i in range(PIECES):
        share.relay(i)
    share.wait()
    for fetch in fetches:
        fetch.wait()
    w.close()


class EarlySum:
    def __init__(self, wires, part, value, over, across, result, pieces, offset=0, got=None):
        w = self.wires = wires
        self.offset, self.got = offset, got
        self.part, self.value, self.over, self.across, self.result = part, value, over, across, result
        self.count, self.half_rows = pieces, value.shape[1]
        self.size = self.half_rows // pieces
        self.over_slots = [[w.slot() for _ in range(pieces)] for _ in range(2)]
        self.across_slots = [w.slot() for _ in range(pieces)]
        self.local_slot = w.local_used
        w.local_used += 2 + pieces

    def span(self, i):
        return pl.ds(i * self.size, self.size)

    def load_copy(self, half):
        start = pl.multiple_of(self.offset + (self.wires.o % 2) * self.half_rows, 16)
        return pltpu.make_async_copy(
            self.part.at[half, pl.ds(start, self.half_rows)],
            self.value.at[half],
            self.wires.local_sem.at[self.local_slot + half],
        )

    def load(self):
        for half in range(2):
            self.load_copy(half).start()

    def over_copy(self, half, i):
        w = self.wires
        start = pl.multiple_of(self.offset + (1 - w.o % 2) * self.half_rows + i * self.size, 16)
        return w.copy(
            self.part.at[half, pl.ds(start, self.size)],
            self.over.at[half, self.span(i)],
            {"o": w.o ^ 1},
            self.over_slots[half][i],
        )

    def across_copy(self, i):
        w = self.wires
        return w.copy(
            self.value.at[1, self.span(i)], self.across.at[self.span(i)], {"x": 1 - w.x}, self.across_slots[i]
        )

    def keep_copy(self, i):
        return pltpu.make_async_copy(
            self.value.at[0, self.span(i)],
            self.result.at[self.span(i)],
            self.wires.local_sem.at[self.local_slot + 2 + i],
        )

    def start(self, half):
        for i in range(self.count):
            self.over_copy(half, i).start()

    def pass_on(self, i):
        if i == 0:
            self.load_copy(1).wait()
        span = self.span(i)
        if self.got is None:
            self.over_copy(1, i).wait_recv()
            add_into(self.value.at[1, span], self.over.at[1, span])
        else:
            add_into(self.value.at[1, span], self.got.at[span])
        self.across_copy(i).start()

    def finish(self, i):
        if i == 0:
            self.load_copy(0).wait()
        self.over_copy(0, i).wait_recv()
        self.across_copy(i).wait_recv()
        span = self.span(i)
        add_into(self.value.at[0, span], self.over.at[0, span], self.across.at[span])
        if self.result is not None:
            self.keep_copy(i).start()

    def close(self):
        for i in range(self.count):
            for half in range(2):
                if half == 0 or self.got is None:
                    self.over_copy(half, i).wait_send()
            self.across_copy(i).wait_send()
            if self.result is not None:
                self.keep_copy(i).wait()


def backward_exchange_kernel(
    psize, grad_gate, grad_up, w_gate, w_up, resid, cot, gain_ref, down_own, down_other, gate_part, up_part,
    grad_resid, g, gain_grad, down_sum, pair_sum,
    near, mid, far, own, part, down_across, down_moved, gate_val, gate_over, gate_across, up_val, up_over, up_across,
    send_sem, recv_sem, local_sem,
):
    w = Wires(send_sem, recv_sem, local_sem)
    gate = EarlySum(w, gate_part, gate_val, gate_over, gate_across, pair_sum.at[0], 2)
    up = EarlySum(w, up_part, up_val, up_over, up_across, pair_sum.at[1], 2)
    gate.load()
    up.load()
    w.greet(partners(w, psize, away=True, over_o=2))
    spans = row_spans(own.shape[0], PIECES)
    reduce = Reduce(w, psize, part, near, mid, far, spans)
    down_copy = w.send(down_other, down_across, {"x": 1 - w.x})
    gate.start(1)
    up.start(1)
    gate.start(0)
    up.start(0)

    def multiply(block):
        def one(n, carry):
            span = pl.ds(pl.multiple_of(n * TILE, TILE), TILE)
            sums = dot_nt(grad_gate[block], w_gate[span, :]) + dot_nt(grad_up[block], w_up[span, :])
            part[block, :, span] = sums.astype(BF16)
            return carry

        lax.fori_loop(0, D // TILE, one, 0)

    reduce.start_with(multiply)
    for i in range(2):
        gate.pass_on(i)
    down_home = w.copy(down_sum, down_moved, {"h": 1 - w.h}, w.slot())
    down_copy.wait_recv()

    def add_down(rows):
        down_sum[rows, :] = (
            down_own[rows, :].astype(F32) + down_across[rows, :].astype(F32)
        ).astype(BF16)

    by_chunks(pl.ds(0, down_sum.shape[0]), add_down)

    @pl.when(jnp.logical_not(w.home))
    def _():
        down_home.start()

    share = Share(w, psize, own, g, spans)
    gain_grad[...] = jnp.zeros(gain_grad.shape, F32)

    def back(rows, total):
        grad, gain_part = norm_back(total, resid[rows, :], cot[rows, :].astype(F32), gain_ref[1:2, :])
        grad_resid[rows, :] = grad
        own[rows, :] = grad.astype(BF16)
        gain_grad[...] += gain_part

    for i in range(PIECES):
        reduce.each(i, back)
        share.send(i)
    for i in range(2):
        up.pass_on(i)
    share.relay(0)
    for i in range(2):
        gate.finish(i)
    for i in range(1, PIECES):
        share.relay(i)
    for i in range(2):
        up.finish(i)
    share.wait()
    gate.close()
    up.close()

    @pl.when(jnp.logical_not(w.home))
    def _():
        down_home.wait_send()

    @pl.when(w.home)
    def _():
        down_home.wait_recv()
        add_into(down_sum, down_moved)

    w.close()


class Spread:
    def __init__(self, wires, value, result):
        w = self.wires = wires
        self.value, self.result = value, result
        self.over_slot, self.near_slot, self.pass_slot = w.slot(), w.slot(), w.slot()
        self.local_slot = w.local_used
        w.local_used += 1

    def rows(self, mine):
        bit = self.wires.o % 2
        return self.result.at[bit if mine else 1 - bit]

    def over_copy(self):
        w = self.wires
        return w.copy(self.value, self.rows(True), {"o": w.o ^ 1}, self.over_slot)

    def near_copy(self):
        return self.wires.copy(self.value, self.rows(True), {"k": 1 - self.wires.k}, self.near_slot)

    def pass_copy(self):
        return self.wires.copy(self.rows(False), self.rows(False), {"k": 1 - self.wires.k}, self.pass_slot)

    def keep_copy(self):
        return pltpu.make_async_copy(
            self.value, self.rows(True), self.wires.local_sem.at[self.local_slot]
        )

    def start(self):
        @pl.when(self.wires.home)
        def _():
            self.over_copy().start()
            self.near_copy().start()
            self.keep_copy().start()

    def relay(self):
        @pl.when(self.wires.home)
        def _():
            self.over_copy().wait_recv()
            self.pass_copy().start()

    def wait(self):
        @pl.when(self.wires.home)
        def _():
            self.over_copy().wait_send()
            self.near_copy().wait_send()
            self.pass_copy().wait_send()
            self.keep_copy().wait()

        @pl.when(jnp.logical_not(self.wires.home))
        def _():
            self.near_copy().wait_recv()
            self.pass_copy().wait_recv()


class SmallSum:
    def __init__(self, wires, psize, osize, value, other, buffers):
        w = self.wires = wires
        self.value, self.other, self.buffers = value, other, buffers
        self.devices = [{"x": 1 - w.x}, {"k": 1 - w.k}]
        self.devices += [{"p": w.p ^ bit} for bit in bits_of(psize)]
        self.devices += [{"h": 1 - w.h}]
        self.devices += [{"o": w.o ^ bit} for bit in bits_of(osize)]
        self.slots = [w.slot() for _ in self.devices]

    def copy(self, step):
        source = self.other if step == 0 else self.value
        return self.wires.copy(source, self.buffers.at[step], self.devices[step], self.slots[step])

    def start(self):
        self.copy(0).start()

    def step(self, step):
        self.copy(step).wait()
        self.value[...] = self.value[...] + self.buffers[step]
        if step + 1 < len(self.devices):
            self.copy(step + 1).start()


class Chain:
    def __init__(self, wires, osize, value, stages, buffers, result, pieces):
        self.wires, self.value, self.stages, self.result = wires, value, stages, result
        self.buffers = buffers
        self.spans = row_spans(value.shape[0], pieces)
        self.slots = [[wires.slot() for _ in self.spans] for _ in stages]
        self.kept = [wires.local_used + i for i in range(pieces)]
        wires.local_used += pieces
        self.other = None

    def copy(self, stage, i):
        w, span = self.wires, self.spans[i]
        kind, slot = self.stages[stage], self.slots[stage][i]
        if kind == "x":
            return w.copy(self.other.at[span], self.buffers[stage].at[span], {"x": 1 - w.x}, slot)
        if kind == "h":
            return w.copy(self.value.at[span], self.buffers[stage].at[span], {"h": 1 - w.h}, slot)
        if kind == "k":
            return w.copy(self.value.at[span], self.result.at[span], {"k": 1 - w.k}, slot)
        return w.copy(self.value.at[span], self.buffers[stage].at[span], {"o": w.o ^ kind}, slot)

    def keep(self, i):
        span = self.spans[i]
        return pltpu.make_async_copy(
            self.value.at[span], self.result.at[span], self.wires.local_sem.at[self.kept[i]]
        )

    def start(self, stage, i):
        w, kind = self.wires, self.stages[stage]
        if kind == "x":
            self.copy(stage, i).start()
        elif kind == "h":
            @pl.when(jnp.logical_not(w.home))
            def _():
                self.copy(stage, i).start()
        else:
            @pl.when(w.home)
            def _():
                self.copy(stage, i).start()
                if kind == "k":
                    self.keep(i).start()

    def add(self, stage, i):
        span = self.spans[i]
        add_into(self.value.at[span], self.buffers[stage].at[span])

    def end(self, stage, i):
        w, kind = self.wires, self.stages[stage]
        if kind == "x":
            self.copy(stage, i).wait_recv()
            self.add(stage, i)
        elif kind == "h":
            @pl.when(w.home)
            def _():
                self.copy(stage, i).wait_recv()
                self.add(stage, i)
        elif kind == "k":
            @pl.when(w.home)
            def _():
                self.copy(stage, i).wait_send()
                self.keep(i).wait()

            @pl.when(jnp.logical_not(w.home))
            def _():
                self.copy(stage, i).wait_recv()
        else:
            @pl.when(w.home)
            def _():
                self.copy(stage, i).wait()
                self.add(stage, i)

    def close(self):
        w = self.wires
        for stage, kind in enumerate(self.stages):
            for i in range(len(self.spans)):
                if kind == "x":
                    self.copy(stage, i).wait_send()
                elif kind == "h":
                    @pl.when(jnp.logical_not(w.home))
                    def _():
                        self.copy(stage, i).wait_send()

    def step(self, stage, i):
        self.end(stage, i)
        if stage + 1 < len(self.stages):
            self.start(stage + 1, i)

    def order(self, first=0):
        return [(stage, i) for stage in range(first, len(self.stages)) for i in range(len(self.spans))]

    def run(self, first=0):
        for stage, i in self.order(first):
            self.step(stage, i)


def leave_kernel(
    psize, osize, pieces, grad_in, weight_in, stream, base, gain_ref, small_in, proj_in, out_own, out_other,
    pair_in, down_in, block, small, first_sum, second_sum, out_sum, up_sum, gate_sum, down_sum,
    near, mid, far, part, kept, first_val, second_val, out_val, up_val, gate_val, down_val, first_bufs,
    second_over, second_across, second_bufs, out_bufs, small_other, small_bufs, gain_acc,
    send_sem, recv_sem, local_sem,
):
    w = Wires(send_sem, recv_sem, local_sem)
    split = first_val.shape[0]
    second = EarlySum(w, proj_in, second_val, second_over, second_across, None, 1, split)
    second.load()
    loads = [
        w.local(source, target)
        for source, target in (
            (pair_in.at[1], up_val), (pair_in.at[0], gate_val), (down_in, down_val), (out_own, out_val),
            (proj_in.at[0, pl.ds(0, split)], first_val),
        )
    ]
    w.greet(partners(w, psize, away=True, over_o=osize))
    rows, half = kept.shape[1], kept.shape[2]
    spans = row_spans(rows, PIECES)
    size = rows // PIECES
    bits = bits_of(osize)

    first = Chain(
        w, osize, first_val, ["x", "h"] + bits + ["k"], [first_bufs.at[i] for i in range(2 + len(bits))],
        first_sum, pieces,
    )
    first.other = proj_in.at[1, pl.ds(0, split)]
    late = Chain(
        w, osize, second_val.at[0], ["h"] + bits[1:], [second_bufs.at[i] for i in range(len(bits))], None, 1
    )
    out = Chain(w, osize, out_val, ["x", "h"] + bits[1:], [out_bufs.at[i] for i in range(1 + len(bits))], None, 1)
    out.other = out_other
    spreads = [Spread(w, up_val, up_sum), Spread(w, gate_val, gate_sum), Spread(w, down_val, down_sum)]
    last_spreads = [Spread(w, out_val, out_sum), Spread(w, second_val.at[0], second_sum)]
    reduce = Reduce(w, psize, part, near, mid, far, spans)
    second.start(1)
    for i in range(pieces):
        first.start(0, i)
    out.start(0, 0)
    second.start(0)
    for load in loads:
        load.wait()
    for spread in spreads:
        spread.start()
    columns = D // TILE

    def multiply(block):
        def one(n, carry):
            span = pl.ds(pl.multiple_of(n * TILE, TILE), TILE)
            part[block, :, span] = dot_nt(grad_in[block], weight_in[span, :]).astype(BF16)
            return carry

        lax.fori_loop(0, columns, one, 0)

    reduce.start_with(multiply)

    near_slots = [w.slot() for _ in spans]
    far_slots = [w.slot() for _ in spans]
    keep_slots = [w.local_used + i for i in range(PIECES)]
    w.local_used += PIECES

    def target(i):
        return block.at[pl.ds(pl.multiple_of(w.k * rows + i * size, 8), size)]

    def same_keep(i):
        return pltpu.make_async_copy(kept.at[0, spans[i]], target(i), local_sem.at[keep_slots[i]])

    def same_send(i):
        return w.copy(kept.at[1, spans[i]], target(i), {"x": 1 - w.x}, near_slots[i])

    def cross_near(i):
        return w.copy(kept.at[0, spans[i]], target(i), {"k": 1 - w.k}, near_slots[i])

    def cross_far(i):
        return w.copy(kept.at[1, spans[i]], target(i), {"k": 1 - w.k, "x": 1 - w.x}, far_slots[i])

    second.pass_on(0)
    first.step(0, 0)
    for i in range(1, pieces):
        first.step(0, i)
        first.step(1, i - 1)
    out.step(0, 0)
    second.finish(0)
    late.start(0, 0)
    first.step(1, pieces - 1)
    gain_acc[...] = jnp.zeros(gain_acc.shape, F32)

    def back(rows_, total):
        grad, gain_part = norm_back(total, stream[rows_, :].astype(F32), base[rows_, :], gain_ref[0:1, :])
        gain_acc[...] += gain_part
        kept[0, rows_, :] = grad[:, :half].astype(BF16)
        kept[1, rows_, :] = grad[:, half:].astype(BF16)

    for i in range(PIECES):
        reduce.each(i, back)

        @pl.when(w.same)
        def _():
            same_send(i).start()
            same_keep(i).start()

        @pl.when(jnp.logical_not(w.same))
        def _():
            cross_near(i).start()
            cross_far(i).start()

    gain_sum = jnp.sum(gain_acc[...], axis=0, keepdims=True)
    row = lax.broadcasted_iota(jnp.int32, (8, half), 0)
    small[...] = jnp.where(row == 0, gain_sum[:, :half], small_in[:, :half])
    small_other[...] = jnp.where(row == 0, gain_sum[:, half:], small_in[:, half:])
    total = SmallSum(w, psize, osize, small, small_other, small_bufs)
    total.start()
    out.run(1)
    last_spreads[0].start()
    steps = [lambda a=a: late.step(*a) for a in late.order(0)] + [last_spreads[1].start]
    steps += [spread.relay for spread in spreads] + [lambda a=a: first.step(*a) for a in first.order(2)]
    steps += [last_spreads[0].relay, last_spreads[1].relay]
    smalls = list(range(len(total.devices)))
    for n, step in enumerate(steps):
        step()
        if n % 2 == 0 and smalls:
            total.step(smalls.pop(0))
    for step in smalls:
        total.step(step)
    for spread in spreads + last_spreads:
        spread.wait()
    for i in range(PIECES):
        @pl.when(w.same)
        def _():
            same_keep(i).wait()
            same_send(i).wait_send()
            cross_near(i).wait_recv()

        @pl.when(jnp.logical_not(w.same))
        def _():
            cross_near(i).wait_send()
            cross_far(i).wait()
            same_send(i).wait_recv()

    for chain in (first, second, late, out):
        chain.close()
    w.close()


ANY = pl.BlockSpec(memory_space=pl.ANY)
VMEM = pl.BlockSpec(memory_space=pltpu.VMEM)
SLOTS = 128


def exchange_call(kernel, name, collective_id, outs, out_specs, in_specs, scratch, args):
    return pl.pallas_call(
        kernel,
        out_shape=outs,
        in_specs=in_specs,
        out_specs=out_specs,
        scratch_shapes=scratch
        + [
            pltpu.SemaphoreType.DMA((SLOTS,)),
            pltpu.SemaphoreType.DMA((SLOTS,)),
            pltpu.SemaphoreType.DMA((SLOTS // 2,)),
        ],
        compiler_params=pltpu.CompilerParams(
            collective_id=collective_id, has_side_effects=True, vmem_limit_bytes=56 << 20
        ),
        name=name,
    )(*args)


def sds(shape, dtype):
    return jax.ShapeDtypeStruct(shape, dtype)


def sum_scratch(psize, rows):
    far = max(psize - 1, 1)
    return [
        pltpu.VMEM((psize, rows, D), BF16),
        pltpu.VMEM((far, rows, D), BF16),
        pltpu.VMEM((far, rows, D), BF16),
    ]


def enter(psize, layer_input, gains, codes, qkv_weight, forget_weight, out_weight):
    rows = layer_input.shape[0] // 2
    half, width = qkv_weight.shape
    columns = width + forget_weight.shape[1]
    return exchange_call(
        functools.partial(enter_kernel, psize),
        "enter",
        1,
        (
            sds((rows, D), BF16),
            sds((2 * psize, rows, D), BF16),
            sds((2, half, columns), BF16),
            sds((out_weight.shape[0], 2 * half), BF16),
            sds((8, D), F32),
            sds((4,) + codes.shape, jnp.int32),
            sds(gains.shape, F32),
        ),
        (VMEM, ANY, ANY, ANY, VMEM, VMEM, VMEM),
        [ANY, VMEM, VMEM, ANY, ANY, ANY],
        [pltpu.VMEM((rows, D), BF16)]
        + [pltpu.VMEM(value.shape, BF16) for value in (qkv_weight, forget_weight, out_weight)],
        (layer_input, gains, codes, qkv_weight, forget_weight, out_weight),
    )


def forward_exchange(psize, attended, w_out, xin, gains, gate_weight, gate_got, up_weight, up_got, down_weight):
    rows = xin.shape[0]
    return exchange_call(
        functools.partial(forward_exchange_kernel, psize),
        "forward_exchange",
        2,
        (
            sds((rows, D), F32),
            sds((2 * psize, rows, D), BF16),
            sds((2,) + gate_weight.shape, BF16),
            sds((2,) + up_weight.shape, BF16),
            sds((down_weight.shape[0], D), BF16),
        ),
        (VMEM, ANY, ANY, ANY, ANY),
        [VMEM, VMEM, VMEM, VMEM, ANY, ANY, ANY, ANY, ANY],
        sum_scratch(psize, rows)
        + [pltpu.VMEM((rows, D), BF16), pltpu.VMEM((2 * psize, rows, D), BF16)]
        + [
            pltpu.VMEM(value.shape, BF16)
            for value in (gate_weight, gate_got, up_weight, up_got, down_weight)
        ],
        (attended, w_out, xin, gains, gate_weight, gate_got, up_weight, up_got, down_weight),
    )


def backward_exchange(
    psize, grad_gate, grad_up, w_gate, w_up, resid, cot, gains, down_own, down_other, gate_part, up_part
):
    rows = resid.shape[0]

    def early(value):
        half_rows = value.shape[1] // 2
        shape = (half_rows, value.shape[2])
        return [
            pltpu.VMEM((2,) + shape, BF16),
            pltpu.VMEM((2,) + shape, BF16),
            pltpu.VMEM(shape, BF16),
        ]

    return exchange_call(
        functools.partial(backward_exchange_kernel, psize),
        "backward_exchange",
        3,
        (
            sds((rows, D), F32),
            sds((2 * psize, rows, D), BF16),
            sds((8, D), F32),
            sds(down_own.shape, BF16),
            sds((2, gate_part.shape[1] // 2, gate_part.shape[2]), BF16),
        ),
        (VMEM, ANY, VMEM, VMEM, ANY),
        [VMEM] * 8 + [ANY, ANY, ANY],
        sum_scratch(psize, rows)
        + [pltpu.VMEM((rows, D), BF16), pltpu.VMEM((2 * psize, rows, D), BF16)]
        + [pltpu.VMEM(down_own.shape, BF16)] * 2
        + early(gate_part)
        + early(up_part),
        (grad_gate, grad_up, w_gate, w_up, resid, cot, gains, down_own, down_other, gate_part, up_part),
    )


def leave(psize, osize, grad, weight, stream, base, gains, small, proj, out_own, out_other, pair, down):
    rows = stream.shape[0]
    bits = len(bits_of(osize))
    half = D // 2
    columns = proj.shape[2]
    split = proj.shape[1] * 3 // 4
    late = (proj.shape[1] - split) // 2

    def scratch(*shape):
        return pltpu.VMEM(shape, BF16)

    def both(shape):
        return sds((2,) + shape, BF16)

    return exchange_call(
        functools.partial(leave_kernel, psize, osize, 3),
        "leave",
        4,
        (
            sds((2 * rows, half), BF16),
            sds((8, half), F32),
            sds((split, columns), BF16),
            both((late, columns)),
            both(out_own.shape),
            both(pair.shape[1:]),
            both(pair.shape[1:]),
            both(down.shape),
        ),
        (ANY, VMEM, ANY, ANY, ANY, ANY, ANY, ANY),
        [VMEM] * 6 + [ANY] * 5,
        sum_scratch(psize, rows)
        + [
            scratch(2 * psize, rows, D),
            scratch(2, rows, half),
            scratch(split, columns),
            scratch(2, late, columns),
            scratch(*out_own.shape),
            scratch(*pair.shape[1:]),
            scratch(*pair.shape[1:]),
            scratch(*down.shape),
            scratch(2 + bits, split, columns),
            scratch(2, late, columns),
            scratch(late, columns),
            scratch(bits, late, columns),
            scratch(1 + bits, *out_own.shape),
            pltpu.VMEM((8, half), F32),
            pltpu.VMEM((3 + len(bits_of(psize)) + bits, 8, half), F32),
            pltpu.VMEM((8, D), F32),
        ],
        (grad, weight, stream, base, gains, small, proj, out_own, out_other, pair, down),
    )


def make_shards(osize, psize):
    count = 2 * psize
    obits = bits_of(osize)

    def shards(
        layer_input,
        attn_gain,
        qkv_weight,
        forget_weight,
        forget_bias,
        out_weight,
        ffn_gain,
        gate_weight,
        up_weight,
        down_weight,
        prompt_doc,
        branch_seg,
        branch_doc,
        out_cotangent,
    ):
        core, xpos = lax.axis_index("k"), lax.axis_index("x")
        hpos, ppos, opos = lax.axis_index("h"), lax.axis_index("p"), lax.axis_index("o")
        home = core == hpos
        same = core == xpos
        heads = forget_weight.shape[1]
        width = heads * 3 * DH
        lane_pad = LANES - heads
        feat = D // 2

        def far_blocks(block):
            return [xor_swap(block, "p", psize, bit) for bit in range(1, psize)]

        def all_blocks(block, far):
            blocks = []
            for near in [block] + far:
                blocks += [near, swap(near, "k")]
            return jnp.concatenate(blocks, axis=0)

        def near_sums(partial):
            size = partial.shape[0] // count
            parts = [partial[i * size : (i + 1) * size] for i in range(count)]
            moved = [swap(parts[i + 1], "k") for i in range(0, count, 2)]
            return [add_parts(parts[i], moved[i // 2]) for i in range(0, count, 2)]

        def far_sums(sums):
            return [xor_swap(sums[bit], "p", psize, bit) for bit in range(1, psize)]

        def total_of(near, far):
            total = near.astype(F32)
            for value in far:
                total = total + value.astype(F32)
            return total

        prompt_len, branch_len = prompt_doc.shape[1], branch_seg.shape[1]
        packed = jnp.concatenate([prompt_doc[0], branch_seg[0], branch_doc[0]])
        code_rows = -(-packed.shape[0] // (8 * LANES)) * 8
        packed = jnp.pad(packed, (0, code_rows * LANES - packed.shape[0])).reshape(code_rows, LANES)
        bias_row = jnp.pad(forget_bias, (0, feat - heads))
        own_gains = jnp.concatenate(
            [jnp.stack([attn_gain, ffn_gain, bias_row]), jnp.zeros((5, feat), F32)]
        )
        forget_wide = jnp.concatenate(
            [forget_weight, jnp.zeros((forget_weight.shape[0], lane_pad), BF16)], axis=1
        )
        first_part, second_part = qkv_weight, forget_wide
        if width % LANES:
            spare = jnp.zeros((qkv_weight.shape[0], LANES - width % LANES), BF16)
            first_part = jnp.concatenate([qkv_weight, forget_wide, spare], axis=1)
        xin, normed_a_all, w_proj, w_out, gains8, codes, far_gains = enter(
            psize, layer_input, own_gains, packed, first_part, second_part, out_weight
        )
        bias = jnp.where(home, own_gains[2, :LANES], far_gains[2, :LANES])
        packed = lax.dynamic_index_in_dim(
            codes, (core ^ xpos) * 2 + (xpos ^ hpos), 0, keepdims=False
        ).reshape(-1)
        prompt_ids = packed[:prompt_len]
        branch_ids = packed[prompt_len : prompt_len + branch_len]
        branch_docs = packed[prompt_len + branch_len : prompt_len + branch_len + branch_doc.shape[1]]
        kcol, qrow, flags = group_codes(prompt_ids, branch_ids, branch_docs)
        normed_a_all = normed_a_all.reshape(-1, D)
        w_proj = w_proj.reshape(D, -1)[:, : width + LANES]

        projected = matmul(normed_a_all, w_proj).reshape(count, -1, width + LANES)
        cot_near, cot_far = take_half(out_cotangent, core), take_half(out_cotangent, 1 - core)
        projected, kcol, qrow, flags, gate_half, up_half, cot_first, cot_near, cot_far = lax.optimization_barrier(
            (
                projected,
                kcol,
                qrow,
                flags,
                take_half(gate_weight, opos % 2),
                take_half(up_weight, opos % 2),
                jnp.where(same, cot_far, cot_near),
                cot_near,
                cot_far,
            )
        )
        gate_got, up_got = fetch_home_away(gate_half), fetch_home_away(up_half)
        cot_first = lax.ppermute(cot_first, ("k", "x"), SPREAD_A)
        cot_second = lax.ppermute(cot_far, ("k", "x"), SPREAD_B)
        attended, *saved = attention_forward(
            projected, bias[None], kcol, qrow, flags, heads, prompt_len
        )
        attended, gate_got, up_got, cot_first, cot_second, *saved = lax.optimization_barrier(
            (attended, gate_got, up_got, cot_first, cot_second, *saved)
        )
        attended = attended.reshape(-1, heads * DH)
        cot = jnp.concatenate(
            [jnp.where(same, cot_near, cot_first), jnp.where(same, cot_first, cot_second)], axis=1
        )
        resid, normed_b_all, w_gate, w_up, w_down = forward_exchange(
            psize, attended.reshape(count, -1, heads * DH), w_out, xin, gains8, gate_weight, gate_got, up_weight, up_got, down_weight
        )
        normed_b_all = normed_b_all.reshape(-1, D)
        w_gate, w_up = w_gate.reshape(D, -1), w_up.reshape(D, -1)
        cot_others = far_blocks(tie(cot, normed_b_all))
        gate_pre = matmul(normed_b_all, w_gate)
        up_pre = matmul(normed_b_all, w_up)
        gate_sig = jax.nn.sigmoid(gate_pre)
        gate_act = gate_pre * gate_sig
        hidden = (gate_act * up_pre).astype(BF16)
        out_part = matmul(hidden, w_down).astype(BF16)
        out_part, *cot_others = lax.optimization_barrier((out_part, *cot_others))
        cot_all = all_blocks(cot, cot_others)

        def finish(total, axis_bits):
            for bit in axis_bits:
                total = add_parts(total, home_swap(total, osize, bit))
            return total

        high = opos % 2 == 1
        down_part = contract_rows(hidden, cot_all).astype(BF16)
        down_keep, down_give = split_rows(down_part, high)
        down_moved = xor_swap(down_give, "o", osize, 1)
        out_sums = near_sums(out_part)
        out_far = far_sums(out_sums)
        grad_hidden = contract_cols(tie(cot_all, out_sums[0]), w_down)
        grad_gate = (grad_hidden * up_pre * gate_sig * (1.0 + gate_pre * (1.0 - gate_sig))).astype(BF16)
        grad_up = (grad_hidden * gate_act).astype(BF16)
        gate_part = contract_rows(normed_b_all, grad_gate).astype(BF16).reshape(2, feat, -1)
        up_part = contract_rows(normed_b_all, grad_up).astype(BF16).reshape(2, feat, -1)
        up_part, gate_part, down_moved, *out_far = lax.optimization_barrier(
            (up_part, gate_part, down_moved, *out_far)
        )
        layer_output = (resid + total_of(out_sums[0], out_far)).astype(BF16)
        down_total = add_parts(down_keep, down_moved)
        grad_resid, grad_branch_all, ffn_gain_part, down_total, pair_total = backward_exchange(
            psize,
            grad_gate.reshape(count, -1, grad_gate.shape[1]),
            grad_up.reshape(count, -1, grad_up.shape[1]),
            w_gate,
            w_up,
            resid,
            cot,
            gains8,
            down_total[:, :feat],
            down_total[:, feat:],
            gate_part,
            up_part,
        )
        grad_branch_all = grad_branch_all.reshape(-1, D)
        grad_attended = contract_cols(grad_branch_all, w_out).astype(BF16)
        out_part = contract_rows(attended, grad_branch_all).astype(BF16)
        out_keep, out_give = split_rows(out_part, high)
        grad_attended, out_keep, out_give, down_total, pair_total, *block_parts = lax.optimization_barrier(
            (grad_attended, out_keep, out_give, down_total, pair_total) + unspread_parts(layer_output, same)
        )
        own_part, near_part, far_part = block_parts
        pair_moved = to_home(pair_total)
        out_moved = xor_swap(out_give, "o", osize, 1)
        near_moved, far_moved = unspread_moves(near_part, far_part)
        grad_proj, bias_sums = attention_backward(
            grad_attended.reshape(count, -1, heads * DH), saved, kcol, qrow, flags, heads, prompt_len
        )
        grad_proj, bias_sums, out_moved, near_moved, far_moved, pair_moved = lax.optimization_barrier(
            (grad_proj, bias_sums, out_moved, near_moved, far_moved, pair_moved)
        )
        layer_output = unspread_join(own_part, near_moved, far_moved, core, same)
        grad_proj = grad_proj.reshape(-1, width + LANES)
        proj_part = contract_rows(normed_a_all, grad_proj).astype(BF16)
        down_total = finish(down_total, obits[1:])
        pair_total = finish(add_parts(pair_total, pair_moved), obits[1:])
        out_total = add_parts(out_keep, out_moved)

        slots = jnp.where(
            (jnp.arange(2 * psize) == core * psize + ppos)[:, None], bias_sums[:1, :heads], 0.0
        ).reshape(-1)
        slots = jnp.concatenate([slots, jnp.zeros((feat - slots.shape[0],), F32)])
        small = jnp.stack([jnp.zeros((D,), F32), jnp.sum(ffn_gain_part, axis=0), jnp.concatenate([slots, slots])])
        small = jnp.concatenate([small, jnp.zeros((5, D), F32)])
        input_grad, small, first_rows, second_rows, out_both, up_both, gate_both, down_both = leave(
            psize,
            osize,
            grad_proj.reshape(count, -1, width + LANES),
            w_proj,
            xin,
            grad_resid,
            gains8,
            small,
            proj_part.reshape(2, feat, -1),
            out_total[:, :feat],
            out_total[:, feat:],
            pair_total,
            down_total,
        )
        proj_grad = jnp.concatenate([first_rows, second_rows.reshape(-1, first_rows.shape[1])], axis=0)
        qkv_grad = proj_grad[:, :width].astype(F32)
        forget_grad = proj_grad[:, width : width + heads].astype(F32)
        bias_all = small[2, : 2 * psize * heads].reshape(2 * psize, heads)
        forget_bias_grad = lax.dynamic_index_in_dim(bias_all, hpos * psize + ppos, 0, keepdims=False)

        def whole(halves):
            return halves.reshape(-1, halves.shape[2]).astype(F32)

        return (
            layer_output,
            input_grad,
            small[0],
            qkv_grad,
            forget_grad,
            forget_bias_grad,
            whole(out_both),
            small[1],
            whole(gate_both),
            whole(up_both),
            whole(down_both),
        )

    return shards


def solution(mesh):
    dp, row, col = mesh.shape["dp"], mesh.shape["row"], mesh.shape["col"]
    osize, psize = dp // 2, col // 2
    assert row == 2
    split = Mesh(mesh.devices.reshape(osize, 2, row, 2, psize), ("o", "k", "x", "h", "p"))
    tokens = P(("o", "k", "h", "p"), "x")
    rows_first = P("x", ("h", "p"))
    cols_first = P(("h", "p"), "x")
    groups = P(("o", "k", "x"), None)
    in_specs = (
        tokens,
        P("x"),
        rows_first,
        rows_first,
        P(("h", "p")),
        cols_first,
        P("x"),
        rows_first,
        rows_first,
        cols_first,
        groups,
        groups,
        groups,
        tokens,
    )
    out_specs = (
        tokens,
        tokens,
        P("x"),
        rows_first,
        rows_first,
        P(("h", "p")),
        cols_first,
        P("x"),
        rows_first,
        rows_first,
        cols_first,
    )
    return jax.shard_map(
        make_shards(osize, psize), mesh=split, in_specs=in_specs, out_specs=out_specs, check_vma=False
    )
```
